32 devices in a mesh: dp: 8 (over z, y), head: 4 (over x, core).
Axes of the slice: x: 2, y: 2, z: 4, core: 2. Of those that a mesh axis runs over, the one named last changes fastest.
Arguments:
- inputs: bfloat16 [16, 2048, 768], P('dp', 'head'), may hold values from -6 to 6
- lengths: int32 [16], P('dp'), may hold values from 1 to 2048, 24576 in all
- w_query: bfloat16 [768, 768], P('head'), may hold values from -0.21875 to 0.21875
- w_key: bfloat16 [768, 768], P('head'), may hold values from -0.21875 to 0.21875
- w_value: bfloat16 [768, 768], P('head'), may hold values from -0.21875 to 0.21875
- w_out: bfloat16 [768, 768], P('head'), may hold values from -1.75 to 1.75
- w_up: bfloat16 [768, 3072], P(None, 'head'), may hold values from -0.21875 to 0.21875
- w_down: bfloat16 [3072, 768], P('head'), may hold values from -0.109375 to 0.109375
- conv_taps: bfloat16 [3, 3, 768], P(None, None, 'head'), may hold values from -3.5 to 3.5
- gain_attn: bfloat16 [768], replicated, may hold values from 0.5 to 1.5
- gain_ff: bfloat16 [768], replicated, may hold values from 0.5 to 1.5
- cotangent: bfloat16 [16, 2048, 768], P('dp', 'head'), may hold values from -6 to 6
Outputs:
- output: float32 [16, 2048, 768], P('dp', 'head')
- grad_input: float32 [16, 2048, 768], P('dp', 'head')
- grad_query: float32 [768, 768], P('head')
- grad_key: float32 [768, 768], P('head')
- grad_value: float32 [768, 768], P('head')
- grad_out: float32 [768, 768], P('head')
- grad_up: float32 [768, 3072], P(None, 'head')
- grad_down: float32 [3072, 768], P('head')
- grad_taps: float32 [3, 3, 768], P(None, None, 'head')
- grad_gain_attn: float32 [768], P('head')
- grad_gain_ff: float32 [768], P('head')
The draws below stay inside these ranges and needn't reach their ends.
Inputs may be any that keep to these rules, and one draw needn't show every extreme that they name: `lengths`: one sequence in every draw has all 2048 positions real.
All inputs are finite; a program needn't handle non-finite values. No bound on the sum of `lengths` on one device may be relied on, other than what follows from the above.
Results may differ from the reference program's by a relative error of at most 0.015.
The reference program's roundings to bfloat16 on the way count: a program that leaves them out, or rounds other values in their place, can miss the bound.
Values may be sent and summed in bfloat16 or wider, within the bound.
No kernel may reach another device: no remote copies, remote signals or barrier semaphores. Data moves between devices by JAX's collectives and lax.ppermute only.
A program may use at most 256 MiB of HBM per device.

```python
import math
import jax
import jax.numpy as jnp
import numpy as np
from jax import lax

D = 768
HEADS = 12
HDIM = 64
FF = 3072
LEN = 2048
SEQS = 16


def levels(key, dims, shards, least, high):
    loudness, own = 1.0, jax.random.fold_in(key, 6)
    for dim, parts in shards:
        heights = jnp.exp(jax.random.uniform(jax.random.fold_in(own, dim), (parts,), jnp.float32, least / len(shards), high / len(shards)))
        loudness = loudness * jnp.repeat(heights, dims[dim] // parts).reshape([-1 if axis == dim else 1 for axis in range(len(dims))])
    return loudness


def profile(amount, total, most, skew):
    loads = [(1 << 20) // math.isqrt(grade ** skew) + 1 for grade in range(2, amount + 1)]
    rest, counts = total - most - (amount - 1), [1] * (amount - 1)
    while rest > 0:
        candidates = [i for i in range(amount - 1) if counts[i] < most]
        whole, budget = sum([loads[i] for i in candidates]), rest
        for i in candidates:
            more = min(most - counts[i], max(1, budget * loads[i] // whole), rest)
            counts[i] = counts[i] + more
            rest = rest - more
    return np.array([most] + counts)


def ragged(stream_key, number_of, total, limit, skew):
    if number_of == 2:
        one = jax.random.randint(stream_key, (), max(1, total - limit), min(limit, total - 1) + 1)
        return jnp.stack([one, total - one])
    tallies = jnp.asarray(profile(number_of, total, limit, skew), jnp.int32)
    twos = (number_of - 1) // 2
    source_of, receiver = tallies[1:1 + 2 * twos:2], tallies[2:2 + 2 * twos:2]
    room = jnp.minimum(source_of - 1, limit - receiver)
    passed = jax.random.randint(jax.random.fold_in(stream_key, 1), (twos,), 0, 1 << 20) % (room + 1)
    tallies = tallies.at[1:1 + 2 * twos:2].set(source_of - passed).at[2:2 + 2 * twos:2].set(receiver + passed)
    return tallies[jax.random.permutation(jax.random.fold_in(stream_key, 2), number_of)]


def scatter_about(key, extent, spread, reach, cuts=(), dtype=jnp.bfloat16):
    values = spread * jax.random.normal(key, extent, jnp.float32)
    if cuts:
        values = values * levels(key, extent, cuts, -0.22, 0.18)
    return jnp.clip(values, -reach, reach).astype(dtype)


def setup_inputs(seed: int = 0) -> dict:
    key_of = jax.random.split(jax.random.key(seed), 13)
    return {
        "inputs": scatter_about(key_of[0], (SEQS, LEN, D), 1.0, 6.0, ((0, 8), (1, 4))),
        "lengths": ragged(key_of[1], SEQS, 3 * LEN * SEQS // 4, LEN, 2).astype(jnp.int32),
        "w_query": scatter_about(key_of[2], (D, D), D ** -0.5, 0.21875, ((0, 4),)),
        "w_key": scatter_about(key_of[3], (D, D), D ** -0.5, 0.21875, ((0, 4),)),
        "w_value": scatter_about(key_of[4], (D, D), D ** -0.5, 0.21875, ((0, 4),)),
        "w_out": scatter_about(key_of[5], (D, D), (max(D // 64, 1)) ** -0.5, 1.75, ((0, 4),)),
        "w_up": scatter_about(key_of[6], (D, FF), D ** -0.5, 0.21875, ((1, 4),)),
        "w_down": scatter_about(key_of[7], (FF, D), FF ** -0.5, 0.109375, ((0, 4),)),
        "conv_taps": scatter_about(key_of[8], (3, 3, D), 3 ** -0.5, 3.5, ((2, 4),)),
        "gain_attn": jnp.clip(1.0 + 0.1 * jax.random.normal(key_of[9], (D,), jnp.float32), 0.5, 1.5).astype(jnp.bfloat16),
        "gain_ff": jnp.clip(1.0 + 0.1 * jax.random.normal(key_of[10], (D,), jnp.float32), 0.5, 1.5).astype(jnp.bfloat16),
        "cotangent": scatter_about(key_of[11], (SEQS, LEN, D), 1.0, 6.0, ((0, 8), (1, 4))),
    }


@jax.custom_vjp
def low(v):
    return lax.optimization_barrier(v.astype(jnp.bfloat16)).astype(jnp.float32)

@jax.custom_vjp
def low_back(v):
    return v

def low_keep(v):
    return (low(v), None)

def low_pass(kept, grad):
    return (grad,)

def back_keep(v):
    return (v, None)

def back_low(kept, grad):
    return (low(grad),)
low.defvjp(low_keep, low_pass)
low_back.defvjp(back_keep, back_low)
epsilon = 1e-06

def matmul(left_op, right_op):
    return jnp.dot(left_op, right_op, precision=lax.Precision.HIGHEST, preferred_element_type=jnp.float32)

def rms_norm(values, gain_vec):
    scaled = values * lax.rsqrt(lax.optimization_barrier(jnp.mean(values * values, axis=-1, keepdims=True)) + epsilon)
    return scaled * gain_vec

def causal_conv(values, conv_row):
    length = values.shape[0]
    padded = jnp.concatenate([jnp.zeros((2, values.shape[1]), jnp.float32), values], axis=0)
    return conv_row[0] * values + conv_row[1] * padded[1:length + 1] + conv_row[2] * padded[0:length]

def attend(queries, key_rows, value_rows, seq_limit):
    length = queries.shape[0]
    block_rows = min(512, length)
    score_scale = HDIM ** (-0.5)
    key_place = jnp.arange(length).astype(jnp.int32)

    def one_block(block_start):
        query_rows = lax.dynamic_slice_in_dim(queries, block_start, block_rows, 0)
        scores = jnp.einsum('qhd,khd->hqk', query_rows, key_rows, precision=lax.Precision.HIGHEST) * score_scale
        scores = low_back(scores)
        query_place = block_start + jnp.arange(block_rows).astype(jnp.int32)
        allowed = (key_place[None, :] <= query_place[:, None]) & (key_place[None, :] < seq_limit)
        masked = jnp.where(allowed[None], scores, -1000000000.0)
        row_top = lax.optimization_barrier(jnp.max(masked, axis=-1, keepdims=True))
        raised = jnp.where(allowed[None], jnp.exp(masked - row_top), 0.0)
        weights_low = low(raised / lax.optimization_barrier(jnp.sum(raised, axis=-1, keepdims=True)))
        return jnp.einsum('hqk,khd->qhd', weights_low, value_rows, precision=lax.Precision.HIGHEST)
    block_starts = (jnp.arange(length // block_rows) * block_rows).astype(jnp.int32)
    outputs = lax.map(jax.checkpoint(one_block), block_starts)
    return outputs.reshape(length, HEADS * HDIM)

def layer(stream, w_query, w_key, w_value, w_out, w_up, w_down, conv_taps, gain_attn, gain_ff, seq_limit):
    length = stream.shape[0]
    normed = low(rms_norm(stream, gain_attn))
    projected = [low(low_back(matmul(normed, weight))) for weight in (w_query, w_key, w_value)]
    mixed = [low(causal_conv(projected[which], conv_taps[which])) for which in range(3)]
    shaped = [item.reshape(length, HEADS, HDIM) for item in mixed]
    attended = attend(shaped[0], shaped[1], shaped[2], seq_limit)
    attended = low(low_back(attended))
    branch = low_back(matmul(attended, w_out))
    middle = stream + branch
    normed_ff = low(rms_norm(middle, gain_ff))
    hidden_pre = low_back(matmul(normed_ff, w_up))
    hidden = low(jnp.square(jax.nn.relu(hidden_pre)))
    ff_out = low_back(matmul(hidden, w_down))
    row_valid = (jnp.arange(length).astype(jnp.int32) < seq_limit)[:, None]
    return jnp.where(row_valid, middle + ff_out, 0.0)

def reference(inputs, lengths, w_query, w_key, w_value, w_out, w_up, w_down, conv_taps, gain_attn, gain_ff, cotangent):
    params = tuple((item.astype(jnp.float32) for item in (w_query, w_key, w_value, w_out, w_up, w_down, conv_taps, gain_attn, gain_ff)))

    def per_sequence(totals, pieces):
        sequence, seq_limit, upstream = pieces

        def forward(stream, *weights):
            return layer(stream, *weights, seq_limit)
        result, pullback = jax.vjp(forward, sequence.astype(jnp.float32), *params)
        grads = pullback(upstream.astype(jnp.float32))
        totals = tuple((first + second for first, second in zip(totals, grads[1:])))
        return (totals, (result, grads[0]))
    zeros_start = tuple((jnp.zeros_like(item) for item in params))
    totals, (outputs, grad_stream) = lax.scan(per_sequence, zeros_start, (inputs, lengths, cotangent))
    return (outputs, grad_stream, totals[0], totals[1], totals[2], totals[3], totals[4], totals[5], totals[6], totals[7], totals[8])
```

```python
import functools

import jax
import jax.numpy as jnp
from jax import lax
from jax.experimental import pallas as pl
from jax.experimental.pallas import tpu as pltpu
from jax.sharding import PartitionSpec as P

HDIM = 64
EPS = 1e-06
bf16 = jnp.bfloat16
f32 = jnp.float32

NN = (((1,), (0,)), ((), ()))
NT = (((1,), (1,)), ((), ()))
TN = (((0,), (0,)), ((), ()))

CORE = [(0, 1), (1, 0), (2, 3), (3, 2)]
XNB = [(0, 2), (2, 0), (1, 3), (3, 1)]


def dot(a, b, dims=NN):
    return lax.dot_general(a, b, dims, preferred_element_type=f32)


def cost(flops, nbytes, trans=0):
    return pl.CostEstimate(flops=int(flops), bytes_accessed=int(nbytes), transcendentals=int(trans))


def sds(shape, dtype):
    return jax.ShapeDtypeStruct(shape, dtype)


def whole(shape):
    zeros = (0,) * len(shape)
    return pl.BlockSpec(shape, lambda *_: zeros, pipeline_mode=pl.Buffered(1))


def grid_spec(grid, ins, outs, scratch=()):
    return pltpu.PrefetchScalarGridSpec(
        num_scalar_prefetch=1, grid=grid, in_specs=ins, out_specs=outs, scratch_shapes=scratch
    )


def norm(x, gain):
    inv = lax.rsqrt(jnp.mean(x * x, axis=-1, keepdims=True) + EPS)
    n = x * inv
    return n, inv, (n * gain).astype(bf16)


def qkv_body(
    meta, x0, x1, x2, x3, w0, w1, w2, w3, gain, taps, h_ref, raw_ref, mix_ref, w_ref, ext
):
    b = pl.program_id(0)
    rows = x0.shape[0]
    part = w0.shape[0]

    @pl.when(b == 0)
    def _():
        for k, piece in enumerate((w0, w1, w2, w3)):
            at = jnp.bitwise_xor(meta[3], k)
            w_ref[pl.ds(pl.multiple_of(at * part, 64), part), :] = piece[...]
        ext[0:8, :] = jnp.zeros((8, ext.shape[1]), f32)

    slot = meta[4 + b]
    x = x0[...]
    for k, other in ((1, x1), (2, x2), (3, x3)):
        x = jnp.where(slot == k, other[...], x)
    _, _, h = norm(x.astype(f32), gain[...].astype(f32))
    h_ref[...] = h
    raw = dot(h, w_ref[...]).astype(bf16)
    raw_ref[...] = raw
    rawf = raw.astype(f32)
    ext[8 : 8 + rows, :] = rawf
    t = taps[...].astype(f32)
    mixed = t[0:1] * rawf + t[1:2] * ext[7 : 7 + rows, :] + t[2:3] * ext[6 : 6 + rows, :]
    mix_ref[...] = mixed.astype(bf16)
    ext[0:8, :] = ext[rows : rows + 8, :]


def qkv_call(meta, xs, ws, gain, taps):
    rows, width = xs[0].shape
    part, cols = ws[0].shape
    length = 4 * rows
    blk = lambda n: pl.BlockSpec((rows, n), lambda b, m: (b, 0))
    return pl.pallas_call(
        qkv_body,
        out_shape=[
            sds((length, width), bf16),
            sds((length, cols), bf16),
            sds((length, cols), bf16),
            sds((width, cols), bf16),
        ],
        grid_spec=grid_spec(
            (4,),
            [whole((rows, width))] * 4
            + [whole((part, cols))] * 4
            + [whole((1, width)), whole((3, cols))],
            [blk(width), blk(cols), blk(cols), pl.BlockSpec((width, cols), lambda b, m: (0, 0))],
            [pltpu.VMEM((rows + 8, cols), f32)],
        ),
        cost_estimate=cost(2 * length * width * cols, 2 * length * (width * 2 + cols * 2)),
        name="qkv",
    )(meta, *xs, *ws, gain, taps)


def two_heads(v):
    lane = lax.broadcasted_iota(jnp.int32, v.shape, 1)
    z = jnp.zeros_like(v)
    return jnp.concatenate([jnp.where(lane < HDIM, v, z), jnp.where(lane < HDIM, z, v)], axis=0)


def limits(i, rows, length):
    lim = jnp.minimum(i * rows + lax.broadcasted_iota(jnp.int32, (1, rows), 1), length - 1)
    return jnp.concatenate([lim, lim], axis=1)


def att_fwd_body(meta, q_ref, k_ref, v_ref, mine_ref, theirs_ref, lse_ref, vt, acc):
    i = pl.program_id(1)
    B = q_ref.shape[0]

    @pl.when(i == 0)
    def _():
        vt[...] = v_ref[...].T

    length = meta[0]
    qq = two_heads(q_ref[...] * bf16(HDIM**-0.5))
    acc[...] = jnp.zeros_like(acc)
    lim = limits(i, B, length)

    def tile(j, carry, masked):
        m, l = carry
        sl = pl.ds(pl.multiple_of(j * B, B), B)
        s = dot(k_ref[sl, :], qq, NT)
        if masked:
            ok = j * B + lax.broadcasted_iota(jnp.int32, (B, 2 * B), 0) <= lim
            s = jnp.where(ok, s, -1e9)
        mn = jnp.maximum(m, jnp.max(s, axis=0, keepdims=True))
        p = jnp.exp(s - mn)
        if masked:
            p = jnp.where(ok, p, 0.0)
        a = jnp.exp(m - mn)
        l = a * l + jnp.sum(p, axis=0, keepdims=True)
        pb = p.astype(bf16)
        for h in range(2):
            r, c = slice(HDIM * h, HDIM * h + HDIM), slice(h * B, h * B + B)
            acc[r, :] = acc[r, :] * a[:, c] + dot(vt[r, sl], pb[:, c])
        return mn, l

    full = jnp.minimum(i, length // B)
    init = (jnp.full((1, 2 * B), -1e9, f32), jnp.zeros((1, 2 * B), f32))
    m, l = lax.fori_loop(0, full, lambda j, c: tile(j, c, False), init)
    last = jnp.minimum(full, pl.num_programs(1) - 1)
    m, l = tile(last, (m, l), True)
    inv = 1.0 / l
    for h in range(2):
        r, c = slice(HDIM * h, HDIM * h + HDIM), slice(h * B, h * B + B)
        acc[r, :] = acc[r, :] * inv[:, c]
    out = acc[...].T.astype(bf16)
    own = jnp.bitwise_and(i, 1) == meta[2]

    @pl.when(own)
    def _():
        mine_ref[...] = out

    @pl.when(jnp.logical_not(own))
    def _():
        theirs_ref[...] = out

    ls = m + jnp.log(l)
    lse_ref[0] = jnp.concatenate([ls[:, :B], ls[:, B:]], axis=0)


def half_map(p, i, m):
    return (jnp.bitwise_xor(i // 2, m[1]), p)


def att_fwd_call(meta, mix):
    length, cols = mix.shape
    width = cols // 3
    pairs = width // 128
    B = length // 4
    half = pl.BlockSpec((B, 128), half_map)
    return pl.pallas_call(
        att_fwd_body,
        out_shape=[
            sds((length // 2, width), bf16),
            sds((length // 2, width), bf16),
            sds((pairs, 2, length), f32),
        ],
        grid_spec=grid_spec(
            (pairs, 4),
            [
                pl.BlockSpec((B, 128), lambda p, i, m: (i, p)),
                pl.BlockSpec((length, 128), lambda p, i, m: (0, pairs + p)),
                pl.BlockSpec((length, 128), lambda p, i, m: (0, 2 * pairs + p)),
            ],
            [half, half, pl.BlockSpec((1, 2, B), lambda p, i, m: (p, 0, i))],
            [pltpu.VMEM((128, length), bf16), pltpu.VMEM((128, B), f32)],
        ),
        cost_estimate=cost(8 * length * length * width, 8 * length * width, 2 * length * length * pairs),
        name="attn_fwd",
    )(meta, mix, mix, mix)


def att_bwd_body(
    meta, q_ref, k_ref, v_ref, om, ot, dm, dt, lse_ref, rq, rk, rv, taps,
    gq, gk, gv, gt, kt, dkt, dvt, dqt, dqs, ext,
):
    i = pl.program_id(1)
    B = q_ref.shape[0]
    L = k_ref.shape[0]

    @pl.when(i == 0)
    def _():
        kt[...] = k_ref[...].T
        dkt[...] = jnp.zeros_like(dkt)
        dvt[...] = jnp.zeros_like(dvt)

    length = meta[0]
    own = jnp.bitwise_and(i, 1) == meta[2]
    q = q_ref[...] * bf16(HDIM**-0.5)
    o = jnp.where(own, om[...], ot[...])
    do = jnp.where(own, dm[...], dt[...])
    qq, dd = two_heads(q), two_heads(do)
    qt, dot_ = q.T, do.T
    od = (o.astype(f32) * do.astype(f32)).T
    delta = jnp.concatenate(
        [jnp.sum(od[:HDIM], axis=0, keepdims=True), jnp.sum(od[HDIM:], axis=0, keepdims=True)],
        axis=1,
    )
    ls = lse_ref[0]
    lse = jnp.concatenate([ls[0:1], ls[1:2]], axis=1)
    dqt[...] = jnp.zeros_like(dqt)
    lim = limits(i, B, length)

    def tile(j, masked):
        sl = pl.ds(pl.multiple_of(j * B, B), B)
        s = dot(k_ref[sl, :], qq, NT)
        dp = dot(v_ref[sl, :], dd, NT)
        p = jnp.exp(s - lse)
        if masked:
            p = jnp.where(j * B + lax.broadcasted_iota(jnp.int32, (B, 2 * B), 0) <= lim, p, 0.0)
        ds = (p * (dp - delta)).astype(bf16)
        pb = p.astype(bf16)
        for h in range(2):
            r, c = slice(HDIM * h, HDIM * h + HDIM), slice(h * B, h * B + B)
            dqt[r, :] += dot(kt[r, sl], ds[:, c])
            dkt[r, sl] += dot(qt[r, :], ds[:, c], NT)
            dvt[r, sl] += dot(dot_[r, :], pb[:, c], NT)

    full = jnp.minimum(i, length // B)

    def step(j, carry):
        tile(j, False)
        return carry

    lax.fori_loop(0, full, step, 0)
    tile(jnp.minimum(full, pl.num_programs(1) - 1), True)
    dqs[pl.ds(pl.multiple_of(i * B, B), B), :] = dqt[...].T * HDIM**-0.5

    @pl.when(i == pl.num_programs(1) - 1)
    def _():
        gt[...] = jnp.zeros_like(gt)
        ext[B : B + 8, :] = jnp.zeros((8, 128), f32)
        for which, (raw, out) in enumerate(((rq, gq), (rk, gk), (rv, gv))):
            t = taps[3 * which : 3 * which + 3, :].astype(f32)
            sums = [jnp.zeros((1, 128), f32)] * 3
            for blk in reversed(range(L // B)):
                sl = slice(blk * B, blk * B + B)
                if which == 0:
                    g = dqs[sl, :]
                elif which == 1:
                    g = dkt[:, sl].T
                else:
                    g = dvt[:, sl].T
                if blk == L // B - 1:
                    ext[B : B + 8, :] = jnp.zeros((8, 128), f32)
                else:
                    ext[B : B + 8, :] = ext[0:8, :]
                ext[0:B, :] = g
                g1, g2 = ext[1 : B + 1, :], ext[2 : B + 2, :]
                out[sl, :] = (t[0:1] * g + t[1:2] * g1 + t[2:3] * g2).astype(bf16)
                r = raw[sl, :].astype(f32)
                for n, gg in enumerate((g, g1, g2)):
                    sums[n] = sums[n] + jnp.sum(r * gg, axis=0, keepdims=True)
            for n in range(3):
                gt[3 * which + n : 3 * which + n + 1, :] = sums[n]


def att_bwd_call(meta, mix, raw, om, ot, dm, dt, lse, taps):
    length, cols = mix.shape
    width = cols // 3
    pairs = width // 128
    B = length // 4
    half = pl.BlockSpec((B, 128), half_map)
    full = lambda k: pl.BlockSpec((length, 128), lambda p, i, m: (0, k * pairs + p))
    return pl.pallas_call(
        att_bwd_body,
        out_shape=[sds((length, width), bf16)] * 3 + [sds((16, width), f32)],
        grid_spec=grid_spec(
            (pairs, 4),
            [
                pl.BlockSpec((B, 128), lambda p, i, m: (i, p)),
                full(1),
                full(2),
                half,
                half,
                half,
                half,
                pl.BlockSpec((1, 2, B), lambda p, i, m: (p, 0, i)),
                full(0),
                full(1),
                full(2),
                pl.BlockSpec((9, 128), lambda p, i, m: (0, p)),
            ],
            [full(0)] * 3 + [pl.BlockSpec((16, 128), lambda p, i, m: (0, p))],
            [
                pltpu.VMEM((128, length), bf16),
                pltpu.VMEM((128, length), f32),
                pltpu.VMEM((128, length), f32),
                pltpu.VMEM((128, B), f32),
                pltpu.VMEM((length, 128), f32),
                pltpu.VMEM((B + 8, 128), f32),
            ],
        ),
        cost_estimate=cost(14 * length * length * width, 20 * length * width, 2 * length * length * pairs),
        name="attn_bwd",
    )(meta, mix, mix, mix, om, ot, dm, dt, lse, raw, raw, raw, taps)


T = 256


def row_valid(meta, i, per):
    block = jnp.where(i < per, meta[3], jnp.bitwise_xor(meta[3], 2))
    start = block * (per * T) + lax.rem(i, per) * T
    return start + lax.broadcasted_iota(jnp.int32, (T, 1), 0) < meta[0]


def mid_body(meta, xo, xx, co, cx, am, at, w, gain, mid_ref, h_ref, g_ref):
    i = pl.program_id(0)
    per = pl.num_programs(0) // 2
    first = i < per
    x = jnp.where(first, xo[...], xx[...]).astype(f32)
    mid = x + dot(jnp.concatenate([am[...], at[...]], axis=1), w[...])
    mid_ref[...] = mid
    h_ref[...] = norm(mid, gain[...].astype(f32))[2]
    ct = jnp.where(first, co[...], cx[...])
    g_ref[...] = jnp.where(row_valid(meta, i, per), ct, jnp.zeros_like(ct))


def own_map(per):
    return lambda i, m: (jnp.minimum(i, per - 1), 0)


def nb_map(per):
    return lambda i, m: (jnp.maximum(i - per, 0), 0)


def mid_call(meta, xo, xx, co, cx, am, at, w, gain):
    rows, width = xo.shape
    per = rows // T
    half = am.shape[1]
    fst, snd = pl.BlockSpec((T, width), own_map(per)), pl.BlockSpec((T, width), nb_map(per))
    blk = lambda n: pl.BlockSpec((T, n), lambda i, m: (i, 0))
    return pl.pallas_call(
        mid_body,
        out_shape=[
            sds((2 * rows, width), f32),
            sds((2 * rows, width), bf16),
            sds((2 * rows, width), bf16),
        ],
        grid_spec=grid_spec(
            (2 * per,),
            [fst, snd, fst, snd, blk(half), blk(half), whole((width, width)), whole((1, width))],
            [blk(width)] * 3,
        ),
        cost_estimate=cost(4 * rows * width * width, 24 * rows * width),
        name="mid",
    )(meta, xo, xx, co, cx, am, at, w, gain)


def ff_body(first, meta, h_ref, g_ref, wu, wd, *rest):
    if first:
        fo, dh, gu, gd, au, ad = rest
    else:
        fi, di, fo, dh, gu, gd, au, ad = rest
    i = pl.program_id(0)
    h, g = h_ref[...], g_ref[...]
    u = dot(h, wu[...])
    r = jnp.maximum(u, 0.0)
    act = (r * r).astype(bf16)
    du = (dot(g, wd[...], NT) * 2.0 * r).astype(bf16)
    f = dot(act, wd[...])
    d = dot(du, wu[...], NT)
    fo[...] = f if first else fi[...] + f
    dh[...] = d if first else di[...] + d
    pu = dot(h, du, TN)
    pd = dot(act, g, TN)

    @pl.when(i == 0)
    def _():
        au[...] = pu
        ad[...] = pd

    @pl.when(i > 0)
    def _():
        au[...] += pu
        ad[...] += pd

    @pl.when(i == pl.num_programs(0) - 1)
    def _():
        gu[...] = au[...].astype(bf16)
        gd[...] = ad[...].astype(bf16)


def ff_call(meta, h, g, wu, wd, carry):
    rows, width = h.shape
    hid = wu.shape[1]
    blk = pl.BlockSpec((T, width), lambda i, m: (i, 0))
    const = lambda s: pl.BlockSpec(s, lambda i, m: (0, 0), pipeline_mode=pl.Buffered(1))
    first = carry is None
    extra = () if first else carry
    return pl.pallas_call(
        functools.partial(ff_body, first),
        out_shape=[
            sds((rows, width), f32),
            sds((rows, width), f32),
            sds((width, hid), bf16),
            sds((hid, width), bf16),
        ],
        grid_spec=grid_spec(
            (rows // T,),
            [blk, blk, const((width, hid)), const((hid, width))] + [blk] * len(extra),
            [blk, blk, const((width, hid)), const((hid, width))],
            [pltpu.VMEM((width, hid), f32), pltpu.VMEM((hid, width), f32)],
        ),
        cost_estimate=cost(12 * rows * width * hid, 20 * rows * width + 8 * width * hid),
        name="ff",
    )(meta, h, g, wu, wd, *extra)


def epi_body(
    meta, mid_ref, f_ref, dh_ref, co, cx, am, at, w, gain,
    oo, ox, dmid_ref, dm_ref, dt_ref, gm, gt, gg, acc,
):
    i = pl.program_id(0)
    per = pl.num_programs(0) // 2
    first = i < per
    ok = row_valid(meta, i, per)
    mid = mid_ref[...]
    out = jnp.where(ok, mid + f_ref[...], 0.0)

    @pl.when(first)
    def _():
        oo[...] = out

    @pl.when(jnp.logical_not(first))
    def _():
        ox[...] = out.astype(bf16)

    g = jnp.where(ok, jnp.where(first, co[...], cx[...]).astype(f32), 0.0)
    gn = gain[...].astype(f32)
    n, inv, _ = norm(mid, gn)
    dh = dh_ref[...]
    dn = dh * gn
    dmid = g + inv * (dn - n * jnp.mean(dn * n, axis=-1, keepdims=True))
    dmid_ref[...] = dmid
    db = dmid.astype(bf16)
    half = am.shape[1]
    da = dot(db, w[...], NT).astype(bf16)
    dm_ref[...] = da[:, :half]
    dt_ref[...] = da[:, half:]
    a = jnp.concatenate([am[...], at[...]], axis=1)
    pg = dot(a, db, TN)
    ps = jnp.sum(dh * n, axis=0, keepdims=True)

    @pl.when(i == 0)
    def _():
        acc[...] = pg
        gg[...] = ps

    @pl.when(i > 0)
    def _():
        acc[...] += pg
        gg[...] += ps

    @pl.when(i == pl.num_programs(0) - 1)
    def _():
        gm[...] = acc[0:half, :].astype(bf16)
        gt[...] = acc[half:, :].astype(bf16)


def epi_call(meta, mid, f, dh, co, cx, am, at, w, gain):
    rows, width = co.shape
    per = rows // T
    half = am.shape[1]
    fst, snd = pl.BlockSpec((T, width), own_map(per)), pl.BlockSpec((T, width), nb_map(per))
    blk = lambda n: pl.BlockSpec((T, n), lambda i, m: (i, 0))
    const = lambda s: pl.BlockSpec(s, lambda i, m: (0, 0), pipeline_mode=pl.Buffered(1))
    return pl.pallas_call(
        epi_body,
        out_shape=[
            sds((rows, width), f32),
            sds((rows, width), bf16),
            sds((2 * rows, width), f32),
            sds((2 * rows, half), bf16),
            sds((2 * rows, half), bf16),
            sds((half, width), bf16),
            sds((half, width), bf16),
            sds((1, width), f32),
        ],
        grid_spec=grid_spec(
            (2 * per,),
            [blk(width)] * 3
            + [fst, snd, blk(half), blk(half), whole((width, width)), whole((1, width))],
            [
                fst,
                snd,
                blk(width),
                blk(half),
                blk(half),
                const((half, width)),
                const((half, width)),
                const((1, width)),
            ],
            [pltpu.VMEM((width, width), f32)],
        ),
        cost_estimate=cost(8 * rows * width * width, 50 * rows * width),
        name="epi",
    )(meta, mid, f, dh, co, cx, am, at, w, gain)


def proj_body(meta, h_ref, q, k, v, w, dm, dt, keep, send, acc):
    b = pl.program_id(0)
    d = jnp.concatenate([q[...], k[...], v[...]], axis=1)
    dh = dot(d, w[...], NT)
    own = jnp.bitwise_and(b, 1) == meta[2]

    @pl.when(own)
    def _():
        dm[...] = dh

    @pl.when(jnp.logical_not(own))
    def _():
        dt[...] = dh.astype(bf16)

    pg = dot(h_ref[...], d, TN)

    @pl.when(b == 0)
    def _():
        acc[...] = pg

    @pl.when(b > 0)
    def _():
        acc[...] += pg

    @pl.when(b == pl.num_programs(0) - 1)
    def _():
        part = keep.shape[1]
        for ref, n, k_ in ((keep, 0, 0), (keep, 1, 2), (send, 0, 1), (send, 1, 3)):
            at = jnp.bitwise_xor(meta[3], k_)
            ref[n] = acc[pl.ds(pl.multiple_of(at * part, 64), part), :].astype(bf16)


def proj_call(meta, h, q, k, v, w):
    length, width = h.shape
    half = q.shape[1]
    B = length // 4
    part = width // 4
    blk = lambda n: pl.BlockSpec((B, n), lambda b, m: (b, 0))
    side = pl.BlockSpec((B, width), lambda b, m: (jnp.bitwise_xor(b // 2, m[1]), 0))
    g = pl.BlockSpec((2, part, 3 * half), lambda b, m: (0, 0, 0), pipeline_mode=pl.Buffered(1))
    return pl.pallas_call(
        proj_body,
        out_shape=[
            sds((length // 2, width), f32),
            sds((length // 2, width), bf16),
            sds((2, part, 3 * half), bf16),
            sds((2, part, 3 * half), bf16),
        ],
        grid_spec=grid_spec(
            (4,),
            [blk(width), blk(half), blk(half), blk(half), whole((width, 3 * half))],
            [side, side, g, g],
            [pltpu.VMEM((width, 3 * half), f32)],
        ),
        cost_estimate=cost(12 * length * width * half, 12 * length * width),
        name="proj",
    )(meta, h, q, k, v, w)


def last_body(meta, xo, xx, dm, dt, dmid, gain, go, gx, gg):
    i = pl.program_id(0)
    per = pl.num_programs(0) // 2
    first = i < per
    x = jnp.where(first, xo[...], xx[...]).astype(f32)
    gn = gain[...].astype(f32)
    n, inv, _ = norm(x, gn)
    dh = dm[...] + dt[...].astype(f32)
    dn = dh * gn
    out = dmid[...] + inv * (dn - n * jnp.mean(dn * n, axis=-1, keepdims=True))

    @pl.when(first)
    def _():
        go[...] = out

    @pl.when(jnp.logical_not(first))
    def _():
        gx[...] = out.astype(bf16)

    ps = jnp.sum(dh * n, axis=0, keepdims=True)

    @pl.when(i == 0)
    def _():
        gg[...] = ps

    @pl.when(i > 0)
    def _():
        gg[...] += ps


def last_call(meta, xo, xx, dm, dt, dmid, gain):
    rows, width = xo.shape
    per = rows // T
    fst, snd = pl.BlockSpec((T, width), own_map(per)), pl.BlockSpec((T, width), nb_map(per))
    blk = pl.BlockSpec((T, width), lambda i, m: (i, 0))
    return pl.pallas_call(
        last_body,
        out_shape=[sds((rows, width), f32), sds((rows, width), bf16), sds((1, width), f32)],
        grid_spec=grid_spec(
            (2 * per,),
            [fst, snd, blk, blk, blk, whole((1, width))],
            [fst, snd, pl.BlockSpec((1, width), lambda i, m: (0, 0))],
        ),
        cost_estimate=cost(40 * rows * width, 30 * rows * width),
        name="last",
    )(meta, xo, xx, dm, dt, dmid, gain)


def flip(size, bit):
    return [(i, i ^ bit) for i in range(size)]


def reduce_dp(v, size):
    me = lax.axis_index("dp")
    bits = []
    bit = 1
    while bit < size:
        bits.append(bit)
        bit *= 2
    for bit in bits:
        half = v.shape[0] // 2
        mine = jnp.where(jnp.bitwise_and(me, bit) > 0, 1, 0)
        send = lax.dynamic_slice_in_dim(v, (1 - mine) * half, half, 0).astype(bf16)
        got = lax.ppermute(send, "dp", flip(size, bit))
        v = lax.dynamic_slice_in_dim(v, mine * half, half, 0) + got.astype(f32)
    v = v.astype(bf16)
    for bit in reversed(bits):
        got = lax.ppermute(v, "dp", flip(size, bit))
        upper = jnp.bitwise_and(me, bit) > 0
        v = jnp.where(upper, jnp.concatenate([got, v], 0), jnp.concatenate([v, got], 0))
    return v


def sum_small(v, size):
    bit = 1
    while bit < size:
        v = v + lax.ppermute(v, "dp", flip(size, bit))
        bit *= 2
    return v


def core_swap(v):
    return lax.ppermute(v, "head", CORE)


def x_swap(v):
    return lax.ppermute(v, "head", XNB)


def local(dp, inputs, lengths, w_query, w_key, w_value, w_out, w_up, w_down, conv_taps, gain_attn, gain_ff, cotangent):
    hd = lax.axis_index("head")
    x, c = hd // 2, hd % 2
    width = inputs.shape[2]
    part = w_query.shape[0]
    pick = lambda v, k: lax.dynamic_index_in_dim(v, k, 0, keepdims=False)
    first = x == 0
    order = lambda own, nb: jnp.where(first, jnp.stack([own, nb]), jnp.stack([nb, own]))

    slots = [jnp.bitwise_xor(hd, b) for b in range(4)]
    slots = [jnp.bitwise_and(s, 1) * 2 + s // 2 for s in slots]
    meta = jnp.stack([pick(lengths, x), x, c, hd, *slots]).astype(jnp.int32)

    x_own, x_nb = pick(inputs, x), x_swap(pick(inputs, 1 - x))
    w3 = jnp.stack([w_query, w_key, w_value], axis=1).reshape(part, 3, 4, part)
    even = w3[:, :, 0::2].reshape(part, -1)
    odd = w3[:, :, 1::2].reshape(part, -1)
    w_mine = jnp.where(c == 0, even, odd)
    w_core = core_swap(jnp.where(c == 0, odd, even))
    w_pair = x_swap(jnp.stack([w_mine, w_core]))
    x_core, x_cnb = core_swap(x_own), core_swap(x_nb)
    taps_nb = x_swap(conv_taps)
    taps = order(conv_taps, taps_nb)
    taps9 = taps.transpose(1, 2, 0, 3).reshape(9, 2 * part)
    taps3 = taps.transpose(2, 1, 0, 3).reshape(3, 6 * part)
    gain1, gain2 = gain_attn.reshape(1, width), gain_ff.reshape(1, width)
    h1, raw, mix, w_full = qkv_call(
        meta, (x_own, x_nb, x_core, x_cnb), (w_mine, w_core, w_pair[0], w_pair[1]), gain1, taps3
    )
    wo_nb = x_swap(w_out)
    wo_mine = order(w_out, wo_nb).reshape(2 * part, width)
    wo = jnp.concatenate([wo_mine, core_swap(wo_mine)], axis=0)
    c_own, c_nb = pick(cotangent, x), x_swap(pick(cotangent, 1 - x))
    up_nb, down_nb = x_swap(w_up), x_swap(w_down)
    up_core, down_core = core_swap(w_up), core_swap(w_down)
    up_cnb, down_cnb = core_swap(up_nb), core_swap(down_nb)

    a_mine, a_send, lse = att_fwd_call(meta, mix)
    a_got = core_swap(a_send)
    mid, h2, g = mid_call(meta, x_own, x_nb, c_own, c_nb, a_mine, a_got, wo, gain2)
    f, dh, gu_c, gd_c = ff_call(meta, h2, g, up_core, down_core, None)
    f, dh, gu_cn, gd_cn = ff_call(meta, h2, g, up_cnb, down_cnb, (f, dh))
    f, dh, gu_n, gd_n = ff_call(meta, h2, g, up_nb, down_nb, (f, dh))
    f, dh, gu_o, gd_o = ff_call(meta, h2, g, w_up, w_down, (f, dh))
    out_own, out_nb, dmid, d_mine, d_send, go_mine, go_send, gg2 = epi_call(
        meta, mid, f, dh, c_own, c_nb, a_mine, a_got, wo, gain2
    )
    d_got = core_swap(d_send)

    both = lambda a, b: a.astype(f32) + b.astype(f32)
    gu_n = both(gu_n, core_swap(gu_cn))
    gd_n = both(gd_n, core_swap(gd_cn))
    gu_o = both(gu_o, core_swap(gu_c))
    gd_o = both(gd_o, core_swap(gd_c))
    gu_o = gu_o + x_swap(gu_n.astype(bf16)).astype(f32)
    gd_o = gd_o + x_swap(gd_n.astype(bf16)).astype(f32)
    go = both(go_mine, core_swap(go_send)).reshape(2, part, width)
    go_o = pick(go, x) + x_swap(pick(go, 1 - x).astype(bf16)).astype(f32)
    grad_up = reduce_dp(gu_o, dp).astype(f32)
    grad_down = reduce_dp(gd_o, dp).astype(f32)
    grad_out = reduce_dp(go_o, dp).astype(f32)
    output = order(out_own, x_swap(out_nb).astype(f32))

    dq, dk, dv, gt = att_bwd_call(meta, mix, raw, a_mine, a_send, d_mine, d_got, lse, taps9)
    dh_mine, dh_send, gp_keep, gp_send = proj_call(meta, h1, dq, dk, dv, w_full)
    gp_got = core_swap(gp_send)
    dh_got = core_swap(dh_send)
    gp = jnp.concatenate([gp_keep, gp_got], axis=2)
    gp_sum = gp[0].astype(f32) + x_swap(gp[1]).astype(f32)
    gp_all = reduce_dp(gp_sum, dp)
    gi_own, gi_nb, gg1 = last_call(meta, x_own, x_nb, dh_mine, dh_got, dmid, gain1)
    grad_input = order(gi_own, x_swap(gi_nb).astype(f32))

    gains = jnp.concatenate([gg1, gg2], axis=0)
    gains = gains + core_swap(gains)
    gains = gains + x_swap(gains)
    gt = gt[:9].reshape(9, 2, part).transpose(1, 0, 2)
    gt = pick(gt, x) + x_swap(pick(gt, 1 - x))
    gains = lax.dynamic_slice_in_dim(gains, hd * part, part, 1)
    small = sum_small(jnp.concatenate([gt, gains], axis=0), dp)
    grad_taps = small[:9].reshape(3, 3, part)

    gp_all = gp_all.astype(f32).reshape(part, 2, 3, 2, part)
    mine, other = gp_all[:, 0], gp_all[:, 1]
    lo = jnp.where(c == 0, mine, other)
    hi = jnp.where(c == 0, other, mine)
    full = jnp.stack([lo, hi], axis=3).reshape(part, 3, width)
    return (
        output,
        grad_input,
        full[:, 0],
        full[:, 1],
        full[:, 2],
        grad_out,
        grad_up,
        grad_down,
        grad_taps,
        small[9],
        small[10],
    )


def solution(mesh):
    placed = (
        P("dp", "head", None),
        P("dp"),
        P("head", None),
        P("head", None),
        P("head", None),
        P("head", None),
        P(None, "head"),
        P("head", None),
        P(None, None, "head"),
        P(),
        P(),
        P("dp", "head", None),
    )
    return jax.shard_map(
        functools.partial(local, mesh.shape["dp"]),
        mesh=mesh,
        in_specs=placed,
        out_specs=(
            P("dp", "head", None),
            P("dp", "head", None),
            P("head", None),
            P("head", None),
            P("head", None),
            P("head", None),
            P(None, "head"),
            P("head", None),
            P(None, None, "head"),
            P("head"),
            P("head"),
        ),
        check_vma=False,
    )
```

```python
import functools

import jax
import jax.numpy as jnp
from jax import lax
from jax.experimental import pallas as pl
from jax.experimental.pallas import tpu as pltpu
from jax.sharding import PartitionSpec as P

HDIM = 64
EPS = 1e-06
bf16 = jnp.bfloat16
f32 = jnp.float32

NN = (((1,), (0,)), ((), ()))
NT = (((1,), (1,)), ((), ()))
TN = (((0,), (0,)), ((), ()))

CORE = [(0, 1), (1, 0), (2, 3), (3, 2)]
XNB = [(0, 2), (2, 0), (1, 3), (3, 1)]


def dot(a, b, dims=NN):
    return lax.dot_general(a, b, dims, preferred_element_type=f32)


def cost(flops, nbytes, trans=0):
    return pl.CostEstimate(flops=int(flops), bytes_accessed=int(nbytes), transcendentals=int(trans))


def sds(shape, dtype):
    return jax.ShapeDtypeStruct(shape, dtype)


def whole(shape):
    zeros = (0,) * len(shape)
    return pl.BlockSpec(shape, lambda *_: zeros, pipeline_mode=pl.Buffered(1))


def grid_spec(grid, ins, outs, scratch=()):
    return pltpu.PrefetchScalarGridSpec(
        num_scalar_prefetch=1, grid=grid, in_specs=ins, out_specs=outs, scratch_shapes=scratch
    )


def length_of(m):
    return m[m[2] // 2]


def x_of(m):
    return m[2] // 2


def core_of(m):
    return lax.rem(m[2], 2)


def norm(x, gain):
    inv = lax.rsqrt(jnp.mean(x * x, axis=-1, keepdims=True) + EPS)
    n = x * inv
    return n, inv, (n * gain).astype(bf16)


def qkv_body(meta, x0, x1, x2, x3, wa, wb, wc, wd, gain, h_ref, raw_ref, mix_ref, w_ref, taps, ext):
    b = pl.program_id(0)
    rows = x0.shape[0]
    part = w_ref.shape[0] // 4
    hd, y = meta[2], meta[3]

    @pl.when(b == 0)
    def _():
        for k, piece in ((0, wa), (1, wb), (2 + y, wc), (3 - y, wd)):
            at = jnp.bitwise_xor(hd, k)
            w_ref[pl.ds(pl.multiple_of(at * part, 64), part), :] = piece[0:part, :]
        near = (wa[part:, :] + wb[part:, :]).astype(f32)
        far = (wc[part:, :] + wd[part:, :]).astype(f32)
        taps[...] = jnp.where(x_of(meta) == core_of(meta), near, far)
        ext[0:8, :] = jnp.zeros((8, ext.shape[1]), f32)

    v = jnp.bitwise_xor(hd, b)
    slot = lax.rem(v, 2) * 2 + v // 2
    x = x0[...]
    for k, other in ((1, x1), (2, x2), (3, x3)):
        x = jnp.where(slot == k, other[...], x)
    _, _, h = norm(x.astype(f32), gain[...].astype(f32))
    h_ref[...] = h
    raw = dot(h, w_ref[...]).astype(bf16)
    raw_ref[...] = raw
    rawf = raw.astype(f32)
    ext[8 : 8 + rows, :] = rawf
    t = taps[...]
    mixed = t[0:1] * rawf + t[1:2] * ext[7 : 7 + rows, :] + t[2:3] * ext[6 : 6 + rows, :]
    mix_ref[...] = mixed.astype(bf16)
    ext[0:8, :] = ext[rows : rows + 8, :]


def qkv_call(meta, xs, ws, gain):
    rows, width = xs[0].shape
    tall, cols = ws[0].shape
    length = 4 * rows
    blk = lambda n: pl.BlockSpec((rows, n), lambda b, m: (b, 0))
    const = lambda r: pl.BlockSpec((r, cols), lambda b, m: (0, 0))
    return pl.pallas_call(
        qkv_body,
        out_shape=[
            sds((length, width), bf16),
            sds((length, cols), bf16),
            sds((length, cols), bf16),
            sds((width, cols), bf16),
            sds((8, cols), f32),
        ],
        grid_spec=grid_spec(
            (4,),
            [whole((rows, width))] * 4 + [whole((tall, cols))] * 4 + [whole((1, width))],
            [blk(width), blk(cols), blk(cols), const(width), const(8)],
            [pltpu.VMEM((rows + 8, cols), f32)],
        ),
        cost_estimate=cost(2 * length * width * cols, 2 * length * (width * 2 + cols * 2)),
        name="qkv",
    )(meta, *xs, *ws, gain)


def two_heads(v):
    lane = lax.broadcasted_iota(jnp.int32, v.shape, 1)
    z = jnp.zeros_like(v)
    return jnp.concatenate([jnp.where(lane < HDIM, v, z), jnp.where(lane < HDIM, z, v)], axis=0)


def causal(first, keys, start, queries):
    key = first + lax.broadcasted_iota(jnp.int32, (keys, queries), 0)
    ok = key <= start + lax.broadcasted_iota(jnp.int32, (keys, queries), 1)
    return jnp.concatenate([ok, ok], axis=1)


def upper(v, axis):
    B = v.shape[axis] // 2
    h = B // 2
    if axis == 0:
        return jnp.concatenate([v[h:B], v[B + h :]], axis=0)
    return jnp.concatenate([v[:, h:B], v[:, B + h :]], axis=1)


def with_bias(k_ref, ka, length):
    L = k_ref.shape[0]
    ka[:, :128] = k_ref[...]
    lane = lax.broadcasted_iota(jnp.int32, (L, 128), 1)
    row = lax.broadcasted_iota(jnp.int32, (L, 128), 0)
    pad = jnp.logical_and(lane == 0, row >= length)
    ka[:, 128:] = jnp.where(pad, -1e9, 0.0).astype(bf16)


def biased(q):
    qq = two_heads(q)
    lane = lax.broadcasted_iota(jnp.int32, qq.shape, 1)
    return jnp.concatenate([qq, jnp.where(lane == 0, 1.0, 0.0).astype(bf16)], axis=1)


def att_fwd_body(meta, q_ref, k_ref, v_ref, mine_ref, theirs_ref, lse_ref, ka, vt, sc):
    i = pl.program_id(1)
    B = q_ref.shape[0]

    @pl.when(i == 0)
    def _():
        vt[...] = v_ref[...].T
        with_bias(k_ref, ka, length_of(meta))

    qq = biased(q_ref[...] * bf16(HDIM**-0.5))
    own = lax.rem(i, 2) == core_of(meta)

    def run(ii):
        m = None
        for j in range(ii + 1):
            ks = slice(j * B, j * B + B)
            s = dot(ka[ks, :], qq, NT)
            if j == ii:
                s = jnp.where(causal(0, B, 0, B), s, -1e9)
            sc[ks, :] = s
            mj = jnp.max(s, axis=0, keepdims=True)
            m = mj if m is None else jnp.maximum(m, mj)
        l = jnp.zeros((1, 2 * B), f32)
        acc = [jnp.zeros((HDIM, B), f32)] * 2
        for j in range(ii + 1):
            ks = slice(j * B, j * B + B)
            p = jnp.exp(sc[ks, :] - m)
            l = l + jnp.sum(p, axis=0, keepdims=True)
            pb = p.astype(bf16)
            for h in range(2):
                r = slice(HDIM * h, HDIM * h + HDIM)
                acc[h] = acc[h] + dot(vt[r, ks], pb[:, h * B : h * B + B])
        inv = 1.0 / l
        out = jnp.concatenate([acc[h] * inv[:, h * B : h * B + B] for h in range(2)], axis=0)
        out = out.T.astype(bf16)

        @pl.when(own)
        def _():
            mine_ref[...] = out

        @pl.when(jnp.logical_not(own))
        def _():
            theirs_ref[...] = out

        ls = m + jnp.log(l)
        lse_ref[0] = jnp.concatenate([ls[:, :B], ls[:, B:]], axis=0)

    for ii in range(4):
        pl.when(i == ii)(functools.partial(run, ii))


def half_map(p, i, m):
    return (jnp.bitwise_xor(i // 2, x_of(m)), p)


def att_fwd_call(meta, mix):
    length, cols = mix.shape
    width = cols // 3
    pairs = width // 128
    B = length // 4
    half = pl.BlockSpec((B, 128), half_map)
    return pl.pallas_call(
        att_fwd_body,
        out_shape=[
            sds((length // 2, width), bf16),
            sds((length // 2, width), bf16),
            sds((pairs, 2, length), f32),
        ],
        grid_spec=grid_spec(
            (pairs, 4),
            [
                pl.BlockSpec((B, 128), lambda p, i, m: (i, p)),
                pl.BlockSpec((length, 128), lambda p, i, m: (0, pairs + p)),
                pl.BlockSpec((length, 128), lambda p, i, m: (0, 2 * pairs + p)),
            ],
            [half, half, pl.BlockSpec((1, 2, B), lambda p, i, m: (p, 0, i))],
            [
                pltpu.VMEM((length, 256), bf16),
                pltpu.VMEM((128, length), bf16),
                pltpu.VMEM((length, 2 * B), f32),
            ],
        ),
        cost_estimate=cost(8 * length * length * width, 8 * length * width, 2 * length * length * pairs),
        name="attn_fwd",
    )(meta, mix, mix, mix)


def att_bwd_body(
    p0, meta, q_ref, k_ref, v_ref, om, ot, dm, dt, lse_ref, rq, rk, rv, taps,
    gq, gk, gv, gt, ka, kt, dkt, dvt, dqs, ext,
):
    i = pl.program_id(1)
    B = q_ref.shape[0]
    L = k_ref.shape[0]
    H = B // 2

    @pl.when(i == 0)
    def _():
        kt[...] = k_ref[...].T
        with_bias(k_ref, ka, length_of(meta))

    own = lax.rem(i, 2) == core_of(meta)
    q = q_ref[...] * bf16(HDIM**-0.5)
    o = jnp.where(own, om[...], ot[...])
    do = jnp.where(own, dm[...], dt[...])
    qq, dd = biased(q), two_heads(do)
    qt, dot_ = q.T, do.T
    od = (o.astype(f32) * do.astype(f32)).T
    delta = jnp.concatenate(
        [jnp.sum(od[:HDIM], axis=0, keepdims=True), jnp.sum(od[HDIM:], axis=0, keepdims=True)],
        axis=1,
    )
    ls = lse_ref[0]
    lse = jnp.concatenate([ls[0:1], ls[1:2]], axis=1)

    def run(ii):
        dq = [jnp.zeros((HDIM, B), f32)] * 2

        def tile(st, n, lo, diagonal):
            w = B - lo
            ks = slice(st, st + n)
            part = upper if lo else lambda v, axis: v
            s = dot(ka[ks, :], part(qq, 0), NT)
            dp = dot(v_ref[ks, :], part(dd, 0), NT)
            p = jnp.exp(s - part(lse, 1))
            if diagonal:
                p = jnp.where(causal(lo, n, lo, w), p, 0.0)
            ds = (p * (dp - part(delta, 1))).astype(bf16)
            pb = p.astype(bf16)
            for h in range(2):
                r, c = slice(HDIM * h, HDIM * h + HDIM), slice(h * w, h * w + w)
                x = dot(kt[r, ks], ds[:, c])
                if lo:
                    x = jnp.concatenate([jnp.zeros((HDIM, lo), f32), x], axis=1)
                dq[h] = dq[h] + x
                a = dot(qt[r, lo:], ds[:, c], NT)
                b = dot(dot_[r, lo:], pb[:, c], NT)
                if diagonal:
                    dkt[r, ks] = a
                    dvt[r, ks] = b
                else:
                    dkt[r, ks] += a
                    dvt[r, ks] += b

        for j in range(ii):
            tile(j * B, B, 0, False)
        tile(ii * B, H, 0, True)
        tile(ii * B + H, H, H, True)
        dqs[ii * B : ii * B + B, :] = jnp.concatenate(dq, axis=0).T * HDIM**-0.5

    for ii in range(4):
        pl.when(i == ii)(functools.partial(run, ii))

    @pl.when(i == pl.num_programs(1) - 1)
    def _():
        gt[...] = jnp.zeros_like(gt)
        ext[...] = jnp.zeros_like(ext)

        def back(n, carry):
            blk = L // B - 1 - n
            sl = pl.ds(pl.multiple_of(blk * B, B), B)
            for which, (raw, out) in enumerate(((rq, gq), (rk, gk), (rv, gv))):
                col = which * (taps.shape[1] // 3) + (p0 + pl.program_id(0)) * 128
                t = taps[:, pl.ds(pl.multiple_of(col, 128), 128)]
                g = dqs[sl, :] if which == 0 else (dkt, dvt)[which - 1][:, sl].T
                ext[which, B : B + 8, :] = ext[which, 0:8, :]
                ext[which, 0:B, :] = g
                g1, g2 = ext[which, 1 : B + 1, :], ext[which, 2 : B + 2, :]
                out[sl, :] = (t[0:1] * g + t[1:2] * g1 + t[2:3] * g2).astype(bf16)
                r = raw[sl, :].astype(f32)
                for k, gg in enumerate((g, g1, g2)):
                    row = slice(3 * which + k, 3 * which + k + 1)
                    gt[row, :] += jnp.sum(r * gg, axis=0, keepdims=True)
            return carry

        lax.fori_loop(0, L // B, back, 0)


def att_bwd_call(meta, mix, raw, om, ot, dm, dt, lse, taps, p0, count):
    length, cols = mix.shape
    pairs = cols // 384
    B = length // 4
    half = pl.BlockSpec((B, 128), lambda p, i, m: (jnp.bitwise_xor(i // 2, x_of(m)), p0 + p))
    full = lambda k: pl.BlockSpec((length, 128), lambda p, i, m: (0, k * pairs + p0 + p))
    outb = pl.BlockSpec((length, 128), lambda p, i, m: (0, p))
    return pl.pallas_call(
        functools.partial(att_bwd_body, p0),
        out_shape=[sds((length, 128 * count), bf16)] * 3 + [sds((16, 128 * count), f32)],
        grid_spec=grid_spec(
            (count, 4),
            [
                pl.BlockSpec((B, 128), lambda p, i, m: (i, p0 + p)),
                full(1),
                full(2),
                half,
                half,
                half,
                half,
                pl.BlockSpec((1, 2, B), lambda p, i, m: (p0 + p, 0, i)),
                full(0),
                full(1),
                full(2),
                whole((8, cols)),
            ],
            [outb] * 3 + [pl.BlockSpec((16, 128), lambda p, i, m: (0, p))],
            [
                pltpu.VMEM((length, 256), bf16),
                pltpu.VMEM((128, length), bf16),
                pltpu.VMEM((128, length), f32),
                pltpu.VMEM((128, length), f32),
                pltpu.VMEM((length, 128), f32),
                pltpu.VMEM((3, B + 8, 128), f32),
            ],
        ),
        cost_estimate=cost(
            14 * length * length * 128 * count, 20 * length * 128 * count, 2 * length * length * count
        ),
        name="attn_bwd",
    )(meta, mix, mix, mix, om, ot, dm, dt, lse, raw, raw, raw, taps)


T = 256


def valid_rows(meta, i, rows):
    per = rows // T
    block = jnp.where(i < per, meta[2], jnp.bitwise_xor(meta[2], 2))
    start = block * rows + lax.rem(i, per) * T
    return start + lax.broadcasted_iota(jnp.int32, (T, 1), 0) < length_of(meta)


def ffn_body(
    meta, xo, xx, co, cx, am, at, gain, wo_o, wo_c, wo_n, wo_cn,
    u_o, u_c, u_n, u_m, u_cn, u_cm, d_o, d_c, d_n, d_m, d_cn, d_cm,
    oo, ox, dm, dt, gg, dmid, gut, gum, gdt, gdm,
    wo, wus, wds, mid, h_s, g_s, fo, dh, act, du, stu, std, sto, gacc, sw, so, sg, sd, st,
):
    rows, width = xo.shape
    part = wo_o.shape[0]
    half = 2 * part
    n = 2 * rows // T
    per = rows // T
    copies = []
    for k, src in ((0, wo_o), (1, wo_c), (2, wo_n), (3, wo_cn)):
        shard = jnp.bitwise_xor(meta[2], k)
        row = jnp.where(shard // 2 == core_of(meta), 0, half) + lax.rem(shard, 2) * part
        cp = pltpu.make_async_copy(src, wo.at[pl.ds(pl.multiple_of(row, 64), part), :], so.at[k])
        cp.start()
        copies.append(cp)
    for k, u, d in ((0, u_c, d_c), (2, u_o, d_o)):
        pltpu.make_async_copy(u, wus.at[k], sw.at[k, 0]).start()
        pltpu.make_async_copy(d, wds.at[k], sw.at[k, 1]).start()
    for k, us, ds in ((1, (u_cn, u_cm), (d_cn, d_cm)), (3, (u_n, u_m), (d_n, d_m))):
        for n_, (u, d) in enumerate(zip(us, ds)):
            count = u.shape[0]
            first = meta[3] if n_ == 0 else 1 - meta[3]
            at_ = pl.ds(pl.multiple_of(first * count, 128), count)
            pltpu.make_async_copy(u, wus.at[k, at_, :], sw.at[k, 0]).start()
            pltpu.make_async_copy(d, wds.at[k, at_, :], sw.at[k, 1]).start()
    for cp in copies:
        cp.wait()
    gn = gain[...].astype(f32)

    def first_rows(i, carry):
        sl = pl.ds(pl.multiple_of(i * T, T), T)
        src = pl.ds(pl.multiple_of(lax.rem(i, per) * T, T), T)
        own = i < per
        x = jnp.where(own, xo[src, :], xx[src, :]).astype(f32)
        a = jnp.concatenate([am[sl, :], at[sl, :]], axis=1)
        m = x + dot(a, wo[...])
        mid[sl, :] = m
        fo[sl, :] = m
        h_s[sl, :] = norm(m, gn)[2]
        ct = jnp.where(own, co[src, :], cx[src, :])
        g_s[sl, :] = jnp.where(valid_rows(meta, i, rows), ct, jnp.zeros_like(ct))
        dh[sl, :] = jnp.zeros((T, width), f32)
        return carry

    lax.fori_loop(0, n, first_rows, 0)

    R = 1024
    C = 768

    def shard(k, carry):
        for cp in (
            pltpu.make_async_copy(u_c, wus.at[k], sw.at[k, 0]),
            pltpu.make_async_copy(d_c, wds.at[k], sw.at[k, 1]),
        ):
            cp.wait()

        def rows_step(t, c2):
            sl = pl.ds(pl.multiple_of(t * R, R), R)
            h, g = h_s[sl, :], g_s[sl, :]
            r = jnp.maximum(dot(h, wus[k]), 0.0)
            a = (r * r).astype(bf16)
            d = (dot(g, wds[k], NT) * 2.0 * r).astype(bf16)
            act[sl, :] = a
            du[sl, :] = d
            fo[sl, :] += dot(a, wds[k])
            dh[sl, :] += dot(d, wus[k], NT)
            return c2

        lax.fori_loop(0, 2 * rows // R, rows_step, 0)
        slot = lax.rem(k, 2)

        @pl.when(k >= 2)
        def _():
            pltpu.make_async_copy(stu.at[slot], gut.at[slot], sg.at[slot, 0]).wait()
            pltpu.make_async_copy(
                std.at[slot], gdt.at[slot, pl.ds(0, width), :], sg.at[slot, 1]
            ).wait()

        def cols_step(t, c2):
            sl = pl.ds(pl.multiple_of(t * C, C), C)
            stu[slot, :, sl] = dot(h_s[...], du[:, sl], TN).astype(bf16)
            std[slot, sl, :] = dot(act[:, sl], g_s[...], TN).astype(bf16)
            return c2

        lax.fori_loop(0, width // C, cols_step, 0)
        for theirs, gu, gd in ((True, gut, gdt), (False, gum, gdm)):

            @pl.when((k < 2) == theirs)
            def _(gu=gu, gd=gd):
                pltpu.make_async_copy(stu.at[slot], gu.at[slot], sg.at[slot, 0]).start()
                pltpu.make_async_copy(
                    std.at[slot], gd.at[slot, pl.ds(0, width), :], sg.at[slot, 1]
                ).start()

        return carry

    lax.fori_loop(0, 4, shard, 0)
    gg[...] = jnp.zeros_like(gg)

    def last_rows(i, carry):
        sl = pl.ds(pl.multiple_of(i * T, T), T)
        dst = pl.ds(pl.multiple_of(lax.rem(i, per) * T, T), T)
        ok = valid_rows(meta, i, rows)
        m = mid[sl, :]
        out = jnp.where(ok, fo[sl, :], 0.0)

        @pl.when(i < per)
        def _():
            oo[dst, :] = out

        @pl.when(i >= per)
        def _():
            ox[dst, :] = out.astype(bf16)

        nm, inv, _ = norm(m, gn)
        d = dh[sl, :]
        dn = d * gn
        r = g_s[sl, :].astype(f32) + inv * (dn - nm * jnp.mean(dn * nm, axis=-1, keepdims=True))
        mid[sl, :] = r
        pltpu.make_async_copy(mid.at[sl, :], dmid.at[sl, :], sd).start()
        db = r.astype(bf16)
        du[sl, :] = db
        da = dot(db, wo[...], NT).astype(bf16)
        dm[sl, :] = da[:, :half]
        dt[sl, :] = da[:, half:]
        gg[...] += jnp.sum(d * nm, axis=0, keepdims=True)
        return carry

    lax.fori_loop(0, n, last_rows, 0)
    gacc[0:half, :] = dot(am[...], du[...], TN)
    gacc[half:, :] = dot(at[...], du[...], TN)
    outs = [pltpu.make_async_copy(mid, dmid, sd)]
    for k, (k_, gd, j) in enumerate(((1, gdt, 0), (3, gdt, 1), (0, gdm, 0), (2, gdm, 1))):
        shard_ = jnp.bitwise_xor(meta[2], k_)
        row = jnp.where(shard_ // 2 == core_of(meta), 0, half) + lax.rem(shard_, 2) * part
        sto[k] = gacc[pl.ds(pl.multiple_of(row, 64), part), :].astype(bf16)
        cp = pltpu.make_async_copy(sto.at[k], gd.at[j, pl.ds(width, part), :], st.at[k])
        cp.start()
        outs.append(cp)
    for slot in range(2):
        outs.append(pltpu.make_async_copy(stu.at[slot], gum.at[slot], sg.at[slot, 0]))
        outs.append(
            pltpu.make_async_copy(std.at[slot], gdm.at[slot, pl.ds(0, width), :], sg.at[slot, 1])
        )
    for cp in outs:
        cp.wait()


def ffn_call(meta, xo, xx, co, cx, am, at, gain, wos, ups, downs):
    rows, width = xo.shape
    half = am.shape[1]
    part = half // 2
    hid = ups[0].shape[1]
    hbm = pl.BlockSpec(memory_space=pl.ANY)
    vm = lambda *shape: whole(shape)
    all_rows = 2 * rows
    return pl.pallas_call(
        ffn_body,
        out_shape=[
            sds((rows, width), f32),
            sds((rows, width), bf16),
            sds((all_rows, half), bf16),
            sds((all_rows, half), bf16),
            sds((1, width), f32),
            sds((all_rows, width), f32),
            sds((2, width, hid), bf16),
            sds((2, width, hid), bf16),
            sds((2, hid + part, width), bf16),
            sds((2, hid + part, width), bf16),
        ],
        grid_spec=grid_spec(
            (1,),
            [vm(rows, width)] * 4 + [vm(all_rows, half)] * 2 + [vm(1, width)] + [hbm] * 16,
            [
                vm(rows, width),
                vm(rows, width),
                vm(all_rows, half),
                vm(all_rows, half),
                vm(1, width),
            ]
            + [hbm] * 5,
            [
                pltpu.VMEM((width, width), bf16),
                pltpu.VMEM((4, width, hid), bf16),
                pltpu.VMEM((4, hid, width), bf16),
                pltpu.VMEM((all_rows, width), f32),
                pltpu.VMEM((all_rows, width), bf16),
                pltpu.VMEM((all_rows, width), bf16),
                pltpu.VMEM((all_rows, width), f32),
                pltpu.VMEM((all_rows, width), f32),
                pltpu.VMEM((all_rows, hid), bf16),
                pltpu.VMEM((all_rows, hid), bf16),
                pltpu.VMEM((2, width, hid), bf16),
                pltpu.VMEM((2, hid, width), bf16),
                pltpu.VMEM((4, part, width), bf16),
                pltpu.VMEM((width, width), f32),
                pltpu.SemaphoreType.DMA((4, 2)),
                pltpu.SemaphoreType.DMA((4,)),
                pltpu.SemaphoreType.DMA((2, 2)),
                pltpu.SemaphoreType.DMA,
                pltpu.SemaphoreType.DMA((4,)),
            ],
        ),
        cost_estimate=cost(
            48 * all_rows * width * hid + 6 * all_rows * width * width, 40 * all_rows * width
        ),
        compiler_params=pltpu.CompilerParams(vmem_limit_bytes=62 * 2**20),
        name="ffn",
    )(meta, xo, xx, co, cx, am, at, gain, *wos, *ups, *downs)


def proj_body(count, meta, h_ref, *refs):
    parts, (w, dm, dt, g_ref, acc) = refs[: 3 * count], refs[3 * count :]
    b = pl.program_id(0)
    d = jnp.concatenate([r[...] for r in parts], axis=1)
    dh = dot(d, w[...], NT)
    own = lax.rem(b, 2) == core_of(meta)

    @pl.when(own)
    def _():
        dm[...] = dh

    @pl.when(jnp.logical_not(own))
    def _():
        dt[...] = dh.astype(bf16)

    pg = dot(h_ref[...], d, TN)

    @pl.when(b == 0)
    def _():
        acc[...] = pg

    @pl.when(b > 0)
    def _():
        acc[...] += pg

    @pl.when(b == pl.num_programs(0) - 1)
    def _():
        g_ref[...] = acc[...].astype(bf16)


def proj_call(meta, h, parts, w):
    length, width = h.shape
    cols = w.shape[1]
    B = length // 4
    blk = lambda n: pl.BlockSpec((B, n), lambda b, m: (b, 0))
    side = pl.BlockSpec((B, width), lambda b, m: (jnp.bitwise_xor(b // 2, x_of(m)), 0))
    g = pl.BlockSpec((width, cols), lambda b, m: (0, 0), pipeline_mode=pl.Buffered(1))
    return pl.pallas_call(
        functools.partial(proj_body, len(parts) // 3),
        out_shape=[
            sds((length // 2, width), f32),
            sds((length // 2, width), bf16),
            sds((width, cols), bf16),
        ],
        grid_spec=grid_spec(
            (4,),
            [blk(width)] + [blk(p.shape[1]) for p in parts] + [whole((width, cols))],
            [side, side, g],
            [pltpu.VMEM((width, cols), f32)],
        ),
        cost_estimate=cost(4 * length * width * cols, 12 * length * width),
        name="proj",
    )(meta, h, *parts, w)


def last_body(meta, xo, xx, dm, dt, dmid, gain, go, gx, gg):
    i = pl.program_id(0)
    per = pl.num_programs(0) // 2
    first = i < per
    x = jnp.where(first, xo[...], xx[...]).astype(f32)
    gn = gain[...].astype(f32)
    n, inv, _ = norm(x, gn)
    dh = dm[...] + dt[...].astype(f32)
    dn = dh * gn
    out = dmid[...] + inv * (dn - n * jnp.mean(dn * n, axis=-1, keepdims=True))

    @pl.when(first)
    def _():
        go[...] = out

    @pl.when(jnp.logical_not(first))
    def _():
        gx[...] = out.astype(bf16)

    ps = jnp.sum(dh * n, axis=0, keepdims=True)

    @pl.when(i == 0)
    def _():
        gg[...] = ps

    @pl.when(i > 0)
    def _():
        gg[...] += ps


def own_map(per):
    return lambda i, m: (jnp.minimum(i, per - 1), 0)


def nb_map(per):
    return lambda i, m: (jnp.maximum(i - per, 0), 0)


def last_call(meta, xo, xx, dm, dt, dmid, gain):
    rows, width = xo.shape
    per = rows // T
    fst, snd = pl.BlockSpec((T, width), own_map(per)), pl.BlockSpec((T, width), nb_map(per))
    blk = pl.BlockSpec((T, width), lambda i, m: (i, 0))
    return pl.pallas_call(
        last_body,
        out_shape=[sds((rows, width), f32), sds((rows, width), bf16), sds((1, width), f32)],
        grid_spec=grid_spec(
            (2 * per,),
            [fst, snd, blk, blk, blk, whole((1, width))],
            [fst, snd, pl.BlockSpec((1, width), lambda i, m: (0, 0))],
        ),
        cost_estimate=cost(40 * rows * width, 30 * rows * width),
        name="last",
    )(meta, xo, xx, dm, dt, dmid, gain)


def flip(size, bit):
    return [(i, i ^ bit) for i in range(size)]


def core_swap(v):
    return lax.ppermute(v, "head", CORE)


def x_swap(v):
    return lax.ppermute(v, "head", XNB)


def after(v, *deps):
    return lax.optimization_barrier((v, *deps))[0]


class DpSum:
    def __init__(self, terms, size):
        self.size = size
        self.y = lax.axis_index("dp") % 2
        self.groups = [[i for i in range(size) if i % 2 == k] for k in range(2)]
        half = terms[0].shape[0] // 2
        part = lambda k: sum(
            lax.dynamic_slice_in_dim(t, k * half, half, 0).astype(f32) for t in terms
        )
        self.send = part(1 - self.y).astype(bf16)
        self.keep = part(self.y)

    def y_swap(self, v):
        return lax.ppermute(v, "dp", flip(self.size, 1))

    def exchange(self, v):
        return lax.all_to_all(v, "dp", 0, 0, tiled=True, axis_index_groups=self.groups)

    def scatter_y(self):
        n = self.size // 2
        v = self.keep + self.y_swap(self.send).astype(f32)
        self.pieces = v.astype(bf16).reshape(n, v.shape[0] // n, v.shape[1])
        return self.pieces

    def scatter_rest(self):
        self.piece = jnp.sum(self.exchange(self.pieces).astype(f32), axis=0).astype(bf16)
        return self.piece

    def gather_rest(self):
        n = self.size // 2
        v = self.exchange(jnp.broadcast_to(self.piece[None], (n, *self.piece.shape)))
        self.part = v.reshape(-1, v.shape[2])
        return self.part

    def gather_y(self):
        got = self.y_swap(self.part)
        upper = self.y == 1
        lo, hi = jnp.where(upper, got, self.part), jnp.where(upper, self.part, got)
        return jnp.concatenate([lo, hi], axis=0).astype(f32)


def local(dp, inputs, lengths, w_query, w_key, w_value, w_out, w_up, w_down, conv_taps, gain_attn, gain_ff, cotangent):
    hd = lax.axis_index("head")
    x, c, y = hd // 2, hd % 2, lax.axis_index("dp") % 2
    width = inputs.shape[2]
    part = w_query.shape[0]
    half = 2 * part
    pick = lambda v, k: lax.dynamic_index_in_dim(v, k, 0, keepdims=False)
    y_swap = lambda v: lax.ppermute(v, "dp", flip(dp, 1))
    mask = (jnp.arange(2) == x)[:, None, None]
    order = lambda own, nb: jnp.where(mask, own[None], nb[None].astype(f32))
    meta = jnp.concatenate([lengths, jnp.stack([hd, y])]).astype(jnp.int32)
    gain1, gain2 = gain_attn.reshape(1, width), gain_ff.reshape(1, width)

    sides = [jnp.concatenate([w[:, k * half : k * half + half] for w in (w_query, w_key, w_value)], axis=1) for k in range(2)]
    tap_rows = jnp.where(
        (jnp.arange(2) == c)[None, None, :, None], conv_taps.transpose(1, 0, 2)[:, :, None, :], 0
    ).reshape(3, 3 * half)
    tap_rows = jnp.pad(tap_rows, ((0, 5), (0, 0)))
    w_mine = jnp.concatenate([jnp.where(c == 0, sides[0], sides[1]), tap_rows], axis=0)
    w_core = core_swap(jnp.concatenate([jnp.where(c == 0, sides[1], sides[0]), tap_rows], axis=0))
    w_got = x_swap(jnp.where(y == 0, w_mine, w_core))
    w_also = y_swap(w_got)
    x_own = pick(inputs, x)
    x_nb = x_swap(pick(inputs, 1 - x))
    x_core, x_cnb = core_swap(x_own), core_swap(x_nb)
    h1, raw, mix, w_full, taps = qkv_call(
        meta, (x_own, x_nb, x_core, x_cnb), (w_mine, w_core, w_got, w_also), gain1
    )

    rows = width // 2
    fetch = lambda w: x_swap(lax.dynamic_slice_in_dim(after(w, w_got, x_nb), y * rows, rows, 0))
    up_n, down_n = fetch(w_up), fetch(w_down)
    wo_n = x_swap(after(w_out, w_got, x_nb))
    c_own, c_nb = pick(cotangent, x), x_swap(after(pick(cotangent, 1 - x), w_got, x_nb))
    up_c, down_c, wo_c = core_swap(w_up), core_swap(w_down), core_swap(w_out)
    a_mine, a_send, lse = att_fwd_call(meta, mix)
    a_got = core_swap(a_send)
    up_m, down_m = y_swap(up_n), y_swap(down_n)
    up_n, down_n, wo_n, up_m, down_m = lax.optimization_barrier((up_n, down_n, wo_n, up_m, down_m, a_mine))[:5]
    wo_cn, up_cn, up_cm, down_cn, down_cm = [core_swap(v) for v in (wo_n, up_n, up_m, down_n, down_m)]
    out_own, out_nb, d_mine, d_send, gg2, dmid, gu_t, gu_m, gd_t, gd_m = ffn_call(
        meta, x_own, x_nb, c_own, c_nb, a_mine, a_got, gain2,
        (w_out, wo_c, wo_n, wo_cn),
        (w_up, up_c, up_n, up_m, up_cn, up_cm),
        (w_down, down_c, down_n, down_m, down_cn, down_cm),
    )
    d_got = core_swap(d_send)

    gu_c, gd_c = core_swap(gu_t), core_swap(gd_t)
    both = lambda a, b: (a.astype(f32) + b.astype(f32)).astype(bf16)
    nu, nd = both(gu_m[1], gu_c[1]), both(gd_m[1], gd_c[1])
    xu, xd = x_swap(nu), x_swap(after(nd, nu))
    q = att_bwd_call(meta, after(mix, nu, nd), raw, a_mine, a_send, d_mine, d_got, lse, taps, 0, width // 256)
    xu, xd = lax.optimization_barrier((xu, xd, q[0]))[:2]
    su = DpSum((gu_m[0], gu_c[0], xu), dp)
    sd = DpSum((gd_m[0], gd_c[0], xd), dp)
    dh_mine, dh_send, gp = proj_call(meta, after(h1, su.send, sd.send), q[:3], w_full)
    dh_got = core_swap(dh_send)

    piece = part // dp
    gp = lax.all_to_all(gp.reshape(4 * dp, piece, 3 * half), ("head", "dp"), 0, 0, tiled=True)
    u1 = su.scatter_y()
    d1 = sd.scatter_y()
    gi_own, gi_nb, gg1 = last_call(meta, x_own, x_nb, dh_mine, dh_got, after(dmid, u1), gain1)
    gi_got = x_swap(gi_nb)
    su.scatter_rest()
    sd.scatter_rest()
    su.gather_rest()
    sd.gather_rest()
    grad_up = su.gather_y()
    gd_all = sd.gather_y()
    grad_down, grad_out = gd_all[: w_down.shape[0]], gd_all[w_down.shape[0] :]
    gp = jnp.sum(gp.reshape(2, 2, dp, piece, 3 * half).astype(f32), axis=(0, 2)).astype(bf16)
    spread = jnp.broadcast_to(gp.reshape(1, 2 * piece, 3 * half), (dp, 2 * piece, 3 * half))
    got = lax.all_to_all(spread, "dp", 0, 0, tiled=True).reshape(dp, 2, piece, 3, half)
    grads = [
        jnp.concatenate([got[:, k, :, w].reshape(part, half) for k in range(2)], axis=1).astype(f32)
        for w in range(3)
    ]

    gt = q[3][:9].reshape(9, 2, part).transpose(1, 0, 2)
    gt = jnp.where(jnp.arange(2)[:, None, None, None] == c, gt[None], 0.0).reshape(4, 9, part)
    gains = jnp.concatenate([gg1, gg2], axis=0).reshape(2, 4, part).transpose(1, 0, 2)
    small = jnp.concatenate([gt, gains, jnp.zeros((4, 5, part), f32)], axis=1)
    small = jnp.broadcast_to(small[:, None], (4, dp, 16, part)).reshape(4 * dp, 16, part)
    small = after(small, spread)
    small = jnp.sum(lax.all_to_all(small, ("head", "dp"), 0, 0, tiled=True), axis=0)
    output = order(out_own, x_swap(out_nb))
    grad_input = order(gi_own, gi_got)
    return (
        output,
        grad_input,
        *grads,
        grad_out,
        grad_up,
        grad_down,
        small[:9].reshape(3, 3, part),
        small[9],
        small[10],
    )


def solution(mesh):
    placed = (
        P("dp", "head", None),
        P("dp"),
        P("head", None),
        P("head", None),
        P("head", None),
        P("head", None),
        P(None, "head"),
        P("head", None),
        P(None, None, "head"),
        P(),
        P(),
        P("dp", "head", None),
    )
    return jax.shard_map(
        functools.partial(local, mesh.shape["dp"]),
        mesh=mesh,
        in_specs=placed,
        out_specs=(
            P("dp", "head", None),
            P("dp", "head", None),
            P("head", None),
            P("head", None),
            P("head", None),
            P("head", None),
            P(None, "head"),
            P("head", None),
            P(None, None, "head"),
            P("head"),
            P("head"),
        ),
        check_vma=False,
    )
```

```python
import functools

import jax
import jax.numpy as jnp
from jax import lax
from jax.experimental import pallas as pl
from jax.experimental.pallas import tpu as pltpu
from jax.sharding import PartitionSpec as P

HDIM = 64
EPS = 1e-06
bf16 = jnp.bfloat16
f32 = jnp.float32

NN = (((1,), (0,)), ((), ()))
NT = (((1,), (1,)), ((), ()))
TN = (((0,), (0,)), ((), ()))

CORE = [(0, 1), (1, 0), (2, 3), (3, 2)]
XNB = [(0, 2), (2, 0), (1, 3), (3, 1)]


def dot(a, b, dims=NN):
    return lax.dot_general(a, b, dims, preferred_element_type=f32)


def cost(flops, nbytes, trans=0):
    return pl.CostEstimate(flops=int(flops), bytes_accessed=int(nbytes), transcendentals=int(trans))


def sds(shape, dtype):
    return jax.ShapeDtypeStruct(shape, dtype)


def whole(shape):
    zeros = (0,) * len(shape)
    return pl.BlockSpec(shape, lambda *_: zeros, pipeline_mode=pl.Buffered(1))


def grid_spec(grid, ins, outs, scratch=()):
    return pltpu.PrefetchScalarGridSpec(
        num_scalar_prefetch=1, grid=grid, in_specs=ins, out_specs=outs, scratch_shapes=scratch
    )


def length_of(m):
    return m[m[2] // 2]


def x_of(m):
    return m[2] // 2


def core_of(m):
    return lax.rem(m[2], 2)


def norm(x, gain):
    inv = lax.rsqrt(jnp.mean(x * x, axis=-1, keepdims=True) + EPS)
    n = x * inv
    return n, inv, (n * gain).astype(bf16)


def qkv_body(meta, x0, x1, x2, x3, wa, wb, wc, wd, gain, h_ref, raw_ref, mix_ref, w_ref, taps, ext):
    b = pl.program_id(0)
    rows = x0.shape[0]
    part = w_ref.shape[0] // 4
    hd = meta[2]

    @pl.when(b == 0)
    def _():
        for k, piece in enumerate((wa, wb, wc, wd)):
            at = jnp.bitwise_xor(hd, k)
            w_ref[pl.ds(pl.multiple_of(at * part, 64), part), :] = piece[0:part, :]
        near = (wa[part:, :] + wb[part:, :]).astype(f32)
        far = (wc[part:, :] + wd[part:, :]).astype(f32)
        taps[...] = jnp.where(x_of(meta) == core_of(meta), near, far)
        ext[0:8, :] = jnp.zeros((8, ext.shape[1]), f32)

    v = jnp.bitwise_xor(hd, b)
    slot = lax.rem(v, 2) * 2 + v // 2
    x = x0[...]
    for k, other in ((1, x1), (2, x2), (3, x3)):
        x = jnp.where(slot == k, other[...], x)
    _, _, h = norm(x.astype(f32), gain[...].astype(f32))
    h_ref[...] = h
    raw = dot(h, w_ref[...]).astype(bf16)
    raw_ref[...] = raw
    rawf = raw.astype(f32)
    ext[8 : 8 + rows, :] = rawf
    t = taps[...]
    mixed = t[0:1] * rawf + t[1:2] * ext[7 : 7 + rows, :] + t[2:3] * ext[6 : 6 + rows, :]
    mix_ref[...] = mixed.astype(bf16)
    ext[0:8, :] = ext[rows : rows + 8, :]


def qkv_call(meta, xs, ws, gain):
    rows, width = xs[0].shape
    tall, cols = ws[0].shape
    length = 4 * rows
    blk = lambda n: pl.BlockSpec((rows, n), lambda b, m: (b, 0))
    const = lambda r: pl.BlockSpec((r, cols), lambda b, m: (0, 0))
    return pl.pallas_call(
        qkv_body,
        out_shape=[
            sds((length, width), bf16),
            sds((length, cols), bf16),
            sds((length, cols), bf16),
            sds((width, cols), bf16),
            sds((8, cols), f32),
        ],
        grid_spec=grid_spec(
            (4,),
            [whole((rows, width))] * 4 + [whole((tall, cols))] * 4 + [whole((1, width))],
            [blk(width), blk(cols), blk(cols), const(width), const(8)],
            [pltpu.VMEM((rows + 8, cols), f32)],
        ),
        cost_estimate=cost(2 * length * width * cols, 2 * length * (width * 2 + cols * 2)),
        name="qkv",
    )(meta, *xs, *ws, gain)


def two_heads(v):
    lane = lax.broadcasted_iota(jnp.int32, v.shape, 1)
    z = jnp.zeros_like(v)
    return jnp.concatenate([jnp.where(lane < HDIM, v, z), jnp.where(lane < HDIM, z, v)], axis=0)


def causal(first, keys, start, queries):
    key = first + lax.broadcasted_iota(jnp.int32, (keys, queries), 0)
    ok = key <= start + lax.broadcasted_iota(jnp.int32, (keys, queries), 1)
    return jnp.concatenate([ok, ok], axis=1)


def upper(v, axis):
    B = v.shape[axis] // 2
    h = B // 2
    if axis == 0:
        return jnp.concatenate([v[h:B], v[B + h :]], axis=0)
    return jnp.concatenate([v[:, h:B], v[:, B + h :]], axis=1)


def with_bias(k_ref, ka, length):
    L = k_ref.shape[0]
    ka[:, :128] = k_ref[...]
    lane = lax.broadcasted_iota(jnp.int32, (L, 128), 1)
    row = lax.broadcasted_iota(jnp.int32, (L, 128), 0)
    pad = jnp.logical_and(lane == 0, row >= length)
    ka[:, 128:] = jnp.where(pad, -1e9, 0.0).astype(bf16)


def biased(q):
    qq = two_heads(q)
    lane = lax.broadcasted_iota(jnp.int32, qq.shape, 1)
    return jnp.concatenate([qq, jnp.where(lane == 0, 1.0, 0.0).astype(bf16)], axis=1)


def att_fwd_body(meta, q_ref, k_ref, v_ref, mine_ref, theirs_ref, lse_ref, ka, vt, sc):
    i = pl.program_id(1)
    B = q_ref.shape[0]

    @pl.when(i == 0)
    def _():
        vt[...] = v_ref[...].T
        with_bias(k_ref, ka, length_of(meta))

    qq = biased(q_ref[...] * bf16(HDIM**-0.5))
    own = lax.rem(i, 2) == core_of(meta)

    def run(ii):
        m = None
        for j in range(ii + 1):
            ks = slice(j * B, j * B + B)
            s = dot(ka[ks, :], qq, NT)
            if j == ii:
                s = jnp.where(causal(0, B, 0, B), s, -1e9)
            sc[ks, :] = s
            mj = jnp.max(s, axis=0, keepdims=True)
            m = mj if m is None else jnp.maximum(m, mj)
        l = jnp.zeros((1, 2 * B), f32)
        acc = [jnp.zeros((HDIM, B), f32)] * 2
        for j in range(ii + 1):
            ks = slice(j * B, j * B + B)
            p = jnp.exp(sc[ks, :] - m)
            l = l + jnp.sum(p, axis=0, keepdims=True)
            pb = p.astype(bf16)
            for h in range(2):
                r = slice(HDIM * h, HDIM * h + HDIM)
                acc[h] = acc[h] + dot(vt[r, ks], pb[:, h * B : h * B + B])
        inv = 1.0 / l
        out = jnp.concatenate([acc[h] * inv[:, h * B : h * B + B] for h in range(2)], axis=0)
        out = out.T.astype(bf16)

        @pl.when(own)
        def _():
            mine_ref[...] = out

        @pl.when(jnp.logical_not(own))
        def _():
            theirs_ref[...] = out

        ls = m + jnp.log(l)
        lse_ref[0] = jnp.concatenate([ls[:, :B], ls[:, B:]], axis=0)

    for ii in range(4):
        pl.when(i == ii)(functools.partial(run, ii))


def half_map(p, i, m):
    return (jnp.bitwise_xor(i // 2, x_of(m)), p)


def att_fwd_call(meta, mix):
    length, cols = mix.shape
    width = cols // 3
    pairs = width // 128
    B = length // 4
    half = pl.BlockSpec((B, 128), half_map)
    return pl.pallas_call(
        att_fwd_body,
        out_shape=[
            sds((length // 2, width), bf16),
            sds((length // 2, width), bf16),
            sds((pairs, 2, length), f32),
        ],
        grid_spec=grid_spec(
            (pairs, 4),
            [
                pl.BlockSpec((B, 128), lambda p, i, m: (i, p)),
                pl.BlockSpec((length, 128), lambda p, i, m: (0, pairs + p)),
                pl.BlockSpec((length, 128), lambda p, i, m: (0, 2 * pairs + p)),
            ],
            [half, half, pl.BlockSpec((1, 2, B), lambda p, i, m: (p, 0, i))],
            [
                pltpu.VMEM((length, 256), bf16),
                pltpu.VMEM((128, length), bf16),
                pltpu.VMEM((length, 2 * B), f32),
            ],
        ),
        cost_estimate=cost(8 * length * length * width, 8 * length * width, 2 * length * length * pairs),
        name="attn_fwd",
    )(meta, mix, mix, mix)


def att_bwd_body(
    p0, aliased, meta, q_ref, k_ref, v_ref, om, ot, dm, dt, lse_ref, rq, rk, rv, taps, *refs
):
    g_ref, gt, ka, kt, dkt, dvt, dqs, ext, stage, sem = refs[1:] if aliased else refs
    i = pl.program_id(1)
    B = q_ref.shape[0]
    L = k_ref.shape[0]
    H = B // 2

    @pl.when(i == 0)
    def _():
        kt[...] = k_ref[...].T
        with_bias(k_ref, ka, length_of(meta))

    own = lax.rem(i, 2) == core_of(meta)
    q = q_ref[...] * bf16(HDIM**-0.5)
    o = jnp.where(own, om[...], ot[...])
    do = jnp.where(own, dm[...], dt[...])
    qq, dd = biased(q), two_heads(do)
    qt, dot_ = q.T, do.T
    od = (o.astype(f32) * do.astype(f32)).T
    delta = jnp.concatenate(
        [jnp.sum(od[:HDIM], axis=0, keepdims=True), jnp.sum(od[HDIM:], axis=0, keepdims=True)],
        axis=1,
    )
    ls = lse_ref[0]
    lse = jnp.concatenate([ls[0:1], ls[1:2]], axis=1)

    def run(ii):
        dq = [jnp.zeros((HDIM, B), f32)] * 2

        def tile(st, n, lo, diagonal):
            w = B - lo
            ks = slice(st, st + n)
            part = upper if lo else lambda v, axis: v
            s = dot(ka[ks, :], part(qq, 0), NT)
            dp = dot(v_ref[ks, :], part(dd, 0), NT)
            p = jnp.exp(s - part(lse, 1))
            if diagonal:
                p = jnp.where(causal(lo, n, lo, w), p, 0.0)
            ds = (p * (dp - part(delta, 1))).astype(bf16)
            pb = p.astype(bf16)
            for h in range(2):
                r, c = slice(HDIM * h, HDIM * h + HDIM), slice(h * w, h * w + w)
                x = dot(kt[r, ks], ds[:, c])
                if lo:
                    x = jnp.concatenate([jnp.zeros((HDIM, lo), f32), x], axis=1)
                dq[h] = dq[h] + x
                a = dot(qt[r, lo:], ds[:, c], NT)
                b = dot(dot_[r, lo:], pb[:, c], NT)
                if diagonal:
                    dkt[r, ks] = a
                    dvt[r, ks] = b
                else:
                    dkt[r, ks] += a
                    dvt[r, ks] += b

        for j in range(ii):
            tile(j * B, B, 0, False)
        tile(ii * B, H, 0, True)
        tile(ii * B + H, H, H, True)
        dqs[ii * B : ii * B + B, :] = jnp.concatenate(dq, axis=0).T * HDIM**-0.5

    for ii in range(4):
        pl.when(i == ii)(functools.partial(run, ii))

    def copies(pair):
        width = g_ref.shape[1] // 3
        return [
            pltpu.make_async_copy(
                stage.at[k],
                g_ref.at[:, pl.ds(pl.multiple_of(k * width + (p0 + pair) * 128, 128), 128)],
                sem.at[k],
            )
            for k in range(3)
        ]

    @pl.when(i == pl.num_programs(1) - 1)
    def _():
        pair = pl.program_id(0)
        gt[...] = jnp.zeros_like(gt)
        ext[...] = jnp.zeros_like(ext)

        @pl.when(pair > 0)
        def _():
            for cp in copies(pair):
                cp.wait()

        def back(n, carry):
            blk = L // B - 1 - n
            sl = pl.ds(pl.multiple_of(blk * B, B), B)
            for which, raw in enumerate((rq, rk, rv)):
                col = which * (taps.shape[1] // 3) + (p0 + pl.program_id(0)) * 128
                t = taps[:, pl.ds(pl.multiple_of(col, 128), 128)]
                g = dqs[sl, :] if which == 0 else (dkt, dvt)[which - 1][:, sl].T
                ext[which, B : B + 8, :] = ext[which, 0:8, :]
                ext[which, 0:B, :] = g
                g1, g2 = ext[which, 1 : B + 1, :], ext[which, 2 : B + 2, :]
                stage[which, sl, :] = (t[0:1] * g + t[1:2] * g1 + t[2:3] * g2).astype(bf16)
                r = raw[sl, :].astype(f32)
                for k, gg in enumerate((g, g1, g2)):
                    row = slice(3 * which + k, 3 * which + k + 1)
                    gt[row, :] += jnp.sum(r * gg, axis=0, keepdims=True)
            return carry

        lax.fori_loop(0, L // B, back, 0)
        for cp in copies(pair):
            cp.start()

        @pl.when(pair == pl.num_programs(0) - 1)
        def _():
            for cp in copies(pair):
                cp.wait()


def att_bwd_call(meta, mix, raw, om, ot, dm, dt, lse, taps, p0, count, into=None):
    length, cols = mix.shape
    pairs = cols // 384
    B = length // 4
    half = pl.BlockSpec((B, 128), lambda p, i, m: (jnp.bitwise_xor(i // 2, x_of(m)), p0 + p))
    full = lambda k: pl.BlockSpec((length, 128), lambda p, i, m: (0, k * pairs + p0 + p))
    return pl.pallas_call(
        functools.partial(att_bwd_body, p0, into is not None),
        out_shape=[sds((length, cols), bf16), sds((16, 128 * count), f32)],
        grid_spec=grid_spec(
            (count, 4),
            [
                pl.BlockSpec((B, 128), lambda p, i, m: (i, p0 + p)),
                full(1),
                full(2),
                half,
                half,
                half,
                half,
                pl.BlockSpec((1, 2, B), lambda p, i, m: (p0 + p, 0, i)),
                full(0),
                full(1),
                full(2),
                whole((8, cols)),
            ]
            + ([] if into is None else [pl.BlockSpec(memory_space=pl.ANY)]),
            [pl.BlockSpec(memory_space=pl.ANY), pl.BlockSpec((16, 128), lambda p, i, m: (0, p))],
            [
                pltpu.VMEM((length, 256), bf16),
                pltpu.VMEM((128, length), bf16),
                pltpu.VMEM((128, length), f32),
                pltpu.VMEM((128, length), f32),
                pltpu.VMEM((length, 128), f32),
                pltpu.VMEM((3, B + 8, 128), f32),
                pltpu.VMEM((3, length, 128), bf16),
                pltpu.SemaphoreType.DMA((3,)),
            ],
        ),
        cost_estimate=cost(
            14 * length * length * 128 * count, 20 * length * 128 * count, 2 * length * length * count
        ),
        name="attn_bwd",
        input_output_aliases={} if into is None else {13: 0},
    )(meta, mix, mix, mix, om, ot, dm, dt, lse, raw, raw, raw, taps, *([] if into is None else [into]))


T = 256


def valid_rows(meta, i, rows):
    per = rows // T
    block = jnp.where(i < per, meta[2], jnp.bitwise_xor(meta[2], 2))
    start = block * rows + lax.rem(i, per) * T
    return start + lax.broadcasted_iota(jnp.int32, (T, 1), 0) < length_of(meta)


def ffn_body(
    meta, xo, xx, co, cx, am, at, gain, wo_o, wo_c, wo_n, wo_cn,
    u_o, d_o, f_c, n0, n1, n2, n3, c0, c1, c2, c3,
    oo, ox, dm, dt, gg, dmid, gu0, gu1, gu2, gu3, gd0, gd1, gd2, gd3,
    wo, wus, wds, mid, h_s, g_s, fo, dh, act, du, stu, std, sto, gacc, sw, so, sg, sd, st,
):
    rows, width = xo.shape
    part = wo_o.shape[0]
    half = 2 * part
    n = 2 * rows // T
    per = rows // T
    copies = []
    for k, src in ((0, wo_o), (1, wo_c), (2, wo_n), (3, wo_cn)):
        shard = jnp.bitwise_xor(meta[2], k)
        row = jnp.where(shard // 2 == core_of(meta), 0, half) + lax.rem(shard, 2) * part
        cp = pltpu.make_async_copy(src, wo.at[pl.ds(pl.multiple_of(row, 64), part), :], so.at[k])
        cp.start()
        copies.append(cp)
    for k, pair in ((0, (f_c.at[0], f_c.at[1])), (2, (u_o, d_o))):
        for n_, src in enumerate(pair):
            pltpu.make_async_copy(src, (wus, wds)[n_].at[k], sw.at[k, n_]).start()
    for k, quarters in ((1, (c0, c1, c2, c3)), (3, (n0, n1, n2, n3))):
        for q_, src in enumerate(quarters):
            count = src.shape[1]
            to = pl.ds(pl.multiple_of(jnp.bitwise_xor(meta[3], q_) * count, 64), count)
            for n_, dst in enumerate((wus, wds)):
                pltpu.make_async_copy(src.at[n_], dst.at[k, to, :], sw.at[k, n_]).start()
    for cp in copies:
        cp.wait()
    gn = gain[...].astype(f32)

    def first_rows(i, carry):
        sl = pl.ds(pl.multiple_of(i * T, T), T)
        src = pl.ds(pl.multiple_of(lax.rem(i, per) * T, T), T)
        own = i < per
        x = jnp.where(own, xo[src, :], xx[src, :]).astype(f32)
        a = jnp.concatenate([am[sl, :], at[sl, :]], axis=1)
        m = x + dot(a, wo[...])
        mid[sl, :] = m
        fo[sl, :] = m
        h_s[sl, :] = norm(m, gn)[2]
        ct = jnp.where(own, co[src, :], cx[src, :])
        g_s[sl, :] = jnp.where(valid_rows(meta, i, rows), ct, jnp.zeros_like(ct))
        dh[sl, :] = jnp.zeros((T, width), f32)
        return carry

    lax.fori_loop(0, n, first_rows, 0)

    R = 1024
    C = 768

    gus, gds = (gu0, gu1, gu2, gu3), (gd0, gd1, gd2, gd3)

    def stores(n_, slot):
        return [
            pltpu.make_async_copy(stu.at[slot], gus[n_], sg.at[slot, 0]),
            pltpu.make_async_copy(std.at[slot], gds[n_].at[pl.ds(0, width), :], sg.at[slot, 1]),
        ]

    def shard(k, carry):
        for cp in (
            pltpu.make_async_copy(u_o, wus.at[k], sw.at[k, 0]),
            pltpu.make_async_copy(d_o, wds.at[k], sw.at[k, 1]),
        ):
            cp.wait()

        def rows_step(t, c2):
            sl = pl.ds(pl.multiple_of(t * R, R), R)
            h, g = h_s[sl, :], g_s[sl, :]
            r = jnp.maximum(dot(h, wus[k]), 0.0)
            a = (r * r).astype(bf16)
            d = (dot(g, wds[k], NT) * 2.0 * r).astype(bf16)
            act[sl, :] = a
            du[sl, :] = d
            fo[sl, :] += dot(a, wds[k])
            dh[sl, :] += dot(d, wus[k], NT)
            return c2

        lax.fori_loop(0, 2 * rows // R, rows_step, 0)
        slot = lax.rem(k, 2)

        @pl.when(k >= 2)
        def _():
            for cp in stores(0, slot):
                cp.wait()

        def cols_step(t, c2):
            sl = pl.ds(pl.multiple_of(t * C, C), C)
            stu[slot, :, sl] = dot(h_s[...], du[:, sl], TN).astype(bf16)
            std[slot, sl, :] = dot(act[:, sl], g_s[...], TN).astype(bf16)
            return c2

        lax.fori_loop(0, width // C, cols_step, 0)
        for n_ in range(4):

            @pl.when(k == n_)
            def _(n_=n_):
                for cp in stores(n_, n_ % 2):
                    cp.start()

        return carry

    lax.fori_loop(0, 4, shard, 0)
    gg[...] = jnp.zeros_like(gg)

    def last_rows(i, carry):
        sl = pl.ds(pl.multiple_of(i * T, T), T)
        dst = pl.ds(pl.multiple_of(lax.rem(i, per) * T, T), T)
        ok = valid_rows(meta, i, rows)
        m = mid[sl, :]
        out = jnp.where(ok, fo[sl, :], 0.0)

        fo[sl, :] = out

        @pl.when(i < per)
        def _():
            own = oo.at[meta[2] // 2, dst, :]
            pltpu.make_async_copy(fo.at[sl, :], own, sd.at[1]).start()

        @pl.when(i >= per)
        def _():
            ox[dst, :] = out.astype(bf16)

        nm, inv, _ = norm(m, gn)
        d = dh[sl, :]
        dn = d * gn
        r = g_s[sl, :].astype(f32) + inv * (dn - nm * jnp.mean(dn * nm, axis=-1, keepdims=True))
        mid[sl, :] = r
        pltpu.make_async_copy(mid.at[sl, :], dmid.at[sl, :], sd.at[0]).start()
        db = r.astype(bf16)
        du[sl, :] = db
        da = dot(db, wo[...], NT).astype(bf16)
        dm[sl, :] = da[:, :half]
        dt[sl, :] = da[:, half:]
        gg[...] += jnp.sum(d * nm, axis=0, keepdims=True)
        return carry

    lax.fori_loop(0, n, last_rows, 0)
    gacc[0:half, :] = dot(am[...], du[...], TN)
    gacc[half:, :] = dot(at[...], du[...], TN)
    outs = [
        pltpu.make_async_copy(mid, dmid, sd.at[0]),
        pltpu.make_async_copy(fo.at[pl.ds(0, rows), :], oo.at[meta[2] // 2], sd.at[1]),
    ]
    for k, k_ in enumerate((1, 3, 0, 2)):
        shard_ = jnp.bitwise_xor(meta[2], k_)
        row = jnp.where(shard_ // 2 == core_of(meta), 0, half) + lax.rem(shard_, 2) * part
        sto[k] = gacc[pl.ds(pl.multiple_of(row, 64), part), :].astype(bf16)
        cp = pltpu.make_async_copy(sto.at[k], gds[k].at[pl.ds(width, part), :], st.at[k])
        cp.start()
        outs.append(cp)
    for slot in range(2):
        outs.extend(stores(2 + slot, slot))
    for cp in outs:
        cp.wait()


def ffn_call(meta, xo, xx, co, cx, am, at, gain, wos, ffs):
    rows, width = xo.shape
    half = am.shape[1]
    part = half // 2
    hid = ffs[0].shape[1]
    hbm = pl.BlockSpec(memory_space=pl.ANY)
    vm = lambda *shape: whole(shape)
    all_rows = 2 * rows
    return pl.pallas_call(
        ffn_body,
        out_shape=[
            sds((2, rows, width), f32),
            sds((rows, width), bf16),
            sds((all_rows, half), bf16),
            sds((all_rows, half), bf16),
            sds((1, width), f32),
            sds((all_rows, width), f32),
        ]
        + [sds((width, hid), bf16)] * 4
        + [sds((hid + part, width), bf16)] * 4,
        grid_spec=grid_spec(
            (1,),
            [vm(rows, width)] * 4 + [vm(all_rows, half)] * 2 + [vm(1, width)] + [hbm] * 15,
            [
                hbm,
                vm(rows, width),
                vm(all_rows, half),
                vm(all_rows, half),
                vm(1, width),
            ]
            + [hbm] * 9,
            [
                pltpu.VMEM((width, width), bf16),
                pltpu.VMEM((4, width, hid), bf16),
                pltpu.VMEM((4, hid, width), bf16),
                pltpu.VMEM((all_rows, width), f32),
                pltpu.VMEM((all_rows, width), bf16),
                pltpu.VMEM((all_rows, width), bf16),
                pltpu.VMEM((all_rows, width), f32),
                pltpu.VMEM((all_rows, width), f32),
                pltpu.VMEM((all_rows, hid), bf16),
                pltpu.VMEM((all_rows, hid), bf16),
                pltpu.VMEM((2, width, hid), bf16),
                pltpu.VMEM((2, hid, width), bf16),
                pltpu.VMEM((4, part, width), bf16),
                pltpu.VMEM((width, width), f32),
                pltpu.SemaphoreType.DMA((4, 2)),
                pltpu.SemaphoreType.DMA((4,)),
                pltpu.SemaphoreType.DMA((2, 2)),
                pltpu.SemaphoreType.DMA((2,)),
                pltpu.SemaphoreType.DMA((4,)),
            ],
        ),
        cost_estimate=cost(
            48 * all_rows * width * hid + 6 * all_rows * width * width, 40 * all_rows * width
        ),
        compiler_params=pltpu.CompilerParams(vmem_limit_bytes=62 * 2**20),
        name="ffn",
    )(meta, xo, xx, co, cx, am, at, gain, *wos, *ffs)


def projg_body(meta, h, d, keep, far, send, also, acc):
    acc[...] = dot(h[...], d[...], TN)
    part = keep.shape[0]
    for ref, k in ((keep, 0), (far, 2), (send, 1), (also, 3)):
        at = jnp.bitwise_xor(meta[2], k)
        ref[...] = acc[pl.ds(pl.multiple_of(at * part, 64), part), :].astype(bf16)


def projg_call(meta, h, d):
    length, width = h.shape
    cols = d.shape[1]
    step = cols // 3
    g = pl.BlockSpec((width // 4, step), lambda j, m: (0, j))
    return pl.pallas_call(
        projg_body,
        out_shape=[sds((width // 4, cols), bf16)] * 4,
        grid_spec=grid_spec(
            (3,),
            [whole((length, width)), pl.BlockSpec((length, step), lambda j, m: (0, j))],
            [g] * 4,
            [pltpu.VMEM((width, step), f32)],
        ),
        cost_estimate=cost(2 * length * width * cols, 2 * length * (width + cols)),
        name="projg",
    )(meta, h, d)


def projd_body(meta, d, w, dm, dt):
    dh = dot(d[...], w[...], NT)
    own = lax.rem(pl.program_id(0), 2) == core_of(meta)

    @pl.when(own)
    def _():
        dm[...] = dh

    @pl.when(jnp.logical_not(own))
    def _():
        dt[...] = dh.astype(bf16)


def projd_call(meta, d, w):
    length, cols = d.shape
    width = w.shape[0]
    B = length // 4
    side = pl.BlockSpec((B, width), lambda b, m: (jnp.bitwise_xor(b // 2, x_of(m)), 0))
    return pl.pallas_call(
        projd_body,
        out_shape=[sds((length // 2, width), f32), sds((length // 2, width), bf16)],
        grid_spec=grid_spec(
            (4,),
            [pl.BlockSpec((B, cols), lambda b, m: (b, 0)), whole((width, cols))],
            [side, side],
        ),
        cost_estimate=cost(2 * length * width * cols, 12 * length * width),
        name="projd",
    )(meta, d, w)


def last_body(meta, xo, xx, dm, dt, dmid, gain, go, gx, gg):
    i = pl.program_id(0)
    per = pl.num_programs(0) // 2
    first = i < per
    x = jnp.where(first, xo[...], xx[...]).astype(f32)
    gn = gain[...].astype(f32)
    n, inv, _ = norm(x, gn)
    dh = dm[...] + dt[...].astype(f32)
    dn = dh * gn
    out = dmid[...] + inv * (dn - n * jnp.mean(dn * n, axis=-1, keepdims=True))

    @pl.when(first)
    def _():
        go[0] = out

    @pl.when(jnp.logical_not(first))
    def _():
        gx[...] = out.astype(bf16)

    ps = jnp.sum(dh * n, axis=0, keepdims=True)

    @pl.when(i == 0)
    def _():
        gg[...] = ps

    @pl.when(i > 0)
    def _():
        gg[...] += ps


def own_map(per):
    return lambda i, m: (jnp.minimum(i, per - 1), 0)


def nb_map(per):
    return lambda i, m: (jnp.maximum(i - per, 0), 0)


def last_call(meta, xo, xx, dm, dt, dmid, gain):
    rows, width = xo.shape
    per = rows // T
    fst, snd = pl.BlockSpec((T, width), own_map(per)), pl.BlockSpec((T, width), nb_map(per))
    blk = pl.BlockSpec((T, width), lambda i, m: (i, 0))
    return pl.pallas_call(
        last_body,
        out_shape=[sds((2, rows, width), f32), sds((rows, width), bf16), sds((1, width), f32)],
        grid_spec=grid_spec(
            (2 * per,),
            [fst, snd, blk, blk, blk, whole((1, width))],
            [pl.BlockSpec((1, T, width), lambda i, m: (x_of(m), jnp.minimum(i, per - 1), 0)), snd, pl.BlockSpec((1, width), lambda i, m: (0, 0))],
        ),
        cost_estimate=cost(40 * rows * width, 30 * rows * width),
        name="last",
    )(meta, xo, xx, dm, dt, dmid, gain)


def flip(size, bit):
    return [(i, i ^ bit) for i in range(size)]


def core_swap(v):
    return lax.ppermute(v, "head", CORE)


def x_swap(v):
    return lax.ppermute(v, "head", XNB)


def after(v, *deps):
    return lax.optimization_barrier((v, *deps))[0]


def halve(terms, index, count):
    rows = terms[0].shape[0] // count
    piece = lambda t, k: lax.dynamic_slice_in_dim(t, jnp.bitwise_xor(index, k) * rows, rows, 0)
    total = lambda k: sum(piece(t, k).astype(f32) for t in terms)
    return [total(k).astype(bf16) for k in range(1, count)], total(0)


def strides(dp):
    out = [1]
    while 2 * out[-1] < dp:
        out.append(2 * out[-1])
    return out


def side(stride):
    return lax.axis_index("dp") // stride % 2


def swap(v, stride, dp):
    return lax.ppermute(v, "dp", flip(dp, stride))


def scatter(terms, stride, dp):
    (send,), keep = halve(terms, side(stride), 2)
    return [keep, swap(send, stride, dp)], send


def gather(v, stride, dp):
    got = swap(v, stride, dp)
    upper = side(stride) == 1
    return jnp.concatenate([jnp.where(upper, got, v), jnp.where(upper, v, got)], axis=0)


def total(terms):
    return sum(t.astype(f32) for t in terms)


def local(dp, inputs, lengths, w_query, w_key, w_value, w_out, w_up, w_down, conv_taps, gain_attn, gain_ff, cotangent):
    hd = lax.axis_index("head")
    x, c, y = hd // 2, hd % 2, lax.axis_index("dp") % 2
    q = lax.axis_index("dp") % 4
    width = inputs.shape[2]
    part = w_query.shape[0]
    half = 2 * part
    pick = lambda v, k: lax.dynamic_index_in_dim(v, k, 0, keepdims=False)
    y_swap = lambda v: lax.ppermute(v, "dp", flip(dp, 1))
    order = lambda own, nb: lax.dynamic_update_slice_in_dim(own, nb[None].astype(f32), 1 - x, 0)
    meta = jnp.concatenate([lengths, jnp.stack([hd, q])]).astype(jnp.int32)
    gain1, gain2 = gain_attn.reshape(1, width), gain_ff.reshape(1, width)

    sides = [jnp.concatenate([w[:, k * half : k * half + half] for w in (w_query, w_key, w_value)], axis=1) for k in range(2)]
    tap_rows = jnp.where(
        (jnp.arange(2) == c)[None, None, :, None], conv_taps.transpose(1, 0, 2)[:, :, None, :], 0
    ).reshape(3, 3 * half)
    tap_rows = jnp.pad(tap_rows, ((0, 5), (0, 0)))
    w_mine = jnp.concatenate([jnp.where(c == 0, sides[0], sides[1]), tap_rows], axis=0)
    w_core = core_swap(jnp.concatenate([jnp.where(c == 0, sides[1], sides[0]), tap_rows], axis=0))
    w_nb, w_cnb = x_swap(w_mine), x_swap(w_core)
    x_own = pick(inputs, x)
    x_nb = x_swap(pick(inputs, 1 - x))
    x_core, x_cnb = core_swap(x_own), core_swap(x_nb)
    h1, raw, mix, w_full, taps = qkv_call(
        meta, (x_own, x_nb, x_core, x_cnb), (w_mine, w_core, w_nb, w_cnb), gain1
    )

    rows = width // 4
    quarter = lambda w: lax.dynamic_slice_in_dim(w, q * rows, rows, 0)
    ff_n = [x_swap(after(jnp.stack([quarter(w_up), quarter(w_down)]), w_nb, w_cnb, x_nb))]
    ff_c = core_swap(jnp.stack([after(w_up, w_nb), w_down]))
    wo_c = core_swap(w_out)
    ff_n += [swap(ff_n[0], k, dp) for k in (1, 2, 3)]
    c_own = pick(cotangent, x)
    wo_n = x_swap(after(w_out, ff_n[0]))
    c_nb = x_swap(after(pick(cotangent, 1 - x), ff_n[0]))
    a_mine, a_send, lse = att_fwd_call(meta, after(mix, ff_n[0], ff_c, wo_c))
    a_got = core_swap(a_send)
    *others, wo_n, c_nb = lax.optimization_barrier((*ff_n[1:], wo_n, c_nb, a_mine))[:-1]
    ff_n = [ff_n[0], *others]
    ff_cn = [core_swap(v) for v in ff_n]
    wo_cn = core_swap(wo_n)
    out_own, out_nb, d_mine, d_send, gg2, dmid, *gw = ffn_call(
        meta, x_own, x_nb, c_own, c_nb, a_mine, a_got, gain2,
        (w_out, wo_c, wo_n, wo_cn),
        (w_up, w_down, ff_c, *ff_n, *ff_cn),
    )
    d_got = core_swap(d_send)

    _, *rest = strides(dp)
    un, dn, do, uo = [core_swap(gw[k]) for k in (1, 5, 4, 0)]
    nu = total((gw[3], un)).astype(bf16)
    xu = x_swap(nu)
    (dn_send,), dn_keep = halve((gw[7], dn), y, 2)
    (do_send,), do_keep = halve((gw[6], do), y, 2)
    yn, yo = y_swap(dn_send), y_swap(do_send)
    out_x = x_swap(after(out_nb, nu))
    pairs = width // 256
    bwd = lambda m, p, n, into: att_bwd_call(
        meta, m, raw, a_mine, a_send, d_mine, d_got, lse, taps, p, n, into
    )
    dall, gt_a = bwd(after(mix, nu, dn_send, do_send), 0, pairs - 1, None)
    xu, yn, yo, out_x = lax.optimization_barrier((xu, yn, yo, out_x, dall))[:4]
    (u_send,), u_keep = halve((gw[2], uo, xu), y, 2)
    nd = total((dn_keep, yn)).astype(bf16)
    yu, xd = y_swap(u_send), x_swap(nd)
    dall, gt_b = bwd(after(mix, u_send, nd), pairs - 1, 1, dall)
    gt = jnp.concatenate([gt_a, gt_b], axis=1)
    yu, xd = lax.optimization_barrier((yu, xd, gt_b))[:2]
    ut, u_send = scatter([u_keep, yu], rest[0], dp)
    dt, d_send = scatter([do_keep, yo, xd], rest[0], dp)
    keep, far, send, also = projg_call(meta, after(h1, u_send, d_send), dall)
    *both, _ = lax.optimization_barrier((*ut, *dt, keep))
    far = x_swap(far)
    got, got_n = core_swap(send), core_swap(also)
    ut, u_send = scatter(both[:2], rest[1], dp)
    dt, d_send = scatter(both[2:], rest[1], dp)
    far2 = x_swap(got_n)
    dh_mine, dh_send = projd_call(meta, after(dall, u_send, d_send, got_n), w_full)
    dh_got = core_swap(dh_send)
    *both, far, far2 = lax.optimization_barrier((*ut, *dt, far, far2, dh_mine))[:-1]
    ut, dt = both[:2], both[2:]
    ga, gb = keep.astype(f32) + far.astype(f32), got.astype(f32) + far2.astype(f32)
    g_send, g_keep = jnp.where(y == 0, gb, ga).astype(bf16), jnp.where(y == 0, ga, gb)
    pt = [g_keep, y_swap(g_send)]
    for stride in rest[2:]:
        ut, dt = scatter(ut, stride, dp)[0], scatter(dt, stride, dp)[0]
    us, ds = [total(t).astype(bf16) for t in (ut, dt)]
    gi_own, gi_nb, gg1 = last_call(meta, x_own, x_nb, dh_mine, dh_got, after(dmid, us, ds, g_send), gain1)
    gi_got = x_swap(gi_nb)
    p_got = lax.optimization_barrier((pt[1], gi_nb))[0]
    pt = [pt[0], p_got]
    for stride in rest:
        pt = scatter(pt, stride, dp)[0]
    ps = total(pt).astype(bf16)
    for stride in reversed(rest):
        us, ds, ps = [gather(v, stride, dp) for v in (us, ds, ps)]
    grad_up = gather(us, 1, dp).astype(f32)
    gd_all = gather(ds, 1, dp).astype(f32)
    grad_down, grad_out = gd_all[: w_down.shape[0]], gd_all[w_down.shape[0] :]
    ps_got = y_swap(ps)
    lo, hi = jnp.where(y == c, ps, ps_got), jnp.where(y == c, ps_got, ps)
    third = lambda v, w: v[:, w * half : w * half + half]
    grads = [jnp.concatenate([third(lo, w), third(hi, w)], axis=1).astype(f32) for w in range(3)]

    gt = gt[:9].reshape(9, 2, part).transpose(1, 0, 2)
    gt = jnp.where(jnp.arange(2)[:, None, None, None] == c, gt[None], 0.0).reshape(4, 9, part)
    gains = jnp.concatenate([gg1, gg2], axis=0).reshape(2, 4, part).transpose(1, 0, 2)
    small = jnp.concatenate([gt, gains, jnp.zeros((4, 5, part), f32)], axis=1)
    small = jnp.broadcast_to(small[:, None], (4, dp, 16, part)).reshape(4 * dp, 16, part)
    small = jnp.sum(lax.all_to_all(small, ("head", "dp"), 0, 0, tiled=True), axis=0)
    output = order(after(out_own, gi_nb), out_x)
    grad_input = order(gi_own, gi_got)
    return (
        output,
        grad_input,
        *grads,
        grad_out,
        grad_up,
        grad_down,
        small[:9].reshape(3, 3, part),
        small[9],
        small[10],
    )


def solution(mesh):
    placed = (
        P("dp", "head", None),
        P("dp"),
        P("head", None),
        P("head", None),
        P("head", None),
        P("head", None),
        P(None, "head"),
        P("head", None),
        P(None, None, "head"),
        P(),
        P(),
        P("dp", "head", None),
    )
    return jax.shard_map(
        functools.partial(local, mesh.shape["dp"]),
        mesh=mesh,
        in_specs=placed,
        out_specs=(
            P("dp", "head", None),
            P("dp", "head", None),
            P("head", None),
            P("head", None),
            P("head", None),
            P("head", None),
            P(None, "head"),
            P("head", None),
            P(None, None, "head"),
            P("head"),
            P("head"),
        ),
        check_vma=False,
    )
```

```python
import functools

import jax
import jax.numpy as jnp
from jax import lax
from jax.experimental import pallas as pl
from jax.experimental.pallas import tpu as pltpu
from jax.sharding import PartitionSpec as P

HDIM = 64
EPS = 1e-06
bf16 = jnp.bfloat16
f32 = jnp.float32

NN = (((1,), (0,)), ((), ()))
NT = (((1,), (1,)), ((), ()))
TN = (((0,), (0,)), ((), ()))

CORE = [(0, 1), (1, 0), (2, 3), (3, 2)]
XNB = [(0, 2), (2, 0), (1, 3), (3, 1)]


def dot(a, b, dims=NN):
    return lax.dot_general(a, b, dims, preferred_element_type=f32)


def cost(flops, nbytes, trans=0):
    return pl.CostEstimate(flops=int(flops), bytes_accessed=int(nbytes), transcendentals=int(trans))


def sds(shape, dtype):
    return jax.ShapeDtypeStruct(shape, dtype)


def whole(shape):
    zeros = (0,) * len(shape)
    return pl.BlockSpec(shape, lambda *_: zeros, pipeline_mode=pl.Buffered(1))


def grid_spec(grid, ins, outs, scratch=()):
    return pltpu.PrefetchScalarGridSpec(
        num_scalar_prefetch=1, grid=grid, in_specs=ins, out_specs=outs, scratch_shapes=scratch
    )


def length_of(m):
    return m[m[2] // 2]


def x_of(m):
    return m[2] // 2


def core_of(m):
    return lax.rem(m[2], 2)


def norm(x, gain):
    inv = lax.rsqrt(jnp.mean(x * x, axis=-1, keepdims=True) + EPS)
    n = x * inv
    return n, inv, (n * gain).astype(bf16)


def qkv_body(meta, x0, x2, x3, wa, wb, pack, gain, h_ref, raw_ref, mix_ref, w_ref, taps, ext):
    b = pl.program_id(0)
    rows = x0.shape[0]
    part = w_ref.shape[0] // 4
    width = x0.shape[1]
    tall = wa.shape[0]
    hd = meta[2]

    @pl.when(b == 0)
    def _():
        def put(k, ref, first):
            at = jnp.bitwise_xor(hd, k) * part
            w_ref[pl.ds(pl.multiple_of(at, 64), part), 0:width] = ref[first : first + part, :]
            for n in range(2):
                row = pl.multiple_of(at + n * (part // 2), 32)
                w_ref[pl.ds(row, part // 2), width:] = ref[
                    first + part : first + part + part // 2, n * (width // 2) : (n + 1) * (width // 2)
                ]

        put(0, wa, 0)
        put(1, wb, 0)
        put(2, pack, rows)
        put(3, pack, rows + tall)
        last = lambda ref, end: ref[end - 16 : end, :].astype(f32)
        near = last(wa, tall) + last(wb, tall)
        far = last(pack, rows + tall) + last(pack, rows + 2 * tall)
        t = jnp.where(x_of(meta) == core_of(meta), near, far)
        taps[...] = jnp.zeros_like(taps)
        taps[0:3, 0:width] = t[0:3]
        taps[0:3, width:] = t[3:6, 0 : width // 2]
        ext[0:8, :] = jnp.zeros((8, ext.shape[1]), f32)

    v = jnp.bitwise_xor(hd, b)
    slot = lax.rem(v, 2) * 2 + v // 2
    x = x0[...]
    for k, other in ((1, pack), (2, x2), (3, x3)):
        x = jnp.where(slot == k, other[0:rows, :], x)
    _, _, h = norm(x.astype(f32), gain[...].astype(f32))
    h_ref[...] = h
    raw = dot(h, w_ref[...]).astype(bf16)
    raw_ref[...] = raw
    rawf = raw.astype(f32)
    ext[8 : 8 + rows, :] = rawf
    t = taps[...]
    mixed = t[0:1] * rawf + t[1:2] * ext[7 : 7 + rows, :] + t[2:3] * ext[6 : 6 + rows, :]
    mix_ref[...] = mixed.astype(bf16)
    ext[0:8, :] = ext[rows : rows + 8, :]


def qkv_call(meta, x_own, x_core, x_cnb, w_mine, w_core, pack, gain):
    rows, width = x_own.shape
    tall = w_mine.shape[0]
    cols = width * 3 // 2
    length = 4 * rows
    blk = lambda n: pl.BlockSpec((rows, n), lambda b, m: (b, 0))
    const = lambda r: pl.BlockSpec((r, cols), lambda b, m: (0, 0))
    return pl.pallas_call(
        qkv_body,
        out_shape=[
            sds((length, width), bf16),
            sds((length, cols), bf16),
            sds((length, cols), bf16),
            sds((width, cols), bf16),
            sds((8, cols), f32),
        ],
        grid_spec=grid_spec(
            (4,),
            [whole((rows, width))] * 3
            + [whole((tall, width))] * 2
            + [whole(pack.shape), whole((1, width))],
            [blk(width), blk(cols), blk(cols), const(width), const(8)],
            [pltpu.VMEM((rows + 8, cols), f32)],
        ),
        cost_estimate=cost(2 * length * width * cols, 2 * length * (width * 2 + cols * 2)),
        name="qkv",
    )(meta, x_own, x_core, x_cnb, w_mine, w_core, pack, gain)


def two_heads(v):
    lane = lax.broadcasted_iota(jnp.int32, v.shape, 1)
    z = jnp.zeros_like(v)
    return jnp.concatenate([jnp.where(lane < HDIM, v, z), jnp.where(lane < HDIM, z, v)], axis=0)


def causal(first, keys, start, queries):
    key = first + lax.broadcasted_iota(jnp.int32, (keys, queries), 0)
    ok = key <= start + lax.broadcasted_iota(jnp.int32, (keys, queries), 1)
    return jnp.concatenate([ok, ok], axis=1)


def upper(v, axis):
    B = v.shape[axis] // 2
    h = B // 2
    if axis == 0:
        return jnp.concatenate([v[h:B], v[B + h :]], axis=0)
    return jnp.concatenate([v[:, h:B], v[:, B + h :]], axis=1)


def with_bias(k_ref, ka, length):
    L = k_ref.shape[0]
    ka[:, :128] = k_ref[...]
    lane = lax.broadcasted_iota(jnp.int32, (L, 128), 1)
    row = lax.broadcasted_iota(jnp.int32, (L, 128), 0)
    pad = jnp.logical_and(lane == 0, row >= length)
    ka[:, 128:] = jnp.where(pad, -1e9, 0.0).astype(bf16)


def biased(q):
    qq = two_heads(q)
    lane = lax.broadcasted_iota(jnp.int32, qq.shape, 1)
    return jnp.concatenate([qq, jnp.where(lane == 0, 1.0, 0.0).astype(bf16)], axis=1)


def att_fwd_body(meta, q_ref, k_ref, v_ref, mine_ref, theirs_ref, lse_ref, ka, vt, sc):
    i = pl.program_id(1)
    B = q_ref.shape[0]

    @pl.when(i == 0)
    def _():
        vt[...] = v_ref[...].T
        with_bias(k_ref, ka, length_of(meta))

    qq = biased(q_ref[...] * bf16(HDIM**-0.5))
    own = lax.rem(i, 2) == core_of(meta)

    def run(ii):
        m = None
        for j in range(ii + 1):
            ks = slice(j * B, j * B + B)
            s = dot(ka[ks, :], qq, NT)
            if j == ii:
                s = jnp.where(causal(0, B, 0, B), s, -1e9)
            sc[ks, :] = s
            mj = jnp.max(s, axis=0, keepdims=True)
            m = mj if m is None else jnp.maximum(m, mj)
        l = jnp.zeros((1, 2 * B), f32)
        acc = [jnp.zeros((HDIM, B), f32)] * 2
        for j in range(ii + 1):
            ks = slice(j * B, j * B + B)
            p = jnp.exp(sc[ks, :] - m)
            l = l + jnp.sum(p, axis=0, keepdims=True)
            pb = p.astype(bf16)
            for h in range(2):
                r = slice(HDIM * h, HDIM * h + HDIM)
                acc[h] = acc[h] + dot(vt[r, ks], pb[:, h * B : h * B + B])
        inv = 1.0 / l
        out = jnp.concatenate([acc[h] * inv[:, h * B : h * B + B] for h in range(2)], axis=0)
        out = out.T.astype(bf16)

        @pl.when(own)
        def _():
            mine_ref[...] = out

        @pl.when(jnp.logical_not(own))
        def _():
            theirs_ref[...] = out

        ls = m + jnp.log(l)
        lse_ref[0] = jnp.concatenate([ls[:, :B], ls[:, B:]], axis=0)

    for ii in range(4):
        pl.when(i == ii)(functools.partial(run, ii))


def half_map(p, i, m):
    return (jnp.bitwise_xor(i // 2, x_of(m)), p)


def att_fwd_call(meta, mix):
    length, cols = mix.shape
    width = cols // 3
    pairs = width // 128
    B = length // 4
    half = pl.BlockSpec((B, 128), half_map)
    return pl.pallas_call(
        att_fwd_body,
        out_shape=[
            sds((length // 2, width), bf16),
            sds((length // 2, width), bf16),
            sds((pairs, 2, length), f32),
        ],
        grid_spec=grid_spec(
            (pairs, 4),
            [
                pl.BlockSpec((B, 128), lambda p, i, m: (i, p)),
                pl.BlockSpec((length, 128), lambda p, i, m: (0, pairs + p)),
                pl.BlockSpec((length, 128), lambda p, i, m: (0, 2 * pairs + p)),
            ],
            [half, half, pl.BlockSpec((1, 2, B), lambda p, i, m: (p, 0, i))],
            [
                pltpu.VMEM((length, 256), bf16),
                pltpu.VMEM((128, length), bf16),
                pltpu.VMEM((length, 2 * B), f32),
            ],
        ),
        cost_estimate=cost(8 * length * length * width, 8 * length * width, 2 * length * length * pairs),
        name="attn_fwd",
    )(meta, mix, mix, mix)


def att_bwd_body(
    p0, aliased, meta, q_ref, k_ref, v_ref, om, ot, dm, dt, lse_ref, rq, rk, rv, taps, *refs
):
    g_ref, gt, ka, kt, dkt, dvt, dqt, dqs, ext, stage, sem = refs[1:] if aliased else refs
    i = pl.program_id(1)
    B = q_ref.shape[0]
    L = k_ref.shape[0]
    H = B // 2

    @pl.when(i == 0)
    def _():
        kt[...] = k_ref[...].T
        with_bias(k_ref, ka, length_of(meta))

    own = lax.rem(i, 2) == core_of(meta)
    q = q_ref[...] * bf16(HDIM**-0.5)
    o = jnp.where(own, om[...], ot[...])
    do = jnp.where(own, dm[...], dt[...])
    qq, dd = biased(q), two_heads(do)
    qt, dot_ = q.T, do.T
    od = (o.astype(f32) * do.astype(f32)).T
    delta = jnp.concatenate(
        [jnp.sum(od[:HDIM], axis=0, keepdims=True), jnp.sum(od[HDIM:], axis=0, keepdims=True)],
        axis=1,
    )
    ls = lse_ref[0]
    lse = jnp.concatenate([ls[0:1], ls[1:2]], axis=1)

    dqt[...] = jnp.zeros_like(dqt)

    def tile(st, n, lo, diagonal):
        w = B - lo
        ks = pl.ds(pl.multiple_of(st, H), n)
        part = upper if lo else lambda v, axis: v
        s = dot(ka[ks, :], part(qq, 0), NT)
        dp = dot(v_ref[ks, :], part(dd, 0), NT)
        p = jnp.exp(s - part(lse, 1))
        if diagonal:
            p = jnp.where(causal(lo, n, lo, w), p, 0.0)
        ds = (p * (dp - part(delta, 1))).astype(bf16)
        pb = p.astype(bf16)
        for h in range(2):
            r, c = slice(HDIM * h, HDIM * h + HDIM), slice(h * w, h * w + w)
            dqt[r, lo:] += dot(kt[r, ks], ds[:, c])
            a = dot(qt[r, lo:], ds[:, c], NT)
            b = dot(dot_[r, lo:], pb[:, c], NT)
            if diagonal:
                dkt[r, ks] = a
                dvt[r, ks] = b
            else:
                dkt[r, ks] += a
                dvt[r, ks] += b

    lax.fori_loop(0, i, lambda j, c: (tile(j * B, B, 0, False), c)[1], 0)
    tile(i * B, H, 0, True)
    tile(i * B + H, H, H, True)
    dqs[pl.ds(pl.multiple_of(i * B, B), B), :] = dqt[...].T * HDIM**-0.5

    def copies(pair):
        width = g_ref.shape[1] // 3
        return [
            pltpu.make_async_copy(
                stage.at[k],
                g_ref.at[:, pl.ds(pl.multiple_of(k * width + (p0 + pair) * 128, 128), 128)],
                sem.at[k],
            )
            for k in range(3)
        ]

    @pl.when(i == pl.num_programs(1) - 1)
    def _():
        pair = pl.program_id(0)
        gt[...] = jnp.zeros_like(gt)
        ext[...] = jnp.zeros_like(ext)

        @pl.when(pair > 0)
        def _():
            for cp in copies(pair):
                cp.wait()

        def back(n, carry):
            blk = L // B - 1 - n
            sl = pl.ds(pl.multiple_of(blk * B, B), B)
            for which, raw in enumerate((rq, rk, rv)):
                col = which * (taps.shape[1] // 3) + (p0 + pl.program_id(0)) * 128
                t = taps[:, pl.ds(pl.multiple_of(col, 128), 128)]
                g = dqs[sl, :] if which == 0 else (dkt, dvt)[which - 1][:, sl].T
                ext[which, B : B + 8, :] = ext[which, 0:8, :]
                ext[which, 0:B, :] = g
                g1, g2 = ext[which, 1 : B + 1, :], ext[which, 2 : B + 2, :]
                stage[which, sl, :] = (t[0:1] * g + t[1:2] * g1 + t[2:3] * g2).astype(bf16)
                r = raw[sl, :].astype(f32)
                for k, gg in enumerate((g, g1, g2)):
                    row = slice(3 * which + k, 3 * which + k + 1)
                    gt[row, :] += jnp.sum(r * gg, axis=0, keepdims=True)
            return carry

        lax.fori_loop(0, L // B, back, 0)
        for cp in copies(pair):
            cp.start()

        @pl.when(pair == pl.num_programs(0) - 1)
        def _():
            for cp in copies(pair):
                cp.wait()


def att_bwd_call(meta, mix, raw, om, ot, dm, dt, lse, taps, p0, count, into=None):
    length, cols = mix.shape
    pairs = cols // 384
    B = length // 4
    half = pl.BlockSpec((B, 128), lambda p, i, m: (jnp.bitwise_xor(i // 2, x_of(m)), p0 + p))
    full = lambda k: pl.BlockSpec((length, 128), lambda p, i, m: (0, k * pairs + p0 + p))
    return pl.pallas_call(
        functools.partial(att_bwd_body, p0, into is not None),
        out_shape=[sds((length, cols), bf16), sds((16, 128 * count), f32)],
        grid_spec=grid_spec(
            (count, 4),
            [
                pl.BlockSpec((B, 128), lambda p, i, m: (i, p0 + p)),
                full(1),
                full(2),
                half,
                half,
                half,
                half,
                pl.BlockSpec((1, 2, B), lambda p, i, m: (p0 + p, 0, i)),
                full(0),
                full(1),
                full(2),
                whole((8, cols)),
            ]
            + ([] if into is None else [pl.BlockSpec(memory_space=pl.ANY)]),
            [pl.BlockSpec(memory_space=pl.ANY), pl.BlockSpec((16, 128), lambda p, i, m: (0, p))],
            [
                pltpu.VMEM((length, 256), bf16),
                pltpu.VMEM((128, length), bf16),
                pltpu.VMEM((128, length), f32),
                pltpu.VMEM((128, length), f32),
                pltpu.VMEM((128, B), f32),
                pltpu.VMEM((length, 128), f32),
                pltpu.VMEM((3, B + 8, 128), f32),
                pltpu.VMEM((3, length, 128), bf16),
                pltpu.SemaphoreType.DMA((3,)),
            ],
        ),
        cost_estimate=cost(
            14 * length * length * 128 * count, 20 * length * 128 * count, 2 * length * length * count
        ),
        name="attn_bwd",
        input_output_aliases={} if into is None else {13: 0},
    )(meta, mix, mix, mix, om, ot, dm, dt, lse, raw, raw, raw, taps, *([] if into is None else [into]))


T = 256


def valid_rows(meta, i, rows):
    per = rows // T
    block = jnp.where(i < per, meta[2], jnp.bitwise_xor(meta[2], 2))
    start = block * rows + lax.rem(i, per) * T
    return start + lax.broadcasted_iota(jnp.int32, (T, 1), 0) < length_of(meta)


def ffn_body(
    meta, xo, xx, co, cx, am, at, gain, wo_o, wo_c, pack, wo_cn,
    u_o, d_o, f_c, n0, n1, n2, n3, c0, c1, c2, c3,
    oo, ox, dm, dt, gg, dmid, gu0, gu1, gu2, gu3, gd0, gd1, gd2, gd3,
    wo, wus, wds, mid, h_s, g_s, fo, dh, act, du, stu, std, sto, gacc, sw, so, sg, sd, st,
):
    rows, width = xo.shape
    part = wo_o.shape[0]
    half = 2 * part
    n = 2 * rows // T
    per = rows // T
    copies = []
    for k, src in ((0, wo_o), (1, wo_c), (2, pack.at[pl.ds(rows, part), :]), (3, wo_cn)):
        shard = jnp.bitwise_xor(meta[2], k)
        row = jnp.where(shard // 2 == core_of(meta), 0, half) + lax.rem(shard, 2) * part
        cp = pltpu.make_async_copy(src, wo.at[pl.ds(pl.multiple_of(row, 64), part), :], so.at[k])
        cp.start()
        copies.append(cp)
    for k, pair in ((0, (f_c.at[0], f_c.at[1])), (2, (u_o, d_o))):
        for n_, src in enumerate(pair):
            pltpu.make_async_copy(src, (wus, wds)[n_].at[k], sw.at[k, n_]).start()
    for k, quarters in ((1, (c0, c1, c2, c3)), (3, (n0, n1, n2, n3))):
        for q_, src in enumerate(quarters):
            count = src.shape[1]
            to = pl.ds(pl.multiple_of(jnp.bitwise_xor(meta[3], q_) * count, 64), count)
            for n_, dst in enumerate((wus, wds)):
                pltpu.make_async_copy(src.at[n_], dst.at[k, to, :], sw.at[k, n_]).start()
    for cp in copies:
        cp.wait()
    gn = gain[...].astype(f32)

    def first_rows(i, carry):
        sl = pl.ds(pl.multiple_of(i * T, T), T)
        src = pl.ds(pl.multiple_of(lax.rem(i, per) * T, T), T)
        own = i < per
        x = jnp.where(own, xo[src, :], xx[src, :]).astype(f32)
        a = jnp.concatenate([am[sl, :], at[sl, :]], axis=1)
        m = x + dot(a, wo[...])
        mid[sl, :] = m
        fo[sl, :] = m
        h_s[sl, :] = norm(m, gn)[2]
        ct = jnp.where(own, co[src, :], cx[src, :])
        g_s[sl, :] = jnp.where(valid_rows(meta, i, rows), ct, jnp.zeros_like(ct))
        dh[sl, :] = jnp.zeros((T, width), f32)
        return carry

    lax.fori_loop(0, n, first_rows, 0)

    R = 1024
    C = 768

    gus, gds = (gu0, gu1, gu2, gu3), (gd0, gd1, gd2, gd3)

    def stores(n_, slot):
        return [
            pltpu.make_async_copy(stu.at[slot], gus[n_], sg.at[slot, 0]),
            pltpu.make_async_copy(std.at[slot], gds[n_].at[pl.ds(0, width), :], sg.at[slot, 1]),
        ]

    def shard(k, carry):
        for cp in (
            pltpu.make_async_copy(u_o, wus.at[k], sw.at[k, 0]),
            pltpu.make_async_copy(d_o, wds.at[k], sw.at[k, 1]),
        ):
            cp.wait()

        def rows_step(t, c2):
            sl = pl.ds(pl.multiple_of(t * R, R), R)
            h, g = h_s[sl, :], g_s[sl, :]
            r = jnp.maximum(dot(h, wus[k]), 0.0)
            a = (r * r).astype(bf16)
            d = (dot(g, wds[k], NT) * 2.0 * r).astype(bf16)
            act[sl, :] = a
            du[sl, :] = d
            fo[sl, :] += dot(a, wds[k])
            dh[sl, :] += dot(d, wus[k], NT)
            return c2

        lax.fori_loop(0, 2 * rows // R, rows_step, 0)
        slot = lax.rem(k, 2)

        @pl.when(k >= 2)
        def _():
            for cp in stores(0, slot):
                cp.wait()

        def cols_step(t, c2):
            sl = pl.ds(pl.multiple_of(t * C, C), C)
            stu[slot, :, sl] = dot(h_s[...], du[:, sl], TN).astype(bf16)
            std[slot, sl, :] = dot(act[:, sl], g_s[...], TN).astype(bf16)
            return c2

        lax.fori_loop(0, width // C, cols_step, 0)
        for n_ in range(4):

            @pl.when(k == n_)
            def _(n_=n_):
                for cp in stores(n_, n_ % 2):
                    cp.start()

        return carry

    lax.fori_loop(0, 4, shard, 0)
    gg[...] = jnp.zeros_like(gg)

    def last_rows(i, carry):
        sl = pl.ds(pl.multiple_of(i * T, T), T)
        dst = pl.ds(pl.multiple_of(lax.rem(i, per) * T, T), T)
        ok = valid_rows(meta, i, rows)
        m = mid[sl, :]
        out = jnp.where(ok, fo[sl, :], 0.0)

        fo[sl, :] = out

        @pl.when(i < per)
        def _():
            own = oo.at[meta[2] // 2, dst, :]
            pltpu.make_async_copy(fo.at[sl, :], own, sd.at[1]).start()

        @pl.when(i >= per)
        def _():
            ox[dst, :] = out.astype(bf16)

        nm, inv, _ = norm(m, gn)
        d = dh[sl, :]
        dn = d * gn
        r = g_s[sl, :].astype(f32) + inv * (dn - nm * jnp.mean(dn * nm, axis=-1, keepdims=True))
        mid[sl, :] = r
        pltpu.make_async_copy(mid.at[sl, :], dmid.at[sl, :], sd.at[0]).start()
        db = r.astype(bf16)
        du[sl, :] = db
        da = dot(db, wo[...], NT).astype(bf16)
        dm[sl, :] = da[:, :half]
        dt[sl, :] = da[:, half:]
        gg[...] += jnp.sum(d * nm, axis=0, keepdims=True)
        return carry

    lax.fori_loop(0, n, last_rows, 0)
    gacc[0:half, :] = dot(am[...], du[...], TN)
    gacc[half:, :] = dot(at[...], du[...], TN)
    outs = [
        pltpu.make_async_copy(mid, dmid, sd.at[0]),
        pltpu.make_async_copy(fo.at[pl.ds(0, rows), :], oo.at[meta[2] // 2], sd.at[1]),
    ]
    for k, k_ in enumerate((1, 3, 0, 2)):
        shard_ = jnp.bitwise_xor(meta[2], k_)
        row = jnp.where(shard_ // 2 == core_of(meta), 0, half) + lax.rem(shard_, 2) * part
        sto[k] = gacc[pl.ds(pl.multiple_of(row, 64), part), :].astype(bf16)
        cp = pltpu.make_async_copy(sto.at[k], gds[k].at[pl.ds(width, part), :], st.at[k])
        cp.start()
        outs.append(cp)
    for slot in range(2):
        outs.extend(stores(2 + slot, slot))
    for cp in outs:
        cp.wait()


def ffn_call(meta, xo, xx, co, cx, am, at, gain, wos, ffs):
    rows, width = xo.shape
    half = am.shape[1]
    part = half // 2
    hid = ffs[0].shape[1]
    hbm = pl.BlockSpec(memory_space=pl.ANY)
    vm = lambda *shape: whole(shape)
    all_rows = 2 * rows
    return pl.pallas_call(
        ffn_body,
        out_shape=[
            sds((2, rows, width), f32),
            sds((rows, width), bf16),
            sds((all_rows, half), bf16),
            sds((all_rows, half), bf16),
            sds((1, width), f32),
            sds((all_rows, width), f32),
        ]
        + [sds((width, hid), bf16)] * 4
        + [sds((hid + part, width), bf16)] * 4,
        grid_spec=grid_spec(
            (1,),
            [vm(rows, width)] * 4 + [vm(all_rows, half)] * 2 + [vm(1, width)] + [hbm] * 15,
            [
                hbm,
                vm(rows, width),
                vm(all_rows, half),
                vm(all_rows, half),
                vm(1, width),
            ]
            + [hbm] * 9,
            [
                pltpu.VMEM((width, width), bf16),
                pltpu.VMEM((4, width, hid), bf16),
                pltpu.VMEM((4, hid, width), bf16),
                pltpu.VMEM((all_rows, width), f32),
                pltpu.VMEM((all_rows, width), bf16),
                pltpu.VMEM((all_rows, width), bf16),
                pltpu.VMEM((all_rows, width), f32),
                pltpu.VMEM((all_rows, width), f32),
                pltpu.VMEM((all_rows, hid), bf16),
                pltpu.VMEM((all_rows, hid), bf16),
                pltpu.VMEM((2, width, hid), bf16),
                pltpu.VMEM((2, hid, width), bf16),
                pltpu.VMEM((4, part, width), bf16),
                pltpu.VMEM((width, width), f32),
                pltpu.SemaphoreType.DMA((4, 2)),
                pltpu.SemaphoreType.DMA((4,)),
                pltpu.SemaphoreType.DMA((2, 2)),
                pltpu.SemaphoreType.DMA((2,)),
                pltpu.SemaphoreType.DMA((4,)),
            ],
        ),
        cost_estimate=cost(
            48 * all_rows * width * hid + 6 * all_rows * width * width, 40 * all_rows * width
        ),
        compiler_params=pltpu.CompilerParams(vmem_limit_bytes=62 * 2**20),
        name="ffn",
    )(meta, xo, xx, co, cx, am, at, gain, *wos, *ffs)


def projg_body(meta, h, d, keep, far, send, also, acc):
    acc[...] = dot(h[...], d[...], TN)
    part = keep.shape[0]
    for ref, k in ((keep, 0), (far, 2), (send, 1), (also, 3)):
        at = jnp.bitwise_xor(meta[2], k)
        ref[...] = acc[pl.ds(pl.multiple_of(at * part, 64), part), :].astype(bf16)


def projg_call(meta, h, d):
    length, width = h.shape
    cols = d.shape[1]
    step = cols // 3
    g = pl.BlockSpec((width // 4, step), lambda j, m: (0, j))
    return pl.pallas_call(
        projg_body,
        out_shape=[sds((width // 4, cols), bf16)] * 4,
        grid_spec=grid_spec(
            (3,),
            [whole((length, width)), pl.BlockSpec((length, step), lambda j, m: (0, j))],
            [g] * 4,
            [pltpu.VMEM((width, step), f32)],
        ),
        cost_estimate=cost(2 * length * width * cols, 2 * length * (width + cols)),
        name="projg",
    )(meta, h, d)


def projd_body(meta, d, w, dm, dt):
    dh = dot(d[...], w[...], NT)
    own = lax.rem(pl.program_id(0), 2) == core_of(meta)

    @pl.when(own)
    def _():
        dm[...] = dh

    @pl.when(jnp.logical_not(own))
    def _():
        dt[...] = dh.astype(bf16)


def projd_call(meta, d, w):
    length, cols = d.shape
    width = w.shape[0]
    B = length // 4
    side = pl.BlockSpec((B, width), lambda b, m: (jnp.bitwise_xor(b // 2, x_of(m)), 0))
    return pl.pallas_call(
        projd_body,
        out_shape=[sds((length // 2, width), f32), sds((length // 2, width), bf16)],
        grid_spec=grid_spec(
            (4,),
            [pl.BlockSpec((B, cols), lambda b, m: (b, 0)), whole((width, cols))],
            [side, side],
        ),
        cost_estimate=cost(2 * length * width * cols, 12 * length * width),
        name="projd",
    )(meta, d, w)


def last_body(meta, xo, xx, dm, dt, dmid, gain, go, gx, gg):
    i = pl.program_id(0)
    per = pl.num_programs(0) // 2
    first = i < per
    x = jnp.where(first, xo[...], xx[...]).astype(f32)
    gn = gain[...].astype(f32)
    n, inv, _ = norm(x, gn)
    dh = dm[...] + dt[...].astype(f32)
    dn = dh * gn
    out = dmid[...] + inv * (dn - n * jnp.mean(dn * n, axis=-1, keepdims=True))

    @pl.when(first)
    def _():
        go[0] = out

    @pl.when(jnp.logical_not(first))
    def _():
        gx[...] = out.astype(bf16)

    ps = jnp.sum(dh * n, axis=0, keepdims=True)

    @pl.when(i == 0)
    def _():
        gg[...] = ps

    @pl.when(i > 0)
    def _():
        gg[...] += ps


def own_map(per):
    return lambda i, m: (jnp.minimum(i, per - 1), 0)


def nb_map(per):
    return lambda i, m: (jnp.maximum(i - per, 0), 0)


def last_call(meta, xo, xx, dm, dt, dmid, gain):
    rows, width = xo.shape
    per = rows // T
    fst, snd = pl.BlockSpec((T, width), own_map(per)), pl.BlockSpec((T, width), nb_map(per))
    blk = pl.BlockSpec((T, width), lambda i, m: (i, 0))
    return pl.pallas_call(
        last_body,
        out_shape=[sds((2, rows, width), f32), sds((rows, width), bf16), sds((1, width), f32)],
        grid_spec=grid_spec(
            (2 * per,),
            [fst, snd, blk, blk, blk, whole((1, width))],
            [pl.BlockSpec((1, T, width), lambda i, m: (x_of(m), jnp.minimum(i, per - 1), 0)), snd, pl.BlockSpec((1, width), lambda i, m: (0, 0))],
        ),
        cost_estimate=cost(40 * rows * width, 30 * rows * width),
        name="last",
    )(meta, xo, xx, dm, dt, dmid, gain)


def flip(size, bit):
    return [(i, i ^ bit) for i in range(size)]


def core_swap(v):
    return lax.ppermute(v, "head", CORE)


def x_swap(v):
    return lax.ppermute(v, "head", XNB)


def after(v, *deps):
    return lax.optimization_barrier((v, *deps))[0]


def halve(terms, index, count):
    rows = terms[0].shape[0] // count
    piece = lambda t, k: lax.dynamic_slice_in_dim(t, jnp.bitwise_xor(index, k) * rows, rows, 0)
    total = lambda k: sum(piece(t, k).astype(f32) for t in terms)
    return [total(k).astype(bf16) for k in range(1, count)], total(0)


def strides(dp):
    out = [1]
    while 2 * out[-1] < dp:
        out.append(2 * out[-1])
    return out


def side(stride):
    return lax.axis_index("dp") // stride % 2


def swap(v, stride, dp):
    return lax.ppermute(v, "dp", flip(dp, stride))


def swap_both(vs, stride, dp):
    got = swap(jnp.concatenate(vs, axis=0), stride, dp)
    out, row = [], 0
    for v in vs:
        out.append(got[row : row + v.shape[0]])
        row += v.shape[0]
    return out


def scatter(sums, stride, dp):
    halves = [halve(terms, side(stride), 2) for terms in sums]
    send = jnp.concatenate([h[0][0] for h in halves], axis=0)
    got = swap(send, stride, dp)
    out, row = [], 0
    for (part,), keep in halves:
        out.append([keep, got[row : row + part.shape[0]]])
        row += part.shape[0]
    return out, send


def join(mine, got, stride):
    upper = side(stride) == 1
    return jnp.concatenate([jnp.where(upper, got, mine), jnp.where(upper, mine, got)], axis=0)


def total(terms):
    return sum(t.astype(f32) for t in terms)


def local(dp, inputs, lengths, w_query, w_key, w_value, w_out, w_up, w_down, conv_taps, gain_attn, gain_ff, cotangent):
    hd = lax.axis_index("head")
    x, c, y = hd // 2, hd % 2, lax.axis_index("dp") % 2
    q = lax.axis_index("dp") % 4
    width = inputs.shape[2]
    part = w_query.shape[0]
    half = 2 * part
    pick = lambda v, k: lax.dynamic_index_in_dim(v, k, 0, keepdims=False)
    y_swap = lambda v: lax.ppermute(v, "dp", flip(dp, 1))
    order = lambda own, nb: lax.dynamic_update_slice_in_dim(own, nb[None].astype(f32), 1 - x, 0)
    meta = jnp.concatenate([lengths, jnp.stack([hd, q])]).astype(jnp.int32)
    gain1, gain2 = gain_attn.reshape(1, width), gain_ff.reshape(1, width)

    mask = (jnp.arange(2) == c)[None, None, :, None]
    tap_rows = jnp.where(mask, conv_taps.transpose(1, 0, 2)[:, :, None, :], 0).reshape(3, 3 * half)
    tap_rows = jnp.concatenate([tap_rows[:, :width], jnp.pad(tap_rows[:, width:], ((0, 0), (0, half)))], axis=0)
    tap_rows = jnp.pad(tap_rows, ((0, 10), (0, 0)))

    def packed(k):
        cut = lambda w: lax.dynamic_slice_in_dim(w, k * half, half, 1)
        fold = cut(w_value)
        return jnp.concatenate(
            [
                jnp.concatenate([cut(w_query), cut(w_key)], axis=1),
                jnp.concatenate([fold[: part // 2], fold[part // 2 :]], axis=1),
                tap_rows,
            ],
            axis=0,
        )

    w_core = core_swap(packed(1 - c))
    w_mine = packed(c)
    x_own = pick(inputs, x)
    rows = x_own.shape[0]
    pack = x_swap(jnp.concatenate([pick(inputs, 1 - x), w_mine, w_core], axis=0))
    x_core, x_cnb = core_swap(x_own), core_swap(pack[:rows])
    h1, raw, mix, w_full, taps = qkv_call(meta, x_own, x_core, x_cnb, w_mine, w_core, pack, gain1)

    count = width // 4
    quarter = lambda w: lax.dynamic_slice_in_dim(w, q * count, count, 0)
    ff_first = x_swap(after(jnp.stack([quarter(w_up), quarter(w_down)]), pack))
    c_own = pick(cotangent, x)
    pack2 = x_swap(after(jnp.concatenate([pick(cotangent, 1 - x), w_out], axis=0), pack))
    ff_c = core_swap(jnp.stack([after(w_up, pack), w_down]))
    wo_c = core_swap(w_out)
    src = after(ff_first, mix)
    ff_n = [swap(src, k, dp) for k in (1, 2, 3)]
    a_mine, a_send, lse = att_fwd_call(meta, after(mix, src, ff_c, wo_c))
    a_got = core_swap(a_send)
    *ff_n, pack2 = lax.optimization_barrier((*ff_n, pack2, a_mine))[:-1]
    ff_n = [src, *ff_n]
    ff_cn = [core_swap(v) for v in ff_n]
    wo_cn = core_swap(pack2[rows:])
    out_own, out_nb, d_mine, d_send, gg2, dmid, *gw = ffn_call(
        meta, x_own, pack, c_own, pack2, a_mine, a_got, gain2,
        (w_out, wo_c, pack2, wo_cn),
        (w_up, w_down, ff_c, *ff_n, *ff_cn),
    )
    d_got = core_swap(d_send)

    _, *rest = strides(dp)
    un, dn, do, uo = [core_swap(gw[k]) for k in (1, 5, 4, 0)]
    nu = total((gw[3], un)).astype(bf16)
    xu = x_swap(nu)
    (dn_send,), dn_keep = halve((gw[7], dn), y, 2)
    (do_send,), do_keep = halve((gw[6], do), y, 2)
    yn, yo = y_swap(dn_send), y_swap(do_send)
    out_x = x_swap(after(out_nb, nu))
    pairs = width // 256
    bwd = lambda m, p, n, into: att_bwd_call(
        meta, m, raw, a_mine, a_send, d_mine, d_got, lse, taps, p, n, into
    )
    dall, gt_a = bwd(after(mix, nu, dn_send, do_send), 0, pairs - 1, None)
    xu, yn, yo, out_x = lax.optimization_barrier((xu, yn, yo, out_x, dall))[:4]
    (u_send,), u_keep = halve((gw[2], uo, xu), y, 2)
    nd = total((dn_keep, yn)).astype(bf16)
    yu, xd = y_swap(u_send), x_swap(nd)
    dall, gt_b = bwd(after(mix, u_send, nd), pairs - 1, 1, dall)
    gt = jnp.concatenate([gt_a, gt_b], axis=1)
    yu, xd = lax.optimization_barrier((yu, xd, gt_b))[:2]
    sums, sent = scatter([[u_keep, yu], [do_keep, yo, xd]], rest[0], dp)
    keep, far, send, also = projg_call(meta, after(h1, sent), dall)
    got, got_n = core_swap(send), core_swap(also)
    far = x_swap(far)
    flat = lax.optimization_barrier((*sums[0], *sums[1], keep))[:-1]
    sums, sent = scatter([flat[:2], flat[2:]], rest[1], dp)
    far2 = x_swap(got_n)
    dh_mine, dh_send = projd_call(meta, after(dall, sent, got_n), w_full)
    dh_got = core_swap(dh_send)
    gi_own, gi_nb, gg1 = last_call(meta, x_own, pack, dh_mine, dh_got, dmid, gain1)
    *flat, far, far2 = lax.optimization_barrier((*sums[0], *sums[1], far, far2, gi_nb))[:-1]
    sums = [flat[:2], flat[2:]]
    for stride in rest[2:]:
        sums, _ = scatter(sums, stride, dp)
    vs = [total(t).astype(bf16) for t in sums]
    ga, gb = keep.astype(f32) + far.astype(f32), got.astype(f32) + far2.astype(f32)
    g_send, g_keep = jnp.where(y == 0, gb, ga).astype(bf16), jnp.where(y == 0, ga, gb)
    pt = [g_keep, y_swap(g_send)]
    gi_got = x_swap(gi_nb)
    for stride in reversed(rest[1:]):
        vs = [join(v, g, stride) for v, g in zip(vs, swap_both(vs, stride, dp))]
    others, across = swap_both(vs, rest[0], dp), swap_both(vs, 1, dp)
    for stride in rest:
        (pt,), _ = scatter([pt], stride, dp)
    ps = total(pt).astype(bf16)
    for stride in reversed(rest):
        ps = join(ps, swap(ps, stride, dp), stride)
    ps_got = y_swap(ps)
    also = swap_both(others, 1, dp)
    whole_of = lambda k: join(
        join(vs[k], others[k], rest[0]), join(across[k], also[k], rest[0]), 1
    ).astype(f32)
    grad_up, gd_all = whole_of(0), whole_of(1)
    grad_down, grad_out = gd_all[: w_down.shape[0]], gd_all[w_down.shape[0] :]
    lo, hi = jnp.where(y == c, ps, ps_got), jnp.where(y == c, ps_got, ps)
    third = lambda v, w: v[:, w * half : w * half + half]
    grads = [jnp.concatenate([third(lo, w), third(hi, w)], axis=1).astype(f32) for w in range(3)]

    gt = gt[:9].reshape(9, 2, part).transpose(1, 0, 2)
    gt = jnp.where(jnp.arange(2)[:, None, None, None] == c, gt[None], 0.0).reshape(4, 9, part)
    gains = jnp.concatenate([gg1, gg2], axis=0).reshape(2, 4, part).transpose(1, 0, 2)
    small = jnp.concatenate([gt, gains, jnp.zeros((4, 5, part), f32)], axis=1)
    small = jnp.broadcast_to(small[:, None], (4, dp, 16, part)).reshape(4 * dp, 16, part)
    small = jnp.sum(lax.all_to_all(small, ("head", "dp"), 0, 0, tiled=True), axis=0)
    output = order(after(out_own, gi_nb), out_x)
    grad_input = order(gi_own, gi_got)
    return (
        output,
        grad_input,
        *grads,
        grad_out,
        grad_up,
        grad_down,
        small[:9].reshape(3, 3, part),
        small[9],
        small[10],
    )


def solution(mesh):
    placed = (
        P("dp", "head", None),
        P("dp"),
        P("head", None),
        P("head", None),
        P("head", None),
        P("head", None),
        P(None, "head"),
        P("head", None),
        P(None, None, "head"),
        P(),
        P(),
        P("dp", "head", None),
    )
    return jax.shard_map(
        functools.partial(local, mesh.shape["dp"]),
        mesh=mesh,
        in_specs=placed,
        out_specs=(
            P("dp", "head", None),
            P("dp", "head", None),
            P("head", None),
            P("head", None),
            P("head", None),
            P("head", None),
            P(None, "head"),
            P("head", None),
            P(None, None, "head"),
            P("head"),
            P("head"),
        ),
        check_vma=False,
    )
```

```python
import functools

import jax
import jax.numpy as jnp
from jax import lax
from jax.experimental import pallas as pl
from jax.experimental.pallas import tpu as pltpu
from jax.sharding import PartitionSpec as P

HDIM = 64
EPS = 1e-06
bf16 = jnp.bfloat16
f32 = jnp.float32

NN = (((1,), (0,)), ((), ()))
NT = (((1,), (1,)), ((), ()))
TN = (((0,), (0,)), ((), ()))

CORE = [(0, 1), (1, 0), (2, 3), (3, 2)]
XNB = [(0, 2), (2, 0), (1, 3), (3, 1)]


def dot(a, b, dims=NN):
    return lax.dot_general(a, b, dims, preferred_element_type=f32)


def cost(flops, nbytes, trans=0):
    return pl.CostEstimate(flops=int(flops), bytes_accessed=int(nbytes), transcendentals=int(trans))


def sds(shape, dtype):
    return jax.ShapeDtypeStruct(shape, dtype)


def whole(shape):
    zeros = (0,) * len(shape)
    return pl.BlockSpec(shape, lambda *_: zeros, pipeline_mode=pl.Buffered(1))


def grid_spec(grid, ins, outs, scratch=()):
    return pltpu.PrefetchScalarGridSpec(
        num_scalar_prefetch=1, grid=grid, in_specs=ins, out_specs=outs, scratch_shapes=scratch
    )


def length_of(m):
    return m[m[2] // 2]


def x_of(m):
    return m[2] // 2


def core_of(m):
    return lax.rem(m[2], 2)


def slot_of(m, b):
    v = jnp.bitwise_xor(m[2], b)
    return lax.rem(v, 2) * 2 + v // 2


def norm(x, gain):
    inv = lax.rsqrt(jnp.mean(x * x, axis=-1, keepdims=True) + EPS)
    n = x * inv
    return n, inv, (n * gain).astype(bf16)


def qkv_body(meta, x0, x2, x3, wa, wb, pack, gain, h_ref, raw_ref, mix_ref, w_ref, taps, ext):
    b = pl.program_id(0)
    rows = x0.shape[0]
    part = w_ref.shape[0] // 4
    width = x0.shape[1]
    tall = wa.shape[0]
    hd = meta[2]

    @pl.when(b == 0)
    def _():
        def put(k, ref, first):
            at = jnp.bitwise_xor(hd, k) * part
            w_ref[pl.ds(pl.multiple_of(at, 64), part), 0:width] = ref[first : first + part, :]
            for n in range(2):
                row = pl.multiple_of(at + n * (part // 2), 32)
                w_ref[pl.ds(row, part // 2), width:] = ref[
                    first + part : first + part + part // 2, n * (width // 2) : (n + 1) * (width // 2)
                ]

        put(0, wa, 0)
        put(1, wb, 0)
        put(2, pack, rows)
        put(3, pack, rows + tall)
        last = lambda ref, end: ref[end - 16 : end, :].astype(f32)
        near = last(wa, tall) + last(wb, tall)
        far = last(pack, rows + tall) + last(pack, rows + 2 * tall)
        t = jnp.where(x_of(meta) == core_of(meta), near, far)
        taps[...] = jnp.zeros_like(taps)
        taps[0:3, 0:width] = t[0:3]
        taps[0:3, width:] = t[3:6, 0 : width // 2]
        ext[0:8, :] = jnp.zeros((8, ext.shape[1]), f32)

    slot = slot_of(meta, b)
    x = x0[...]
    for k, other in ((1, pack), (2, x2), (3, x3)):
        x = jnp.where(slot == k, other[0:rows, :], x)
    _, _, h = norm(x.astype(f32), gain[...].astype(f32))
    h_ref[...] = h
    raw = dot(h, w_ref[...]).astype(bf16)
    raw_ref[...] = raw
    rawf = raw.astype(f32)
    ext[8 : 8 + rows, :] = rawf
    t = taps[...]
    mixed = t[0:1] * rawf + t[1:2] * ext[7 : 7 + rows, :] + t[2:3] * ext[6 : 6 + rows, :]
    mix_ref[...] = mixed.astype(bf16)
    ext[0:8, :] = ext[rows : rows + 8, :]


def qkv_call(meta, x_own, x_core, x_cnb, w_mine, w_core, pack, gain):
    rows, width = x_own.shape
    tall = w_mine.shape[0]
    cols = width * 3 // 2
    length = 4 * rows
    blk = lambda n: pl.BlockSpec((rows, n), lambda b, m: (b, 0))
    const = lambda r: pl.BlockSpec((r, cols), lambda b, m: (0, 0))
    return pl.pallas_call(
        qkv_body,
        out_shape=[
            sds((length, width), bf16),
            sds((length, cols), bf16),
            sds((length, cols), bf16),
            sds((width, cols), bf16),
            sds((8, cols), f32),
        ],
        grid_spec=grid_spec(
            (4,),
            [whole((rows, width))] * 3
            + [whole((tall, width))] * 2
            + [whole(pack.shape), whole((1, width))],
            [
                pl.BlockSpec((rows, width), lambda b, m: (slot_of(m, b), 0)),
                blk(cols),
                blk(cols),
                const(width),
                const(8),
            ],
            [pltpu.VMEM((rows + 8, cols), f32)],
        ),
        cost_estimate=cost(2 * length * width * cols, 2 * length * (width * 2 + cols * 2)),
        name="qkv",
    )(meta, x_own, x_core, x_cnb, w_mine, w_core, pack, gain)


def two_heads(v):
    lane = lax.broadcasted_iota(jnp.int32, v.shape, 1)
    z = jnp.zeros_like(v)
    return jnp.concatenate([jnp.where(lane < HDIM, v, z), jnp.where(lane < HDIM, z, v)], axis=0)


def causal(first, keys, start, queries):
    key = first + lax.broadcasted_iota(jnp.int32, (keys, queries), 0)
    ok = key <= start + lax.broadcasted_iota(jnp.int32, (keys, queries), 1)
    return jnp.concatenate([ok, ok], axis=1)


def upper(v, axis):
    B = v.shape[axis] // 2
    h = B // 2
    if axis == 0:
        return jnp.concatenate([v[h:B], v[B + h :]], axis=0)
    return jnp.concatenate([v[:, h:B], v[:, B + h :]], axis=1)


def with_bias(k_ref, ka, length):
    L = k_ref.shape[0]
    ka[:, :128] = k_ref[...]
    lane = lax.broadcasted_iota(jnp.int32, (L, 128), 1)
    row = lax.broadcasted_iota(jnp.int32, (L, 128), 0)
    pad = jnp.logical_and(lane == 0, row >= length)
    ka[:, 128:] = jnp.where(pad, -1e9, 0.0).astype(bf16)


def biased(q):
    qq = two_heads(q)
    lane = lax.broadcasted_iota(jnp.int32, qq.shape, 1)
    return jnp.concatenate([qq, jnp.where(lane == 0, 1.0, 0.0).astype(bf16)], axis=1)


def att_fwd_body(meta, q_ref, k_ref, v_ref, mine_ref, theirs_ref, lse_ref, ka, vt, sc):
    i = pl.program_id(1)
    B = q_ref.shape[0]

    @pl.when(i == 0)
    def _():
        vt[...] = v_ref[...].T
        with_bias(k_ref, ka, length_of(meta))

    qq = biased(q_ref[...] * bf16(HDIM**-0.5))
    own = lax.rem(i, 2) == core_of(meta)

    def run(ii):
        m = None
        for j in range(ii + 1):
            ks = slice(j * B, j * B + B)
            s = dot(ka[ks, :], qq, NT)
            if j == ii:
                s = jnp.where(causal(0, B, 0, B), s, -1e9)
            sc[ks, :] = s
            mj = jnp.max(s, axis=0, keepdims=True)
            m = mj if m is None else jnp.maximum(m, mj)
        l = jnp.zeros((1, 2 * B), f32)
        acc = [jnp.zeros((HDIM, B), f32)] * 2
        for j in range(ii + 1):
            ks = slice(j * B, j * B + B)
            p = jnp.exp(sc[ks, :] - m)
            l = l + jnp.sum(p, axis=0, keepdims=True)
            pb = p.astype(bf16)
            for h in range(2):
                r = slice(HDIM * h, HDIM * h + HDIM)
                acc[h] = acc[h] + dot(vt[r, ks], pb[:, h * B : h * B + B])
        inv = 1.0 / l
        out = jnp.concatenate([acc[h] * inv[:, h * B : h * B + B] for h in range(2)], axis=0)
        out = out.T.astype(bf16)

        @pl.when(own)
        def _():
            mine_ref[...] = out

        @pl.when(jnp.logical_not(own))
        def _():
            theirs_ref[...] = out

        ls = m + jnp.log(l)
        lse_ref[0] = jnp.concatenate([ls[:, :B], ls[:, B:]], axis=0)

    for ii in range(4):
        pl.when(i == ii)(functools.partial(run, ii))


def half_map(p, i, m):
    return (jnp.bitwise_xor(i // 2, x_of(m)), p)


def att_fwd_call(meta, mix):
    length, cols = mix.shape
    width = cols // 3
    pairs = width // 128
    B = length // 4
    half = pl.BlockSpec((B, 128), half_map)
    return pl.pallas_call(
        att_fwd_body,
        out_shape=[
            sds((length // 2, width), bf16),
            sds((length // 2, width), bf16),
            sds((pairs, 2, length), f32),
        ],
        grid_spec=grid_spec(
            (pairs, 4),
            [
                pl.BlockSpec((B, 128), lambda p, i, m: (i, p)),
                pl.BlockSpec((length, 128), lambda p, i, m: (0, pairs + p)),
                pl.BlockSpec((length, 128), lambda p, i, m: (0, 2 * pairs + p)),
            ],
            [half, half, pl.BlockSpec((1, 2, B), lambda p, i, m: (p, 0, i))],
            [
                pltpu.VMEM((length, 256), bf16),
                pltpu.VMEM((128, length), bf16),
                pltpu.VMEM((length, 2 * B), f32),
            ],
        ),
        cost_estimate=cost(8 * length * length * width, 8 * length * width, 2 * length * length * pairs),
        name="attn_fwd",
    )(meta, mix, mix, mix)


def att_bwd_body(
    p0, aliased, meta, q_ref, k_ref, v_ref, om, ot, dm, dt, lse_ref, rq, rk, rv, taps, *refs
):
    gm_ref, gt_ref, gt, ka, kt, dkt, dvt, dqt, dqs, ext, stage, sem = refs[2:] if aliased else refs
    i = pl.program_id(1)
    B = q_ref.shape[0]
    L = k_ref.shape[0]
    H = B // 2

    @pl.when(i == 0)
    def _():
        kt[...] = k_ref[...].T
        with_bias(k_ref, ka, length_of(meta))

    own = lax.rem(i, 2) == core_of(meta)
    q = q_ref[...] * bf16(HDIM**-0.5)
    o = jnp.where(own, om[...], ot[...])
    do = jnp.where(own, dm[...], dt[...])
    qq, dd = biased(q), two_heads(do)
    qt, dot_ = q.T, do.T
    od = (o.astype(f32) * do.astype(f32)).T
    delta = jnp.concatenate(
        [jnp.sum(od[:HDIM], axis=0, keepdims=True), jnp.sum(od[HDIM:], axis=0, keepdims=True)],
        axis=1,
    )
    ls = lse_ref[0]
    lse = jnp.concatenate([ls[0:1], ls[1:2]], axis=1)

    dqt[...] = jnp.zeros_like(dqt)

    def tile(st, n, lo, diagonal):
        w = B - lo
        ks = pl.ds(pl.multiple_of(st, H), n)
        part = upper if lo else lambda v, axis: v
        s = dot(ka[ks, :], part(qq, 0), NT)
        dp = dot(v_ref[ks, :], part(dd, 0), NT)
        p = jnp.exp(s - part(lse, 1))
        if diagonal:
            p = jnp.where(causal(lo, n, lo, w), p, 0.0)
        ds = (p * (dp - part(delta, 1))).astype(bf16)
        pb = p.astype(bf16)
        for h in range(2):
            r, c = slice(HDIM * h, HDIM * h + HDIM), slice(h * w, h * w + w)
            dqt[r, lo:] += dot(kt[r, ks], ds[:, c])
            a = dot(qt[r, lo:], ds[:, c], NT)
            b = dot(dot_[r, lo:], pb[:, c], NT)
            if diagonal:
                dkt[r, ks] = a
                dvt[r, ks] = b
            else:
                dkt[r, ks] += a
                dvt[r, ks] += b

    lax.fori_loop(0, i, lambda j, c: (tile(j * B, B, 0, False), c)[1], 0)
    tile(i * B, H, 0, True)
    tile(i * B + H, H, H, True)
    dqs[pl.ds(pl.multiple_of(i * B, B), B), :] = dqt[...].T * HDIM**-0.5

    def copies(pair):
        width = gm_ref.shape[1] // 3
        for b in range(L // B):
            to = pl.ds(pl.multiple_of(jnp.bitwise_xor(b // 2, x_of(meta)) * B, B), B)
            for k in range(3):
                col = pl.ds(pl.multiple_of(k * width + (p0 + pair) * 128, 128), 128)
                src = stage.at[k, pl.ds(b * B, B), :]
                yield b, lambda g, to=to, col=col, src=src, k=k: pltpu.make_async_copy(
                    src, g.at[to, col], sem.at[k]
                )

    def send(pair):
        for b, copy in copies(pair):
            own = core_of(meta) == b % 2

            @pl.when(own)
            def _(copy=copy):
                copy(gm_ref).start()

            @pl.when(jnp.logical_not(own))
            def _(copy=copy):
                copy(gt_ref).start()

    def finish(pair):
        for _, copy in copies(pair):
            copy(gm_ref).wait()

    @pl.when(i == pl.num_programs(1) - 1)
    def _():
        pair = pl.program_id(0)
        gt[...] = jnp.zeros_like(gt)
        ext[...] = jnp.zeros_like(ext)

        @pl.when(pair > 0)
        def _():
            finish(pair)

        def back(n, carry):
            blk = L // B - 1 - n
            sl = pl.ds(pl.multiple_of(blk * B, B), B)
            for which, raw in enumerate((rq, rk, rv)):
                col = which * (taps.shape[1] // 3) + (p0 + pl.program_id(0)) * 128
                t = taps[:, pl.ds(pl.multiple_of(col, 128), 128)]
                g = dqs[sl, :] if which == 0 else (dkt, dvt)[which - 1][:, sl].T
                ext[which, B : B + 8, :] = ext[which, 0:8, :]
                ext[which, 0:B, :] = g
                g1, g2 = ext[which, 1 : B + 1, :], ext[which, 2 : B + 2, :]
                stage[which, sl, :] = (t[0:1] * g + t[1:2] * g1 + t[2:3] * g2).astype(bf16)
                r = raw[sl, :].astype(f32)
                for k, gg in enumerate((g, g1, g2)):
                    row = slice(3 * which + k, 3 * which + k + 1)
                    gt[row, :] += jnp.sum(r * gg, axis=0, keepdims=True)
            return carry

        lax.fori_loop(0, L // B, back, 0)
        send(pair)

        @pl.when(pair == pl.num_programs(0) - 1)
        def _():
            finish(pair)


def att_bwd_call(meta, mix, raw, om, ot, dm, dt, lse, taps, p0, count, into=None):
    length, cols = mix.shape
    pairs = cols // 384
    B = length // 4
    half = pl.BlockSpec((B, 128), lambda p, i, m: (jnp.bitwise_xor(i // 2, x_of(m)), p0 + p))
    full = lambda k: pl.BlockSpec((length, 128), lambda p, i, m: (0, k * pairs + p0 + p))
    return pl.pallas_call(
        functools.partial(att_bwd_body, p0, into is not None),
        out_shape=[sds((length // 2, cols), bf16)] * 2 + [sds((16, 128 * count), f32)],
        grid_spec=grid_spec(
            (count, 4),
            [
                pl.BlockSpec((B, 128), lambda p, i, m: (i, p0 + p)),
                full(1),
                full(2),
                half,
                half,
                half,
                half,
                pl.BlockSpec((1, 2, B), lambda p, i, m: (p0 + p, 0, i)),
                full(0),
                full(1),
                full(2),
                whole((8, cols)),
            ]
            + ([] if into is None else [pl.BlockSpec(memory_space=pl.ANY)] * 2),
            [pl.BlockSpec(memory_space=pl.ANY)] * 2 + [pl.BlockSpec((16, 128), lambda p, i, m: (0, p))],
            [
                pltpu.VMEM((length, 256), bf16),
                pltpu.VMEM((128, length), bf16),
                pltpu.VMEM((128, length), f32),
                pltpu.VMEM((128, length), f32),
                pltpu.VMEM((128, B), f32),
                pltpu.VMEM((length, 128), f32),
                pltpu.VMEM((3, B + 8, 128), f32),
                pltpu.VMEM((3, length, 128), bf16),
                pltpu.SemaphoreType.DMA((3,)),
            ],
        ),
        cost_estimate=cost(
            14 * length * length * 128 * count, 20 * length * 128 * count, 2 * length * length * count
        ),
        name="attn_bwd",
        input_output_aliases={} if into is None else {13: 0, 14: 1},
    )(meta, mix, mix, mix, om, ot, dm, dt, lse, raw, raw, raw, taps, *(into or ()))


T = 256


def valid_rows(meta, i, rows):
    per = rows // T
    block = jnp.where(i < per, meta[2], jnp.bitwise_xor(meta[2], 2))
    start = block * rows + lax.rem(i, per) * T
    return start + lax.broadcasted_iota(jnp.int32, (T, 1), 0) < length_of(meta)


def ffn_body(
    meta, xo, xx, co, cx, am, at, gain, wo_o, wo_c, pack,
    u_o, d_o, f_c, n0, n1, n2, n3, c0, c1, c2, c3,
    oo, ox, dm, dt, gg, dmid, gu0, gu1, gu2, gu3, gd0, gd1, gd2, gd3,
    wo, wus, wds, mid, h_s, g_s, fo, dh, act, du, stu, std, sto, gacc, sw, so, sg, sd, st,
):
    rows, width = xo.shape
    part = wo_o.shape[0]
    half = 2 * part
    n = 2 * rows // T
    per = rows // T
    copies = []
    for k, src in ((0, wo_o), (1, wo_c), (2, pack.at[pl.ds(rows, part), :]), (3, pack.at[pl.ds(rows + part, part), :])):
        shard = jnp.bitwise_xor(meta[2], k)
        row = jnp.where(shard // 2 == core_of(meta), 0, half) + lax.rem(shard, 2) * part
        cp = pltpu.make_async_copy(src, wo.at[pl.ds(pl.multiple_of(row, 64), part), :], so.at[k])
        cp.start()
        copies.append(cp)
    for k, pair in ((0, (f_c.at[0], f_c.at[1])), (2, (u_o, d_o))):
        for n_, src in enumerate(pair):
            pltpu.make_async_copy(src, (wus, wds)[n_].at[k], sw.at[k, n_]).start()
    for k, quarters in ((1, (c0, c1, c2, c3)), (3, (n0, n1, n2, n3))):
        for q_, src in enumerate(quarters):
            count = src.shape[1]
            to = pl.ds(pl.multiple_of(jnp.bitwise_xor(meta[3], q_) * count, 64), count)
            for n_, dst in enumerate((wus, wds)):
                pltpu.make_async_copy(src.at[n_], dst.at[k, to, :], sw.at[k, n_]).start()
    for cp in copies:
        cp.wait()
    gn = gain[...].astype(f32)

    def first_rows(i, carry):
        sl = pl.ds(pl.multiple_of(i * T, T), T)
        src = pl.ds(pl.multiple_of(lax.rem(i, per) * T, T), T)
        own = i < per
        x = jnp.where(own, xo[src, :], xx[src, :]).astype(f32)
        a = jnp.concatenate([am[sl, :], at[sl, :]], axis=1)
        m = x + dot(a, wo[...])
        mid[sl, :] = m
        fo[sl, :] = m
        h_s[sl, :] = norm(m, gn)[2]
        ct = jnp.where(own, co[src, :], cx[src, :])
        g_s[sl, :] = jnp.where(valid_rows(meta, i, rows), ct, jnp.zeros_like(ct))
        dh[sl, :] = jnp.zeros((T, width), f32)
        return carry

    lax.fori_loop(0, n, first_rows, 0)

    R = 1024
    C = 768

    gus, gds = (gu0, gu1, gu2, gu3), (gd0, gd1, gd2, gd3)

    def stores(n_, slot):
        return [
            pltpu.make_async_copy(stu.at[slot], gus[n_], sg.at[slot, 0]),
            pltpu.make_async_copy(std.at[slot], gds[n_].at[pl.ds(0, width), :], sg.at[slot, 1]),
        ]

    def shard(k, carry):
        for cp in (
            pltpu.make_async_copy(u_o, wus.at[k], sw.at[k, 0]),
            pltpu.make_async_copy(d_o, wds.at[k], sw.at[k, 1]),
        ):
            cp.wait()

        def rows_step(t, c2):
            sl = pl.ds(pl.multiple_of(t * R, R), R)
            h, g = h_s[sl, :], g_s[sl, :]
            r = jnp.maximum(dot(h, wus[k]), 0.0)
            a = (r * r).astype(bf16)
            d = (dot(g, wds[k], NT) * 2.0 * r).astype(bf16)
            act[sl, :] = a
            du[sl, :] = d
            fo[sl, :] += dot(a, wds[k])
            dh[sl, :] += dot(d, wus[k], NT)
            return c2

        lax.fori_loop(0, 2 * rows // R, rows_step, 0)
        slot = lax.rem(k, 2)

        @pl.when(k >= 2)
        def _():
            for cp in stores(0, slot):
                cp.wait()

        def cols_step(t, c2):
            sl = pl.ds(pl.multiple_of(t * C, C), C)
            stu[slot, :, sl] = dot(h_s[...], du[:, sl], TN).astype(bf16)
            std[slot, sl, :] = dot(act[:, sl], g_s[...], TN).astype(bf16)
            return c2

        lax.fori_loop(0, width // C, cols_step, 0)
        for n_ in range(4):

            @pl.when(k == n_)
            def _(n_=n_):
                for cp in stores(n_, n_ % 2):
                    cp.start()

        return carry

    lax.fori_loop(0, 4, shard, 0)
    gg[...] = jnp.zeros_like(gg)

    def last_rows(i, carry):
        sl = pl.ds(pl.multiple_of(i * T, T), T)
        dst = pl.ds(pl.multiple_of(lax.rem(i, per) * T, T), T)
        ok = valid_rows(meta, i, rows)
        m = mid[sl, :]
        out = jnp.where(ok, fo[sl, :], 0.0)

        fo[sl, :] = out

        @pl.when(i < per)
        def _():
            own = oo.at[meta[2] // 2, dst, :]
            pltpu.make_async_copy(fo.at[sl, :], own, sd.at[1]).start()

        @pl.when(i >= per)
        def _():
            ox[dst, :] = out.astype(bf16)

        nm, inv, _ = norm(m, gn)
        d = dh[sl, :]
        dn = d * gn
        r = g_s[sl, :].astype(f32) + inv * (dn - nm * jnp.mean(dn * nm, axis=-1, keepdims=True))
        mid[sl, :] = r
        pltpu.make_async_copy(mid.at[sl, :], dmid.at[sl, :], sd.at[0]).start()
        db = r.astype(bf16)
        du[sl, :] = db
        da = dot(db, wo[...], NT).astype(bf16)
        dm[sl, :] = da[:, :half]
        dt[sl, :] = da[:, half:]
        gg[...] += jnp.sum(d * nm, axis=0, keepdims=True)
        return carry

    lax.fori_loop(0, n, last_rows, 0)
    gacc[0:half, :] = dot(am[...], du[...], TN)
    gacc[half:, :] = dot(at[...], du[...], TN)
    outs = [
        pltpu.make_async_copy(mid, dmid, sd.at[0]),
        pltpu.make_async_copy(fo.at[pl.ds(0, rows), :], oo.at[meta[2] // 2], sd.at[1]),
    ]
    for k, k_ in enumerate((1, 3, 0, 2)):
        shard_ = jnp.bitwise_xor(meta[2], k_)
        row = jnp.where(shard_ // 2 == core_of(meta), 0, half) + lax.rem(shard_, 2) * part
        sto[k] = gacc[pl.ds(pl.multiple_of(row, 64), part), :].astype(bf16)
        cp = pltpu.make_async_copy(sto.at[k], gds[k].at[pl.ds(width, part), :], st.at[k])
        cp.start()
        outs.append(cp)
    for slot in range(2):
        outs.extend(stores(2 + slot, slot))
    for cp in outs:
        cp.wait()


def ffn_call(meta, xo, xx, co, cx, am, at, gain, wos, ffs):
    rows, width = xo.shape
    half = am.shape[1]
    part = half // 2
    hid = ffs[0].shape[1]
    hbm = pl.BlockSpec(memory_space=pl.ANY)
    vm = lambda *shape: whole(shape)
    all_rows = 2 * rows
    return pl.pallas_call(
        ffn_body,
        out_shape=[
            sds((2, rows, width), f32),
            sds((rows, width), bf16),
            sds((all_rows, half), bf16),
            sds((all_rows, half), bf16),
            sds((1, width), f32),
            sds((all_rows, width), f32),
        ]
        + [sds((width, hid), bf16)] * 4
        + [sds((hid + part, width), bf16)] * 4,
        grid_spec=grid_spec(
            (1,),
            [vm(rows, width)] * 4 + [vm(all_rows, half)] * 2 + [vm(1, width)] + [hbm] * 14,
            [
                hbm,
                vm(rows, width),
                vm(all_rows, half),
                vm(all_rows, half),
                vm(1, width),
            ]
            + [hbm] * 9,
            [
                pltpu.VMEM((width, width), bf16),
                pltpu.VMEM((4, width, hid), bf16),
                pltpu.VMEM((4, hid, width), bf16),
                pltpu.VMEM((all_rows, width), f32),
                pltpu.VMEM((all_rows, width), bf16),
                pltpu.VMEM((all_rows, width), bf16),
                pltpu.VMEM((all_rows, width), f32),
                pltpu.VMEM((all_rows, width), f32),
                pltpu.VMEM((all_rows, hid), bf16),
                pltpu.VMEM((all_rows, hid), bf16),
                pltpu.VMEM((2, width, hid), bf16),
                pltpu.VMEM((2, hid, width), bf16),
                pltpu.VMEM((4, part, width), bf16),
                pltpu.VMEM((width, width), f32),
                pltpu.SemaphoreType.DMA((4, 2)),
                pltpu.SemaphoreType.DMA((4,)),
                pltpu.SemaphoreType.DMA((2, 2)),
                pltpu.SemaphoreType.DMA((2,)),
                pltpu.SemaphoreType.DMA((4,)),
            ],
        ),
        cost_estimate=cost(
            48 * all_rows * width * hid + 6 * all_rows * width * width, 40 * all_rows * width
        ),
        compiler_params=pltpu.CompilerParams(vmem_limit_bytes=62 * 2**20),
        name="ffn",
    )(meta, xo, xx, co, cx, am, at, gain, *wos, *ffs)


def projg_body(meta, h, dm, dt, keep, far, send, acc):
    rows = dm.shape[0]
    acc[...] = dot(h[0:rows, :], dm[...], TN) + dot(h[rows:, :], dt[...], TN)
    part = keep.shape[0]
    for ref, k, row in ((keep, 0, 0), (far, 2, 0), (send, 1, 0), (send, 3, part)):
        at = jnp.bitwise_xor(meta[2], k)
        ref[row : row + part, :] = acc[pl.ds(pl.multiple_of(at * part, 64), part), :].astype(bf16)


def projg_call(meta, h, dm, dt):
    length, width = h.shape
    cols = dm.shape[1]
    step = cols // 3
    d = pl.BlockSpec((length // 2, step), lambda j, m: (0, j))
    g = lambda rows: pl.BlockSpec((rows, step), lambda j, m: (0, j))
    part = width // 4
    return pl.pallas_call(
        projg_body,
        out_shape=[sds((rows, cols), bf16) for rows in (part, part, 2 * part)],
        grid_spec=grid_spec(
            (3,),
            [whole((length, width)), d, d],
            [g(part), g(part), g(2 * part)],
            [pltpu.VMEM((width, step), f32)],
        ),
        cost_estimate=cost(length, length),
        name="projg",
    )(meta, h, dm, dt)


def last_body(meta, xo, xx, dm, dt, wm, wt, dmid, gain, go, gx, gg):
    i = pl.program_id(0)
    per = pl.num_programs(0) // 2
    first = i < per
    x = jnp.where(first, xo[...], xx[...]).astype(f32)
    gn = gain[...].astype(f32)
    n, inv, _ = norm(x, gn)
    dh = dot(dm[...], wm[...], NT) + dot(dt[...], wt[...], NT)
    dn = dh * gn
    out = dmid[...] + inv * (dn - n * jnp.mean(dn * n, axis=-1, keepdims=True))

    @pl.when(first)
    def _():
        go[0] = out

    @pl.when(jnp.logical_not(first))
    def _():
        gx[...] = out.astype(bf16)

    ps = jnp.sum(dh * n, axis=0, keepdims=True)

    @pl.when(i == 0)
    def _():
        gg[...] = ps

    @pl.when(i > 0)
    def _():
        gg[...] += ps


def own_map(per):
    return lambda i, m: (jnp.minimum(i, per - 1), 0)


def nb_map(per):
    return lambda i, m: (jnp.maximum(i - per, 0), 0)


def last_call(meta, xo, xx, dm, dt, wm, wt, dmid, gain):
    rows, width = xo.shape
    cols = dm.shape[1]
    per = rows // T
    fst, snd = pl.BlockSpec((T, width), own_map(per)), pl.BlockSpec((T, width), nb_map(per))
    blk = lambda n: pl.BlockSpec((T, n), lambda i, m: (i, 0))
    return pl.pallas_call(
        last_body,
        out_shape=[sds((2, rows, width), f32), sds((rows, width), bf16), sds((1, width), f32)],
        grid_spec=grid_spec(
            (2 * per,),
            [fst, snd, blk(cols), blk(cols)]
            + [whole((width, cols))] * 2
            + [blk(width), whole((1, width))],
            [
                pl.BlockSpec((1, T, width), lambda i, m: (x_of(m), jnp.minimum(i, per - 1), 0)),
                snd,
                pl.BlockSpec((1, width), lambda i, m: (0, 0)),
            ],
        ),
        cost_estimate=cost(rows, rows),
        name="last",
    )(meta, xo, xx, dm, dt, wm, wt, dmid, gain)


def flip(size, bit):
    return [(i, i ^ bit) for i in range(size)]


def core_swap(v):
    return lax.ppermute(v, "head", CORE)


def x_swap(v):
    return lax.ppermute(v, "head", XNB)


def after(v, *deps):
    return lax.optimization_barrier((v, *deps))[0]


def halve(terms, index, count):
    rows = terms[0].shape[0] // count
    piece = lambda t, k: lax.dynamic_slice_in_dim(t, jnp.bitwise_xor(index, k) * rows, rows, 0)
    total = lambda k: sum(piece(t, k).astype(f32) for t in terms)
    return [total(k).astype(bf16) for k in range(1, count)], total(0)


def strides(dp):
    out = [1]
    while 2 * out[-1] < dp:
        out.append(2 * out[-1])
    return out


def side(stride):
    return lax.axis_index("dp") // stride % 2


def swap(v, stride, dp):
    return lax.ppermute(v, "dp", flip(dp, stride))


def swap_both(vs, stride, dp):
    got = swap(jnp.concatenate(vs, axis=0), stride, dp)
    out, row = [], 0
    for v in vs:
        out.append(got[row : row + v.shape[0]])
        row += v.shape[0]
    return out


def scatter(sums, stride, dp):
    halves = [halve(terms, side(stride), 2) for terms in sums]
    send = jnp.concatenate([h[0][0] for h in halves], axis=0)
    got = swap(send, stride, dp)
    out, row = [], 0
    for (part,), keep in halves:
        out.append([keep, got[row : row + part.shape[0]]])
        row += part.shape[0]
    return out, send


def join(mine, got, stride):
    upper = side(stride) == 1
    return jnp.concatenate([jnp.where(upper, got, mine), jnp.where(upper, mine, got)], axis=0)


def total(terms):
    return sum(t.astype(f32) for t in terms)


def local(dp, inputs, lengths, w_query, w_key, w_value, w_out, w_up, w_down, conv_taps, gain_attn, gain_ff, cotangent):
    hd = lax.axis_index("head")
    x, c, y = hd // 2, hd % 2, lax.axis_index("dp") % 2
    q = lax.axis_index("dp") % 4
    width = inputs.shape[2]
    part = w_query.shape[0]
    half = 2 * part
    pick = lambda v, k: lax.dynamic_index_in_dim(v, k, 0, keepdims=False)
    y_swap = lambda v: lax.ppermute(v, "dp", flip(dp, 1))
    order = lambda own, nb: lax.dynamic_update_slice_in_dim(own, nb[None].astype(f32), 1 - x, 0)
    meta = jnp.concatenate([lengths, jnp.stack([hd, q])]).astype(jnp.int32)
    gain1, gain2 = gain_attn.reshape(1, width), gain_ff.reshape(1, width)

    mask = (jnp.arange(2) == c)[None, None, :, None]
    tap_rows = jnp.where(mask, conv_taps.transpose(1, 0, 2)[:, :, None, :], 0).reshape(3, 3 * half)
    tap_rows = jnp.concatenate([tap_rows[:, :width], jnp.pad(tap_rows[:, width:], ((0, 0), (0, half)))], axis=0)
    tap_rows = jnp.pad(tap_rows, ((0, 10), (0, 0)))

    def packed(k):
        cut = lambda w: lax.dynamic_slice_in_dim(w, k * half, half, 1)
        fold = cut(w_value)
        return jnp.concatenate(
            [
                jnp.concatenate([cut(w_query), cut(w_key)], axis=1),
                jnp.concatenate([fold[: part // 2], fold[part // 2 :]], axis=1),
                tap_rows,
            ],
            axis=0,
        )

    w_core = core_swap(packed(1 - c))
    w_mine = packed(c)
    x_own = pick(inputs, x)
    rows = x_own.shape[0]
    pack = x_swap(jnp.concatenate([pick(inputs, 1 - x), w_mine, w_core], axis=0))
    x_core = core_swap(x_own)
    count = width // 4
    quarter = lambda w: lax.dynamic_slice_in_dim(w, q * count, count, 0)
    wo_c = core_swap(w_out)
    c_own = pick(cotangent, x)
    ff_src = jnp.stack([quarter(w_up), quarter(w_down)])
    ff_own = jnp.stack([w_up, w_down])
    pack2 = jnp.concatenate([pick(cotangent, 1 - x), w_out, wo_c], axis=0)
    pack, ff_src, ff_own, pack2, c_own, meta, x_core = lax.optimization_barrier(
        (pack, ff_src, ff_own, pack2, c_own, meta, x_core)
    )
    x_cnb = core_swap(pack[:rows])
    h1, raw, mix, w_full, taps = qkv_call(meta, x_own, x_core, x_cnb, w_mine, w_core, pack, gain1)

    ff_first, pack2 = x_swap(ff_src), x_swap(pack2)
    ff_c = core_swap(ff_own)
    src = after(ff_first, mix)
    ff_n = [swap(src, k, dp) for k in (1, 2, 3)]
    a_mine, a_send, lse = att_fwd_call(meta, after(mix, src, ff_c))
    a_got = core_swap(a_send)
    w_other = core_swap(w_full)
    *ff_n, pack2 = lax.optimization_barrier((*ff_n, pack2, a_mine))[:-1]
    ff_n = [src, *ff_n]
    ff_cn = [core_swap(v) for v in ff_n]
    out_own, out_nb, d_mine, d_send, gg2, dmid, *gw = ffn_call(
        meta, x_own, pack, c_own, pack2, a_mine, a_got, after(gain2, w_other),
        (w_out, wo_c, pack2),
        (w_up, w_down, ff_c, *ff_n, *ff_cn),
    )
    d_got = core_swap(d_send)

    _, *rest = strides(dp)
    un, dn, do, uo = [core_swap(gw[k]) for k in (1, 5, 4, 0)]
    nu = total((gw[3], un)).astype(bf16)
    xu = x_swap(nu)
    (dn_send,), dn_keep = halve((gw[7], dn), y, 2)
    (do_send,), do_keep = halve((gw[6], do), y, 2)
    yn, yo = y_swap(dn_send), y_swap(do_send)
    out_x = x_swap(after(out_nb, nu))
    pairs = width // 256
    bwd = lambda m, p, n, into: att_bwd_call(
        meta, m, raw, a_mine, a_send, d_mine, d_got, lse, taps, p, n, into
    )
    *dall, gt_a = bwd(after(mix, nu, dn_send, do_send), 0, pairs - 1, None)
    xu, yn, yo, out_x = lax.optimization_barrier((xu, yn, yo, out_x, gt_a))[:4]
    (u_send,), u_keep = halve((gw[2], uo, xu), y, 2)
    nd = total((dn_keep, yn)).astype(bf16)
    yu, xd = y_swap(u_send), x_swap(nd)
    p_mine, p_theirs, gt_b = bwd(after(mix, u_send, nd), pairs - 1, 1, dall)
    p_got = core_swap(p_theirs)
    gt = jnp.concatenate([gt_a, gt_b], axis=1)
    yu, xd = lax.optimization_barrier((yu, xd, gt_b))[:2]
    sums, sent = scatter([[u_keep, yu], [do_keep, yo, xd]], rest[0], dp)
    keep, far, send = projg_call(meta, after(h1, sent), p_mine, p_theirs)
    flat = lax.optimization_barrier((*sums[0], *sums[1], keep))[:-1]
    sums, sent = scatter([flat[:2], flat[2:]], rest[1], dp)
    got = core_swap(after(send, sent))
    far = x_swap(jnp.concatenate([far, got[part:]], axis=0))
    gi_own, gi_nb, gg1 = last_call(
        meta, x_own, pack, p_mine, p_got, w_full, w_other, after(dmid, sent), gain1
    )
    *flat, far, gt = lax.optimization_barrier((*sums[0], *sums[1], far, gt, gi_nb))[:-1]
    far, far2 = far[:part], far[part:]
    sums = [flat[:2], flat[2:]]
    for stride in rest[2:]:
        sums, _ = scatter(sums, stride, dp)
    vs = [total(t).astype(bf16) for t in sums]
    ga, gb = keep.astype(f32) + far.astype(f32), got[:part].astype(f32) + far2.astype(f32)
    g_send, g_keep = jnp.where(y == 0, gb, ga).astype(bf16), jnp.where(y == 0, ga, gb)
    pt = [g_keep, y_swap(g_send)]
    gi_got = x_swap(gi_nb)
    for stride in reversed(rest[1:]):
        vs = [join(v, g, stride) for v, g in zip(vs, swap_both(vs, stride, dp))]
    others, across = swap_both(vs, rest[0], dp), swap_both(vs, 1, dp)
    for stride in rest:
        (pt,), _ = scatter([pt], stride, dp)
    ps = total(pt).astype(bf16)
    for stride in reversed(rest):
        ps = join(ps, swap(ps, stride, dp), stride)
    ps_got = y_swap(ps)
    also = swap_both(others, 1, dp)
    whole_of = lambda k: join(
        join(vs[k], others[k], rest[0]), join(across[k], also[k], rest[0]), 1
    ).astype(f32)
    grad_up, gd_all = whole_of(0), whole_of(1)
    grad_down, grad_out = gd_all[: w_down.shape[0]], gd_all[w_down.shape[0] :]
    lo, hi = jnp.where(y == c, ps, ps_got), jnp.where(y == c, ps_got, ps)
    third = lambda v, w: v[:, w * half : w * half + half]
    grads = [jnp.concatenate([third(lo, w), third(hi, w)], axis=1).astype(f32) for w in range(3)]

    gt = gt[:9].reshape(9, 2, part).transpose(1, 0, 2)
    gt = jnp.where(jnp.arange(2)[:, None, None, None] == c, gt[None], 0.0).reshape(4, 9, part)
    gains = jnp.concatenate([gg1, gg2], axis=0).reshape(2, 4, part).transpose(1, 0, 2)
    small = jnp.concatenate([gt, gains, jnp.zeros((4, 5, part), f32)], axis=1)
    small = jnp.broadcast_to(small[:, None], (4, dp, 16, part)).reshape(4 * dp, 16, part)
    small = jnp.sum(lax.all_to_all(small, ("head", "dp"), 0, 0, tiled=True), axis=0)
    output = order(after(out_own, gi_nb), out_x)
    grad_input = order(gi_own, gi_got)
    return (
        output,
        grad_input,
        *grads,
        grad_out,
        grad_up,
        grad_down,
        small[:9].reshape(3, 3, part),
        small[9],
        small[10],
    )


def solution(mesh):
    placed = (
        P("dp", "head", None),
        P("dp"),
        P("head", None),
        P("head", None),
        P("head", None),
        P("head", None),
        P(None, "head"),
        P("head", None),
        P(None, None, "head"),
        P(),
        P(),
        P("dp", "head", None),
    )
    return jax.shard_map(
        functools.partial(local, mesh.shape["dp"]),
        mesh=mesh,
        in_specs=placed,
        out_specs=(
            P("dp", "head", None),
            P("dp", "head", None),
            P("head", None),
            P("head", None),
            P("head", None),
            P("head", None),
            P(None, "head"),
            P("head", None),
            P(None, None, "head"),
            P("head"),
            P("head"),
        ),
        check_vma=False,
    )
```

```python
import functools

import jax
import jax.numpy as jnp
from jax import lax
from jax.experimental import pallas as pl
from jax.experimental.pallas import tpu as pltpu
from jax.sharding import PartitionSpec as P

HDIM = 64
EPS = 1e-06
bf16 = jnp.bfloat16
f32 = jnp.float32

NN = (((1,), (0,)), ((), ()))
NT = (((1,), (1,)), ((), ()))
TN = (((0,), (0,)), ((), ()))

CORE = [(0, 1), (1, 0), (2, 3), (3, 2)]
XNB = [(0, 2), (2, 0), (1, 3), (3, 1)]


def dot(a, b, dims=NN):
    return lax.dot_general(a, b, dims, preferred_element_type=f32)


def cost(flops, nbytes, trans=0):
    return pl.CostEstimate(flops=int(flops), bytes_accessed=int(nbytes), transcendentals=int(trans))


def sds(shape, dtype):
    return jax.ShapeDtypeStruct(shape, dtype)


def whole(shape):
    zeros = (0,) * len(shape)
    return pl.BlockSpec(shape, lambda *_: zeros, pipeline_mode=pl.Buffered(1))


def grid_spec(grid, ins, outs, scratch=()):
    return pltpu.PrefetchScalarGridSpec(
        num_scalar_prefetch=1, grid=grid, in_specs=ins, out_specs=outs, scratch_shapes=scratch
    )


def length_of(m):
    return m[m[2] // 2]


def x_of(m):
    return m[2] // 2


def core_of(m):
    return lax.rem(m[2], 2)


def slot_of(m, b):
    v = jnp.bitwise_xor(m[2], b)
    return lax.rem(v, 2) * 2 + v // 2


def norm(x, gain):
    inv = lax.rsqrt(jnp.mean(x * x, axis=-1, keepdims=True) + EPS)
    n = x * inv
    return n, inv, (n * gain).astype(bf16)


def qkv_body(meta, x0, x2, x3, wa, wb, pack, gain, h_ref, raw_ref, mix_ref, w_ref, taps, ext):
    b = pl.program_id(0)
    rows = x0.shape[0]
    part = w_ref.shape[0] // 4
    width = x0.shape[1]
    tall = wa.shape[0]
    hd = meta[2]

    @pl.when(b == 0)
    def _():
        def put(k, ref, first):
            at = jnp.bitwise_xor(hd, k) * part
            w_ref[pl.ds(pl.multiple_of(at, 64), part), 0:width] = ref[first : first + part, :]
            for n in range(2):
                row = pl.multiple_of(at + n * (part // 2), 32)
                w_ref[pl.ds(row, part // 2), width:] = ref[
                    first + part : first + part + part // 2, n * (width // 2) : (n + 1) * (width // 2)
                ]

        put(0, wa, 0)
        put(1, wb, 0)
        put(2, pack, rows)
        put(3, pack, rows + tall)
        last = lambda ref, end: ref[end - 16 : end, :].astype(f32)
        near = last(wa, tall) + last(wb, tall)
        far = last(pack, rows + tall) + last(pack, rows + 2 * tall)
        t = jnp.where(x_of(meta) == core_of(meta), near, far)
        taps[...] = jnp.zeros_like(taps)
        taps[0:3, 0:width] = t[0:3]
        taps[0:3, width:] = t[3:6, 0 : width // 2]
        ext[0:8, :] = jnp.zeros((8, ext.shape[1]), f32)

    slot = slot_of(meta, b)
    x = x0[...]
    for k, other in ((1, pack), (2, x2), (3, x3)):
        x = jnp.where(slot == k, other[0:rows, :], x)
    _, _, h = norm(x.astype(f32), gain[...].astype(f32))
    h_ref[...] = h
    raw = dot(h, w_ref[...]).astype(bf16)
    raw_ref[...] = raw
    rawf = raw.astype(f32)
    ext[8 : 8 + rows, :] = rawf
    t = taps[...]
    mixed = t[0:1] * rawf + t[1:2] * ext[7 : 7 + rows, :] + t[2:3] * ext[6 : 6 + rows, :]
    mix_ref[...] = mixed.astype(bf16)
    ext[0:8, :] = ext[rows : rows + 8, :]


def qkv_call(meta, x_own, x_core, x_cnb, w_mine, w_core, pack, gain):
    rows, width = x_own.shape
    tall = w_mine.shape[0]
    cols = width * 3 // 2
    length = 4 * rows
    blk = lambda n: pl.BlockSpec((rows, n), lambda b, m: (b, 0))
    const = lambda r: pl.BlockSpec((r, cols), lambda b, m: (0, 0))
    return pl.pallas_call(
        qkv_body,
        out_shape=[
            sds((length, width), bf16),
            sds((length, cols), bf16),
            sds((length, cols), bf16),
            sds((width, cols), bf16),
            sds((8, cols), f32),
        ],
        grid_spec=grid_spec(
            (4,),
            [whole((rows, width))] * 3
            + [whole((tall, width))] * 2
            + [whole(pack.shape), whole((1, width))],
            [
                pl.BlockSpec((rows, width), lambda b, m: (slot_of(m, b), 0)),
                blk(cols),
                blk(cols),
                const(width),
                const(8),
            ],
            [pltpu.VMEM((rows + 8, cols), f32)],
        ),
        cost_estimate=cost(2 * length * width * cols, 2 * length * (width * 2 + cols * 2)),
        name="qkv",
    )(meta, x_own, x_core, x_cnb, w_mine, w_core, pack, gain)


def two_heads(v):
    lane = lax.broadcasted_iota(jnp.int32, v.shape, 1)
    z = jnp.zeros_like(v)
    return jnp.concatenate([jnp.where(lane < HDIM, v, z), jnp.where(lane < HDIM, z, v)], axis=0)


def causal(first, keys, start, queries):
    key = first + lax.broadcasted_iota(jnp.int32, (keys, queries), 0)
    ok = key <= start + lax.broadcasted_iota(jnp.int32, (keys, queries), 1)
    return jnp.concatenate([ok, ok], axis=1)


def upper(v, axis):
    B = v.shape[axis] // 2
    h = B // 2
    if axis == 0:
        return jnp.concatenate([v[h:B], v[B + h :]], axis=0)
    return jnp.concatenate([v[:, h:B], v[:, B + h :]], axis=1)


def with_bias(k_ref, ka, length):
    L = k_ref.shape[0]
    ka[:, :128] = k_ref[...]
    lane = lax.broadcasted_iota(jnp.int32, (L, 128), 1)
    row = lax.broadcasted_iota(jnp.int32, (L, 128), 0)
    pad = jnp.logical_and(lane == 0, row >= length)
    ka[:, 128:] = jnp.where(pad, -1e9, 0.0).astype(bf16)


def biased(q):
    qq = two_heads(q)
    lane = lax.broadcasted_iota(jnp.int32, qq.shape, 1)
    return jnp.concatenate([qq, jnp.where(lane == 0, 1.0, 0.0).astype(bf16)], axis=1)


def att_fwd_body(meta, q_ref, k_ref, v_ref, mine_ref, theirs_ref, lse_ref, ka, vt, sc):
    i = pl.program_id(1)
    B = q_ref.shape[0]

    @pl.when(i == 0)
    def _():
        vt[...] = v_ref[...].T
        with_bias(k_ref, ka, length_of(meta))

    qq = biased(q_ref[...] * bf16(HDIM**-0.5))
    own = lax.rem(i, 2) == core_of(meta)

    def run(ii):
        m = None
        for j in range(ii + 1):
            ks = slice(j * B, j * B + B)
            s = dot(ka[ks, :], qq, NT)
            if j == ii:
                s = jnp.where(causal(0, B, 0, B), s, -1e9)
            sc[ks, :] = s
            mj = jnp.max(s, axis=0, keepdims=True)
            m = mj if m is None else jnp.maximum(m, mj)
        l = jnp.zeros((1, 2 * B), f32)
        acc = [jnp.zeros((HDIM, B), f32)] * 2
        for j in range(ii + 1):
            ks = slice(j * B, j * B + B)
            p = jnp.exp(sc[ks, :] - m)
            l = l + jnp.sum(p, axis=0, keepdims=True)
            pb = p.astype(bf16)
            for h in range(2):
                r = slice(HDIM * h, HDIM * h + HDIM)
                acc[h] = acc[h] + dot(vt[r, ks], pb[:, h * B : h * B + B])
        inv = 1.0 / l
        out = jnp.concatenate([acc[h] * inv[:, h * B : h * B + B] for h in range(2)], axis=0)
        out = out.T.astype(bf16)

        @pl.when(own)
        def _():
            mine_ref[...] = out

        @pl.when(jnp.logical_not(own))
        def _():
            theirs_ref[...] = out

        ls = m + jnp.log(l)
        lse_ref[0] = jnp.concatenate([ls[:, :B], ls[:, B:]], axis=0)

    for ii in range(4):
        pl.when(i == ii)(functools.partial(run, ii))


def half_map(p, i, m):
    return (jnp.bitwise_xor(i // 2, x_of(m)), p)


def att_fwd_call(meta, mix):
    length, cols = mix.shape
    width = cols // 3
    pairs = width // 128
    B = length // 4
    half = pl.BlockSpec((B, 128), half_map)
    return pl.pallas_call(
        att_fwd_body,
        out_shape=[
            sds((length // 2, width), bf16),
            sds((length // 2, width), bf16),
            sds((pairs, 2, length), f32),
        ],
        grid_spec=grid_spec(
            (pairs, 4),
            [
                pl.BlockSpec((B, 128), lambda p, i, m: (i, p)),
                pl.BlockSpec((length, 128), lambda p, i, m: (0, pairs + p)),
                pl.BlockSpec((length, 128), lambda p, i, m: (0, 2 * pairs + p)),
            ],
            [half, half, pl.BlockSpec((1, 2, B), lambda p, i, m: (p, 0, i))],
            [
                pltpu.VMEM((length, 256), bf16),
                pltpu.VMEM((128, length), bf16),
                pltpu.VMEM((length, 2 * B), f32),
            ],
        ),
        cost_estimate=cost(8 * length * length * width, 8 * length * width, 2 * length * length * pairs),
        name="attn_fwd",
    )(meta, mix, mix, mix)


def att_bwd_body(
    p0, aliased, meta, q_ref, k_ref, v_ref, om, ot, dm, dt, lse_ref, rq, rk, rv, taps, *refs
):
    gm_ref, gt_ref, gt, ka, kt, dkt, dvt, dqt, dqs, ext, stage, sem = refs[2:] if aliased else refs
    i = pl.program_id(1)
    B = q_ref.shape[0]
    L = k_ref.shape[0]
    H = B // 2

    @pl.when(i == 0)
    def _():
        kt[...] = k_ref[...].T
        with_bias(k_ref, ka, length_of(meta))

    own = lax.rem(i, 2) == core_of(meta)
    q = q_ref[...] * bf16(HDIM**-0.5)
    o = jnp.where(own, om[...], ot[...])
    do = jnp.where(own, dm[...], dt[...])
    qq, dd = biased(q), two_heads(do)
    qt, dot_ = q.T, do.T
    od = (o.astype(f32) * do.astype(f32)).T
    delta = jnp.concatenate(
        [jnp.sum(od[:HDIM], axis=0, keepdims=True), jnp.sum(od[HDIM:], axis=0, keepdims=True)],
        axis=1,
    )
    ls = lse_ref[0]
    lse = jnp.concatenate([ls[0:1], ls[1:2]], axis=1)

    dqt[...] = jnp.zeros_like(dqt)

    def tile(st, n, lo, diagonal):
        w = B - lo
        ks = pl.ds(pl.multiple_of(st, H), n)
        part = upper if lo else lambda v, axis: v
        s = dot(ka[ks, :], part(qq, 0), NT)
        dp = dot(v_ref[ks, :], part(dd, 0), NT)
        p = jnp.exp(s - part(lse, 1))
        if diagonal:
            p = jnp.where(causal(lo, n, lo, w), p, 0.0)
        ds = (p * (dp - part(delta, 1))).astype(bf16)
        pb = p.astype(bf16)
        for h in range(2):
            r, c = slice(HDIM * h, HDIM * h + HDIM), slice(h * w, h * w + w)
            dqt[r, lo:] += dot(kt[r, ks], ds[:, c])
            a = dot(qt[r, lo:], ds[:, c], NT)
            b = dot(dot_[r, lo:], pb[:, c], NT)
            if diagonal:
                dkt[r, ks] = a
                dvt[r, ks] = b
            else:
                dkt[r, ks] += a
                dvt[r, ks] += b

    lax.fori_loop(0, i, lambda j, c: (tile(j * B, B, 0, False), c)[1], 0)
    tile(i * B, H, 0, True)
    tile(i * B + H, H, H, True)
    dqs[pl.ds(pl.multiple_of(i * B, B), B), :] = dqt[...].T * HDIM**-0.5

    def copies(pair):
        width = gm_ref.shape[1] // 3
        for b in range(L // B):
            to = pl.ds(pl.multiple_of(jnp.bitwise_xor(b // 2, x_of(meta)) * B, B), B)
            for k in range(3):
                col = pl.ds(pl.multiple_of(k * width + (p0 + pair) * 128, 128), 128)
                src = stage.at[k, pl.ds(b * B, B), :]
                yield b, lambda g, to=to, col=col, src=src, k=k: pltpu.make_async_copy(
                    src, g.at[to, col], sem.at[k]
                )

    def send(pair):
        for b, copy in copies(pair):
            own = core_of(meta) == b % 2

            @pl.when(own)
            def _(copy=copy):
                copy(gm_ref).start()

            @pl.when(jnp.logical_not(own))
            def _(copy=copy):
                copy(gt_ref).start()

    def finish(pair):
        for _, copy in copies(pair):
            copy(gm_ref).wait()

    @pl.when(i == pl.num_programs(1) - 1)
    def _():
        pair = pl.program_id(0)
        gt[...] = jnp.zeros_like(gt)
        ext[...] = jnp.zeros_like(ext)

        @pl.when(pair > 0)
        def _():
            finish(pair)

        def back(n, carry):
            blk = L // B - 1 - n
            sl = pl.ds(pl.multiple_of(blk * B, B), B)
            for which, raw in enumerate((rq, rk, rv)):
                col = which * (taps.shape[1] // 3) + (p0 + pl.program_id(0)) * 128
                t = taps[:, pl.ds(pl.multiple_of(col, 128), 128)]
                g = dqs[sl, :] if which == 0 else (dkt, dvt)[which - 1][:, sl].T
                ext[which, B : B + 8, :] = ext[which, 0:8, :]
                ext[which, 0:B, :] = g
                g1, g2 = ext[which, 1 : B + 1, :], ext[which, 2 : B + 2, :]
                stage[which, sl, :] = (t[0:1] * g + t[1:2] * g1 + t[2:3] * g2).astype(bf16)
                r = raw[sl, :].astype(f32)
                for k, gg in enumerate((g, g1, g2)):
                    row = slice(3 * which + k, 3 * which + k + 1)
                    gt[row, :] += jnp.sum(r * gg, axis=0, keepdims=True)
            return carry

        lax.fori_loop(0, L // B, back, 0)
        send(pair)

        @pl.when(pair == pl.num_programs(0) - 1)
        def _():
            finish(pair)


def att_bwd_call(meta, mix, raw, om, ot, dm, dt, lse, taps, p0, count, into=None):
    length, cols = mix.shape
    pairs = cols // 384
    B = length // 4
    half = pl.BlockSpec((B, 128), lambda p, i, m: (jnp.bitwise_xor(i // 2, x_of(m)), p0 + p))
    full = lambda k: pl.BlockSpec((length, 128), lambda p, i, m: (0, k * pairs + p0 + p))
    return pl.pallas_call(
        functools.partial(att_bwd_body, p0, into is not None),
        out_shape=[sds((length // 2, cols), bf16)] * 2 + [sds((16, 128 * count), f32)],
        grid_spec=grid_spec(
            (count, 4),
            [
                pl.BlockSpec((B, 128), lambda p, i, m: (i, p0 + p)),
                full(1),
                full(2),
                half,
                half,
                half,
                half,
                pl.BlockSpec((1, 2, B), lambda p, i, m: (p0 + p, 0, i)),
                full(0),
                full(1),
                full(2),
                whole((8, cols)),
            ]
            + ([] if into is None else [pl.BlockSpec(memory_space=pl.ANY)] * 2),
            [pl.BlockSpec(memory_space=pl.ANY)] * 2 + [pl.BlockSpec((16, 128), lambda p, i, m: (0, p))],
            [
                pltpu.VMEM((length, 256), bf16),
                pltpu.VMEM((128, length), bf16),
                pltpu.VMEM((128, length), f32),
                pltpu.VMEM((128, length), f32),
                pltpu.VMEM((128, B), f32),
                pltpu.VMEM((length, 128), f32),
                pltpu.VMEM((3, B + 8, 128), f32),
                pltpu.VMEM((3, length, 128), bf16),
                pltpu.SemaphoreType.DMA((3,)),
            ],
        ),
        cost_estimate=cost(
            14 * length * length * 128 * count, 20 * length * 128 * count, 2 * length * length * count
        ),
        name="attn_bwd",
        input_output_aliases={} if into is None else {13: 0, 14: 1},
    )(meta, mix, mix, mix, om, ot, dm, dt, lse, raw, raw, raw, taps, *(into or ()))


T = 256


def valid_rows(meta, i, rows):
    per = rows // T
    block = jnp.where(i < per, meta[2], jnp.bitwise_xor(meta[2], 2))
    start = block * rows + lax.rem(i, per) * T
    return start + lax.broadcasted_iota(jnp.int32, (T, 1), 0) < length_of(meta)


def ffn_body(
    meta, xo, xx, co, cx, am, at, gain, wo_o, wo_c, pack,
    u_o, d_o, f_c, n0, n1, n2, n3, c0, c1, c2, c3,
    oo, ox, dm, dt, gg, dmid, gu0, gu1, gu2, gu3, gd0, gd1, gd2, gd3,
    wo, wus, wds, mid, h_s, g_s, fo, dh, act, du, stu, std, sto, gacc, sw, so, sg, sd, st,
):
    rows, width = xo.shape
    part = wo_o.shape[0]
    half = 2 * part
    n = 2 * rows // T
    per = rows // T
    copies = []
    for k, src in ((0, wo_o), (1, wo_c), (2, pack.at[pl.ds(rows, part), :]), (3, pack.at[pl.ds(rows + part, part), :])):
        shard = jnp.bitwise_xor(meta[2], k)
        row = jnp.where(shard // 2 == core_of(meta), 0, half) + lax.rem(shard, 2) * part
        cp = pltpu.make_async_copy(src, wo.at[pl.ds(pl.multiple_of(row, 64), part), :], so.at[k])
        cp.start()
        copies.append(cp)
    for k, pair in ((0, (f_c.at[0], f_c.at[1])), (2, (u_o, d_o))):
        for n_, src in enumerate(pair):
            pltpu.make_async_copy(src, (wus, wds)[n_].at[k], sw.at[k, n_]).start()
    for k, quarters in ((1, (c0, c1, c2, c3)), (3, (n0, n1, n2, n3))):
        for q_, src in enumerate(quarters):
            count = src.shape[1]
            to = pl.ds(pl.multiple_of(jnp.bitwise_xor(meta[3], q_) * count, 64), count)
            for n_, dst in enumerate((wus, wds)):
                pltpu.make_async_copy(src.at[n_], dst.at[k, to, :], sw.at[k, n_]).start()
    for cp in copies:
        cp.wait()
    gn = gain[...].astype(f32)

    def first_rows(i, carry):
        sl = pl.ds(pl.multiple_of(i * T, T), T)
        src = pl.ds(pl.multiple_of(lax.rem(i, per) * T, T), T)
        own = i < per
        x = jnp.where(own, xo[src, :], xx[src, :]).astype(f32)
        a = jnp.concatenate([am[sl, :], at[sl, :]], axis=1)
        m = x + dot(a, wo[...])
        mid[sl, :] = m
        fo[sl, :] = m
        h_s[sl, :] = norm(m, gn)[2]
        ct = jnp.where(own, co[src, :], cx[src, :])
        g_s[sl, :] = jnp.where(valid_rows(meta, i, rows), ct, jnp.zeros_like(ct))
        dh[sl, :] = jnp.zeros((T, width), f32)
        return carry

    lax.fori_loop(0, n, first_rows, 0)

    R = 1024
    C = 768

    gus, gds = (gu0, gu1, gu2, gu3), (gd0, gd1, gd2, gd3)

    def stores(n_, slot):
        return [
            pltpu.make_async_copy(stu.at[slot], gus[n_], sg.at[slot, 0]),
            pltpu.make_async_copy(std.at[slot], gds[n_].at[pl.ds(0, width), :], sg.at[slot, 1]),
        ]

    def shard(k, carry):
        for cp in (
            pltpu.make_async_copy(u_o, wus.at[k], sw.at[k, 0]),
            pltpu.make_async_copy(d_o, wds.at[k], sw.at[k, 1]),
        ):
            cp.wait()

        def rows_step(t, c2):
            sl = pl.ds(pl.multiple_of(t * R, R), R)
            h, g = h_s[sl, :], g_s[sl, :]
            r = jnp.maximum(dot(h, wus[k]), 0.0)
            a = (r * r).astype(bf16)
            d = (dot(g, wds[k], NT) * 2.0 * r).astype(bf16)
            act[sl, :] = a
            du[sl, :] = d
            fo[sl, :] += dot(a, wds[k])
            dh[sl, :] += dot(d, wus[k], NT)
            return c2

        lax.fori_loop(0, 2 * rows // R, rows_step, 0)
        slot = lax.rem(k, 2)

        @pl.when(k >= 2)
        def _():
            for cp in stores(0, slot):
                cp.wait()

        def cols_step(t, c2):
            sl = pl.ds(pl.multiple_of(t * C, C), C)
            stu[slot, :, sl] = dot(h_s[...], du[:, sl], TN).astype(bf16)
            std[slot, sl, :] = dot(act[:, sl], g_s[...], TN).astype(bf16)
            return c2

        lax.fori_loop(0, width // C, cols_step, 0)
        for n_ in range(4):

            @pl.when(k == n_)
            def _(n_=n_):
                for cp in stores(n_, n_ % 2):
                    cp.start()

        return carry

    lax.fori_loop(0, 4, shard, 0)
    gg[...] = jnp.zeros_like(gg)

    def last_rows(i, carry):
        sl = pl.ds(pl.multiple_of(i * T, T), T)
        dst = pl.ds(pl.multiple_of(lax.rem(i, per) * T, T), T)
        ok = valid_rows(meta, i, rows)
        m = mid[sl, :]
        out = jnp.where(ok, fo[sl, :], 0.0)

        fo[sl, :] = out

        @pl.when(i < per)
        def _():
            own = oo.at[meta[2] // 2, dst, :]
            pltpu.make_async_copy(fo.at[sl, :], own, sd.at[1]).start()

        @pl.when(i >= per)
        def _():
            ox[dst, :] = out.astype(bf16)

        nm, inv, _ = norm(m, gn)
        d = dh[sl, :]
        dn = d * gn
        r = g_s[sl, :].astype(f32) + inv * (dn - nm * jnp.mean(dn * nm, axis=-1, keepdims=True))
        mid[sl, :] = r
        pltpu.make_async_copy(mid.at[sl, :], dmid.at[sl, :], sd.at[0]).start()
        db = r.astype(bf16)
        du[sl, :] = db
        da = dot(db, wo[...], NT).astype(bf16)
        dm[sl, :] = da[:, :half]
        dt[sl, :] = da[:, half:]
        gg[...] += jnp.sum(d * nm, axis=0, keepdims=True)
        return carry

    lax.fori_loop(0, n, last_rows, 0)
    gacc[0:half, :] = dot(am[...], du[...], TN)
    gacc[half:, :] = dot(at[...], du[...], TN)
    outs = [
        pltpu.make_async_copy(mid, dmid, sd.at[0]),
        pltpu.make_async_copy(fo.at[pl.ds(0, rows), :], oo.at[meta[2] // 2], sd.at[1]),
    ]
    for k, k_ in enumerate((1, 3, 0, 2)):
        shard_ = jnp.bitwise_xor(meta[2], k_)
        row = jnp.where(shard_ // 2 == core_of(meta), 0, half) + lax.rem(shard_, 2) * part
        sto[k] = gacc[pl.ds(pl.multiple_of(row, 64), part), :].astype(bf16)
        cp = pltpu.make_async_copy(sto.at[k], gds[k].at[pl.ds(width, part), :], st.at[k])
        cp.start()
        outs.append(cp)
    for slot in range(2):
        outs.extend(stores(2 + slot, slot))
    for cp in outs:
        cp.wait()


def ffn_call(meta, xo, xx, co, cx, am, at, gain, wos, ffs):
    rows, width = xo.shape
    half = am.shape[1]
    part = half // 2
    hid = ffs[0].shape[1]
    hbm = pl.BlockSpec(memory_space=pl.ANY)
    vm = lambda *shape: whole(shape)
    all_rows = 2 * rows
    return pl.pallas_call(
        ffn_body,
        out_shape=[
            sds((2, rows, width), f32),
            sds((rows, width), bf16),
            sds((all_rows, half), bf16),
            sds((all_rows, half), bf16),
            sds((1, width), f32),
            sds((all_rows, width), f32),
        ]
        + [sds((width, hid), bf16)] * 4
        + [sds((hid + part, width), bf16)] * 4,
        grid_spec=grid_spec(
            (1,),
            [vm(rows, width)] * 4 + [vm(all_rows, half)] * 2 + [vm(1, width)] + [hbm] * 14,
            [
                hbm,
                vm(rows, width),
                vm(all_rows, half),
                vm(all_rows, half),
                vm(1, width),
            ]
            + [hbm] * 9,
            [
                pltpu.VMEM((width, width), bf16),
                pltpu.VMEM((4, width, hid), bf16),
                pltpu.VMEM((4, hid, width), bf16),
                pltpu.VMEM((all_rows, width), f32),
                pltpu.VMEM((all_rows, width), bf16),
                pltpu.VMEM((all_rows, width), bf16),
                pltpu.VMEM((all_rows, width), f32),
                pltpu.VMEM((all_rows, width), f32),
                pltpu.VMEM((all_rows, hid), bf16),
                pltpu.VMEM((all_rows, hid), bf16),
                pltpu.VMEM((2, width, hid), bf16),
                pltpu.VMEM((2, hid, width), bf16),
                pltpu.VMEM((4, part, width), bf16),
                pltpu.VMEM((width, width), f32),
                pltpu.SemaphoreType.DMA((4, 2)),
                pltpu.SemaphoreType.DMA((4,)),
                pltpu.SemaphoreType.DMA((2, 2)),
                pltpu.SemaphoreType.DMA((2,)),
                pltpu.SemaphoreType.DMA((4,)),
            ],
        ),
        cost_estimate=cost(
            48 * all_rows * width * hid + 6 * all_rows * width * width, 40 * all_rows * width
        ),
        compiler_params=pltpu.CompilerParams(vmem_limit_bytes=62 * 2**20),
        name="ffn",
    )(meta, xo, xx, co, cx, am, at, gain, *wos, *ffs)


def projg_body(meta, h, dm, dt, keep, far, send, acc):
    rows = dm.shape[0]
    acc[...] = dot(h[0:rows, :], dm[...], TN) + dot(h[rows:, :], dt[...], TN)
    part = keep.shape[0]
    for ref, k, row in ((keep, 0, 0), (far, 2, 0), (send, 1, 0), (send, 3, part)):
        at = jnp.bitwise_xor(meta[2], k)
        ref[row : row + part, :] = acc[pl.ds(pl.multiple_of(at * part, 64), part), :].astype(bf16)


def projg_call(meta, h, dm, dt):
    length, width = h.shape
    cols = dm.shape[1]
    step = cols // 3
    d = pl.BlockSpec((length // 2, step), lambda j, m: (0, j))
    g = lambda rows: pl.BlockSpec((rows, step), lambda j, m: (0, j))
    part = width // 4
    return pl.pallas_call(
        projg_body,
        out_shape=[sds((rows, cols), bf16) for rows in (part, part, 2 * part)],
        grid_spec=grid_spec(
            (3,),
            [whole((length, width)), d, d],
            [g(part), g(part), g(2 * part)],
            [pltpu.VMEM((width, step), f32)],
        ),
        cost_estimate=cost(length, length),
        name="projg",
    )(meta, h, dm, dt)


def last_body(meta, xo, xx, dm, dt, wm, wt, dmid, gain, go, gx, gg):
    i = pl.program_id(0)
    per = pl.num_programs(0) // 2
    first = i < per
    x = jnp.where(first, xo[...], xx[...]).astype(f32)
    gn = gain[...].astype(f32)
    n, inv, _ = norm(x, gn)
    dh = dot(dm[...], wm[...], NT) + dot(dt[...], wt[...], NT)
    dn = dh * gn
    out = dmid[...] + inv * (dn - n * jnp.mean(dn * n, axis=-1, keepdims=True))

    @pl.when(first)
    def _():
        go[0] = out

    @pl.when(jnp.logical_not(first))
    def _():
        gx[...] = out.astype(bf16)

    ps = jnp.sum(dh * n, axis=0, keepdims=True)

    @pl.when(i == 0)
    def _():
        gg[...] = ps

    @pl.when(i > 0)
    def _():
        gg[...] += ps


def own_map(per):
    return lambda i, m: (jnp.minimum(i, per - 1), 0)


def nb_map(per):
    return lambda i, m: (jnp.maximum(i - per, 0), 0)


def last_call(meta, xo, xx, dm, dt, wm, wt, dmid, gain):
    rows, width = xo.shape
    cols = dm.shape[1]
    per = rows // T
    fst, snd = pl.BlockSpec((T, width), own_map(per)), pl.BlockSpec((T, width), nb_map(per))
    blk = lambda n: pl.BlockSpec((T, n), lambda i, m: (i, 0))
    return pl.pallas_call(
        last_body,
        out_shape=[sds((2, rows, width), f32), sds((rows, width), bf16), sds((1, width), f32)],
        grid_spec=grid_spec(
            (2 * per,),
            [fst, snd, blk(cols), blk(cols)]
            + [whole((width, cols))] * 2
            + [blk(width), whole((1, width))],
            [
                pl.BlockSpec((1, T, width), lambda i, m: (x_of(m), jnp.minimum(i, per - 1), 0)),
                snd,
                pl.BlockSpec((1, width), lambda i, m: (0, 0)),
            ],
        ),
        cost_estimate=cost(rows, rows),
        name="last",
    )(meta, xo, xx, dm, dt, wm, wt, dmid, gain)


def flip(size, bit):
    return [(i, i ^ bit) for i in range(size)]


def core_swap(v):
    return lax.ppermute(v, "head", CORE)


def x_swap(v):
    return lax.ppermute(v, "head", XNB)


def after(v, *deps):
    return lax.optimization_barrier((v, *deps))[0]


def halve(terms, index, count):
    rows = terms[0].shape[0] // count
    piece = lambda t, k: lax.dynamic_slice_in_dim(t, jnp.bitwise_xor(index, k) * rows, rows, 0)
    total = lambda k: sum(piece(t, k).astype(f32) for t in terms)
    return [total(k).astype(bf16) for k in range(1, count)], total(0)


def strides(dp):
    out = [1]
    while 2 * out[-1] < dp:
        out.append(2 * out[-1])
    return out


def side(stride):
    return lax.axis_index("dp") // stride % 2


def swap(v, stride, dp):
    return lax.ppermute(v, "dp", flip(dp, stride))


def rows_as(got, vs):
    out, row = [], 0
    for v in vs:
        out.append(got[row : row + v.shape[0]])
        row += v.shape[0]
    return out


def swap_both(vs, stride, dp):
    return rows_as(swap(jnp.concatenate(vs, axis=0), stride, dp), vs)


def scatter(sums, stride, dp):
    halves = [halve(terms, side(stride), 2) for terms in sums]
    send = jnp.concatenate([h[0][0] for h in halves], axis=0)
    got = swap(send, stride, dp)
    out, row = [], 0
    for (part,), keep in halves:
        out.append([keep, got[row : row + part.shape[0]]])
        row += part.shape[0]
    return out, send


def join(mine, got, stride):
    upper = side(stride) == 1
    return jnp.concatenate([jnp.where(upper, got, mine), jnp.where(upper, mine, got)], axis=0)


def total(terms):
    return sum(t.astype(f32) for t in terms)


def local(dp, inputs, lengths, w_query, w_key, w_value, w_out, w_up, w_down, conv_taps, gain_attn, gain_ff, cotangent):
    hd = lax.axis_index("head")
    x, c, y = hd // 2, hd % 2, lax.axis_index("dp") % 2
    q = lax.axis_index("dp") % 4
    width = inputs.shape[2]
    part = w_query.shape[0]
    half = 2 * part
    pick = lambda v, k: lax.dynamic_index_in_dim(v, k, 0, keepdims=False)
    y_swap = lambda v: lax.ppermute(v, "dp", flip(dp, 1))
    order = lambda own, nb: lax.dynamic_update_slice_in_dim(own, nb[None].astype(f32), 1 - x, 0)
    meta = jnp.concatenate([lengths, jnp.stack([hd, q])]).astype(jnp.int32)
    gain1, gain2 = gain_attn.reshape(1, width), gain_ff.reshape(1, width)

    mask = (jnp.arange(2) == c)[None, None, :, None]
    tap_rows = jnp.where(mask, conv_taps.transpose(1, 0, 2)[:, :, None, :], 0).reshape(3, 3 * half)
    tap_rows = jnp.concatenate([tap_rows[:, :width], jnp.pad(tap_rows[:, width:], ((0, 0), (0, half)))], axis=0)
    tap_rows = jnp.pad(tap_rows, ((0, 10), (0, 0)))

    def packed(k):
        cut = lambda w: lax.dynamic_slice_in_dim(w, k * half, half, 1)
        fold = cut(w_value)
        return jnp.concatenate(
            [
                jnp.concatenate([cut(w_query), cut(w_key)], axis=1),
                jnp.concatenate([fold[: part // 2], fold[part // 2 :]], axis=1),
                tap_rows,
            ],
            axis=0,
        )

    w_core = core_swap(packed(1 - c))
    w_mine = packed(c)
    x_own = pick(inputs, x)
    rows = x_own.shape[0]
    pack = x_swap(jnp.concatenate([pick(inputs, 1 - x), w_mine, w_core], axis=0))
    x_core = core_swap(x_own)
    count = width // 4
    quarter = lambda w: lax.dynamic_slice_in_dim(w, q * count, count, 0)
    wo_c = core_swap(w_out)
    c_own = pick(cotangent, x)
    ff_src = jnp.stack([quarter(w_up), quarter(w_down)])
    ff_own = jnp.stack([w_up, w_down])
    pack2 = jnp.concatenate([pick(cotangent, 1 - x), w_out, wo_c], axis=0)
    pack, ff_src, ff_own, pack2, c_own, meta, x_core = lax.optimization_barrier(
        (pack, ff_src, ff_own, pack2, c_own, meta, x_core)
    )
    x_cnb = core_swap(pack[:rows])
    h1, raw, mix, w_full, taps = qkv_call(meta, x_own, x_core, x_cnb, w_mine, w_core, pack, gain1)

    ff_first, pack2 = x_swap(ff_src), x_swap(pack2)
    ff_c = core_swap(ff_own)
    src = after(ff_first, mix)
    ff_n = [swap(src, k, dp) for k in (1, 2, 3)]
    a_mine, a_send, lse = att_fwd_call(meta, after(mix, src, ff_c))
    a_got = core_swap(a_send)
    w_other = core_swap(w_full)
    *ff_n, pack2 = lax.optimization_barrier((*ff_n, pack2, a_mine))[:-1]
    ff_n = [src, *ff_n]
    ff_cn = [core_swap(v) for v in ff_n]
    out_own, out_nb, d_mine, d_send, gg2, dmid, *gw = ffn_call(
        meta, x_own, pack, c_own, pack2, a_mine, a_got, after(gain2, w_other),
        (w_out, wo_c, pack2),
        (w_up, w_down, ff_c, *ff_n, *ff_cn),
    )
    d_got = core_swap(d_send)

    _, *rest = strides(dp)
    un, dn, do, uo = [core_swap(gw[k]) for k in (1, 5, 4, 0)]
    nu = total((gw[3], un)).astype(bf16)
    xu = x_swap(nu)
    (dn_send,), dn_keep = halve((gw[7], dn), y, 2)
    (do_send,), do_keep = halve((gw[6], do), y, 2)
    yn, yo = y_swap(dn_send), y_swap(do_send)
    out_x = x_swap(after(out_nb, nu))
    pairs = width // 256
    bwd = lambda m, p, n, into: att_bwd_call(
        meta, m, raw, a_mine, a_send, d_mine, d_got, lse, taps, p, n, into
    )
    *dall, gt_a = bwd(after(mix, nu, dn_send, do_send), 0, pairs - 1, None)
    xu, yn, yo, out_x = lax.optimization_barrier((xu, yn, yo, out_x, gt_a))[:4]
    (u_send,), u_keep = halve((gw[2], uo, xu), y, 2)
    nd = total((dn_keep, yn)).astype(bf16)
    yu, xd = y_swap(u_send), x_swap(nd)
    p_mine, p_theirs, gt_b = bwd(after(mix, u_send, nd), pairs - 1, 1, dall)
    p_got = core_swap(p_theirs)
    gt = jnp.concatenate([gt_a, gt_b], axis=1)
    yu, xd = lax.optimization_barrier((yu, xd, gt_b))[:2]
    sums, sent = scatter([[u_keep, yu], [do_keep, yo, xd]], rest[0], dp)
    keep, far, send = projg_call(meta, after(h1, sent), p_mine, p_theirs)
    flat = lax.optimization_barrier((*sums[0], *sums[1], keep))[:-1]
    sums, sent = scatter([flat[:2], flat[2:]], rest[1], dp)
    got = core_swap(after(send, sent))
    far = x_swap(jnp.concatenate([far, got[part:]], axis=0))
    gi_own, gi_nb, gg1 = last_call(
        meta, x_own, pack, p_mine, p_got, w_full, w_other, after(dmid, sent), gain1
    )
    *flat, gt = lax.optimization_barrier((*sums[0], *sums[1], gt, gi_nb))[:-1]
    sums = [flat[:2], flat[2:]]
    for stride in rest[2:]:
        sums, _ = scatter(sums, stride, dp)
    vs = [total(t).astype(bf16) for t in sums]
    far = after(far, *vs)
    far, far2 = far[:part], far[part:]
    ga, gb = keep.astype(f32) + far.astype(f32), got[:part].astype(f32) + far2.astype(f32)
    g_send, g_keep = jnp.where(y == 0, gb, ga).astype(bf16), jnp.where(y == 0, ga, gb)
    pt = [g_keep, y_swap(g_send)]
    gi_got = x_swap(after(gi_nb, g_send))
    for stride in reversed(rest[1:]):
        vs = [join(v, g, stride) for v, g in zip(vs, swap_both(vs, stride, dp))]
    (pt,), sent = scatter([pt], rest[0], dp)
    *vs, _ = lax.optimization_barrier((*vs, sent))
    packed_vs = jnp.concatenate(vs, axis=0)
    near_got = swap(packed_vs, rest[0], dp)
    across = rows_as(y_swap(packed_vs), vs)
    for stride in rest[1:]:
        (pt,), _ = scatter([pt], stride, dp)
    others, also = rows_as(near_got, vs), rows_as(y_swap(near_got), vs)
    ps = after(total(pt).astype(bf16), near_got)
    for stride in reversed(rest):
        ps = join(ps, swap(ps, stride, dp), stride)
    ps_got = y_swap(ps)
    whole_of = lambda k: join(
        join(vs[k], others[k], rest[0]), join(across[k], also[k], rest[0]), 1
    ).astype(f32)
    grad_up, gd_all = whole_of(0), whole_of(1)
    grad_down, grad_out = gd_all[: w_down.shape[0]], gd_all[w_down.shape[0] :]
    lo, hi = jnp.where(y == c, ps, ps_got), jnp.where(y == c, ps_got, ps)
    third = lambda v, w: v[:, w * half : w * half + half]
    grads = [jnp.concatenate([third(lo, w), third(hi, w)], axis=1).astype(f32) for w in range(3)]

    gt = gt[:9].reshape(9, 2, part).transpose(1, 0, 2)
    gt = jnp.where(jnp.arange(2)[:, None, None, None] == c, gt[None], 0.0).reshape(4, 9, part)
    gains = jnp.concatenate([gg1, gg2], axis=0).reshape(2, 4, part).transpose(1, 0, 2)
    small = jnp.concatenate([gt, gains, jnp.zeros((4, 5, part), f32)], axis=1)
    small = jnp.broadcast_to(small[:, None], (4, dp, 16, part)).reshape(4 * dp, 16, part)
    small = jnp.sum(lax.all_to_all(small, ("head", "dp"), 0, 0, tiled=True), axis=0)
    output = order(after(out_own, g_send), out_x)
    grad_input = order(after(gi_own, ps), gi_got)
    return (
        output,
        grad_input,
        *grads,
        grad_out,
        grad_up,
        grad_down,
        small[:9].reshape(3, 3, part),
        small[9],
        small[10],
    )


def solution(mesh):
    placed = (
        P("dp", "head", None),
        P("dp"),
        P("head", None),
        P("head", None),
        P("head", None),
        P("head", None),
        P(None, "head"),
        P("head", None),
        P(None, None, "head"),
        P(),
        P(),
        P("dp", "head", None),
    )
    return jax.shard_map(
        functools.partial(local, mesh.shape["dp"]),
        mesh=mesh,
        in_specs=placed,
        out_specs=(
            P("dp", "head", None),
            P("dp", "head", None),
            P("head", None),
            P("head", None),
            P("head", None),
            P("head", None),
            P(None, "head"),
            P("head", None),
            P(None, None, "head"),
            P("head"),
            P("head"),
        ),
        check_vma=False,
    )
```

```python
import functools

import jax
import jax.numpy as jnp
from jax import lax
from jax.experimental import pallas as pl
from jax.experimental.pallas import tpu as pltpu
from jax.sharding import PartitionSpec as P

HDIM = 64
EPS = 1e-06
bf16 = jnp.bfloat16
f32 = jnp.float32

NN = (((1,), (0,)), ((), ()))
NT = (((1,), (1,)), ((), ()))
TN = (((0,), (0,)), ((), ()))

CORE = [(0, 1), (1, 0), (2, 3), (3, 2)]
XNB = [(0, 2), (2, 0), (1, 3), (3, 1)]


def dot(a, b, dims=NN):
    return lax.dot_general(a, b, dims, preferred_element_type=f32)


def cost(flops, nbytes, trans=0):
    return pl.CostEstimate(flops=int(flops), bytes_accessed=int(nbytes), transcendentals=int(trans))


def sds(shape, dtype):
    return jax.ShapeDtypeStruct(shape, dtype)


def whole(shape):
    zeros = (0,) * len(shape)
    return pl.BlockSpec(shape, lambda *_: zeros, pipeline_mode=pl.Buffered(1))


def grid_spec(grid, ins, outs, scratch=()):
    return pltpu.PrefetchScalarGridSpec(
        num_scalar_prefetch=1, grid=grid, in_specs=ins, out_specs=outs, scratch_shapes=scratch
    )


def length_of(m):
    return m[m[2] // 2]


def x_of(m):
    return m[2] // 2


def core_of(m):
    return lax.rem(m[2], 2)


def slot_of(m, b):
    v = jnp.bitwise_xor(m[2], b)
    return lax.rem(v, 2) * 2 + v // 2


def norm(x, gain):
    inv = lax.rsqrt(jnp.mean(x * x, axis=-1, keepdims=True) + EPS)
    n = x * inv
    return n, inv, (n * gain).astype(bf16)


def qkv_body(meta, x0, x2, x3, wa, wb, pack, gain, h_ref, raw_ref, mix_ref, w_ref, taps, ext):
    b = pl.program_id(0)
    rows = x0.shape[0]
    part = w_ref.shape[0] // 4
    width = x0.shape[1]
    tall = wa.shape[0]
    hd = meta[2]

    @pl.when(b == 0)
    def _():
        def put(k, ref, first):
            at = jnp.bitwise_xor(hd, k) * part
            w_ref[pl.ds(pl.multiple_of(at, 64), part), 0:width] = ref[first : first + part, :]
            for n in range(2):
                row = pl.multiple_of(at + n * (part // 2), 32)
                w_ref[pl.ds(row, part // 2), width:] = ref[
                    first + part : first + part + part // 2, n * (width // 2) : (n + 1) * (width // 2)
                ]

        put(0, wa, 0)
        put(1, wb, 0)
        put(2, pack, rows)
        put(3, pack, rows + tall)
        last = lambda ref, end: ref[end - 16 : end, :].astype(f32)
        near = last(wa, tall) + last(wb, tall)
        far = last(pack, rows + tall) + last(pack, rows + 2 * tall)
        t = jnp.where(x_of(meta) == core_of(meta), near, far)
        taps[...] = jnp.zeros_like(taps)
        taps[0:3, 0:width] = t[0:3]
        taps[0:3, width:] = t[3:6, 0 : width // 2]
        ext[0:8, :] = jnp.zeros((8, ext.shape[1]), f32)

    slot = slot_of(meta, b)
    step = ext.shape[0] - 8

    def some(n, carry):
        sl = pl.ds(pl.multiple_of(n * step, step), step)
        x = x0[sl, :]
        for k, other in ((1, pack), (2, x2), (3, x3)):
            x = jnp.where(slot == k, other[sl, :], x)
        _, _, h = norm(x.astype(f32), gain[...].astype(f32))
        h_ref[sl, :] = h
        raw = dot(h, w_ref[...]).astype(bf16)
        raw_ref[sl, :] = raw
        rawf = raw.astype(f32)
        ext[8:, :] = rawf
        t = taps[...]
        mixed = t[0:1] * rawf + t[1:2] * ext[7 : 7 + step, :] + t[2:3] * ext[6 : 6 + step, :]
        mix_ref[sl, :] = mixed.astype(bf16)
        ext[0:8, :] = ext[step:, :]
        return carry

    lax.fori_loop(0, rows // step, some, 0)


def qkv_call(meta, x_own, x_core, x_cnb, w_mine, w_core, pack, gain):
    rows, width = x_own.shape
    tall = w_mine.shape[0]
    cols = width * 3 // 2
    length = 4 * rows
    blk = lambda n: pl.BlockSpec((rows, n), lambda b, m: (b, 0))
    const = lambda r: pl.BlockSpec((r, cols), lambda b, m: (0, 0))
    return pl.pallas_call(
        qkv_body,
        out_shape=[
            sds((length, width), bf16),
            sds((length, cols), bf16),
            sds((length, cols), bf16),
            sds((width, cols), bf16),
            sds((8, cols), f32),
        ],
        grid_spec=grid_spec(
            (4,),
            [whole((rows, width))] * 3
            + [whole((tall, width))] * 2
            + [whole(pack.shape), whole((1, width))],
            [
                pl.BlockSpec((rows, width), lambda b, m: (slot_of(m, b), 0)),
                blk(cols),
                blk(cols),
                const(width),
                const(8),
            ],
            [pltpu.VMEM((T + 8, cols), f32)],
        ),
        cost_estimate=cost(2 * length * width * cols, 2 * length * (width * 2 + cols * 2)),
        name="qkv",
    )(meta, x_own, x_core, x_cnb, w_mine, w_core, pack, gain)


def two_heads(v):
    lane = lax.broadcasted_iota(jnp.int32, v.shape, 1)
    z = jnp.zeros_like(v)
    return jnp.concatenate([jnp.where(lane < HDIM, v, z), jnp.where(lane < HDIM, z, v)], axis=0)


def causal(first, keys, start, queries):
    key = first + lax.broadcasted_iota(jnp.int32, (keys, queries), 0)
    ok = key <= start + lax.broadcasted_iota(jnp.int32, (keys, queries), 1)
    return jnp.concatenate([ok, ok], axis=1)


def upper(v, axis):
    B = v.shape[axis] // 2
    h = B // 2
    if axis == 0:
        return jnp.concatenate([v[h:B], v[B + h :]], axis=0)
    return jnp.concatenate([v[:, h:B], v[:, B + h :]], axis=1)


def with_bias(k_ref, ka, length):
    L = k_ref.shape[0]
    ka[:, :128] = k_ref[...]
    lane = lax.broadcasted_iota(jnp.int32, (L, 128), 1)
    row = lax.broadcasted_iota(jnp.int32, (L, 128), 0)
    pad = jnp.logical_and(lane == 0, row >= length)
    ka[:, 128:] = jnp.where(pad, -1e9, 0.0).astype(bf16)


def biased(q):
    qq = two_heads(q)
    lane = lax.broadcasted_iota(jnp.int32, qq.shape, 1)
    return jnp.concatenate([qq, jnp.where(lane == 0, 1.0, 0.0).astype(bf16)], axis=1)


def att_fwd_body(meta, q_ref, k_ref, v_ref, mine_ref, theirs_ref, lse_ref, ka, vt, sc):
    i = pl.program_id(1)
    B = q_ref.shape[0]

    @pl.when(i == 0)
    def _():
        vt[...] = v_ref[...].T
        with_bias(k_ref, ka, length_of(meta))

    qq = biased(q_ref[...] * bf16(HDIM**-0.5))
    own = lax.rem(i, 2) == core_of(meta)

    def run(ii):
        m = None
        for j in range(ii + 1):
            ks = slice(j * B, j * B + B)
            s = dot(ka[ks, :], qq, NT)
            if j == ii:
                s = jnp.where(causal(0, B, 0, B), s, -1e9)
            sc[ks, :] = s
            mj = jnp.max(s, axis=0, keepdims=True)
            m = mj if m is None else jnp.maximum(m, mj)
        l = jnp.zeros((1, 2 * B), f32)
        acc = [jnp.zeros((HDIM, B), f32)] * 2
        for j in range(ii + 1):
            ks = slice(j * B, j * B + B)
            p = jnp.exp(sc[ks, :] - m)
            l = l + jnp.sum(p, axis=0, keepdims=True)
            pb = p.astype(bf16)
            for h in range(2):
                r = slice(HDIM * h, HDIM * h + HDIM)
                acc[h] = acc[h] + dot(vt[r, ks], pb[:, h * B : h * B + B])
        inv = 1.0 / l
        out = jnp.concatenate([acc[h] * inv[:, h * B : h * B + B] for h in range(2)], axis=0)
        out = out.T.astype(bf16)

        @pl.when(own)
        def _():
            mine_ref[...] = out

        @pl.when(jnp.logical_not(own))
        def _():
            theirs_ref[...] = out

        ls = m + jnp.log(l)
        lse_ref[0] = jnp.concatenate([ls[:, :B], ls[:, B:]], axis=0)

    for ii in range(4):
        pl.when(i == ii)(functools.partial(run, ii))


def half_map(p, i, m):
    return (jnp.bitwise_xor(i // 2, x_of(m)), p)


def att_fwd_call(meta, mix):
    length, cols = mix.shape
    width = cols // 3
    pairs = width // 128
    B = length // 4
    half = pl.BlockSpec((B, 128), half_map)
    return pl.pallas_call(
        att_fwd_body,
        out_shape=[
            sds((length // 2, width), bf16),
            sds((length // 2, width), bf16),
            sds((pairs, 2, length), f32),
        ],
        grid_spec=grid_spec(
            (pairs, 4),
            [
                pl.BlockSpec((B, 128), lambda p, i, m: (i, p)),
                pl.BlockSpec((length, 128), lambda p, i, m: (0, pairs + p)),
                pl.BlockSpec((length, 128), lambda p, i, m: (0, 2 * pairs + p)),
            ],
            [half, half, pl.BlockSpec((1, 2, B), lambda p, i, m: (p, 0, i))],
            [
                pltpu.VMEM((length, 256), bf16),
                pltpu.VMEM((128, length), bf16),
                pltpu.VMEM((length, 2 * B), f32),
            ],
        ),
        cost_estimate=cost(8 * length * length * width, 8 * length * width, 2 * length * length * pairs),
        name="attn_fwd",
    )(meta, mix, mix, mix)


def att_bwd_body(
    p0, aliased, meta, q_ref, k_ref, v_ref, om, ot, dm, dt, lse_ref, rq, rk, rv, taps, *refs
):
    gm_ref, gt_ref, gt, ka, kt, dkt, dvt, dqt, dqs, ext, stage, sem = refs[2:] if aliased else refs
    i = pl.program_id(1)
    B = q_ref.shape[0]
    L = k_ref.shape[0]
    H = B // 2

    @pl.when(i == 0)
    def _():
        kt[...] = k_ref[...].T
        with_bias(k_ref, ka, length_of(meta))

    own = lax.rem(i, 2) == core_of(meta)
    q = q_ref[...] * bf16(HDIM**-0.5)
    o = jnp.where(own, om[...], ot[...])
    do = jnp.where(own, dm[...], dt[...])
    qq, dd = biased(q), two_heads(do)
    qt, dot_ = q.T, do.T
    od = (o.astype(f32) * do.astype(f32)).T
    delta = jnp.concatenate(
        [jnp.sum(od[:HDIM], axis=0, keepdims=True), jnp.sum(od[HDIM:], axis=0, keepdims=True)],
        axis=1,
    )
    ls = lse_ref[0]
    lse = jnp.concatenate([ls[0:1], ls[1:2]], axis=1)

    dqt[...] = jnp.zeros_like(dqt)

    def tile(st, n, lo, diagonal):
        w = B - lo
        ks = pl.ds(pl.multiple_of(st, H), n)
        part = upper if lo else lambda v, axis: v
        s = dot(ka[ks, :], part(qq, 0), NT)
        dp = dot(v_ref[ks, :], part(dd, 0), NT)
        p = jnp.exp(s - part(lse, 1))
        if diagonal:
            p = jnp.where(causal(lo, n, lo, w), p, 0.0)
        ds = (p * (dp - part(delta, 1))).astype(bf16)
        pb = p.astype(bf16)
        for h in range(2):
            r, c = slice(HDIM * h, HDIM * h + HDIM), slice(h * w, h * w + w)
            dqt[r, lo:] += dot(kt[r, ks], ds[:, c])
            a = dot(qt[r, lo:], ds[:, c], NT)
            b = dot(dot_[r, lo:], pb[:, c], NT)
            if diagonal:
                dkt[r, ks] = a
                dvt[r, ks] = b
            else:
                dkt[r, ks] += a
                dvt[r, ks] += b

    lax.fori_loop(0, i, lambda j, c: (tile(j * B, B, 0, False), c)[1], 0)
    tile(i * B, H, 0, True)
    tile(i * B + H, H, H, True)
    dqs[pl.ds(pl.multiple_of(i * B, B), B), :] = dqt[...].T * HDIM**-0.5

    def copies(pair):
        width = gm_ref.shape[1] // 3
        for b in range(L // B):
            to = pl.ds(pl.multiple_of(jnp.bitwise_xor(b // 2, x_of(meta)) * B, B), B)
            for k in range(3):
                col = pl.ds(pl.multiple_of(k * width + (p0 + pair) * 128, 128), 128)
                src = stage.at[k, pl.ds(b * B, B), :]
                yield b, lambda g, to=to, col=col, src=src, k=k: pltpu.make_async_copy(
                    src, g.at[to, col], sem.at[k]
                )

    def send(pair):
        for b, copy in copies(pair):
            own = core_of(meta) == b % 2

            @pl.when(own)
            def _(copy=copy):
                copy(gm_ref).start()

            @pl.when(jnp.logical_not(own))
            def _(copy=copy):
                copy(gt_ref).start()

    def finish(pair):
        for _, copy in copies(pair):
            copy(gm_ref).wait()

    @pl.when(i == pl.num_programs(1) - 1)
    def _():
        pair = pl.program_id(0)
        gt[...] = jnp.zeros_like(gt)
        ext[...] = jnp.zeros_like(ext)

        @pl.when(pair > 0)
        def _():
            finish(pair)

        def back(n, carry):
            blk = L // B - 1 - n
            sl = pl.ds(pl.multiple_of(blk * B, B), B)
            for which, raw in enumerate((rq, rk, rv)):
                col = which * (taps.shape[1] // 3) + (p0 + pl.program_id(0)) * 128
                t = taps[:, pl.ds(pl.multiple_of(col, 128), 128)]
                g = dqs[sl, :] if which == 0 else (dkt, dvt)[which - 1][:, sl].T
                ext[which, B : B + 8, :] = ext[which, 0:8, :]
                ext[which, 0:B, :] = g
                g1, g2 = ext[which, 1 : B + 1, :], ext[which, 2 : B + 2, :]
                stage[which, sl, :] = (t[0:1] * g + t[1:2] * g1 + t[2:3] * g2).astype(bf16)
                r = raw[sl, :].astype(f32)
                for k, gg in enumerate((g, g1, g2)):
                    row = slice(3 * which + k, 3 * which + k + 1)
                    gt[row, :] += jnp.sum(r * gg, axis=0, keepdims=True)
            return carry

        lax.fori_loop(0, L // B, back, 0)
        send(pair)

        @pl.when(pair == pl.num_programs(0) - 1)
        def _():
            finish(pair)


def att_bwd_call(meta, mix, raw, om, ot, dm, dt, lse, taps, p0, count, into=None):
    length, cols = mix.shape
    pairs = cols // 384
    B = length // 4
    half = pl.BlockSpec((B, 128), lambda p, i, m: (jnp.bitwise_xor(i // 2, x_of(m)), p0 + p))
    full = lambda k: pl.BlockSpec((length, 128), lambda p, i, m: (0, k * pairs + p0 + p))
    return pl.pallas_call(
        functools.partial(att_bwd_body, p0, into is not None),
        out_shape=[sds((length // 2, cols), bf16)] * 2 + [sds((16, 128 * count), f32)],
        grid_spec=grid_spec(
            (count, 4),
            [
                pl.BlockSpec((B, 128), lambda p, i, m: (i, p0 + p)),
                full(1),
                full(2),
                half,
                half,
                half,
                half,
                pl.BlockSpec((1, 2, B), lambda p, i, m: (p0 + p, 0, i)),
                full(0),
                full(1),
                full(2),
                whole((8, cols)),
            ]
            + ([] if into is None else [pl.BlockSpec(memory_space=pl.ANY)] * 2),
            [pl.BlockSpec(memory_space=pl.ANY)] * 2 + [pl.BlockSpec((16, 128), lambda p, i, m: (0, p))],
            [
                pltpu.VMEM((length, 256), bf16),
                pltpu.VMEM((128, length), bf16),
                pltpu.VMEM((128, length), f32),
                pltpu.VMEM((128, length), f32),
                pltpu.VMEM((128, B), f32),
                pltpu.VMEM((length, 128), f32),
                pltpu.VMEM((3, B + 8, 128), f32),
                pltpu.VMEM((3, length, 128), bf16),
                pltpu.SemaphoreType.DMA((3,)),
            ],
        ),
        cost_estimate=cost(
            14 * length * length * 128 * count, 20 * length * 128 * count, 2 * length * length * count
        ),
        name="attn_bwd",
        input_output_aliases={} if into is None else {13: 0, 14: 1},
    )(meta, mix, mix, mix, om, ot, dm, dt, lse, raw, raw, raw, taps, *(into or ()))


T = 256


def valid_rows(meta, i, rows):
    per = rows // T
    block = jnp.where(i < per, meta[2], jnp.bitwise_xor(meta[2], 2))
    start = block * rows + lax.rem(i, per) * T
    return start + lax.broadcasted_iota(jnp.int32, (T, 1), 0) < length_of(meta)


def ffn_body(
    meta, xo, xx, co, cx, am, at, gain, wo_o, wo_c, pack,
    u_o, d_o, f_c, n0, n1, n2, n3, c0, c1, c2, c3,
    oo, ox, dm, dt, gg, dmid, gu0, gu1, gu2, gu3, gd0, gd1, gd2, gd3,
    wo, wus, wds, mid, h_s, g_s, fo, dh, act, du, stu, std, sto, gacc, sw, so, sg, sd, st,
):
    rows, width = xo.shape
    part = wo_o.shape[0]
    half = 2 * part
    n = 2 * rows // T
    per = rows // T
    copies = []
    for k, src in ((0, wo_o), (1, wo_c), (2, pack.at[pl.ds(rows, part), :]), (3, pack.at[pl.ds(rows + part, part), :])):
        shard = jnp.bitwise_xor(meta[2], k)
        row = jnp.where(shard // 2 == core_of(meta), 0, half) + lax.rem(shard, 2) * part
        cp = pltpu.make_async_copy(src, wo.at[pl.ds(pl.multiple_of(row, 64), part), :], so.at[k])
        cp.start()
        copies.append(cp)
    for k, pair in ((0, (f_c.at[0], f_c.at[1])), (2, (u_o, d_o))):
        for n_, src in enumerate(pair):
            pltpu.make_async_copy(src, (wus, wds)[n_].at[k], sw.at[k, n_]).start()
    for k, quarters in ((1, (c0, c1, c2, c3)), (3, (n0, n1, n2, n3))):
        for q_, src in enumerate(quarters):
            count = src.shape[1]
            to = pl.ds(pl.multiple_of(jnp.bitwise_xor(meta[3], q_) * count, 64), count)
            for n_, dst in enumerate((wus, wds)):
                pltpu.make_async_copy(src.at[n_], dst.at[k, to, :], sw.at[k, n_]).start()
    for cp in copies:
        cp.wait()
    gn = gain[...].astype(f32)

    def first_rows(i, carry):
        sl = pl.ds(pl.multiple_of(i * T, T), T)
        src = pl.ds(pl.multiple_of(lax.rem(i, per) * T, T), T)
        own = i < per
        x = jnp.where(own, xo[src, :], xx[src, :]).astype(f32)
        a = jnp.concatenate([am[sl, :], at[sl, :]], axis=1)
        m = x + dot(a, wo[...])
        mid[sl, :] = m
        fo[sl, :] = m
        h_s[sl, :] = norm(m, gn)[2]
        ct = jnp.where(own, co[src, :], cx[src, :])
        g_s[sl, :] = jnp.where(valid_rows(meta, i, rows), ct, jnp.zeros_like(ct))
        dh[sl, :] = jnp.zeros((T, width), f32)
        return carry

    lax.fori_loop(0, n, first_rows, 0)

    R = 512
    C = 768

    gus, gds = (gu0, gu1, gu2, gu3), (gd0, gd1, gd2, gd3)

    def stores(n_, slot):
        return [
            pltpu.make_async_copy(stu.at[slot], gus[n_], sg.at[slot, 0]),
            pltpu.make_async_copy(std.at[slot], gds[n_].at[pl.ds(0, width), :], sg.at[slot, 1]),
        ]

    def shard(k, carry):
        for cp in (
            pltpu.make_async_copy(u_o, wus.at[k], sw.at[k, 0]),
            pltpu.make_async_copy(d_o, wds.at[k], sw.at[k, 1]),
        ):
            cp.wait()

        def rows_step(t, c2):
            sl = pl.ds(pl.multiple_of(t * R, R), R)
            h, g = h_s[sl, :], g_s[sl, :]
            r = jnp.maximum(dot(h, wus[k]), 0.0)
            a = (r * r).astype(bf16)
            d = (dot(g, wds[k], NT) * 2.0 * r).astype(bf16)
            act[sl, :] = a
            du[sl, :] = d
            fo[sl, :] += dot(a, wds[k])
            dh[sl, :] += dot(d, wus[k], NT)
            return c2

        lax.fori_loop(0, 2 * rows // R, rows_step, 0)
        slot = lax.rem(k, 2)

        @pl.when(k >= 2)
        def _():
            for cp in stores(0, slot):
                cp.wait()

        def cols_step(t, c2):
            sl = pl.ds(pl.multiple_of(t * C, C), C)
            stu[slot, :, sl] = dot(h_s[...], du[:, sl], TN).astype(bf16)
            std[slot, sl, :] = dot(act[:, sl], g_s[...], TN).astype(bf16)
            return c2

        lax.fori_loop(0, width // C, cols_step, 0)
        for n_ in range(4):

            @pl.when(k == n_)
            def _(n_=n_):
                for cp in stores(n_, n_ % 2):
                    cp.start()

        return carry

    lax.fori_loop(0, 4, shard, 0)
    gg[...] = jnp.zeros_like(gg)

    def last_rows(i, carry):
        sl = pl.ds(pl.multiple_of(i * T, T), T)
        dst = pl.ds(pl.multiple_of(lax.rem(i, per) * T, T), T)
        ok = valid_rows(meta, i, rows)
        m = mid[sl, :]
        out = jnp.where(ok, fo[sl, :], 0.0)

        fo[sl, :] = out

        @pl.when(i < per)
        def _():
            own = oo.at[meta[2] // 2, dst, :]
            pltpu.make_async_copy(fo.at[sl, :], own, sd.at[1]).start()

        @pl.when(i >= per)
        def _():
            ox[dst, :] = out.astype(bf16)

        nm, inv, _ = norm(m, gn)
        d = dh[sl, :]
        dn = d * gn
        r = g_s[sl, :].astype(f32) + inv * (dn - nm * jnp.mean(dn * nm, axis=-1, keepdims=True))
        mid[sl, :] = r
        pltpu.make_async_copy(mid.at[sl, :], dmid.at[sl, :], sd.at[0]).start()
        db = r.astype(bf16)
        du[sl, :] = db
        da = dot(db, wo[...], NT).astype(bf16)
        dm[sl, :] = da[:, :half]
        dt[sl, :] = da[:, half:]
        gg[...] += jnp.sum(d * nm, axis=0, keepdims=True)
        return carry

    lax.fori_loop(0, n, last_rows, 0)
    gacc[0:half, :] = dot(am[...], du[...], TN)
    gacc[half:, :] = dot(at[...], du[...], TN)
    outs = [
        pltpu.make_async_copy(mid, dmid, sd.at[0]),
        pltpu.make_async_copy(fo.at[pl.ds(0, rows), :], oo.at[meta[2] // 2], sd.at[1]),
    ]
    for k, k_ in enumerate((1, 3, 0, 2)):
        shard_ = jnp.bitwise_xor(meta[2], k_)
        row = jnp.where(shard_ // 2 == core_of(meta), 0, half) + lax.rem(shard_, 2) * part
        sto[k] = gacc[pl.ds(pl.multiple_of(row, 64), part), :].astype(bf16)
        cp = pltpu.make_async_copy(sto.at[k], gds[k].at[pl.ds(width, part), :], st.at[k])
        cp.start()
        outs.append(cp)
    for slot in range(2):
        outs.extend(stores(2 + slot, slot))
    for cp in outs:
        cp.wait()


def ffn_call(meta, xo, xx, co, cx, am, at, gain, wos, ffs):
    rows, width = xo.shape
    half = am.shape[1]
    part = half // 2
    hid = ffs[0].shape[1]
    hbm = pl.BlockSpec(memory_space=pl.ANY)
    vm = lambda *shape: whole(shape)
    all_rows = 2 * rows
    return pl.pallas_call(
        ffn_body,
        out_shape=[
            sds((2, rows, width), f32),
            sds((rows, width), bf16),
            sds((all_rows, half), bf16),
            sds((all_rows, half), bf16),
            sds((1, width), f32),
            sds((all_rows, width), f32),
        ]
        + [sds((width, hid), bf16)] * 4
        + [sds((hid + part, width), bf16)] * 4,
        grid_spec=grid_spec(
            (1,),
            [vm(rows, width)] * 4 + [vm(all_rows, half)] * 2 + [vm(1, width)] + [hbm] * 14,
            [
                hbm,
                vm(rows, width),
                vm(all_rows, half),
                vm(all_rows, half),
                vm(1, width),
            ]
            + [hbm] * 9,
            [
                pltpu.VMEM((width, width), bf16),
                pltpu.VMEM((4, width, hid), bf16),
                pltpu.VMEM((4, hid, width), bf16),
                pltpu.VMEM((all_rows, width), f32),
                pltpu.VMEM((all_rows, width), bf16),
                pltpu.VMEM((all_rows, width), bf16),
                pltpu.VMEM((all_rows, width), f32),
                pltpu.VMEM((all_rows, width), f32),
                pltpu.VMEM((all_rows, hid), bf16),
                pltpu.VMEM((all_rows, hid), bf16),
                pltpu.VMEM((2, width, hid), bf16),
                pltpu.VMEM((2, hid, width), bf16),
                pltpu.VMEM((4, part, width), bf16),
                pltpu.VMEM((width, width), f32),
                pltpu.SemaphoreType.DMA((4, 2)),
                pltpu.SemaphoreType.DMA((4,)),
                pltpu.SemaphoreType.DMA((2, 2)),
                pltpu.SemaphoreType.DMA((2,)),
                pltpu.SemaphoreType.DMA((4,)),
            ],
        ),
        cost_estimate=cost(
            48 * all_rows * width * hid + 6 * all_rows * width * width, 40 * all_rows * width
        ),
        compiler_params=pltpu.CompilerParams(vmem_limit_bytes=62 * 2**20),
        name="ffn",
    )(meta, xo, xx, co, cx, am, at, gain, *wos, *ffs)


def projg_body(meta, h, dm, dt, keep, far, send, acc):
    rows = dm.shape[0]
    acc[...] = dot(h[0:rows, :], dm[...], TN) + dot(h[rows:, :], dt[...], TN)
    part = keep.shape[0]
    for ref, k, row in ((keep, 0, 0), (far, 2, 0), (send, 1, 0), (send, 3, part)):
        at = jnp.bitwise_xor(meta[2], k)
        ref[row : row + part, :] = acc[pl.ds(pl.multiple_of(at * part, 64), part), :].astype(bf16)


def projg_call(meta, h, dm, dt):
    length, width = h.shape
    cols = dm.shape[1]
    step = cols // 3
    d = pl.BlockSpec((length // 2, step), lambda j, m: (0, j))
    g = lambda rows: pl.BlockSpec((rows, step), lambda j, m: (0, j))
    part = width // 4
    return pl.pallas_call(
        projg_body,
        out_shape=[sds((rows, cols), bf16) for rows in (part, part, 2 * part)],
        grid_spec=grid_spec(
            (3,),
            [whole((length, width)), d, d],
            [g(part), g(part), g(2 * part)],
            [pltpu.VMEM((width, step), f32)],
        ),
        cost_estimate=cost(length, length),
        name="projg",
    )(meta, h, dm, dt)


def last_body(meta, xo, xx, dm, dt, wm, wt, dmid, gain, go, gx, gg):
    i = pl.program_id(0)
    per = pl.num_programs(0) // 2
    first = i < per
    x = jnp.where(first, xo[...], xx[...]).astype(f32)
    gn = gain[...].astype(f32)
    n, inv, _ = norm(x, gn)
    dh = dot(dm[...], wm[...], NT) + dot(dt[...], wt[...], NT)
    dn = dh * gn
    out = dmid[...] + inv * (dn - n * jnp.mean(dn * n, axis=-1, keepdims=True))

    @pl.when(first)
    def _():
        go[0] = out

    @pl.when(jnp.logical_not(first))
    def _():
        gx[...] = out.astype(bf16)

    ps = jnp.sum(dh * n, axis=0, keepdims=True)

    @pl.when(i == 0)
    def _():
        gg[...] = ps

    @pl.when(i > 0)
    def _():
        gg[...] += ps


def own_map(per):
    return lambda i, m: (jnp.minimum(i, per - 1), 0)


def nb_map(per):
    return lambda i, m: (jnp.maximum(i - per, 0), 0)


def last_call(meta, xo, xx, dm, dt, wm, wt, dmid, gain):
    rows, width = xo.shape
    cols = dm.shape[1]
    per = rows // T
    fst, snd = pl.BlockSpec((T, width), own_map(per)), pl.BlockSpec((T, width), nb_map(per))
    blk = lambda n: pl.BlockSpec((T, n), lambda i, m: (i, 0))
    return pl.pallas_call(
        last_body,
        out_shape=[sds((2, rows, width), f32), sds((rows, width), bf16), sds((1, width), f32)],
        grid_spec=grid_spec(
            (2 * per,),
            [fst, snd, blk(cols), blk(cols)]
            + [whole((width, cols))] * 2
            + [blk(width), whole((1, width))],
            [
                pl.BlockSpec((1, T, width), lambda i, m: (x_of(m), jnp.minimum(i, per - 1), 0)),
                snd,
                pl.BlockSpec((1, width), lambda i, m: (0, 0)),
            ],
        ),
        cost_estimate=cost(rows, rows),
        name="last",
    )(meta, xo, xx, dm, dt, wm, wt, dmid, gain)


def flip(size, bit):
    return [(i, i ^ bit) for i in range(size)]


def core_swap(v):
    return lax.ppermute(v, "head", CORE)


def x_swap(v):
    return lax.ppermute(v, "head", XNB)


def after(v, *deps):
    return lax.optimization_barrier((v, *deps))[0]


def halve(terms, index, count):
    rows = terms[0].shape[0] // count
    piece = lambda t, k: lax.dynamic_slice_in_dim(t, jnp.bitwise_xor(index, k) * rows, rows, 0)
    total = lambda k: sum(piece(t, k).astype(f32) for t in terms)
    return [total(k).astype(bf16) for k in range(1, count)], total(0)


def strides(dp):
    out = [1]
    while 2 * out[-1] < dp:
        out.append(2 * out[-1])
    return out


def side(stride):
    return lax.axis_index("dp") // stride % 2


def swap(v, stride, dp):
    return lax.ppermute(v, "dp", flip(dp, stride))


def rows_as(got, vs):
    out, row = [], 0
    for v in vs:
        out.append(got[row : row + v.shape[0]])
        row += v.shape[0]
    return out


def swap_both(vs, stride, dp):
    return rows_as(swap(jnp.concatenate(vs, axis=0), stride, dp), vs)


def scatter(sums, stride, dp):
    halves = [halve(terms, side(stride), 2) for terms in sums]
    send = jnp.concatenate([h[0][0] for h in halves], axis=0)
    got = swap(send, stride, dp)
    out, row = [], 0
    for (part,), keep in halves:
        out.append([keep, got[row : row + part.shape[0]]])
        row += part.shape[0]
    return out, send


def join(mine, got, stride):
    upper = side(stride) == 1
    return jnp.concatenate([jnp.where(upper, got, mine), jnp.where(upper, mine, got)], axis=0)


def total(terms):
    return sum(t.astype(f32) for t in terms)


def local(dp, inputs, lengths, w_query, w_key, w_value, w_out, w_up, w_down, conv_taps, gain_attn, gain_ff, cotangent):
    hd = lax.axis_index("head")
    x, c, y = hd // 2, hd % 2, lax.axis_index("dp") % 2
    q = lax.axis_index("dp") % 4
    width = inputs.shape[2]
    part = w_query.shape[0]
    half = 2 * part
    pick = lambda v, k: lax.dynamic_index_in_dim(v, k, 0, keepdims=False)
    y_swap = lambda v: lax.ppermute(v, "dp", flip(dp, 1))
    order = lambda own, nb: lax.dynamic_update_slice_in_dim(own, nb[None].astype(f32), 1 - x, 0)
    meta = jnp.concatenate([lengths, jnp.stack([hd, q])]).astype(jnp.int32)
    gain1, gain2 = gain_attn.reshape(1, width), gain_ff.reshape(1, width)

    mask = (jnp.arange(2) == c)[None, None, :, None]
    tap_rows = jnp.where(mask, conv_taps.transpose(1, 0, 2)[:, :, None, :], 0).reshape(3, 3 * half)
    tap_rows = jnp.concatenate([tap_rows[:, :width], jnp.pad(tap_rows[:, width:], ((0, 0), (0, half)))], axis=0)
    tap_rows = jnp.pad(tap_rows, ((0, 10), (0, 0)))

    def packed(k):
        cut = lambda w: lax.dynamic_slice_in_dim(w, k * half, half, 1)
        fold = cut(w_value)
        return jnp.concatenate(
            [
                jnp.concatenate([cut(w_query), cut(w_key)], axis=1),
                jnp.concatenate([fold[: part // 2], fold[part // 2 :]], axis=1),
                tap_rows,
            ],
            axis=0,
        )

    w_core = core_swap(packed(1 - c))
    w_mine = packed(c)
    x_own = pick(inputs, x)
    rows = x_own.shape[0]
    pack = x_swap(jnp.concatenate([pick(inputs, 1 - x), w_mine, w_core], axis=0))
    x_core = core_swap(x_own)
    count = width // 4
    quarter = lambda w: lax.dynamic_slice_in_dim(w, q * count, count, 0)
    wo_c = core_swap(w_out)
    c_own = pick(cotangent, x)
    ff_src = jnp.stack([quarter(w_up), quarter(w_down)])
    ff_own = jnp.stack([w_up, w_down])
    pack2 = jnp.concatenate([pick(cotangent, 1 - x), w_out, wo_c], axis=0)
    pack, ff_src, ff_own, pack2, c_own, meta, x_core = lax.optimization_barrier(
        (pack, ff_src, ff_own, pack2, c_own, meta, x_core)
    )
    x_cnb = core_swap(pack[:rows])
    h1, raw, mix, w_full, taps = qkv_call(meta, x_own, x_core, x_cnb, w_mine, w_core, pack, gain1)

    ff_first, pack2 = x_swap(ff_src), x_swap(pack2)
    ff_c = core_swap(ff_own)
    src = after(ff_first, mix)
    ff_n = [swap(src, k, dp) for k in (1, 2, 3)]
    a_mine, a_send, lse = att_fwd_call(meta, after(mix, src, ff_c))
    a_got = core_swap(a_send)
    w_other = core_swap(w_full)
    *ff_n, pack2 = lax.optimization_barrier((*ff_n, pack2, a_mine))[:-1]
    ff_n = [src, *ff_n]
    ff_cn = [core_swap(v) for v in ff_n]
    out_own, out_nb, d_mine, d_send, gg2, dmid, *gw = ffn_call(
        meta, x_own, pack, c_own, pack2, a_mine, a_got, after(gain2, w_other),
        (w_out, wo_c, pack2),
        (w_up, w_down, ff_c, *ff_n, *ff_cn),
    )
    d_got = core_swap(d_send)

    _, *rest = strides(dp)
    un, dn, do, uo = [core_swap(gw[k]) for k in (1, 5, 4, 0)]
    nu = total((gw[3], un)).astype(bf16)
    xu = x_swap(nu)
    (dn_send,), dn_keep = halve((gw[7], dn), y, 2)
    (do_send,), do_keep = halve((gw[6], do), y, 2)
    yn, yo = y_swap(dn_send), y_swap(do_send)
    out_x = x_swap(after(out_nb, nu))
    pairs = width // 256
    bwd = lambda m, p, n, into: att_bwd_call(
        meta, m, raw, a_mine, a_send, d_mine, d_got, lse, taps, p, n, into
    )
    *dall, gt_a = bwd(after(mix, nu, dn_send, do_send), 0, pairs - 1, None)
    xu, yn, yo, out_x = lax.optimization_barrier((xu, yn, yo, out_x, gt_a))[:4]
    (u_send,), u_keep = halve((gw[2], uo, xu), y, 2)
    nd = total((dn_keep, yn)).astype(bf16)
    yu, xd = y_swap(u_send), x_swap(nd)
    p_mine, p_theirs, gt_b = bwd(after(mix, u_send, nd), pairs - 1, 1, dall)
    p_got = core_swap(p_theirs)
    gt = jnp.concatenate([gt_a, gt_b], axis=1)
    yu, xd = lax.optimization_barrier((yu, xd, gt_b))[:2]
    sums, sent = scatter([[u_keep, yu], [do_keep, yo, xd]], rest[0], dp)
    keep, far, send = projg_call(meta, after(h1, sent), p_mine, p_theirs)
    flat = lax.optimization_barrier((*sums[0], *sums[1], keep))[:-1]
    sums, sent = scatter([flat[:2], flat[2:]], rest[1], dp)
    got = core_swap(after(send, sent))
    far = x_swap(jnp.concatenate([far, got[part:]], axis=0))
    gi_own, gi_nb, gg1 = last_call(
        meta, x_own, pack, p_mine, p_got, w_full, w_other, after(dmid, sent), gain1
    )
    *flat, gt, gg1 = lax.optimization_barrier((*sums[0], *sums[1], gt, x_swap(core_swap(gg1))))
    sums = [flat[:2], flat[2:]]
    for stride in rest[2:]:
        sums, _ = scatter(sums, stride, dp)
    vs = [total(t).astype(bf16) for t in sums]
    far = after(far, *vs)
    far, far2 = far[:part], far[part:]
    ga, gb = keep.astype(f32) + far.astype(f32), got[:part].astype(f32) + far2.astype(f32)
    g_send, g_keep = jnp.where(y == 0, gb, ga).astype(bf16), jnp.where(y == 0, ga, gb)
    pt = [g_keep, y_swap(g_send)]
    gi_got = x_swap(after(gi_nb, g_send))
    for stride in reversed(rest[1:]):
        vs = [join(v, g, stride) for v, g in zip(vs, swap_both(vs, stride, dp))]
    (pt,), sent = scatter([pt], rest[0], dp)
    *vs, _ = lax.optimization_barrier((*vs, sent))
    packed_vs = jnp.concatenate(vs, axis=0)
    near_got = swap(packed_vs, rest[0], dp)
    across = rows_as(y_swap(packed_vs), vs)
    for stride in rest[1:]:
        (pt,), _ = scatter([pt], stride, dp)
    others, also = rows_as(near_got, vs), rows_as(y_swap(near_got), vs)
    ps = after(total(pt).astype(bf16), near_got)
    for stride in reversed(rest):
        ps = join(ps, swap(ps, stride, dp), stride)
    ps_got = y_swap(ps)
    whole_of = lambda k: join(
        join(vs[k], others[k], rest[0]), join(across[k], also[k], rest[0]), 1
    ).astype(f32)
    grad_up, gd_all = whole_of(0), whole_of(1)
    grad_down, grad_out = gd_all[: w_down.shape[0]], gd_all[w_down.shape[0] :]
    lo, hi = jnp.where(y == c, ps, ps_got), jnp.where(y == c, ps_got, ps)
    third = lambda v, w: v[:, w * half : w * half + half]
    grads = [jnp.concatenate([third(lo, w), third(hi, w)], axis=1).astype(f32) for w in range(3)]

    gt = gt[:9].reshape(9, 2, part).transpose(1, 0, 2)
    gt = jnp.where(jnp.arange(2)[:, None, None, None] == c, gt[None], 0.0).reshape(4, 9, part)
    gains = jnp.concatenate([gg1, gg2], axis=0).reshape(2, 4, part).transpose(1, 0, 2)
    small = jnp.concatenate([gt, gains, jnp.zeros((4, 5, part), f32)], axis=1)
    small = jnp.broadcast_to(small[:, None], (4, dp, 16, part)).reshape(4 * dp, 16, part)
    small = jnp.sum(lax.all_to_all(small, ("head", "dp"), 0, 0, tiled=True), axis=0)
    output = order(after(out_own, g_send), out_x)
    grad_input = order(after(gi_own, ps), gi_got)
    return (
        output,
        grad_input,
        *grads,
        grad_out,
        grad_up,
        grad_down,
        small[:9].reshape(3, 3, part),
        small[9],
        small[10],
    )


def solution(mesh):
    placed = (
        P("dp", "head", None),
        P("dp"),
        P("head", None),
        P("head", None),
        P("head", None),
        P("head", None),
        P(None, "head"),
        P("head", None),
        P(None, None, "head"),
        P(),
        P(),
        P("dp", "head", None),
    )
    return jax.shard_map(
        functools.partial(local, mesh.shape["dp"]),
        mesh=mesh,
        in_specs=placed,
        out_specs=(
            P("dp", "head", None),
            P("dp", "head", None),
            P("head", None),
            P("head", None),
            P("head", None),
            P("head", None),
            P(None, "head"),
            P("head", None),
            P(None, None, "head"),
            P("head"),
            P("head"),
        ),
        check_vma=False,
    )
```

```python
import functools

import jax
import jax.numpy as jnp
from jax import lax
from jax.experimental import pallas as pl
from jax.experimental.pallas import tpu as pltpu
from jax.sharding import PartitionSpec as P

HDIM = 64
EPS = 1e-06
bf16 = jnp.bfloat16
f32 = jnp.float32

NN = (((1,), (0,)), ((), ()))
NT = (((1,), (1,)), ((), ()))
TN = (((0,), (0,)), ((), ()))

CORE = [(0, 1), (1, 0), (2, 3), (3, 2)]
XNB = [(0, 2), (2, 0), (1, 3), (3, 1)]


def dot(a, b, dims=NN):
    return lax.dot_general(a, b, dims, preferred_element_type=f32)


def cost(flops, nbytes, trans=0):
    return pl.CostEstimate(flops=int(flops), bytes_accessed=int(nbytes), transcendentals=int(trans))


def sds(shape, dtype):
    return jax.ShapeDtypeStruct(shape, dtype)


def whole(shape):
    zeros = (0,) * len(shape)
    return pl.BlockSpec(shape, lambda *_: zeros, pipeline_mode=pl.Buffered(1))


def grid_spec(grid, ins, outs, scratch=()):
    return pltpu.PrefetchScalarGridSpec(
        num_scalar_prefetch=1, grid=grid, in_specs=ins, out_specs=outs, scratch_shapes=scratch
    )


def length_of(m):
    return m[m[2] // 2]


def x_of(m):
    return m[2] // 2


def core_of(m):
    return lax.rem(m[2], 2)


def slot_of(m, b):
    v = jnp.bitwise_xor(m[2], b)
    return lax.rem(v, 2) * 2 + v // 2


def norm(x, gain):
    inv = lax.rsqrt(jnp.mean(x * x, axis=-1, keepdims=True) + EPS)
    n = x * inv
    return n, inv, (n * gain).astype(bf16)


def qkv_body(meta, x0, x1, x2, x3, wa, wb, pack, gain, h_ref, raw_ref, mix_ref, w_ref, taps, ext):
    b = pl.program_id(0)
    rows = x0.shape[0]
    part = w_ref.shape[0] // 4
    width = x0.shape[1]
    tall = wa.shape[0]
    hd = meta[2]

    @pl.when(b == 0)
    def _():
        def put(k, ref, first):
            at = jnp.bitwise_xor(hd, k) * part
            w_ref[pl.ds(pl.multiple_of(at, 64), part), 0:width] = ref[first : first + part, :]
            for n in range(2):
                row = pl.multiple_of(at + n * (part // 2), 32)
                w_ref[pl.ds(row, part // 2), width:] = ref[
                    first + part : first + part + part // 2, n * (width // 2) : (n + 1) * (width // 2)
                ]

        put(0, wa, 0)
        put(1, wb, 0)
        put(2, pack, 0)
        put(3, pack, tall)
        last = lambda ref, end: ref[end - 16 : end, :].astype(f32)
        near = last(wa, tall) + last(wb, tall)
        far = last(pack, tall) + last(pack, 2 * tall)
        t = jnp.where(x_of(meta) == core_of(meta), near, far)
        taps[...] = jnp.zeros_like(taps)
        taps[0:3, 0:width] = t[0:3]
        taps[0:3, width:] = t[3:6, 0 : width // 2]
        ext[0:8, :] = jnp.zeros((8, ext.shape[1]), f32)

    slot = slot_of(meta, b)
    step = ext.shape[0] - 8

    def some(n, carry):
        sl = pl.ds(pl.multiple_of(n * step, step), step)
        x = x0[sl, :]
        for k, other in ((1, x1), (2, x2), (3, x3)):
            x = jnp.where(slot == k, other[sl, :], x)
        _, _, h = norm(x.astype(f32), gain[...].astype(f32))
        h_ref[sl, :] = h
        raw = dot(h, w_ref[...]).astype(bf16)
        raw_ref[sl, :] = raw
        rawf = raw.astype(f32)
        ext[8:, :] = rawf
        t = taps[...]
        mixed = t[0:1] * rawf + t[1:2] * ext[7 : 7 + step, :] + t[2:3] * ext[6 : 6 + step, :]
        mix_ref[sl, :] = mixed.astype(bf16)
        ext[0:8, :] = ext[step:, :]
        return carry

    lax.fori_loop(0, rows // step, some, 0)


def qkv_call(meta, x_own, x_nb, x_core, x_cnb, w_mine, w_core, pack, gain):
    rows, width = x_own.shape
    tall = w_mine.shape[0]
    cols = width * 3 // 2
    length = 4 * rows
    blk = lambda n: pl.BlockSpec((rows, n), lambda b, m: (b, 0))
    const = lambda r: pl.BlockSpec((r, cols), lambda b, m: (0, 0))
    return pl.pallas_call(
        qkv_body,
        out_shape=[
            sds((length, width), bf16),
            sds((length, cols), bf16),
            sds((length, cols), bf16),
            sds((width, cols), bf16),
            sds((8, cols), f32),
        ],
        grid_spec=grid_spec(
            (4,),
            [whole((rows, width))] * 4
            + [whole((tall, width))] * 2
            + [whole(pack.shape), whole((1, width))],
            [
                pl.BlockSpec((rows, width), lambda b, m: (slot_of(m, b), 0)),
                blk(cols),
                blk(cols),
                const(width),
                const(8),
            ],
            [pltpu.VMEM((T + 8, cols), f32)],
        ),
        cost_estimate=cost(2 * length * width * cols, 2 * length * (width * 2 + cols * 2)),
        name="qkv",
    )(meta, x_own, x_nb, x_core, x_cnb, w_mine, w_core, pack, gain)


def two_heads(v):
    lane = lax.broadcasted_iota(jnp.int32, v.shape, 1)
    z = jnp.zeros_like(v)
    return jnp.concatenate([jnp.where(lane < HDIM, v, z), jnp.where(lane < HDIM, z, v)], axis=0)


def causal(first, keys, start, queries):
    key = first + lax.broadcasted_iota(jnp.int32, (keys, queries), 0)
    ok = key <= start + lax.broadcasted_iota(jnp.int32, (keys, queries), 1)
    return jnp.concatenate([ok, ok], axis=1)


def upper(v, axis):
    B = v.shape[axis] // 2
    h = B // 2
    if axis == 0:
        return jnp.concatenate([v[h:B], v[B + h :]], axis=0)
    return jnp.concatenate([v[:, h:B], v[:, B + h :]], axis=1)


def with_bias(k_ref, ka, length):
    L = k_ref.shape[0]
    ka[:, :128] = k_ref[...]
    lane = lax.broadcasted_iota(jnp.int32, (L, 128), 1)
    row = lax.broadcasted_iota(jnp.int32, (L, 128), 0)
    pad = jnp.logical_and(lane == 0, row >= length)
    ka[:, 128:] = jnp.where(pad, -1e9, 0.0).astype(bf16)


def biased(q):
    qq = two_heads(q)
    lane = lax.broadcasted_iota(jnp.int32, qq.shape, 1)
    return jnp.concatenate([qq, jnp.where(lane == 0, 1.0, 0.0).astype(bf16)], axis=1)


def att_fwd_body(meta, q_ref, k_ref, v_ref, mine_ref, theirs_ref, lse_ref, ka, vt, sc):
    i = pl.program_id(1)
    B = q_ref.shape[0]

    @pl.when(i == 0)
    def _():
        vt[...] = v_ref[...].T
        with_bias(k_ref, ka, length_of(meta))

    qq = biased(q_ref[...] * bf16(HDIM**-0.5))
    own = lax.rem(i, 2) == core_of(meta)

    def run(ii):
        m = None
        for j in range(ii + 1):
            ks = slice(j * B, j * B + B)
            s = dot(ka[ks, :], qq, NT)
            if j == ii:
                s = jnp.where(causal(0, B, 0, B), s, -1e9)
            sc[ks, :] = s
            mj = jnp.max(s, axis=0, keepdims=True)
            m = mj if m is None else jnp.maximum(m, mj)
        l = jnp.zeros((1, 2 * B), f32)
        acc = [jnp.zeros((HDIM, B), f32)] * 2
        for j in range(ii + 1):
            ks = slice(j * B, j * B + B)
            p = jnp.exp(sc[ks, :] - m)
            l = l + jnp.sum(p, axis=0, keepdims=True)
            pb = p.astype(bf16)
            for h in range(2):
                r = slice(HDIM * h, HDIM * h + HDIM)
                acc[h] = acc[h] + dot(vt[r, ks], pb[:, h * B : h * B + B])
        inv = 1.0 / l
        out = jnp.concatenate([acc[h] * inv[:, h * B : h * B + B] for h in range(2)], axis=0)
        out = out.T.astype(bf16)

        @pl.when(own)
        def _():
            mine_ref[...] = out

        @pl.when(jnp.logical_not(own))
        def _():
            theirs_ref[...] = out

        ls = m + jnp.log(l)
        lse_ref[0] = jnp.concatenate([ls[:, :B], ls[:, B:]], axis=0)

    for ii in range(4):
        pl.when(i == ii)(functools.partial(run, ii))


def half_map(p, i, m):
    return (jnp.bitwise_xor(i // 2, x_of(m)), p)


def att_fwd_call(meta, mix):
    length, cols = mix.shape
    width = cols // 3
    pairs = width // 128
    B = length // 4
    half = pl.BlockSpec((B, 128), half_map)
    return pl.pallas_call(
        att_fwd_body,
        out_shape=[
            sds((length // 2, width), bf16),
            sds((length // 2, width), bf16),
            sds((pairs, 2, length), f32),
        ],
        grid_spec=grid_spec(
            (pairs, 4),
            [
                pl.BlockSpec((B, 128), lambda p, i, m: (i, p)),
                pl.BlockSpec((length, 128), lambda p, i, m: (0, pairs + p)),
                pl.BlockSpec((length, 128), lambda p, i, m: (0, 2 * pairs + p)),
            ],
            [half, half, pl.BlockSpec((1, 2, B), lambda p, i, m: (p, 0, i))],
            [
                pltpu.VMEM((length, 256), bf16),
                pltpu.VMEM((128, length), bf16),
                pltpu.VMEM((length, 2 * B), f32),
            ],
        ),
        cost_estimate=cost(8 * length * length * width, 8 * length * width, 2 * length * length * pairs),
        name="attn_fwd",
    )(meta, mix, mix, mix)


def att_bwd_body(
    p0, aliased, meta, q_ref, k_ref, v_ref, om, ot, dm, dt, lse_ref, rq, rk, rv, taps, *refs
):
    gm_ref, gt_ref, gt, ka, kt, dkt, dvt, dqt, dqs, ext, stage, sem = refs[2:] if aliased else refs
    i = pl.program_id(1)
    B = q_ref.shape[0]
    L = k_ref.shape[0]
    H = B // 2

    @pl.when(i == 0)
    def _():
        kt[...] = k_ref[...].T
        with_bias(k_ref, ka, length_of(meta))

    own = lax.rem(i, 2) == core_of(meta)
    q = q_ref[...] * bf16(HDIM**-0.5)
    o = jnp.where(own, om[...], ot[...])
    do = jnp.where(own, dm[...], dt[...])
    qq, dd = biased(q), two_heads(do)
    qt, dot_ = q.T, do.T
    od = (o.astype(f32) * do.astype(f32)).T
    delta = jnp.concatenate(
        [jnp.sum(od[:HDIM], axis=0, keepdims=True), jnp.sum(od[HDIM:], axis=0, keepdims=True)],
        axis=1,
    )
    ls = lse_ref[0]
    lse = jnp.concatenate([ls[0:1], ls[1:2]], axis=1)

    dqt[...] = jnp.zeros_like(dqt)

    def tile(st, n, lo, diagonal):
        w = B - lo
        ks = pl.ds(pl.multiple_of(st, H), n)
        part = upper if lo else lambda v, axis: v
        s = dot(ka[ks, :], part(qq, 0), NT)
        dp = dot(v_ref[ks, :], part(dd, 0), NT)
        p = jnp.exp(s - part(lse, 1))
        if diagonal:
            p = jnp.where(causal(lo, n, lo, w), p, 0.0)
        ds = (p * (dp - part(delta, 1))).astype(bf16)
        pb = p.astype(bf16)
        for h in range(2):
            r, c = slice(HDIM * h, HDIM * h + HDIM), slice(h * w, h * w + w)
            dqt[r, lo:] += dot(kt[r, ks], ds[:, c])
            a = dot(qt[r, lo:], ds[:, c], NT)
            b = dot(dot_[r, lo:], pb[:, c], NT)
            if diagonal:
                dkt[r, ks] = a
                dvt[r, ks] = b
            else:
                dkt[r, ks] += a
                dvt[r, ks] += b

    lax.fori_loop(0, i, lambda j, c: (tile(j * B, B, 0, False), c)[1], 0)
    tile(i * B, H, 0, True)
    tile(i * B + H, H, H, True)
    dqs[pl.ds(pl.multiple_of(i * B, B), B), :] = dqt[...].T * HDIM**-0.5

    def copies(pair):
        width = gm_ref.shape[1] // 3
        for b in range(L // B):
            to = pl.ds(pl.multiple_of(jnp.bitwise_xor(b // 2, x_of(meta)) * B, B), B)
            for k in range(3):
                col = pl.ds(pl.multiple_of(k * width + (p0 + pair) * 128, 128), 128)
                src = stage.at[k, pl.ds(b * B, B), :]
                yield b, lambda g, to=to, col=col, src=src, k=k: pltpu.make_async_copy(
                    src, g.at[to, col], sem.at[k]
                )

    def send(pair):
        for b, copy in copies(pair):
            own = core_of(meta) == b % 2

            @pl.when(own)
            def _(copy=copy):
                copy(gm_ref).start()

            @pl.when(jnp.logical_not(own))
            def _(copy=copy):
                copy(gt_ref).start()

    def finish(pair):
        for _, copy in copies(pair):
            copy(gm_ref).wait()

    @pl.when(i == pl.num_programs(1) - 1)
    def _():
        pair = pl.program_id(0)
        gt[...] = jnp.zeros_like(gt)
        ext[...] = jnp.zeros_like(ext)

        @pl.when(pair > 0)
        def _():
            finish(pair)

        def back(n, carry):
            blk = L // B - 1 - n
            sl = pl.ds(pl.multiple_of(blk * B, B), B)
            for which, raw in enumerate((rq, rk, rv)):
                col = which * (taps.shape[1] // 3) + (p0 + pl.program_id(0)) * 128
                t = taps[:, pl.ds(pl.multiple_of(col, 128), 128)]
                g = dqs[sl, :] if which == 0 else (dkt, dvt)[which - 1][:, sl].T
                ext[which, B : B + 8, :] = ext[which, 0:8, :]
                ext[which, 0:B, :] = g
                g1, g2 = ext[which, 1 : B + 1, :], ext[which, 2 : B + 2, :]
                stage[which, sl, :] = (t[0:1] * g + t[1:2] * g1 + t[2:3] * g2).astype(bf16)
                r = raw[sl, :].astype(f32)
                for k, gg in enumerate((g, g1, g2)):
                    row = slice(3 * which + k, 3 * which + k + 1)
                    gt[row, :] += jnp.sum(r * gg, axis=0, keepdims=True)
            return carry

        lax.fori_loop(0, L // B, back, 0)
        send(pair)

        @pl.when(pair == pl.num_programs(0) - 1)
        def _():
            finish(pair)


def att_bwd_call(meta, mix, raw, om, ot, dm, dt, lse, taps, p0, count, into=None):
    length, cols = mix.shape
    pairs = cols // 384
    B = length // 4
    half = pl.BlockSpec((B, 128), lambda p, i, m: (jnp.bitwise_xor(i // 2, x_of(m)), p0 + p))
    full = lambda k: pl.BlockSpec((length, 128), lambda p, i, m: (0, k * pairs + p0 + p))
    return pl.pallas_call(
        functools.partial(att_bwd_body, p0, into is not None),
        out_shape=[sds((length // 2, cols), bf16)] * 2 + [sds((16, 128 * count), f32)],
        grid_spec=grid_spec(
            (count, 4),
            [
                pl.BlockSpec((B, 128), lambda p, i, m: (i, p0 + p)),
                full(1),
                full(2),
                half,
                half,
                half,
                half,
                pl.BlockSpec((1, 2, B), lambda p, i, m: (p0 + p, 0, i)),
                full(0),
                full(1),
                full(2),
                whole((8, cols)),
            ]
            + ([] if into is None else [pl.BlockSpec(memory_space=pl.ANY)] * 2),
            [pl.BlockSpec(memory_space=pl.ANY)] * 2 + [pl.BlockSpec((16, 128), lambda p, i, m: (0, p))],
            [
                pltpu.VMEM((length, 256), bf16),
                pltpu.VMEM((128, length), bf16),
                pltpu.VMEM((128, length), f32),
                pltpu.VMEM((128, length), f32),
                pltpu.VMEM((128, B), f32),
                pltpu.VMEM((length, 128), f32),
                pltpu.VMEM((3, B + 8, 128), f32),
                pltpu.VMEM((3, length, 128), bf16),
                pltpu.SemaphoreType.DMA((3,)),
            ],
        ),
        cost_estimate=cost(
            14 * length * length * 128 * count, 20 * length * 128 * count, 2 * length * length * count
        ),
        name="attn_bwd",
        input_output_aliases={} if into is None else {13: 0, 14: 1},
    )(meta, mix, mix, mix, om, ot, dm, dt, lse, raw, raw, raw, taps, *(into or ()))


T = 256


def valid_rows(meta, i, rows):
    per = rows // T
    block = jnp.where(i < per, meta[2], jnp.bitwise_xor(meta[2], 2))
    start = block * rows + lax.rem(i, per) * T
    return start + lax.broadcasted_iota(jnp.int32, (T, 1), 0) < length_of(meta)


def ffn_body(
    meta, xo, xx, co, cx, am, at, gain, wo_o, wo_c, pack,
    u_o, d_o, f_c, n0, n1, n2, n3, c0, c1, c2, c3,
    oo, ox, dm, dt, gg, dmid, gu0, gu1, gu2, gu3, gd0, gd1, gd2, gd3,
    wo, wus, wds, mid, h_s, g_s, fo, dh, act, du, stu, std, sto, gacc, sw, so, sg, sd, st,
):
    rows, width = xo.shape
    part = wo_o.shape[0]
    half = 2 * part
    n = 2 * rows // T
    per = rows // T
    copies = []
    for k, src in ((0, wo_o), (1, wo_c), (2, pack.at[pl.ds(rows, part), :]), (3, pack.at[pl.ds(rows + part, part), :])):
        shard = jnp.bitwise_xor(meta[2], k)
        row = jnp.where(shard // 2 == core_of(meta), 0, half) + lax.rem(shard, 2) * part
        cp = pltpu.make_async_copy(src, wo.at[pl.ds(pl.multiple_of(row, 64), part), :], so.at[k])
        cp.start()
        copies.append(cp)
    for k, pair in ((0, (f_c.at[0], f_c.at[1])), (2, (u_o, d_o))):
        for n_, src in enumerate(pair):
            pltpu.make_async_copy(src, (wus, wds)[n_].at[k], sw.at[k, n_]).start()
    for k, quarters in ((1, (c0, c1, c2, c3)), (3, (n0, n1, n2, n3))):
        for q_, src in enumerate(quarters):
            count = src.shape[1]
            to = pl.ds(pl.multiple_of(jnp.bitwise_xor(meta[3], q_) * count, 64), count)
            for n_, dst in enumerate((wus, wds)):
                pltpu.make_async_copy(src.at[n_], dst.at[k, to, :], sw.at[k, n_]).start()
    for cp in copies:
        cp.wait()
    gn = gain[...].astype(f32)

    def first_rows(i, carry):
        sl = pl.ds(pl.multiple_of(i * T, T), T)
        src = pl.ds(pl.multiple_of(lax.rem(i, per) * T, T), T)
        own = i < per
        x = jnp.where(own, xo[src, :], xx[src, :]).astype(f32)
        a = jnp.concatenate([am[sl, :], at[sl, :]], axis=1)
        m = x + dot(a, wo[...])
        mid[sl, :] = m
        fo[sl, :] = m
        h_s[sl, :] = norm(m, gn)[2]
        ct = jnp.where(own, co[src, :], cx[src, :])
        g_s[sl, :] = jnp.where(valid_rows(meta, i, rows), ct, jnp.zeros_like(ct))
        dh[sl, :] = jnp.zeros((T, width), f32)
        return carry

    lax.fori_loop(0, n, first_rows, 0)

    R = 512
    C = 768

    gus, gds = (gu0, gu1, gu2, gu3), (gd0, gd1, gd2, gd3)

    def stores(n_, slot):
        return [
            pltpu.make_async_copy(stu.at[slot], gus[n_], sg.at[slot, 0]),
            pltpu.make_async_copy(std.at[slot], gds[n_].at[pl.ds(0, width), :], sg.at[slot, 1]),
        ]

    def shard(k, carry):
        for cp in (
            pltpu.make_async_copy(u_o, wus.at[k], sw.at[k, 0]),
            pltpu.make_async_copy(d_o, wds.at[k], sw.at[k, 1]),
        ):
            cp.wait()

        def rows_step(t, c2):
            sl = pl.ds(pl.multiple_of(t * R, R), R)
            h, g = h_s[sl, :], g_s[sl, :]
            r = jnp.maximum(dot(h, wus[k]), 0.0)
            a = (r * r).astype(bf16)
            d = (dot(g, wds[k], NT) * 2.0 * r).astype(bf16)
            act[sl, :] = a
            du[sl, :] = d
            fo[sl, :] += dot(a, wds[k])
            dh[sl, :] += dot(d, wus[k], NT)
            return c2

        lax.fori_loop(0, 2 * rows // R, rows_step, 0)
        slot = lax.rem(k, 2)

        @pl.when(k >= 2)
        def _():
            for cp in stores(0, slot):
                cp.wait()

        def cols_step(t, c2):
            sl = pl.ds(pl.multiple_of(t * C, C), C)
            stu[slot, :, sl] = dot(h_s[...], du[:, sl], TN).astype(bf16)
            std[slot, sl, :] = dot(act[:, sl], g_s[...], TN).astype(bf16)
            return c2

        lax.fori_loop(0, width // C, cols_step, 0)
        for n_ in range(4):

            @pl.when(k == n_)
            def _(n_=n_):
                for cp in stores(n_, n_ % 2):
                    cp.start()

        return carry

    lax.fori_loop(0, 4, shard, 0)
    gg[...] = jnp.zeros_like(gg)

    def last_rows(i, carry):
        sl = pl.ds(pl.multiple_of(i * T, T), T)
        dst = pl.ds(pl.multiple_of(lax.rem(i, per) * T, T), T)
        ok = valid_rows(meta, i, rows)
        m = mid[sl, :]
        out = jnp.where(ok, fo[sl, :], 0.0)

        fo[sl, :] = out

        @pl.when(i < per)
        def _():
            own = oo.at[meta[2] // 2, dst, :]
            pltpu.make_async_copy(fo.at[sl, :], own, sd.at[1]).start()

        @pl.when(i >= per)
        def _():
            ox[dst, :] = out.astype(bf16)

        nm, inv, _ = norm(m, gn)
        d = dh[sl, :]
        dn = d * gn
        r = g_s[sl, :].astype(f32) + inv * (dn - nm * jnp.mean(dn * nm, axis=-1, keepdims=True))
        mid[sl, :] = r
        pltpu.make_async_copy(mid.at[sl, :], dmid.at[sl, :], sd.at[0]).start()
        db = r.astype(bf16)
        du[sl, :] = db
        da = dot(db, wo[...], NT).astype(bf16)
        dm[sl, :] = da[:, :half]
        dt[sl, :] = da[:, half:]
        gg[...] += jnp.sum(d * nm, axis=0, keepdims=True)
        return carry

    lax.fori_loop(0, n, last_rows, 0)
    gacc[0:half, :] = dot(am[...], du[...], TN)
    gacc[half:, :] = dot(at[...], du[...], TN)
    outs = [
        pltpu.make_async_copy(mid, dmid, sd.at[0]),
        pltpu.make_async_copy(fo.at[pl.ds(0, rows), :], oo.at[meta[2] // 2], sd.at[1]),
    ]
    for k, k_ in enumerate((1, 3, 0, 2)):
        shard_ = jnp.bitwise_xor(meta[2], k_)
        row = jnp.where(shard_ // 2 == core_of(meta), 0, half) + lax.rem(shard_, 2) * part
        sto[k] = gacc[pl.ds(pl.multiple_of(row, 64), part), :].astype(bf16)
        cp = pltpu.make_async_copy(sto.at[k], gds[k].at[pl.ds(width, part), :], st.at[k])
        cp.start()
        outs.append(cp)
    for slot in range(2):
        outs.extend(stores(2 + slot, slot))
    for cp in outs:
        cp.wait()


def ffn_call(meta, xo, xx, co, cx, am, at, gain, wos, ffs):
    rows, width = xo.shape
    half = am.shape[1]
    part = half // 2
    hid = ffs[0].shape[1]
    hbm = pl.BlockSpec(memory_space=pl.ANY)
    vm = lambda *shape: whole(shape)
    all_rows = 2 * rows
    return pl.pallas_call(
        ffn_body,
        out_shape=[
            sds((2, rows, width), f32),
            sds((rows, width), bf16),
            sds((all_rows, half), bf16),
            sds((all_rows, half), bf16),
            sds((1, width), f32),
            sds((all_rows, width), f32),
        ]
        + [sds((width, hid), bf16)] * 4
        + [sds((hid + part, width), bf16)] * 4,
        grid_spec=grid_spec(
            (1,),
            [vm(rows, width)] * 4 + [vm(all_rows, half)] * 2 + [vm(1, width)] + [hbm] * 14,
            [
                hbm,
                vm(rows, width),
                vm(all_rows, half),
                vm(all_rows, half),
                vm(1, width),
            ]
            + [hbm] * 9,
            [
                pltpu.VMEM((width, width), bf16),
                pltpu.VMEM((4, width, hid), bf16),
                pltpu.VMEM((4, hid, width), bf16),
                pltpu.VMEM((all_rows, width), f32),
                pltpu.VMEM((all_rows, width), bf16),
                pltpu.VMEM((all_rows, width), bf16),
                pltpu.VMEM((all_rows, width), f32),
                pltpu.VMEM((all_rows, width), f32),
                pltpu.VMEM((all_rows, hid), bf16),
                pltpu.VMEM((all_rows, hid), bf16),
                pltpu.VMEM((2, width, hid), bf16),
                pltpu.VMEM((2, hid, width), bf16),
                pltpu.VMEM((4, part, width), bf16),
                pltpu.VMEM((width, width), f32),
                pltpu.SemaphoreType.DMA((4, 2)),
                pltpu.SemaphoreType.DMA((4,)),
                pltpu.SemaphoreType.DMA((2, 2)),
                pltpu.SemaphoreType.DMA((2,)),
                pltpu.SemaphoreType.DMA((4,)),
            ],
        ),
        cost_estimate=cost(
            48 * all_rows * width * hid + 6 * all_rows * width * width, 40 * all_rows * width
        ),
        compiler_params=pltpu.CompilerParams(vmem_limit_bytes=62 * 2**20),
        name="ffn",
    )(meta, xo, xx, co, cx, am, at, gain, *wos, *ffs)


def projg_body(meta, h, dm, dt, keep, far, send, acc):
    rows = dm.shape[0]
    acc[...] = dot(h[0:rows, :], dm[...], TN) + dot(h[rows:, :], dt[...], TN)
    part = keep.shape[0]
    for ref, k, row in ((keep, 0, 0), (far, 2, 0), (send, 1, 0), (send, 3, part)):
        at = jnp.bitwise_xor(meta[2], k)
        ref[row : row + part, :] = acc[pl.ds(pl.multiple_of(at * part, 64), part), :].astype(bf16)


def projg_call(meta, h, dm, dt):
    length, width = h.shape
    cols = dm.shape[1]
    step = cols // 3
    d = pl.BlockSpec((length // 2, step), lambda j, m: (0, j))
    g = lambda rows: pl.BlockSpec((rows, step), lambda j, m: (0, j))
    part = width // 4
    return pl.pallas_call(
        projg_body,
        out_shape=[sds((rows, cols), bf16) for rows in (part, part, 2 * part)],
        grid_spec=grid_spec(
            (3,),
            [whole((length, width)), d, d],
            [g(part), g(part), g(2 * part)],
            [pltpu.VMEM((width, step), f32)],
        ),
        cost_estimate=cost(length, length),
        name="projg",
    )(meta, h, dm, dt)


def last_body(meta, xo, xx, dm, dt, wm, wt, dmid, gain, go, gx, gg):
    i = pl.program_id(0)
    per = pl.num_programs(0) // 2
    first = i < per
    x = jnp.where(first, xo[...], xx[...]).astype(f32)
    gn = gain[...].astype(f32)
    n, inv, _ = norm(x, gn)
    dh = dot(dm[...], wm[...], NT) + dot(dt[...], wt[...], NT)
    dn = dh * gn
    out = dmid[...] + inv * (dn - n * jnp.mean(dn * n, axis=-1, keepdims=True))

    @pl.when(first)
    def _():
        go[0] = out

    @pl.when(jnp.logical_not(first))
    def _():
        gx[...] = out.astype(bf16)

    ps = jnp.sum(dh * n, axis=0, keepdims=True)

    @pl.when(i == 0)
    def _():
        gg[...] = ps

    @pl.when(i > 0)
    def _():
        gg[...] += ps


def own_map(per):
    return lambda i, m: (jnp.minimum(i, per - 1), 0)


def nb_map(per):
    return lambda i, m: (jnp.maximum(i - per, 0), 0)


def last_call(meta, xo, xx, dm, dt, wm, wt, dmid, gain):
    rows, width = xo.shape
    cols = dm.shape[1]
    per = rows // T
    fst, snd = pl.BlockSpec((T, width), own_map(per)), pl.BlockSpec((T, width), nb_map(per))
    blk = lambda n: pl.BlockSpec((T, n), lambda i, m: (i, 0))
    return pl.pallas_call(
        last_body,
        out_shape=[sds((2, rows, width), f32), sds((rows, width), bf16), sds((1, width), f32)],
        grid_spec=grid_spec(
            (2 * per,),
            [fst, snd, blk(cols), blk(cols)]
            + [whole((width, cols))] * 2
            + [blk(width), whole((1, width))],
            [
                pl.BlockSpec((1, T, width), lambda i, m: (x_of(m), jnp.minimum(i, per - 1), 0)),
                snd,
                pl.BlockSpec((1, width), lambda i, m: (0, 0)),
            ],
        ),
        cost_estimate=cost(rows, rows),
        name="last",
    )(meta, xo, xx, dm, dt, wm, wt, dmid, gain)


def flip(size, bit):
    return [(i, i ^ bit) for i in range(size)]


def core_swap(v):
    return lax.ppermute(v, "head", CORE)


def x_swap(v):
    return lax.ppermute(v, "head", XNB)


def after(v, *deps):
    return lax.optimization_barrier((v, *deps))[0]


def halve(terms, index, count):
    rows = terms[0].shape[0] // count
    piece = lambda t, k: lax.dynamic_slice_in_dim(t, jnp.bitwise_xor(index, k) * rows, rows, 0)
    total = lambda k: sum(piece(t, k).astype(f32) for t in terms)
    return [total(k).astype(bf16) for k in range(1, count)], total(0)


def strides(dp):
    out = [1]
    while 2 * out[-1] < dp:
        out.append(2 * out[-1])
    return out


def side(stride):
    return lax.axis_index("dp") // stride % 2


def swap(v, stride, dp):
    return lax.ppermute(v, "dp", flip(dp, stride))


def rows_as(got, vs):
    out, row = [], 0
    for v in vs:
        out.append(got[row : row + v.shape[0]])
        row += v.shape[0]
    return out


def swap_both(vs, stride, dp):
    return rows_as(swap(jnp.concatenate(vs, axis=0), stride, dp), vs)


def scatter(sums, stride, dp):
    halves = [halve(terms, side(stride), 2) for terms in sums]
    send = jnp.concatenate([h[0][0] for h in halves], axis=0)
    got = swap(send, stride, dp)
    out, row = [], 0
    for (part,), keep in halves:
        out.append([keep, got[row : row + part.shape[0]]])
        row += part.shape[0]
    return out, send


def join(mine, got, stride):
    upper = side(stride) == 1
    return jnp.concatenate([jnp.where(upper, got, mine), jnp.where(upper, mine, got)], axis=0)


def total(terms):
    return sum(t.astype(f32) for t in terms)


def local(dp, inputs, lengths, w_query, w_key, w_value, w_out, w_up, w_down, conv_taps, gain_attn, gain_ff, cotangent):
    hd = lax.axis_index("head")
    x, c, y = hd // 2, hd % 2, lax.axis_index("dp") % 2
    q = lax.axis_index("dp") % 4
    width = inputs.shape[2]
    part = w_query.shape[0]
    half = 2 * part
    pick = lambda v, k: lax.dynamic_index_in_dim(v, k, 0, keepdims=False)
    y_swap = lambda v: lax.ppermute(v, "dp", flip(dp, 1))
    order = lambda own, nb: lax.dynamic_update_slice_in_dim(own, nb[None].astype(f32), 1 - x, 0)
    meta = jnp.concatenate([lengths, jnp.stack([hd, q])]).astype(jnp.int32)
    gain1, gain2 = gain_attn.reshape(1, width), gain_ff.reshape(1, width)

    mask = (jnp.arange(2) == c)[None, None, :, None]
    tap_rows = jnp.where(mask, conv_taps.transpose(1, 0, 2)[:, :, None, :], 0).reshape(3, 3 * half)
    tap_rows = jnp.concatenate([tap_rows[:, :width], jnp.pad(tap_rows[:, width:], ((0, 0), (0, half)))], axis=0)
    tap_rows = jnp.pad(tap_rows, ((0, 10), (0, 0)))

    def packed(k):
        cut = lambda w: lax.dynamic_slice_in_dim(w, k * half, half, 1)
        fold = cut(w_value)
        return jnp.concatenate(
            [
                jnp.concatenate([cut(w_query), cut(w_key)], axis=1),
                jnp.concatenate([fold[: part // 2], fold[part // 2 :]], axis=1),
                tap_rows,
            ],
            axis=0,
        )

    w_core = core_swap(packed(1 - c))
    w_mine = packed(c)
    x_own = pick(inputs, x)
    rows = x_own.shape[0]
    x_nb = x_swap(pick(inputs, 1 - x))
    pack = x_swap(jnp.concatenate([w_mine, w_core], axis=0))
    x_core = core_swap(x_own)
    count = width // 4
    quarter = lambda w: lax.dynamic_slice_in_dim(w, q * count, count, 0)
    wo_c = core_swap(w_out)
    c_own = pick(cotangent, x)
    ff_src = jnp.stack([quarter(w_up), quarter(w_down)])
    ff_own = jnp.stack([w_up, w_down])
    pack2 = jnp.concatenate([pick(cotangent, 1 - x), w_out, wo_c], axis=0)
    x_nb, ff_src, ff_own, pack2, c_own, meta, x_core, pack = lax.optimization_barrier(
        (x_nb, ff_src, ff_own, pack2, c_own, meta, x_core, pack)
    )
    x_cnb = core_swap(x_nb)
    h1, raw, mix, w_full, taps = qkv_call(meta, x_own, x_nb, x_core, x_cnb, w_mine, w_core, pack, gain1)

    ff_first, pack2 = x_swap(ff_src), x_swap(pack2)
    ff_c = core_swap(ff_own)
    src = after(ff_first, mix)
    ff_n = [swap(src, k, dp) for k in (1, 2, 3)]
    a_mine, a_send, lse = att_fwd_call(meta, after(mix, src, ff_c))
    a_got = core_swap(a_send)
    w_other = core_swap(w_full)
    *ff_n, pack2 = lax.optimization_barrier((*ff_n, pack2, a_mine))[:-1]
    ff_n = [src, *ff_n]
    ff_cn = [core_swap(v) for v in ff_n]
    out_own, out_nb, d_mine, d_send, gg2, dmid, *gw = ffn_call(
        meta, x_own, x_nb, c_own, pack2, a_mine, a_got, after(gain2, w_other),
        (w_out, wo_c, pack2),
        (w_up, w_down, ff_c, *ff_n, *ff_cn),
    )
    d_got = core_swap(d_send)

    _, *rest = strides(dp)
    un, dn, do, uo = [core_swap(gw[k]) for k in (1, 5, 4, 0)]
    nu = total((gw[3], un)).astype(bf16)
    xu = x_swap(nu)
    (dn_send,), dn_keep = halve((gw[7], dn), y, 2)
    (do_send,), do_keep = halve((gw[6], do), y, 2)
    yn, yo = y_swap(dn_send), y_swap(do_send)
    out_x = x_swap(after(out_nb, nu))
    pairs = width // 256
    bwd = lambda m, p, n, into: att_bwd_call(
        meta, m, raw, a_mine, a_send, d_mine, d_got, lse, taps, p, n, into
    )
    *dall, gt_a = bwd(after(mix, nu, dn_send, do_send), 0, pairs - 1, None)
    xu, yn, yo, out_x = lax.optimization_barrier((xu, yn, yo, out_x, gt_a))[:4]
    (u_send,), u_keep = halve((gw[2], uo, xu), y, 2)
    nd = total((dn_keep, yn)).astype(bf16)
    yu, xd = y_swap(u_send), x_swap(nd)
    p_mine, p_theirs, gt_b = bwd(after(mix, u_send, nd), pairs - 1, 1, dall)
    p_got = core_swap(p_theirs)
    gt = jnp.concatenate([gt_a, gt_b], axis=1)
    yu, xd = lax.optimization_barrier((yu, xd, gt_b))[:2]
    sums, sent = scatter([[u_keep, yu], [do_keep, yo, xd]], rest[0], dp)
    keep, far, send = projg_call(meta, after(h1, sent), p_mine, p_theirs)
    flat = lax.optimization_barrier((*sums[0], *sums[1], keep))[:-1]
    sums, sent = scatter([flat[:2], flat[2:]], rest[1], dp)
    got = core_swap(after(send, sent))
    far = x_swap(jnp.concatenate([far, got[part:]], axis=0))
    gi_own, gi_nb, gg1 = last_call(
        meta, x_own, x_nb, p_mine, p_got, w_full, w_other, after(dmid, sent), gain1
    )
    *flat, gt, gg1 = lax.optimization_barrier((*sums[0], *sums[1], gt, x_swap(core_swap(gg1))))
    sums = [flat[:2], flat[2:]]
    for stride in rest[2:]:
        sums, _ = scatter(sums, stride, dp)
    vs = [total(t).astype(bf16) for t in sums]
    far = after(far, *vs)
    far, far2 = far[:part], far[part:]
    ga, gb = keep.astype(f32) + far.astype(f32), got[:part].astype(f32) + far2.astype(f32)
    g_send, g_keep = jnp.where(y == 0, gb, ga).astype(bf16), jnp.where(y == 0, ga, gb)
    pt = [g_keep, y_swap(g_send)]
    gi_got = x_swap(after(gi_nb, g_send))
    for stride in reversed(rest[1:]):
        *got_v, pt[1] = lax.optimization_barrier((*swap_both(vs, stride, dp), pt[1]))
        vs = [join(v, g, stride) for v, g in zip(vs, got_v)]
    (pt,), sent = scatter([pt], rest[0], dp)
    *vs, _ = lax.optimization_barrier((*vs, sent))
    packed_vs = jnp.concatenate(vs, axis=0)
    near_got = swap(packed_vs, rest[0], dp)
    across = rows_as(y_swap(packed_vs), vs)
    for stride in rest[1:]:
        (pt,), _ = scatter([pt], stride, dp)
    others, also = rows_as(near_got, vs), rows_as(y_swap(near_got), vs)
    ps = after(total(pt).astype(bf16), near_got)
    for stride in reversed(rest):
        ps = join(ps, swap(ps, stride, dp), stride)
    ps_got = y_swap(ps)
    whole_of = lambda k: join(
        join(vs[k], others[k], rest[0]), join(across[k], also[k], rest[0]), 1
    ).astype(f32)
    grad_up, gd_all = whole_of(0), whole_of(1)
    grad_down, grad_out = gd_all[: w_down.shape[0]], gd_all[w_down.shape[0] :]
    lo, hi = jnp.where(y == c, ps, ps_got), jnp.where(y == c, ps_got, ps)
    third = lambda v, w: v[:, w * half : w * half + half]
    grads = [jnp.concatenate([third(lo, w), third(hi, w)], axis=1).astype(f32) for w in range(3)]

    gt = gt[:9].reshape(9, 2, part).transpose(1, 0, 2)
    gt = jnp.where(jnp.arange(2)[:, None, None, None] == c, gt[None], 0.0).reshape(4, 9, part)
    gains = jnp.concatenate([gg1, gg2], axis=0).reshape(2, 4, part).transpose(1, 0, 2)
    small = jnp.concatenate([gt, gains, jnp.zeros((4, 5, part), f32)], axis=1)
    small = jnp.broadcast_to(small[:, None], (4, dp, 16, part)).reshape(4 * dp, 16, part)
    small = jnp.sum(lax.all_to_all(small, ("head", "dp"), 0, 0, tiled=True), axis=0)
    output = order(after(out_own, g_send), out_x)
    grad_input = order(after(gi_own, ps), gi_got)
    return (
        output,
        grad_input,
        *grads,
        grad_out,
        grad_up,
        grad_down,
        small[:9].reshape(3, 3, part),
        small[9],
        small[10],
    )


def solution(mesh):
    placed = (
        P("dp", "head", None),
        P("dp"),
        P("head", None),
        P("head", None),
        P("head", None),
        P("head", None),
        P(None, "head"),
        P("head", None),
        P(None, None, "head"),
        P(),
        P(),
        P("dp", "head", None),
    )
    return jax.shard_map(
        functools.partial(local, mesh.shape["dp"]),
        mesh=mesh,
        in_specs=placed,
        out_specs=(
            P("dp", "head", None),
            P("dp", "head", None),
            P("head", None),
            P("head", None),
            P("head", None),
            P("head", None),
            P(None, "head"),
            P("head", None),
            P(None, None, "head"),
            P("head"),
            P("head"),
        ),
        check_vma=False,
    )
```

```python
import functools

import jax
import jax.numpy as jnp
from jax import lax
from jax.experimental import pallas as pl
from jax.experimental.pallas import tpu as pltpu
from jax.sharding import PartitionSpec as P

HDIM = 64
EPS = 1e-06
bf16 = jnp.bfloat16
f32 = jnp.float32

NN = (((1,), (0,)), ((), ()))
NT = (((1,), (1,)), ((), ()))
TN = (((0,), (0,)), ((), ()))

CORE = [(0, 1), (1, 0), (2, 3), (3, 2)]
XNB = [(0, 2), (2, 0), (1, 3), (3, 1)]


def dot(a, b, dims=NN):
    return lax.dot_general(a, b, dims, preferred_element_type=f32)


def cost(flops, nbytes, trans=0):
    return pl.CostEstimate(flops=int(flops), bytes_accessed=int(nbytes), transcendentals=int(trans))


def sds(shape, dtype):
    return jax.ShapeDtypeStruct(shape, dtype)


def whole(shape):
    zeros = (0,) * len(shape)
    return pl.BlockSpec(shape, lambda *_: zeros, pipeline_mode=pl.Buffered(1))


def grid_spec(grid, ins, outs, scratch=()):
    return pltpu.PrefetchScalarGridSpec(
        num_scalar_prefetch=1, grid=grid, in_specs=ins, out_specs=outs, scratch_shapes=scratch
    )


def length_of(m):
    return m[m[2] // 2]


def x_of(m):
    return m[2] // 2


def core_of(m):
    return lax.rem(m[2], 2)


def slot_of(m, b):
    v = jnp.bitwise_xor(m[2], b)
    return lax.rem(v, 2) * 2 + v // 2


def norm(x, gain):
    inv = lax.rsqrt(jnp.mean(x * x, axis=-1, keepdims=True) + EPS)
    n = x * inv
    return n, inv, (n * gain).astype(bf16)


def qkv_body(meta, x0, x1, x2, x3, wa, wb, pack, gain, h_ref, raw_ref, mix_ref, w_ref, taps, ext):
    b = pl.program_id(0)
    rows = x0.shape[0]
    part = w_ref.shape[0] // 4
    width = x0.shape[1]
    tall = wa.shape[0]
    hd = meta[2]

    @pl.when(b == 0)
    def _():
        def put(k, ref, first):
            at = jnp.bitwise_xor(hd, k) * part
            w_ref[pl.ds(pl.multiple_of(at, 64), part), 0:width] = ref[first : first + part, :]
            for n in range(2):
                row = pl.multiple_of(at + n * (part // 2), 32)
                w_ref[pl.ds(row, part // 2), width:] = ref[
                    first + part : first + part + part // 2, n * (width // 2) : (n + 1) * (width // 2)
                ]

        put(0, wa, 0)
        put(1, wb, 0)
        put(2, pack, 0)
        put(3, pack, tall)
        last = lambda ref, end: ref[end - 16 : end, :].astype(f32)
        near = last(wa, tall) + last(wb, tall)
        far = last(pack, tall) + last(pack, 2 * tall)
        t = jnp.where(x_of(meta) == core_of(meta), near, far)
        taps[...] = jnp.zeros_like(taps)
        taps[0:3, 0:width] = t[0:3]
        taps[0:3, width:] = t[3:6, 0 : width // 2]
        ext[0:8, :] = jnp.zeros((8, ext.shape[1]), f32)

    slot = slot_of(meta, b)
    step = ext.shape[0] - 8

    def some(n, carry):
        sl = pl.ds(pl.multiple_of(n * step, step), step)
        x = x0[sl, :]
        for k, other in ((1, x1), (2, x2), (3, x3)):
            x = jnp.where(slot == k, other[sl, :], x)
        _, _, h = norm(x.astype(f32), gain[...].astype(f32))
        h_ref[sl, :] = h
        raw = dot(h, w_ref[...]).astype(bf16)
        raw_ref[sl, :] = raw
        rawf = raw.astype(f32)
        ext[8:, :] = rawf
        t = taps[...]
        mixed = t[0:1] * rawf + t[1:2] * ext[7 : 7 + step, :] + t[2:3] * ext[6 : 6 + step, :]
        mix_ref[sl, :] = mixed.astype(bf16)
        ext[0:8, :] = ext[step:, :]
        return carry

    lax.fori_loop(0, rows // step, some, 0)


def qkv_call(meta, x_own, x_nb, x_core, x_cnb, w_mine, w_core, pack, gain):
    rows, width = x_own.shape
    tall = w_mine.shape[0]
    cols = width * 3 // 2
    length = 4 * rows
    blk = lambda n: pl.BlockSpec((rows, n), lambda b, m: (b, 0))
    const = lambda r: pl.BlockSpec((r, cols), lambda b, m: (0, 0))
    return pl.pallas_call(
        qkv_body,
        out_shape=[
            sds((length, width), bf16),
            sds((length, cols), bf16),
            sds((length, cols), bf16),
            sds((width, cols), bf16),
            sds((8, cols), f32),
        ],
        grid_spec=grid_spec(
            (4,),
            [whole((rows, width))] * 4
            + [whole((tall, width))] * 2
            + [whole(pack.shape), whole((1, width))],
            [
                pl.BlockSpec((rows, width), lambda b, m: (slot_of(m, b), 0)),
                blk(cols),
                blk(cols),
                const(width),
                const(8),
            ],
            [pltpu.VMEM((T + 8, cols), f32)],
        ),
        cost_estimate=cost(2 * length * width * cols, 2 * length * (width * 2 + cols * 2)),
        name="qkv",
    )(meta, x_own, x_nb, x_core, x_cnb, w_mine, w_core, pack, gain)


def two_heads(v):
    lane = lax.broadcasted_iota(jnp.int32, v.shape, 1)
    z = jnp.zeros_like(v)
    return jnp.concatenate([jnp.where(lane < HDIM, v, z), jnp.where(lane < HDIM, z, v)], axis=0)


def causal(first, keys, start, queries):
    key = first + lax.broadcasted_iota(jnp.int32, (keys, queries), 0)
    ok = key <= start + lax.broadcasted_iota(jnp.int32, (keys, queries), 1)
    return jnp.concatenate([ok, ok], axis=1)


def upper(v, axis):
    B = v.shape[axis] // 2
    h = B // 2
    if axis == 0:
        return jnp.concatenate([v[h:B], v[B + h :]], axis=0)
    return jnp.concatenate([v[:, h:B], v[:, B + h :]], axis=1)


def with_bias(k_ref, ka, length):
    L = k_ref.shape[0]
    ka[:, :128] = k_ref[...]
    lane = lax.broadcasted_iota(jnp.int32, (L, 128), 1)
    row = lax.broadcasted_iota(jnp.int32, (L, 128), 0)
    pad = jnp.logical_and(lane == 0, row >= length)
    ka[:, 128:] = jnp.where(pad, -1e9, 0.0).astype(bf16)


def biased(q):
    qq = two_heads(q)
    lane = lax.broadcasted_iota(jnp.int32, qq.shape, 1)
    return jnp.concatenate([qq, jnp.where(lane == 0, 1.0, 0.0).astype(bf16)], axis=1)


def att_fwd_body(meta, q_ref, k_ref, v_ref, mine_ref, theirs_ref, lse_ref, ka, vt, sc):
    i = pl.program_id(1)
    B = q_ref.shape[0]

    @pl.when(i == 0)
    def _():
        vt[...] = v_ref[...].T
        with_bias(k_ref, ka, length_of(meta))

    qq = biased(q_ref[...] * bf16(HDIM**-0.5))
    own = lax.rem(i, 2) == core_of(meta)

    def run(ii):
        m = None
        for j in range(ii + 1):
            ks = slice(j * B, j * B + B)
            s = dot(ka[ks, :], qq, NT)
            if j == ii:
                s = jnp.where(causal(0, B, 0, B), s, -1e9)
            sc[ks, :] = s
            mj = jnp.max(s, axis=0, keepdims=True)
            m = mj if m is None else jnp.maximum(m, mj)
        l = jnp.zeros((1, 2 * B), f32)
        acc = [jnp.zeros((HDIM, B), f32)] * 2
        for j in range(ii + 1):
            ks = slice(j * B, j * B + B)
            p = jnp.exp(sc[ks, :] - m)
            l = l + jnp.sum(p, axis=0, keepdims=True)
            pb = p.astype(bf16)
            for h in range(2):
                r = slice(HDIM * h, HDIM * h + HDIM)
                acc[h] = acc[h] + dot(vt[r, ks], pb[:, h * B : h * B + B])
        inv = 1.0 / l
        out = jnp.concatenate([acc[h] * inv[:, h * B : h * B + B] for h in range(2)], axis=0)
        out = out.T.astype(bf16)

        @pl.when(own)
        def _():
            mine_ref[...] = out

        @pl.when(jnp.logical_not(own))
        def _():
            theirs_ref[...] = out

        ls = m + jnp.log(l)
        lse_ref[0] = jnp.concatenate([ls[:, :B], ls[:, B:]], axis=0)

    for ii in range(4):
        pl.when(i == ii)(functools.partial(run, ii))


def half_map(p, i, m):
    return (jnp.bitwise_xor(i // 2, x_of(m)), p)


def att_fwd_call(meta, mix):
    length, cols = mix.shape
    width = cols // 3
    pairs = width // 128
    B = length // 4
    half = pl.BlockSpec((B, 128), half_map)
    return pl.pallas_call(
        att_fwd_body,
        out_shape=[
            sds((length // 2, width), bf16),
            sds((length // 2, width), bf16),
            sds((pairs, 2, length), f32),
        ],
        grid_spec=grid_spec(
            (pairs, 4),
            [
                pl.BlockSpec((B, 128), lambda p, i, m: (i, p)),
                pl.BlockSpec((length, 128), lambda p, i, m: (0, pairs + p)),
                pl.BlockSpec((length, 128), lambda p, i, m: (0, 2 * pairs + p)),
            ],
            [half, half, pl.BlockSpec((1, 2, B), lambda p, i, m: (p, 0, i))],
            [
                pltpu.VMEM((length, 256), bf16),
                pltpu.VMEM((128, length), bf16),
                pltpu.VMEM((length, 2 * B), f32),
            ],
        ),
        cost_estimate=cost(8 * length * length * width, 8 * length * width, 2 * length * length * pairs),
        name="attn_fwd",
    )(meta, mix, mix, mix)


def att_bwd_body(
    p0, aliased, meta, q_ref, k_ref, v_ref, om, ot, dm, dt, lse_ref, rq, rk, rv, taps, *refs
):
    gm_ref, gt_ref, gt, ka, kt, dkt, dvt, dqt, dqs, ext, stage, sem = refs[2:] if aliased else refs
    i = pl.program_id(1)
    B = q_ref.shape[0]
    L = k_ref.shape[0]
    H = B // 2

    @pl.when(i == 0)
    def _():
        kt[...] = k_ref[...].T
        with_bias(k_ref, ka, length_of(meta))

    own = lax.rem(i, 2) == core_of(meta)
    q = q_ref[...] * bf16(HDIM**-0.5)
    o = jnp.where(own, om[...], ot[...])
    do = jnp.where(own, dm[...], dt[...])
    qq, dd = biased(q), two_heads(do)
    qt, dot_ = q.T, do.T
    od = (o.astype(f32) * do.astype(f32)).T
    delta = jnp.concatenate(
        [jnp.sum(od[:HDIM], axis=0, keepdims=True), jnp.sum(od[HDIM:], axis=0, keepdims=True)],
        axis=1,
    )
    ls = lse_ref[0]
    lse = jnp.concatenate([ls[0:1], ls[1:2]], axis=1)

    dqt[...] = jnp.zeros_like(dqt)

    def tile(st, n, lo, diagonal):
        w = B - lo
        ks = pl.ds(pl.multiple_of(st, H), n)
        part = upper if lo else lambda v, axis: v
        s = dot(ka[ks, :], part(qq, 0), NT)
        dp = dot(v_ref[ks, :], part(dd, 0), NT)
        p = jnp.exp(s - part(lse, 1))
        if diagonal:
            p = jnp.where(causal(lo, n, lo, w), p, 0.0)
        ds = (p * (dp - part(delta, 1))).astype(bf16)
        pb = p.astype(bf16)
        for h in range(2):
            r, c = slice(HDIM * h, HDIM * h + HDIM), slice(h * w, h * w + w)
            dqt[r, lo:] += dot(kt[r, ks], ds[:, c])
            a = dot(qt[r, lo:], ds[:, c], NT)
            b = dot(dot_[r, lo:], pb[:, c], NT)
            if diagonal:
                dkt[r, ks] = a
                dvt[r, ks] = b
            else:
                dkt[r, ks] += a
                dvt[r, ks] += b

    lax.fori_loop(0, i, lambda j, c: (tile(j * B, B, 0, False), c)[1], 0)
    tile(i * B, H, 0, True)
    tile(i * B + H, H, H, True)
    dqs[pl.ds(pl.multiple_of(i * B, B), B), :] = dqt[...].T * HDIM**-0.5

    def copies(pair):
        width = gm_ref.shape[1] // 3
        for b in range(L // B):
            to = pl.ds(pl.multiple_of(jnp.bitwise_xor(b // 2, x_of(meta)) * B, B), B)
            for k in range(3):
                col = pl.ds(pl.multiple_of(k * width + (p0 + pair) * 128, 128), 128)
                src = stage.at[k, pl.ds(b * B, B), :]
                yield b, lambda g, to=to, col=col, src=src, k=k: pltpu.make_async_copy(
                    src, g.at[to, col], sem.at[k]
                )

    def send(pair):
        for b, copy in copies(pair):
            own = core_of(meta) == b % 2

            @pl.when(own)
            def _(copy=copy):
                copy(gm_ref).start()

            @pl.when(jnp.logical_not(own))
            def _(copy=copy):
                copy(gt_ref).start()

    def finish(pair):
        for _, copy in copies(pair):
            copy(gm_ref).wait()

    @pl.when(i == pl.num_programs(1) - 1)
    def _():
        pair = pl.program_id(0)
        gt[...] = jnp.zeros_like(gt)
        ext[...] = jnp.zeros_like(ext)

        @pl.when(pair > 0)
        def _():
            finish(pair)

        def back(n, carry):
            blk = L // B - 1 - n
            sl = pl.ds(pl.multiple_of(blk * B, B), B)
            for which, raw in enumerate((rq, rk, rv)):
                col = which * (taps.shape[1] // 3) + (p0 + pl.program_id(0)) * 128
                t = taps[:, pl.ds(pl.multiple_of(col, 128), 128)]
                g = dqs[sl, :] if which == 0 else (dkt, dvt)[which - 1][:, sl].T
                ext[which, B : B + 8, :] = ext[which, 0:8, :]
                ext[which, 0:B, :] = g
                g1, g2 = ext[which, 1 : B + 1, :], ext[which, 2 : B + 2, :]
                stage[which, sl, :] = (t[0:1] * g + t[1:2] * g1 + t[2:3] * g2).astype(bf16)
                r = raw[sl, :].astype(f32)
                for k, gg in enumerate((g, g1, g2)):
                    row = slice(3 * which + k, 3 * which + k + 1)
                    gt[row, :] += jnp.sum(r * gg, axis=0, keepdims=True)
            return carry

        lax.fori_loop(0, L // B, back, 0)
        send(pair)

        @pl.when(pair == pl.num_programs(0) - 1)
        def _():
            finish(pair)


def att_bwd_call(meta, mix, raw, om, ot, dm, dt, lse, taps, p0, count, into=None):
    length, cols = mix.shape
    pairs = cols // 384
    B = length // 4
    half = pl.BlockSpec((B, 128), lambda p, i, m: (jnp.bitwise_xor(i // 2, x_of(m)), p0 + p))
    full = lambda k: pl.BlockSpec((length, 128), lambda p, i, m: (0, k * pairs + p0 + p))
    return pl.pallas_call(
        functools.partial(att_bwd_body, p0, into is not None),
        out_shape=[sds((length // 2, cols), bf16)] * 2 + [sds((16, 128 * count), f32)],
        grid_spec=grid_spec(
            (count, 4),
            [
                pl.BlockSpec((B, 128), lambda p, i, m: (i, p0 + p)),
                full(1),
                full(2),
                half,
                half,
                half,
                half,
                pl.BlockSpec((1, 2, B), lambda p, i, m: (p0 + p, 0, i)),
                full(0),
                full(1),
                full(2),
                whole((8, cols)),
            ]
            + ([] if into is None else [pl.BlockSpec(memory_space=pl.ANY)] * 2),
            [pl.BlockSpec(memory_space=pl.ANY)] * 2 + [pl.BlockSpec((16, 128), lambda p, i, m: (0, p))],
            [
                pltpu.VMEM((length, 256), bf16),
                pltpu.VMEM((128, length), bf16),
                pltpu.VMEM((128, length), f32),
                pltpu.VMEM((128, length), f32),
                pltpu.VMEM((128, B), f32),
                pltpu.VMEM((length, 128), f32),
                pltpu.VMEM((3, B + 8, 128), f32),
                pltpu.VMEM((3, length, 128), bf16),
                pltpu.SemaphoreType.DMA((3,)),
            ],
        ),
        cost_estimate=cost(
            14 * length * length * 128 * count, 20 * length * 128 * count, 2 * length * length * count
        ),
        name="attn_bwd",
        input_output_aliases={} if into is None else {13: 0, 14: 1},
    )(meta, mix, mix, mix, om, ot, dm, dt, lse, raw, raw, raw, taps, *(into or ()))


T = 256


def valid_rows(meta, i, rows):
    per = rows // T
    block = jnp.where(i < per, meta[2], jnp.bitwise_xor(meta[2], 2))
    start = block * rows + lax.rem(i, per) * T
    return start + lax.broadcasted_iota(jnp.int32, (T, 1), 0) < length_of(meta)


def ffn_body(
    meta, xo, xx, co, cx, am, at, gain, wo_o, wo_c, pack,
    u_o, d_o, f_c, n0, n1, n2, n3, c0, c1, c2, c3,
    oo, ox, dm, dt, gg, dmid, gu0, gu1, gu2, gu3, gd0, gd1, gd2, gd3,
    wo, wus, wds, mid, h_s, g_s, fo, dh, act, du, stu, std, sto, gacc, sw, so, sg, sd, st,
):
    rows, width = xo.shape
    part = wo_o.shape[0]
    half = 2 * part
    n = 2 * rows // T
    per = rows // T
    copies = []
    for k, src in ((0, wo_o), (1, wo_c), (2, pack.at[pl.ds(rows, part), :]), (3, pack.at[pl.ds(rows + part, part), :])):
        shard = jnp.bitwise_xor(meta[2], k)
        row = jnp.where(shard // 2 == core_of(meta), 0, half) + lax.rem(shard, 2) * part
        cp = pltpu.make_async_copy(src, wo.at[pl.ds(pl.multiple_of(row, 64), part), :], so.at[k])
        cp.start()
        copies.append(cp)
    for k, pair in ((0, (f_c.at[0], f_c.at[1])), (2, (u_o, d_o))):
        for n_, src in enumerate(pair):
            pltpu.make_async_copy(src, (wus, wds)[n_].at[k], sw.at[k, n_]).start()
    for k, quarters in ((1, (c0, c1, c2, c3)), (3, (n0, n1, n2, n3))):
        for q_, src in enumerate(quarters):
            count = src.shape[1]
            to = pl.ds(pl.multiple_of(jnp.bitwise_xor(meta[3], q_) * count, 64), count)
            for n_, dst in enumerate((wus, wds)):
                pltpu.make_async_copy(src.at[n_], dst.at[k, to, :], sw.at[k, n_]).start()
    for cp in copies:
        cp.wait()
    gn = gain[...].astype(f32)

    def first_rows(i, carry):
        sl = pl.ds(pl.multiple_of(i * T, T), T)
        src = pl.ds(pl.multiple_of(lax.rem(i, per) * T, T), T)
        own = i < per
        x = jnp.where(own, xo[src, :], xx[src, :]).astype(f32)
        a = jnp.concatenate([am[sl, :], at[sl, :]], axis=1)
        m = x + dot(a, wo[...])
        mid[sl, :] = m
        fo[sl, :] = m
        h_s[sl, :] = norm(m, gn)[2]
        ct = jnp.where(own, co[src, :], cx[src, :])
        g_s[sl, :] = jnp.where(valid_rows(meta, i, rows), ct, jnp.zeros_like(ct))
        dh[sl, :] = jnp.zeros((T, width), f32)
        return carry

    lax.fori_loop(0, n, first_rows, 0)

    R = 512
    C = 768

    gus, gds = (gu0, gu1, gu2, gu3), (gd0, gd1, gd2, gd3)

    def stores(n_, slot):
        return [
            pltpu.make_async_copy(stu.at[slot], gus[n_], sg.at[slot, 0]),
            pltpu.make_async_copy(std.at[slot], gds[n_].at[pl.ds(0, width), :], sg.at[slot, 1]),
        ]

    def shard(k, carry):
        for cp in (
            pltpu.make_async_copy(u_o, wus.at[k], sw.at[k, 0]),
            pltpu.make_async_copy(d_o, wds.at[k], sw.at[k, 1]),
        ):
            cp.wait()

        def rows_step(t, c2):
            sl = pl.ds(pl.multiple_of(t * R, R), R)
            h, g = h_s[sl, :], g_s[sl, :]
            r = jnp.maximum(dot(h, wus[k]), 0.0)
            a = (r * r).astype(bf16)
            d = (dot(g, wds[k], NT) * 2.0 * r).astype(bf16)
            act[sl, :] = a
            du[sl, :] = d
            fo[sl, :] += dot(a, wds[k])
            dh[sl, :] += dot(d, wus[k], NT)
            return c2

        lax.fori_loop(0, 2 * rows // R, rows_step, 0)
        slot = lax.rem(k, 2)

        @pl.when(k >= 2)
        def _():
            for cp in stores(0, slot):
                cp.wait()

        def cols_step(t, c2):
            sl = pl.ds(pl.multiple_of(t * C, C), C)
            stu[slot, :, sl] = dot(h_s[...], du[:, sl], TN).astype(bf16)
            std[slot, sl, :] = dot(act[:, sl], g_s[...], TN).astype(bf16)
            return c2

        lax.fori_loop(0, width // C, cols_step, 0)
        for n_ in range(4):

            @pl.when(k == n_)
            def _(n_=n_):
                for cp in stores(n_, n_ % 2):
                    cp.start()

        return carry

    lax.fori_loop(0, 4, shard, 0)
    gg[...] = jnp.zeros_like(gg)

    def last_rows(i, carry):
        sl = pl.ds(pl.multiple_of(i * T, T), T)
        dst = pl.ds(pl.multiple_of(lax.rem(i, per) * T, T), T)
        ok = valid_rows(meta, i, rows)
        m = mid[sl, :]
        out = jnp.where(ok, fo[sl, :], 0.0)

        fo[sl, :] = out

        @pl.when(i < per)
        def _():
            own = oo.at[meta[2] // 2, dst, :]
            pltpu.make_async_copy(fo.at[sl, :], own, sd.at[1]).start()

        @pl.when(i >= per)
        def _():
            ox[dst, :] = out.astype(bf16)

        nm, inv, _ = norm(m, gn)
        d = dh[sl, :]
        dn = d * gn
        r = g_s[sl, :].astype(f32) + inv * (dn - nm * jnp.mean(dn * nm, axis=-1, keepdims=True))
        mid[sl, :] = r
        pltpu.make_async_copy(mid.at[sl, :], dmid.at[sl, :], sd.at[0]).start()
        db = r.astype(bf16)
        du[sl, :] = db
        da = dot(db, wo[...], NT).astype(bf16)
        dm[sl, :] = da[:, :half]
        dt[sl, :] = da[:, half:]
        gg[...] += jnp.sum(d * nm, axis=0, keepdims=True)
        return carry

    lax.fori_loop(0, n, last_rows, 0)
    gacc[0:half, :] = dot(am[...], du[...], TN)
    gacc[half:, :] = dot(at[...], du[...], TN)
    outs = [
        pltpu.make_async_copy(mid, dmid, sd.at[0]),
        pltpu.make_async_copy(fo.at[pl.ds(0, rows), :], oo.at[meta[2] // 2], sd.at[1]),
    ]
    for k, k_ in enumerate((1, 3, 0, 2)):
        shard_ = jnp.bitwise_xor(meta[2], k_)
        row = jnp.where(shard_ // 2 == core_of(meta), 0, half) + lax.rem(shard_, 2) * part
        sto[k] = gacc[pl.ds(pl.multiple_of(row, 64), part), :].astype(bf16)
        cp = pltpu.make_async_copy(sto.at[k], gds[k].at[pl.ds(width, part), :], st.at[k])
        cp.start()
        outs.append(cp)
    for slot in range(2):
        outs.extend(stores(2 + slot, slot))
    for cp in outs:
        cp.wait()


def ffn_call(meta, xo, xx, co, cx, am, at, gain, wos, ffs):
    rows, width = xo.shape
    half = am.shape[1]
    part = half // 2
    hid = ffs[0].shape[1]
    hbm = pl.BlockSpec(memory_space=pl.ANY)
    vm = lambda *shape: whole(shape)
    all_rows = 2 * rows
    return pl.pallas_call(
        ffn_body,
        out_shape=[
            sds((2, rows, width), f32),
            sds((rows, width), bf16),
            sds((all_rows, half), bf16),
            sds((all_rows, half), bf16),
            sds((1, width), f32),
            sds((all_rows, width), f32),
        ]
        + [sds((width, hid), bf16)] * 4
        + [sds((hid + part, width), bf16)] * 4,
        grid_spec=grid_spec(
            (1,),
            [vm(rows, width)] * 4 + [vm(all_rows, half)] * 2 + [vm(1, width)] + [hbm] * 14,
            [
                hbm,
                vm(rows, width),
                vm(all_rows, half),
                vm(all_rows, half),
                vm(1, width),
            ]
            + [hbm] * 9,
            [
                pltpu.VMEM((width, width), bf16),
                pltpu.VMEM((4, width, hid), bf16),
                pltpu.VMEM((4, hid, width), bf16),
                pltpu.VMEM((all_rows, width), f32),
                pltpu.VMEM((all_rows, width), bf16),
                pltpu.VMEM((all_rows, width), bf16),
                pltpu.VMEM((all_rows, width), f32),
                pltpu.VMEM((all_rows, width), f32),
                pltpu.VMEM((all_rows, hid), bf16),
                pltpu.VMEM((all_rows, hid), bf16),
                pltpu.VMEM((2, width, hid), bf16),
                pltpu.VMEM((2, hid, width), bf16),
                pltpu.VMEM((4, part, width), bf16),
                pltpu.VMEM((width, width), f32),
                pltpu.SemaphoreType.DMA((4, 2)),
                pltpu.SemaphoreType.DMA((4,)),
                pltpu.SemaphoreType.DMA((2, 2)),
                pltpu.SemaphoreType.DMA((2,)),
                pltpu.SemaphoreType.DMA((4,)),
            ],
        ),
        cost_estimate=cost(
            48 * all_rows * width * hid + 6 * all_rows * width * width, 40 * all_rows * width
        ),
        compiler_params=pltpu.CompilerParams(vmem_limit_bytes=62 * 2**20),
        name="ffn",
    )(meta, xo, xx, co, cx, am, at, gain, *wos, *ffs)


def projg_body(meta, h, dm, dt, keep, far, send, acc):
    rows = dm.shape[0]
    acc[...] = dot(h[0:rows, :], dm[...], TN) + dot(h[rows:, :], dt[...], TN)
    part = keep.shape[0]
    for ref, k, row in ((keep, 0, 0), (far, 2, 0), (send, 1, 0), (send, 3, part)):
        at = jnp.bitwise_xor(meta[2], k)
        ref[row : row + part, :] = acc[pl.ds(pl.multiple_of(at * part, 64), part), :].astype(bf16)


def projg_call(meta, h, dm, dt):
    length, width = h.shape
    cols = dm.shape[1]
    step = cols // 3
    d = pl.BlockSpec((length // 2, step), lambda j, m: (0, j))
    g = lambda rows: pl.BlockSpec((rows, step), lambda j, m: (0, j))
    part = width // 4
    return pl.pallas_call(
        projg_body,
        out_shape=[sds((rows, cols), bf16) for rows in (part, part, 2 * part)],
        grid_spec=grid_spec(
            (3,),
            [whole((length, width)), d, d],
            [g(part), g(part), g(2 * part)],
            [pltpu.VMEM((width, step), f32)],
        ),
        cost_estimate=cost(length, length),
        name="projg",
    )(meta, h, dm, dt)


def last_body(meta, xo, xx, dm, dt, wm, wt, dmid, gain, go, gx, gg):
    i = pl.program_id(0)
    per = pl.num_programs(0) // 2
    first = i < per
    x = jnp.where(first, xo[...], xx[...]).astype(f32)
    gn = gain[...].astype(f32)
    n, inv, _ = norm(x, gn)
    dh = dot(dm[...], wm[...], NT) + dot(dt[...], wt[...], NT)
    dn = dh * gn
    out = dmid[...] + inv * (dn - n * jnp.mean(dn * n, axis=-1, keepdims=True))

    @pl.when(first)
    def _():
        go[0] = out

    @pl.when(jnp.logical_not(first))
    def _():
        gx[...] = out.astype(bf16)

    ps = jnp.sum(dh * n, axis=0, keepdims=True)

    @pl.when(i == 0)
    def _():
        gg[...] = ps

    @pl.when(i > 0)
    def _():
        gg[...] += ps


def own_map(per):
    return lambda i, m: (jnp.minimum(i, per - 1), 0)


def nb_map(per):
    return lambda i, m: (jnp.maximum(i - per, 0), 0)


def last_call(meta, xo, xx, dm, dt, wm, wt, dmid, gain):
    rows, width = xo.shape
    cols = dm.shape[1]
    per = rows // T
    fst, snd = pl.BlockSpec((T, width), own_map(per)), pl.BlockSpec((T, width), nb_map(per))
    blk = lambda n: pl.BlockSpec((T, n), lambda i, m: (i, 0))
    return pl.pallas_call(
        last_body,
        out_shape=[sds((2, rows, width), f32), sds((rows, width), bf16), sds((1, width), f32)],
        grid_spec=grid_spec(
            (2 * per,),
            [fst, snd, blk(cols), blk(cols)]
            + [whole((width, cols))] * 2
            + [blk(width), whole((1, width))],
            [
                pl.BlockSpec((1, T, width), lambda i, m: (x_of(m), jnp.minimum(i, per - 1), 0)),
                snd,
                pl.BlockSpec((1, width), lambda i, m: (0, 0)),
            ],
        ),
        cost_estimate=cost(rows, rows),
        name="last",
    )(meta, xo, xx, dm, dt, wm, wt, dmid, gain)


def flip(size, bit):
    return [(i, i ^ bit) for i in range(size)]


def core_swap(v):
    return lax.ppermute(v, "head", CORE)


def x_swap(v):
    return lax.ppermute(v, "head", XNB)


def after(v, *deps):
    return lax.optimization_barrier((v, *deps))[0]


def halve(terms, index, count):
    rows = terms[0].shape[0] // count
    piece = lambda t, k: lax.dynamic_slice_in_dim(t, jnp.bitwise_xor(index, k) * rows, rows, 0)
    total = lambda k: sum(piece(t, k).astype(f32) for t in terms)
    return [total(k).astype(bf16) for k in range(1, count)], total(0)


def strides(dp):
    out = [1]
    while 2 * out[-1] < dp:
        out.append(2 * out[-1])
    return out


def side(stride):
    return lax.axis_index("dp") // stride % 2


def swap(v, stride, dp):
    return lax.ppermute(v, "dp", flip(dp, stride))


def rows_as(got, vs):
    out, row = [], 0
    for v in vs:
        out.append(got[row : row + v.shape[0]])
        row += v.shape[0]
    return out


def swap_both(vs, stride, dp):
    return rows_as(swap(jnp.concatenate(vs, axis=0), stride, dp), vs)


def scatter(sums, stride, dp):
    halves = [halve(terms, side(stride), 2) for terms in sums]
    send = jnp.concatenate([h[0][0] for h in halves], axis=0)
    got = swap(send, stride, dp)
    out, row = [], 0
    for (part,), keep in halves:
        out.append([keep, got[row : row + part.shape[0]]])
        row += part.shape[0]
    return out, send


def join(mine, got, stride):
    upper = side(stride) == 1
    return jnp.concatenate([jnp.where(upper, got, mine), jnp.where(upper, mine, got)], axis=0)


def total(terms):
    return sum(t.astype(f32) for t in terms)


def local(dp, inputs, lengths, w_query, w_key, w_value, w_out, w_up, w_down, conv_taps, gain_attn, gain_ff, cotangent):
    hd = lax.axis_index("head")
    x, c, y = hd // 2, hd % 2, lax.axis_index("dp") % 2
    q = lax.axis_index("dp") % 4
    width = inputs.shape[2]
    part = w_query.shape[0]
    half = 2 * part
    pick = lambda v, k: lax.dynamic_index_in_dim(v, k, 0, keepdims=False)
    y_swap = lambda v: lax.ppermute(v, "dp", flip(dp, 1))
    order = lambda own, nb: lax.dynamic_update_slice_in_dim(own, nb[None].astype(f32), 1 - x, 0)
    meta = jnp.concatenate([lengths, jnp.stack([hd, q])]).astype(jnp.int32)
    gain1, gain2 = gain_attn.reshape(1, width), gain_ff.reshape(1, width)

    mask = (jnp.arange(2) == c)[None, None, :, None]
    tap_rows = jnp.where(mask, conv_taps.transpose(1, 0, 2)[:, :, None, :], 0).reshape(3, 3 * half)
    tap_rows = jnp.concatenate([tap_rows[:, :width], jnp.pad(tap_rows[:, width:], ((0, 0), (0, half)))], axis=0)
    tap_rows = jnp.pad(tap_rows, ((0, 10), (0, 0)))

    def packed(k):
        cut = lambda w: lax.dynamic_slice_in_dim(w, k * half, half, 1)
        fold = cut(w_value)
        return jnp.concatenate(
            [
                jnp.concatenate([cut(w_query), cut(w_key)], axis=1),
                jnp.concatenate([fold[: part // 2], fold[part // 2 :]], axis=1),
                tap_rows,
            ],
            axis=0,
        )

    w_core = core_swap(packed(1 - c))
    w_mine = packed(c)
    x_own = pick(inputs, x)
    rows = x_own.shape[0]
    x_nb = x_swap(pick(inputs, 1 - x))
    pack = x_swap(jnp.concatenate([w_mine, w_core], axis=0))
    x_core = core_swap(x_own)
    count = width // 4
    quarter = lambda w: lax.dynamic_slice_in_dim(w, q * count, count, 0)
    wo_c = core_swap(w_out)
    c_own = pick(cotangent, x)
    ff_src = jnp.stack([quarter(w_up), quarter(w_down)])
    ff_own = jnp.stack([w_up, w_down])
    pack2 = jnp.concatenate([pick(cotangent, 1 - x), w_out, wo_c], axis=0)
    x_nb, ff_src, ff_own, pack2, c_own, meta, x_core, pack = lax.optimization_barrier(
        (x_nb, ff_src, ff_own, pack2, c_own, meta, x_core, pack)
    )
    x_cnb = core_swap(x_nb)
    h1, raw, mix, w_full, taps = qkv_call(meta, x_own, x_nb, x_core, x_cnb, w_mine, w_core, pack, gain1)

    ff_first, pack2 = x_swap(ff_src), x_swap(pack2)
    ff_c = core_swap(ff_own)
    src = after(ff_first, mix)
    ff_n = [swap(src, k, dp) for k in (1, 2, 3)]
    a_mine, a_send, lse = att_fwd_call(meta, after(mix, src, ff_c))
    a_got = core_swap(a_send)
    w_other = core_swap(w_full)
    *ff_n, pack2 = lax.optimization_barrier((*ff_n, pack2, a_mine))[:-1]
    ff_n = [src, *ff_n]
    ff_cn = [core_swap(v) for v in ff_n]
    out_own, out_nb, d_mine, d_send, gg2, dmid, *gw = ffn_call(
        meta, x_own, x_nb, c_own, pack2, a_mine, a_got, after(gain2, w_other),
        (w_out, wo_c, pack2),
        (w_up, w_down, ff_c, *ff_n, *ff_cn),
    )
    d_got = core_swap(d_send)

    _, *rest = strides(dp)
    un, dn, do, uo = [core_swap(gw[k]) for k in (1, 5, 4, 0)]
    nu = total((gw[3], un)).astype(bf16)
    xu = x_swap(nu)
    (dn_send,), dn_keep = halve((gw[7], dn), y, 2)
    (do_send,), do_keep = halve((gw[6], do), y, 2)
    yn, yo = y_swap(dn_send), y_swap(do_send)
    out_x = x_swap(after(out_nb, nu))
    pairs = width // 256
    bwd = lambda m, p, n, into: att_bwd_call(
        meta, m, raw, a_mine, a_send, d_mine, d_got, lse, taps, p, n, into
    )
    *dall, gt_a = bwd(after(mix, nu, dn_send, do_send), 0, pairs - 1, None)
    xu, yn, yo, out_x = lax.optimization_barrier((xu, yn, yo, out_x, gt_a))[:4]
    (u_send,), u_keep = halve((gw[2], uo, xu), y, 2)
    nd = total((dn_keep, yn)).astype(bf16)
    yu, xd = y_swap(u_send), x_swap(nd)
    p_mine, p_theirs, gt_b = bwd(after(mix, u_send, nd), pairs - 1, 1, dall)
    p_got = core_swap(p_theirs)
    gt = jnp.concatenate([gt_a, gt_b], axis=1)
    yu, xd = lax.optimization_barrier((yu, xd, gt_b))[:2]
    sums, sent = scatter([[u_keep, yu], [do_keep, yo, xd]], rest[0], dp)
    keep, far, send = projg_call(meta, after(h1, sent), p_mine, p_theirs)
    flat = lax.optimization_barrier((*sums[0], *sums[1], keep))[:-1]
    sums, sent = scatter([flat[:2], flat[2:]], rest[1], dp)
    got = core_swap(after(send, sent))
    far, far2 = x_swap(far), x_swap(got[part:])
    gi_own, gi_nb, gg1 = last_call(
        meta, x_own, x_nb, p_mine, p_got, w_full, w_other, after(dmid, sent), gain1
    )
    *flat, gt, gg1 = lax.optimization_barrier((*sums[0], *sums[1], gt, x_swap(core_swap(gg1))))
    sums = [flat[:2], flat[2:]]
    for stride in rest[2:]:
        sums, _ = scatter(sums, stride, dp)
    vs = [total(t).astype(bf16) for t in sums]
    far, far2 = lax.optimization_barrier((far, far2, *vs))[:2]
    ga, gb = keep.astype(f32) + far.astype(f32), got[:part].astype(f32) + far2.astype(f32)
    g_send, g_keep = jnp.where(y == 0, gb, ga).astype(bf16), jnp.where(y == 0, ga, gb)
    pt = [g_keep, y_swap(g_send)]
    gi_got = x_swap(after(gi_nb, g_send))
    for stride in reversed(rest[1:]):
        cat = jnp.concatenate(vs, axis=0)
        first_cat = cat if stride == rest[-1] else first_cat
        got_v = swap(cat, stride, dp)
        vs = [join(v, g, stride) for v, g in zip(vs, rows_as(got_v, vs))]
    (pt,), sent = scatter([pt], rest[0], dp)
    packed_vs = jnp.concatenate(vs, axis=0)
    near_got = swap(packed_vs, rest[0], dp)
    across = rows_as(y_swap(packed_vs), vs)
    for stride in rest[1:]:
        (pt,), _ = scatter([pt], stride, dp)
    others, also = rows_as(near_got, vs), rows_as(y_swap(near_got), vs)
    ps = after(total(pt).astype(bf16), near_got)
    for stride in reversed(rest):
        ps = join(ps, swap(ps, stride, dp), stride)
    ps_got = y_swap(ps)
    whole_of = lambda k: join(
        join(vs[k], others[k], rest[0]), join(across[k], also[k], rest[0]), 1
    ).astype(f32)
    grad_up, gd_all = whole_of(0), whole_of(1)
    grad_down, grad_out = gd_all[: w_down.shape[0]], gd_all[w_down.shape[0] :]
    lo, hi = jnp.where(y == c, ps, ps_got), jnp.where(y == c, ps_got, ps)
    third = lambda v, w: v[:, w * half : w * half + half]
    grads = [jnp.concatenate([third(lo, w), third(hi, w)], axis=1).astype(f32) for w in range(3)]

    gt = gt[:9].reshape(9, 2, part).transpose(1, 0, 2)
    gt = jnp.where(jnp.arange(2)[:, None, None, None] == c, gt[None], 0.0).reshape(4, 9, part)
    gains = jnp.concatenate([gg1, gg2], axis=0).reshape(2, 4, part).transpose(1, 0, 2)
    small = jnp.concatenate([gt, gains, jnp.zeros((4, 5, part), f32)], axis=1)
    small = after(small, first_cat)
    small = jnp.broadcast_to(small[:, None], (4, dp, 16, part)).reshape(4 * dp, 16, part)
    small = jnp.sum(lax.all_to_all(small, ("head", "dp"), 0, 0, tiled=True), axis=0)
    output = order(after(out_own, g_send), out_x)
    grad_input = order(after(gi_own, ps), gi_got)
    return (
        output,
        grad_input,
        *grads,
        grad_out,
        grad_up,
        grad_down,
        small[:9].reshape(3, 3, part),
        small[9],
        small[10],
    )


def solution(mesh):
    placed = (
        P("dp", "head", None),
        P("dp"),
        P("head", None),
        P("head", None),
        P("head", None),
        P("head", None),
        P(None, "head"),
        P("head", None),
        P(None, None, "head"),
        P(),
        P(),
        P("dp", "head", None),
    )
    return jax.shard_map(
        functools.partial(local, mesh.shape["dp"]),
        mesh=mesh,
        in_specs=placed,
        out_specs=(
            P("dp", "head", None),
            P("dp", "head", None),
            P("head", None),
            P("head", None),
            P("head", None),
            P("head", None),
            P(None, "head"),
            P("head", None),
            P(None, None, "head"),
            P("head"),
            P("head"),
        ),
        check_vma=False,
    )
```

```python
import functools

import jax
import jax.numpy as jnp
from jax import lax
from jax.experimental import pallas as pl
from jax.experimental.pallas import tpu as pltpu
from jax.sharding import PartitionSpec as P

HDIM = 64
EPS = 1e-06
bf16 = jnp.bfloat16
f32 = jnp.float32

NN = (((1,), (0,)), ((), ()))
NT = (((1,), (1,)), ((), ()))
TN = (((0,), (0,)), ((), ()))

CORE = [(0, 1), (1, 0), (2, 3), (3, 2)]
XNB = [(0, 2), (2, 0), (1, 3), (3, 1)]


def dot(a, b, dims=NN):
    return lax.dot_general(a, b, dims, preferred_element_type=f32)


def cost(flops, nbytes, trans=0):
    return pl.CostEstimate(flops=int(flops), bytes_accessed=int(nbytes), transcendentals=int(trans))


def sds(shape, dtype):
    return jax.ShapeDtypeStruct(shape, dtype)


def whole(shape):
    zeros = (0,) * len(shape)
    return pl.BlockSpec(shape, lambda *_: zeros, pipeline_mode=pl.Buffered(1))


def grid_spec(grid, ins, outs, scratch=()):
    return pltpu.PrefetchScalarGridSpec(
        num_scalar_prefetch=1, grid=grid, in_specs=ins, out_specs=outs, scratch_shapes=scratch
    )


def length_of(m):
    return m[m[2] // 2]


def x_of(m):
    return m[2] // 2


def core_of(m):
    return lax.rem(m[2], 2)


def slot_of(m, b):
    v = jnp.bitwise_xor(m[2], b)
    return lax.rem(v, 2) * 2 + v // 2


def norm(x, gain):
    inv = lax.rsqrt(jnp.mean(x * x, axis=-1, keepdims=True) + EPS)
    n = x * inv
    return n, inv, (n * gain).astype(bf16)


def qkv_body(meta, x0, x1, x2, x3, wa, wb, pack, gain, h_ref, raw_ref, mix_ref, w_ref, taps, ext):
    b = pl.program_id(0)
    rows = x0.shape[0]
    part = w_ref.shape[0] // 4
    width = x0.shape[1]
    tall = wa.shape[0]
    hd = meta[2]

    @pl.when(b == 0)
    def _():
        def put(k, ref, first):
            at = jnp.bitwise_xor(hd, k) * part
            w_ref[pl.ds(pl.multiple_of(at, 64), part), 0:width] = ref[first : first + part, :]
            for n in range(2):
                row = pl.multiple_of(at + n * (part // 2), 32)
                w_ref[pl.ds(row, part // 2), width:] = ref[
                    first + part : first + part + part // 2, n * (width // 2) : (n + 1) * (width // 2)
                ]

        put(0, wa, 0)
        put(1, wb, 0)
        put(2, pack, 0)
        put(3, pack, tall)
        last = lambda ref, end: ref[end - 16 : end, :].astype(f32)
        near = last(wa, tall) + last(wb, tall)
        far = last(pack, tall) + last(pack, 2 * tall)
        t = jnp.where(x_of(meta) == core_of(meta), near, far)
        taps[...] = jnp.zeros_like(taps)
        taps[0:3, 0:width] = t[0:3]
        taps[0:3, width:] = t[3:6, 0 : width // 2]
        ext[0:8, :] = jnp.zeros((8, ext.shape[1]), f32)

    slot = slot_of(meta, b)
    step = ext.shape[0] - 8

    def some(n, carry):
        sl = pl.ds(pl.multiple_of(n * step, step), step)
        x = x0[sl, :]
        for k, other in ((1, x1), (2, x2), (3, x3)):
            x = jnp.where(slot == k, other[sl, :], x)
        _, _, h = norm(x.astype(f32), gain[...].astype(f32))
        h_ref[sl, :] = h
        raw = dot(h, w_ref[...]).astype(bf16)
        raw_ref[sl, :] = raw
        rawf = raw.astype(f32)
        ext[8:, :] = rawf
        t = taps[...]
        mixed = t[0:1] * rawf + t[1:2] * ext[7 : 7 + step, :] + t[2:3] * ext[6 : 6 + step, :]
        mix_ref[sl, :] = mixed.astype(bf16)
        ext[0:8, :] = ext[step:, :]
        return carry

    lax.fori_loop(0, rows // step, some, 0)


def qkv_call(meta, x_own, x_nb, x_core, x_cnb, w_mine, w_core, pack, gain):
    rows, width = x_own.shape
    tall = w_mine.shape[0]
    cols = width * 3 // 2
    length = 4 * rows
    blk = lambda n: pl.BlockSpec((rows, n), lambda b, m: (b, 0))
    const = lambda r: pl.BlockSpec((r, cols), lambda b, m: (0, 0))
    return pl.pallas_call(
        qkv_body,
        out_shape=[
            sds((length, width), bf16),
            sds((length, cols), bf16),
            sds((length, cols), bf16),
            sds((width, cols), bf16),
            sds((8, cols), f32),
        ],
        grid_spec=grid_spec(
            (4,),
            [whole((rows, width))] * 4
            + [whole((tall, width))] * 2
            + [whole(pack.shape), whole((1, width))],
            [
                pl.BlockSpec((rows, width), lambda b, m: (slot_of(m, b), 0)),
                blk(cols),
                blk(cols),
                const(width),
                const(8),
            ],
            [pltpu.VMEM((T + 8, cols), f32)],
        ),
        cost_estimate=cost(2 * length * width * cols, 2 * length * (width * 2 + cols * 2)),
        name="qkv",
    )(meta, x_own, x_nb, x_core, x_cnb, w_mine, w_core, pack, gain)


def two_heads(v):
    lane = lax.broadcasted_iota(jnp.int32, v.shape, 1)
    z = jnp.zeros_like(v)
    return jnp.concatenate([jnp.where(lane < HDIM, v, z), jnp.where(lane < HDIM, z, v)], axis=0)


def causal(first, keys, start, queries):
    key = first + lax.broadcasted_iota(jnp.int32, (keys, queries), 0)
    ok = key <= start + lax.broadcasted_iota(jnp.int32, (keys, queries), 1)
    return jnp.concatenate([ok, ok], axis=1)


def upper(v, axis):
    B = v.shape[axis] // 2
    h = B // 2
    if axis == 0:
        return jnp.concatenate([v[h:B], v[B + h :]], axis=0)
    return jnp.concatenate([v[:, h:B], v[:, B + h :]], axis=1)


def with_bias(k_ref, ka, length):
    L = k_ref.shape[0]
    ka[:, :128] = k_ref[...]
    lane = lax.broadcasted_iota(jnp.int32, (L, 128), 1)
    row = lax.broadcasted_iota(jnp.int32, (L, 128), 0)
    pad = jnp.logical_and(lane == 0, row >= length)
    ka[:, 128:] = jnp.where(pad, -1e9, 0.0).astype(bf16)


def biased(q):
    qq = two_heads(q)
    lane = lax.broadcasted_iota(jnp.int32, qq.shape, 1)
    return jnp.concatenate([qq, jnp.where(lane == 0, 1.0, 0.0).astype(bf16)], axis=1)


def att_fwd_body(meta, q_ref, k_ref, v_ref, mine_ref, theirs_ref, lse_ref, ka, vt, sc):
    i = pl.program_id(1)
    B = q_ref.shape[0]

    @pl.when(i == 0)
    def _():
        vt[...] = v_ref[...].T
        with_bias(k_ref, ka, length_of(meta))

    qq = biased(q_ref[...] * bf16(HDIM**-0.5))
    own = lax.rem(i, 2) == core_of(meta)

    def run(ii):
        m = None
        for j in range(ii + 1):
            ks = slice(j * B, j * B + B)
            s = dot(ka[ks, :], qq, NT)
            if j == ii:
                s = jnp.where(causal(0, B, 0, B), s, -1e9)
            sc[ks, :] = s
            mj = jnp.max(s, axis=0, keepdims=True)
            m = mj if m is None else jnp.maximum(m, mj)
        l = jnp.zeros((1, 2 * B), f32)
        acc = [jnp.zeros((HDIM, B), f32)] * 2
        for j in range(ii + 1):
            ks = slice(j * B, j * B + B)
            p = jnp.exp(sc[ks, :] - m)
            l = l + jnp.sum(p, axis=0, keepdims=True)
            pb = p.astype(bf16)
            for h in range(2):
                r = slice(HDIM * h, HDIM * h + HDIM)
                acc[h] = acc[h] + dot(vt[r, ks], pb[:, h * B : h * B + B])
        inv = 1.0 / l
        out = jnp.concatenate([acc[h] * inv[:, h * B : h * B + B] for h in range(2)], axis=0)
        out = out.T.astype(bf16)

        @pl.when(own)
        def _():
            mine_ref[...] = out

        @pl.when(jnp.logical_not(own))
        def _():
            theirs_ref[...] = out

        ls = m + jnp.log(l)
        lse_ref[0] = jnp.concatenate([ls[:, :B], ls[:, B:]], axis=0)

    for ii in range(4):
        pl.when(i == ii)(functools.partial(run, ii))


def half_map(p, i, m):
    return (jnp.bitwise_xor(i // 2, x_of(m)), p)


def att_fwd_call(meta, mix):
    length, cols = mix.shape
    width = cols // 3
    pairs = width // 128
    B = length // 4
    half = pl.BlockSpec((B, 128), half_map)
    return pl.pallas_call(
        att_fwd_body,
        out_shape=[
            sds((length // 2, width), bf16),
            sds((length // 2, width), bf16),
            sds((pairs, 2, length), f32),
        ],
        grid_spec=grid_spec(
            (pairs, 4),
            [
                pl.BlockSpec((B, 128), lambda p, i, m: (i, p)),
                pl.BlockSpec((length, 128), lambda p, i, m: (0, pairs + p)),
                pl.BlockSpec((length, 128), lambda p, i, m: (0, 2 * pairs + p)),
            ],
            [half, half, pl.BlockSpec((1, 2, B), lambda p, i, m: (p, 0, i))],
            [
                pltpu.VMEM((length, 256), bf16),
                pltpu.VMEM((128, length), bf16),
                pltpu.VMEM((length, 2 * B), f32),
            ],
        ),
        cost_estimate=cost(8 * length * length * width, 8 * length * width, 2 * length * length * pairs),
        name="attn_fwd",
    )(meta, mix, mix, mix)


def att_bwd_body(
    p0, aliased, meta, q_ref, k_ref, v_ref, om, ot, dm, dt, lse_ref, rq, rk, rv, taps, *refs
):
    gm_ref, gt_ref, gt, ka, kt, dkt, dvt, dqt, dqs, ext, stage, sem = refs[2:] if aliased else refs
    i = pl.program_id(1)
    B = q_ref.shape[0]
    L = k_ref.shape[0]
    H = B // 2

    @pl.when(i == 0)
    def _():
        kt[...] = k_ref[...].T
        with_bias(k_ref, ka, length_of(meta))

    own = lax.rem(i, 2) == core_of(meta)
    q = q_ref[...] * bf16(HDIM**-0.5)
    o = jnp.where(own, om[...], ot[...])
    do = jnp.where(own, dm[...], dt[...])
    qq, dd = biased(q), two_heads(do)
    qt, dot_ = q.T, do.T
    od = (o.astype(f32) * do.astype(f32)).T
    delta = jnp.concatenate(
        [jnp.sum(od[:HDIM], axis=0, keepdims=True), jnp.sum(od[HDIM:], axis=0, keepdims=True)],
        axis=1,
    )
    ls = lse_ref[0]
    lse = jnp.concatenate([ls[0:1], ls[1:2]], axis=1)

    dqt[...] = jnp.zeros_like(dqt)

    def tile(st, n, lo, diagonal):
        w = B - lo
        ks = pl.ds(pl.multiple_of(st, H), n)
        part = upper if lo else lambda v, axis: v
        s = dot(ka[ks, :], part(qq, 0), NT)
        dp = dot(v_ref[ks, :], part(dd, 0), NT)
        p = jnp.exp(s - part(lse, 1))
        if diagonal:
            p = jnp.where(causal(lo, n, lo, w), p, 0.0)
        ds = (p * (dp - part(delta, 1))).astype(bf16)
        pb = p.astype(bf16)
        for h in range(2):
            r, c = slice(HDIM * h, HDIM * h + HDIM), slice(h * w, h * w + w)
            dqt[r, lo:] += dot(kt[r, ks], ds[:, c])
            a = dot(qt[r, lo:], ds[:, c], NT)
            b = dot(dot_[r, lo:], pb[:, c], NT)
            if diagonal:
                dkt[r, ks] = a
                dvt[r, ks] = b
            else:
                dkt[r, ks] += a
                dvt[r, ks] += b

    lax.fori_loop(0, i, lambda j, c: (tile(j * B, B, 0, False), c)[1], 0)
    tile(i * B, H, 0, True)
    tile(i * B + H, H, H, True)
    dqs[pl.ds(pl.multiple_of(i * B, B), B), :] = dqt[...].T * HDIM**-0.5

    def copies(pair):
        width = gm_ref.shape[1] // 3
        for b in range(L // B):
            to = pl.ds(pl.multiple_of(jnp.bitwise_xor(b // 2, x_of(meta)) * B, B), B)
            for k in range(3):
                col = pl.ds(pl.multiple_of(k * width + (p0 + pair) * 128, 128), 128)
                src = stage.at[k, pl.ds(b * B, B), :]
                yield b, lambda g, to=to, col=col, src=src, k=k: pltpu.make_async_copy(
                    src, g.at[to, col], sem.at[k]
                )

    def send(pair):
        for b, copy in copies(pair):
            own = core_of(meta) == b % 2

            @pl.when(own)
            def _(copy=copy):
                copy(gm_ref).start()

            @pl.when(jnp.logical_not(own))
            def _(copy=copy):
                copy(gt_ref).start()

    def finish(pair):
        for _, copy in copies(pair):
            copy(gm_ref).wait()

    @pl.when(i == pl.num_programs(1) - 1)
    def _():
        pair = pl.program_id(0)
        gt[...] = jnp.zeros_like(gt)
        ext[...] = jnp.zeros_like(ext)

        @pl.when(pair > 0)
        def _():
            finish(pair)

        def back(n, carry):
            blk = L // B - 1 - n
            sl = pl.ds(pl.multiple_of(blk * B, B), B)
            for which, raw in enumerate((rq, rk, rv)):
                col = which * (taps.shape[1] // 3) + (p0 + pl.program_id(0)) * 128
                t = taps[:, pl.ds(pl.multiple_of(col, 128), 128)]
                g = dqs[sl, :] if which == 0 else (dkt, dvt)[which - 1][:, sl].T
                ext[which, B : B + 8, :] = ext[which, 0:8, :]
                ext[which, 0:B, :] = g
                g1, g2 = ext[which, 1 : B + 1, :], ext[which, 2 : B + 2, :]
                stage[which, sl, :] = (t[0:1] * g + t[1:2] * g1 + t[2:3] * g2).astype(bf16)
                r = raw[sl, :].astype(f32)
                for k, gg in enumerate((g, g1, g2)):
                    row = slice(3 * which + k, 3 * which + k + 1)
                    gt[row, :] += jnp.sum(r * gg, axis=0, keepdims=True)
            return carry

        lax.fori_loop(0, L // B, back, 0)
        send(pair)

        @pl.when(pair == pl.num_programs(0) - 1)
        def _():
            finish(pair)


def att_bwd_call(meta, mix, raw, om, ot, dm, dt, lse, taps, p0, count, into=None):
    length, cols = mix.shape
    pairs = cols // 384
    B = length // 4
    half = pl.BlockSpec((B, 128), lambda p, i, m: (jnp.bitwise_xor(i // 2, x_of(m)), p0 + p))
    full = lambda k: pl.BlockSpec((length, 128), lambda p, i, m: (0, k * pairs + p0 + p))
    return pl.pallas_call(
        functools.partial(att_bwd_body, p0, into is not None),
        out_shape=[sds((length // 2, cols), bf16)] * 2 + [sds((16, 128 * count), f32)],
        grid_spec=grid_spec(
            (count, 4),
            [
                pl.BlockSpec((B, 128), lambda p, i, m: (i, p0 + p)),
                full(1),
                full(2),
                half,
                half,
                half,
                half,
                pl.BlockSpec((1, 2, B), lambda p, i, m: (p0 + p, 0, i)),
                full(0),
                full(1),
                full(2),
                whole((8, cols)),
            ]
            + ([] if into is None else [pl.BlockSpec(memory_space=pl.ANY)] * 2),
            [pl.BlockSpec(memory_space=pl.ANY)] * 2 + [pl.BlockSpec((16, 128), lambda p, i, m: (0, p))],
            [
                pltpu.VMEM((length, 256), bf16),
                pltpu.VMEM((128, length), bf16),
                pltpu.VMEM((128, length), f32),
                pltpu.VMEM((128, length), f32),
                pltpu.VMEM((128, B), f32),
                pltpu.VMEM((length, 128), f32),
                pltpu.VMEM((3, B + 8, 128), f32),
                pltpu.VMEM((3, length, 128), bf16),
                pltpu.SemaphoreType.DMA((3,)),
            ],
        ),
        cost_estimate=cost(
            14 * length * length * 128 * count, 20 * length * 128 * count, 2 * length * length * count
        ),
        name="attn_bwd",
        input_output_aliases={} if into is None else {13: 0, 14: 1},
    )(meta, mix, mix, mix, om, ot, dm, dt, lse, raw, raw, raw, taps, *(into or ()))


T = 256


def valid_rows(meta, i, rows):
    per = rows // T
    block = jnp.where(i < per, meta[2], jnp.bitwise_xor(meta[2], 2))
    start = block * rows + lax.rem(i, per) * T
    return start + lax.broadcasted_iota(jnp.int32, (T, 1), 0) < length_of(meta)


def ffn_body(
    meta, xo, xx, co, cx, am, at, gain, wo_o, wo_c, pack,
    u_o, d_o, f_c, n0, n1, n2, n3, c0, c1, c2, c3,
    oo, ox, dm, dt, gg, dmid, gu0, gu1, gu2, gu3, gd0, gd1, gd2, gd3,
    wo, wus, wds, mid, h_s, g_s, fo, dh, act, du, stu, std, sto, gacc, sw, so, sg, sd, st,
):
    rows, width = xo.shape
    part = wo_o.shape[0]
    half = 2 * part
    n = 2 * rows // T
    per = rows // T
    copies = []
    for k, src in ((0, wo_o), (1, wo_c), (2, pack.at[pl.ds(rows, part), :]), (3, pack.at[pl.ds(rows + part, part), :])):
        shard = jnp.bitwise_xor(meta[2], k)
        row = jnp.where(shard // 2 == core_of(meta), 0, half) + lax.rem(shard, 2) * part
        cp = pltpu.make_async_copy(src, wo.at[pl.ds(pl.multiple_of(row, 64), part), :], so.at[k])
        cp.start()
        copies.append(cp)
    for k, pair in ((0, (f_c.at[0], f_c.at[1])), (2, (u_o, d_o))):
        for n_, src in enumerate(pair):
            pltpu.make_async_copy(src, (wus, wds)[n_].at[k], sw.at[k, n_]).start()
    for k, quarters in ((1, (c0, c1, c2, c3)), (3, (n0, n1, n2, n3))):
        for q_, src in enumerate(quarters):
            count = src.shape[1]
            to = pl.ds(pl.multiple_of(jnp.bitwise_xor(meta[3], q_) * count, 64), count)
            for n_, dst in enumerate((wus, wds)):
                pltpu.make_async_copy(src.at[n_], dst.at[k, to, :], sw.at[k, n_]).start()
    for cp in copies:
        cp.wait()
    gn = gain[...].astype(f32)

    def first_rows(i, carry):
        sl = pl.ds(pl.multiple_of(i * T, T), T)
        src = pl.ds(pl.multiple_of(lax.rem(i, per) * T, T), T)
        own = i < per
        x = jnp.where(own, xo[src, :], xx[src, :]).astype(f32)
        a = jnp.concatenate([am[sl, :], at[sl, :]], axis=1)
        m = x + dot(a, wo[...])
        mid[sl, :] = m
        fo[sl, :] = m
        h_s[sl, :] = norm(m, gn)[2]
        ct = jnp.where(own, co[src, :], cx[src, :])
        g_s[sl, :] = jnp.where(valid_rows(meta, i, rows), ct, jnp.zeros_like(ct))
        dh[sl, :] = jnp.zeros((T, width), f32)
        return carry

    lax.fori_loop(0, n, first_rows, 0)

    R = 512
    C = 768

    gus, gds = (gu0, gu1, gu2, gu3), (gd0, gd1, gd2, gd3)

    def stores(n_, slot):
        return [
            pltpu.make_async_copy(stu.at[slot], gus[n_], sg.at[slot, 0]),
            pltpu.make_async_copy(std.at[slot], gds[n_].at[pl.ds(0, width), :], sg.at[slot, 1]),
        ]

    def shard(k, carry):
        for cp in (
            pltpu.make_async_copy(u_o, wus.at[k], sw.at[k, 0]),
            pltpu.make_async_copy(d_o, wds.at[k], sw.at[k, 1]),
        ):
            cp.wait()

        def rows_step(t, c2):
            sl = pl.ds(pl.multiple_of(t * R, R), R)
            h, g = h_s[sl, :], g_s[sl, :]
            r = jnp.maximum(dot(h, wus[k]), 0.0)
            a = (r * r).astype(bf16)
            d = (dot(g, wds[k], NT) * 2.0 * r).astype(bf16)
            act[sl, :] = a
            du[sl, :] = d
            fo[sl, :] += dot(a, wds[k])
            dh[sl, :] += dot(d, wus[k], NT)
            return c2

        lax.fori_loop(0, 2 * rows // R, rows_step, 0)
        slot = lax.rem(k, 2)

        @pl.when(k >= 2)
        def _():
            for cp in stores(0, slot):
                cp.wait()

        def cols_step(t, c2):
            sl = pl.ds(pl.multiple_of(t * C, C), C)
            stu[slot, :, sl] = dot(h_s[...], du[:, sl], TN).astype(bf16)
            std[slot, sl, :] = dot(act[:, sl], g_s[...], TN).astype(bf16)
            return c2

        lax.fori_loop(0, width // C, cols_step, 0)
        for n_ in range(4):

            @pl.when(k == n_)
            def _(n_=n_):
                for cp in stores(n_, n_ % 2):
                    cp.start()

        return carry

    lax.fori_loop(0, 4, shard, 0)
    gg[...] = jnp.zeros_like(gg)

    def last_rows(i, carry):
        sl = pl.ds(pl.multiple_of(i * T, T), T)
        dst = pl.ds(pl.multiple_of(lax.rem(i, per) * T, T), T)
        ok = valid_rows(meta, i, rows)
        m = mid[sl, :]
        out = jnp.where(ok, fo[sl, :], 0.0)

        fo[sl, :] = out

        @pl.when(i < per)
        def _():
            own = oo.at[meta[2] // 2, dst, :]
            pltpu.make_async_copy(fo.at[sl, :], own, sd.at[1]).start()

        @pl.when(i >= per)
        def _():
            ox[dst, :] = out.astype(bf16)

        nm, inv, _ = norm(m, gn)
        d = dh[sl, :]
        dn = d * gn
        r = g_s[sl, :].astype(f32) + inv * (dn - nm * jnp.mean(dn * nm, axis=-1, keepdims=True))
        mid[sl, :] = r
        pltpu.make_async_copy(mid.at[sl, :], dmid.at[sl, :], sd.at[0]).start()
        db = r.astype(bf16)
        du[sl, :] = db
        da = dot(db, wo[...], NT).astype(bf16)
        dm[sl, :] = da[:, :half]
        dt[sl, :] = da[:, half:]
        gg[...] += jnp.sum(d * nm, axis=0, keepdims=True)
        return carry

    lax.fori_loop(0, n, last_rows, 0)
    gacc[0:half, :] = dot(am[...], du[...], TN)
    gacc[half:, :] = dot(at[...], du[...], TN)
    outs = [
        pltpu.make_async_copy(mid, dmid, sd.at[0]),
        pltpu.make_async_copy(fo.at[pl.ds(0, rows), :], oo.at[meta[2] // 2], sd.at[1]),
    ]
    for k, k_ in enumerate((1, 3, 0, 2)):
        shard_ = jnp.bitwise_xor(meta[2], k_)
        row = jnp.where(shard_ // 2 == core_of(meta), 0, half) + lax.rem(shard_, 2) * part
        sto[k] = gacc[pl.ds(pl.multiple_of(row, 64), part), :].astype(bf16)
        cp = pltpu.make_async_copy(sto.at[k], gds[k].at[pl.ds(width, part), :], st.at[k])
        cp.start()
        outs.append(cp)
    for slot in range(2):
        outs.extend(stores(2 + slot, slot))
    for cp in outs:
        cp.wait()


def ffn_call(meta, xo, xx, co, cx, am, at, gain, wos, ffs):
    rows, width = xo.shape
    half = am.shape[1]
    part = half // 2
    hid = ffs[0].shape[1]
    hbm = pl.BlockSpec(memory_space=pl.ANY)
    vm = lambda *shape: whole(shape)
    all_rows = 2 * rows
    return pl.pallas_call(
        ffn_body,
        out_shape=[
            sds((2, rows, width), f32),
            sds((rows, width), bf16),
            sds((all_rows, half), bf16),
            sds((all_rows, half), bf16),
            sds((1, width), f32),
            sds((all_rows, width), f32),
        ]
        + [sds((width, hid), bf16)] * 4
        + [sds((hid + part, width), bf16)] * 4,
        grid_spec=grid_spec(
            (1,),
            [vm(rows, width)] * 4 + [vm(all_rows, half)] * 2 + [vm(1, width)] + [hbm] * 14,
            [
                hbm,
                vm(rows, width),
                vm(all_rows, half),
                vm(all_rows, half),
                vm(1, width),
            ]
            + [hbm] * 9,
            [
                pltpu.VMEM((width, width), bf16),
                pltpu.VMEM((4, width, hid), bf16),
                pltpu.VMEM((4, hid, width), bf16),
                pltpu.VMEM((all_rows, width), f32),
                pltpu.VMEM((all_rows, width), bf16),
                pltpu.VMEM((all_rows, width), bf16),
                pltpu.VMEM((all_rows, width), f32),
                pltpu.VMEM((all_rows, width), f32),
                pltpu.VMEM((all_rows, hid), bf16),
                pltpu.VMEM((all_rows, hid), bf16),
                pltpu.VMEM((2, width, hid), bf16),
                pltpu.VMEM((2, hid, width), bf16),
                pltpu.VMEM((4, part, width), bf16),
                pltpu.VMEM((width, width), f32),
                pltpu.SemaphoreType.DMA((4, 2)),
                pltpu.SemaphoreType.DMA((4,)),
                pltpu.SemaphoreType.DMA((2, 2)),
                pltpu.SemaphoreType.DMA((2,)),
                pltpu.SemaphoreType.DMA((4,)),
            ],
        ),
        cost_estimate=cost(
            48 * all_rows * width * hid + 6 * all_rows * width * width, 40 * all_rows * width
        ),
        compiler_params=pltpu.CompilerParams(vmem_limit_bytes=62 * 2**20),
        name="ffn",
    )(meta, xo, xx, co, cx, am, at, gain, *wos, *ffs)


def projg_body(meta, h, dm, dt, keep, far, send, acc):
    rows = dm.shape[0]
    acc[...] = dot(h[0:rows, :], dm[...], TN) + dot(h[rows:, :], dt[...], TN)
    part = keep.shape[0]
    for ref, k, row in ((keep, 0, 0), (far, 2, 0), (send, 1, 0), (send, 3, part)):
        at = jnp.bitwise_xor(meta[2], k)
        ref[row : row + part, :] = acc[pl.ds(pl.multiple_of(at * part, 64), part), :].astype(bf16)


def projg_call(meta, h, dm, dt):
    length, width = h.shape
    cols = dm.shape[1]
    step = cols // 3
    d = pl.BlockSpec((length // 2, step), lambda j, m: (0, j))
    g = lambda rows: pl.BlockSpec((rows, step), lambda j, m: (0, j))
    part = width // 4
    return pl.pallas_call(
        projg_body,
        out_shape=[sds((rows, cols), bf16) for rows in (part, part, 2 * part)],
        grid_spec=grid_spec(
            (3,),
            [whole((length, width)), d, d],
            [g(part), g(part), g(2 * part)],
            [pltpu.VMEM((width, step), f32)],
        ),
        cost_estimate=cost(length, length),
        name="projg",
    )(meta, h, dm, dt)


def last_body(meta, xo, xx, dm, dt, wm, wt, dmid, gain, go, gx, gg):
    i = pl.program_id(0)
    per = pl.num_programs(0) // 2
    first = i < per
    x = jnp.where(first, xo[...], xx[...]).astype(f32)
    gn = gain[...].astype(f32)
    n, inv, _ = norm(x, gn)
    dh = dot(dm[...], wm[...], NT) + dot(dt[...], wt[...], NT)
    dn = dh * gn
    out = dmid[...] + inv * (dn - n * jnp.mean(dn * n, axis=-1, keepdims=True))

    @pl.when(first)
    def _():
        go[0] = out

    @pl.when(jnp.logical_not(first))
    def _():
        gx[...] = out.astype(bf16)

    ps = jnp.sum(dh * n, axis=0, keepdims=True)

    @pl.when(i == 0)
    def _():
        gg[...] = ps

    @pl.when(i > 0)
    def _():
        gg[...] += ps


def own_map(per):
    return lambda i, m: (jnp.minimum(i, per - 1), 0)


def nb_map(per):
    return lambda i, m: (jnp.maximum(i - per, 0), 0)


def last_call(meta, xo, xx, dm, dt, wm, wt, dmid, gain):
    rows, width = xo.shape
    cols = dm.shape[1]
    per = rows // T
    fst, snd = pl.BlockSpec((T, width), own_map(per)), pl.BlockSpec((T, width), nb_map(per))
    blk = lambda n: pl.BlockSpec((T, n), lambda i, m: (i, 0))
    return pl.pallas_call(
        last_body,
        out_shape=[sds((2, rows, width), f32), sds((rows, width), bf16), sds((1, width), f32)],
        grid_spec=grid_spec(
            (2 * per,),
            [fst, snd, blk(cols), blk(cols)]
            + [whole((width, cols))] * 2
            + [blk(width), whole((1, width))],
            [
                pl.BlockSpec((1, T, width), lambda i, m: (x_of(m), jnp.minimum(i, per - 1), 0)),
                snd,
                pl.BlockSpec((1, width), lambda i, m: (0, 0)),
            ],
        ),
        cost_estimate=cost(rows, rows),
        name="last",
    )(meta, xo, xx, dm, dt, wm, wt, dmid, gain)


def flip(size, bit):
    return [(i, i ^ bit) for i in range(size)]


def core_swap(v):
    return lax.ppermute(v, "head", CORE)


def x_swap(v):
    return lax.ppermute(v, "head", XNB)


def after(v, *deps):
    return lax.optimization_barrier((v, *deps))[0]


def halve(terms, index, count):
    rows = terms[0].shape[0] // count
    piece = lambda t, k: lax.dynamic_slice_in_dim(t, jnp.bitwise_xor(index, k) * rows, rows, 0)
    total = lambda k: sum(piece(t, k).astype(f32) for t in terms)
    return [total(k).astype(bf16) for k in range(1, count)], total(0)


def strides(dp):
    out = [1]
    while 2 * out[-1] < dp:
        out.append(2 * out[-1])
    return out


def side(stride):
    return lax.axis_index("dp") // stride % 2


def swap(v, stride, dp):
    return lax.ppermute(v, "dp", flip(dp, stride))


def rows_as(got, vs):
    out, row = [], 0
    for v in vs:
        out.append(got[row : row + v.shape[0]])
        row += v.shape[0]
    return out


def swap_both(vs, stride, dp):
    return rows_as(swap(jnp.concatenate(vs, axis=0), stride, dp), vs)


def scatter(sums, stride, dp):
    halves = [halve(terms, side(stride), 2) for terms in sums]
    send = jnp.concatenate([h[0][0] for h in halves], axis=0)
    got = swap(send, stride, dp)
    out, row = [], 0
    for (part,), keep in halves:
        out.append([keep, got[row : row + part.shape[0]]])
        row += part.shape[0]
    return out, send


def join(mine, got, stride):
    upper = side(stride) == 1
    return jnp.concatenate([jnp.where(upper, got, mine), jnp.where(upper, mine, got)], axis=0)


def scatter4(terms, dp):
    sends, keep = halve(terms, lax.axis_index("dp") // 2 % 4, 4)
    return [keep] + [swap(v, 2 * k, dp) for k, v in enumerate(sends, 1)]


def gather4(v, dp):
    index = lax.axis_index("dp") // 2 % 4
    parts = [v] + [swap(v, 2 * k, dp) for k in (1, 2, 3)]

    def block(j):
        out = parts[0]
        for k in (1, 2, 3):
            out = jnp.where(jnp.bitwise_xor(index, j) == k, parts[k], out)
        return out

    return jnp.concatenate([block(j) for j in range(4)], axis=0)


def total(terms):
    return sum(t.astype(f32) for t in terms)


def local(dp, inputs, lengths, w_query, w_key, w_value, w_out, w_up, w_down, conv_taps, gain_attn, gain_ff, cotangent):
    hd = lax.axis_index("head")
    x, c, y = hd // 2, hd % 2, lax.axis_index("dp") % 2
    q = lax.axis_index("dp") % 4
    width = inputs.shape[2]
    part = w_query.shape[0]
    half = 2 * part
    pick = lambda v, k: lax.dynamic_index_in_dim(v, k, 0, keepdims=False)
    y_swap = lambda v: lax.ppermute(v, "dp", flip(dp, 1))
    order = lambda own, nb: lax.dynamic_update_slice_in_dim(own, nb[None].astype(f32), 1 - x, 0)
    meta = jnp.concatenate([lengths, jnp.stack([hd, q])]).astype(jnp.int32)
    gain1, gain2 = gain_attn.reshape(1, width), gain_ff.reshape(1, width)

    mask = (jnp.arange(2) == c)[None, None, :, None]
    tap_rows = jnp.where(mask, conv_taps.transpose(1, 0, 2)[:, :, None, :], 0).reshape(3, 3 * half)
    tap_rows = jnp.concatenate([tap_rows[:, :width], jnp.pad(tap_rows[:, width:], ((0, 0), (0, half)))], axis=0)
    tap_rows = jnp.pad(tap_rows, ((0, 10), (0, 0)))

    def packed(k):
        cut = lambda w: lax.dynamic_slice_in_dim(w, k * half, half, 1)
        fold = cut(w_value)
        return jnp.concatenate(
            [
                jnp.concatenate([cut(w_query), cut(w_key)], axis=1),
                jnp.concatenate([fold[: part // 2], fold[part // 2 :]], axis=1),
                tap_rows,
            ],
            axis=0,
        )

    w_core = core_swap(packed(1 - c))
    w_mine = packed(c)
    x_own = pick(inputs, x)
    rows = x_own.shape[0]
    x_nb = x_swap(pick(inputs, 1 - x))
    pack = x_swap(jnp.concatenate([w_mine, w_core], axis=0))
    x_core = core_swap(x_own)
    count = width // 4
    quarter = lambda w: lax.dynamic_slice_in_dim(w, q * count, count, 0)
    wo_c = core_swap(w_out)
    c_own = pick(cotangent, x)
    ff_src = jnp.stack([quarter(w_up), quarter(w_down)])
    ff_own = jnp.stack([w_up, w_down])
    pack2 = jnp.concatenate([pick(cotangent, 1 - x), w_out, wo_c], axis=0)
    x_nb, ff_src, ff_own, pack2, c_own, meta, x_core, pack = lax.optimization_barrier(
        (x_nb, ff_src, ff_own, pack2, c_own, meta, x_core, pack)
    )
    x_cnb = core_swap(x_nb)
    h1, raw, mix, w_full, taps = qkv_call(meta, x_own, x_nb, x_core, x_cnb, w_mine, w_core, pack, gain1)

    ff_first, pack2 = x_swap(ff_src), x_swap(pack2)
    ff_c = core_swap(ff_own)
    src = after(ff_first, mix)
    ff_n = [swap(src, k, dp) for k in (1, 2, 3)]
    a_mine, a_send, lse = att_fwd_call(meta, after(mix, src, ff_c))
    a_got = core_swap(a_send)
    w_other = core_swap(w_full)
    *ff_n, pack2 = lax.optimization_barrier((*ff_n, pack2, a_mine))[:-1]
    ff_n = [src, *ff_n]
    ff_cn = [core_swap(v) for v in ff_n]
    out_own, out_nb, d_mine, d_send, gg2, dmid, *gw = ffn_call(
        meta, x_own, x_nb, c_own, pack2, a_mine, a_got, after(gain2, w_other),
        (w_out, wo_c, pack2),
        (w_up, w_down, ff_c, *ff_n, *ff_cn),
    )
    d_got = core_swap(d_send)

    _, *rest = strides(dp)
    un, dn, do, uo = [core_swap(gw[k]) for k in (1, 5, 4, 0)]
    nu = total((gw[3], un)).astype(bf16)
    xu = x_swap(nu)
    (dn_send,), dn_keep = halve((gw[7], dn), y, 2)
    (do_send,), do_keep = halve((gw[6], do), y, 2)
    yn, yo = y_swap(dn_send), y_swap(do_send)
    out_x = x_swap(after(out_nb, nu))
    pairs = width // 256
    bwd = lambda m, p, n, into: att_bwd_call(
        meta, m, raw, a_mine, a_send, d_mine, d_got, lse, taps, p, n, into
    )
    *dall, gt_a = bwd(after(mix, nu, dn_send, do_send), 0, pairs - 1, None)
    xu, yn, yo, out_x = lax.optimization_barrier((xu, yn, yo, out_x, gt_a))[:4]
    (u_send,), u_keep = halve((gw[2], uo, xu), y, 2)
    nd = total((dn_keep, yn)).astype(bf16)
    yu, xd = y_swap(u_send), x_swap(nd)
    p_mine, p_theirs, gt_b = bwd(after(mix, u_send, nd), pairs - 1, 1, dall)
    p_got = core_swap(p_theirs)
    gt = jnp.concatenate([gt_a, gt_b], axis=1)
    yu, xd = lax.optimization_barrier((yu, xd, gt_b))[:2]
    sums, sent = scatter([[u_keep, yu], [do_keep, yo, xd]], rest[0], dp)
    keep, far, send = projg_call(meta, after(h1, sent), p_mine, p_theirs)
    flat = lax.optimization_barrier((*sums[0], *sums[1], keep))[:-1]
    sums, sent = scatter([flat[:2], flat[2:]], rest[1], dp)
    got = core_swap(after(send, sent))
    far, far2 = x_swap(far), x_swap(got[part:])
    gi_own, gi_nb, gg1 = last_call(
        meta, x_own, x_nb, p_mine, p_got, w_full, w_other, after(dmid, sent), gain1
    )
    *flat, gt, gg1 = lax.optimization_barrier((*sums[0], *sums[1], gt, x_swap(core_swap(gg1))))
    sums = [flat[:2], flat[2:]]
    for stride in rest[2:]:
        sums, _ = scatter(sums, stride, dp)
    vs = [total(t).astype(bf16) for t in sums]
    far, far2 = lax.optimization_barrier((far, far2, *vs))[:2]
    ga, gb = keep.astype(f32) + far.astype(f32), got[:part].astype(f32) + far2.astype(f32)
    g_send, g_keep = jnp.where(y == 0, gb, ga).astype(bf16), jnp.where(y == 0, ga, gb)
    pt = [g_keep, y_swap(g_send)]
    gi_got = x_swap(after(gi_nb, g_send))
    for stride in reversed(rest[1:]):
        cat = jnp.concatenate(vs, axis=0)
        first_cat = cat if stride == rest[-1] else first_cat
        got_v = swap(cat, stride, dp)
        vs = [join(v, g, stride) for v, g in zip(vs, rows_as(got_v, vs))]
    pt = scatter4(pt, dp)
    packed_vs = jnp.concatenate(vs, axis=0)
    near_got = swap(packed_vs, rest[0], dp)
    across = rows_as(y_swap(packed_vs), vs)
    for stride in rest[2:]:
        (pt,), _ = scatter([pt], stride, dp)
    others, also = rows_as(near_got, vs), rows_as(y_swap(near_got), vs)
    ps = total(pt).astype(bf16)
    for stride in reversed(rest[2:]):
        ps = join(ps, swap(ps, stride, dp), stride)
    ps = gather4(ps, dp)
    ps_got = y_swap(ps)
    whole_of = lambda k: join(
        join(vs[k], others[k], rest[0]), join(across[k], also[k], rest[0]), 1
    ).astype(f32)
    grad_up, gd_all = whole_of(0), whole_of(1)
    grad_down, grad_out = gd_all[: w_down.shape[0]], gd_all[w_down.shape[0] :]
    lo, hi = jnp.where(y == c, ps, ps_got), jnp.where(y == c, ps_got, ps)
    third = lambda v, w: v[:, w * half : w * half + half]
    grads = [jnp.concatenate([third(lo, w), third(hi, w)], axis=1).astype(f32) for w in range(3)]

    gt = gt[:9].reshape(9, 2, part).transpose(1, 0, 2)
    gt = jnp.where(jnp.arange(2)[:, None, None, None] == c, gt[None], 0.0).reshape(4, 9, part)
    gains = jnp.concatenate([gg1, gg2], axis=0).reshape(2, 4, part).transpose(1, 0, 2)
    small = jnp.concatenate([gt, gains, jnp.zeros((4, 5, part), f32)], axis=1)
    small = after(small, first_cat)
    small = jnp.broadcast_to(small[:, None], (4, dp, 16, part)).reshape(4 * dp, 16, part)
    small = jnp.sum(lax.all_to_all(small, ("head", "dp"), 0, 0, tiled=True), axis=0)
    output = order(after(out_own, g_send), out_x)
    grad_input = order(after(gi_own, ps), gi_got)
    return (
        output,
        grad_input,
        *grads,
        grad_out,
        grad_up,
        grad_down,
        small[:9].reshape(3, 3, part),
        small[9],
        small[10],
    )


def solution(mesh):
    placed = (
        P("dp", "head", None),
        P("dp"),
        P("head", None),
        P("head", None),
        P("head", None),
        P("head", None),
        P(None, "head"),
        P("head", None),
        P(None, None, "head"),
        P(),
        P(),
        P("dp", "head", None),
    )
    return jax.shard_map(
        functools.partial(local, mesh.shape["dp"]),
        mesh=mesh,
        in_specs=placed,
        out_specs=(
            P("dp", "head", None),
            P("dp", "head", None),
            P("head", None),
            P("head", None),
            P("head", None),
            P("head", None),
            P(None, "head"),
            P("head", None),
            P(None, None, "head"),
            P("head"),
            P("head"),
        ),
        check_vma=False,
    )
```

```python
import functools

import jax
import jax.numpy as jnp
from jax import lax
from jax.experimental import pallas as pl
from jax.experimental.pallas import tpu as pltpu
from jax.sharding import PartitionSpec as P

HDIM = 64
EPS = 1e-06
bf16 = jnp.bfloat16
f32 = jnp.float32

NN = (((1,), (0,)), ((), ()))
NT = (((1,), (1,)), ((), ()))
TN = (((0,), (0,)), ((), ()))

CORE = [(0, 1), (1, 0), (2, 3), (3, 2)]
XNB = [(0, 2), (2, 0), (1, 3), (3, 1)]


def dot(a, b, dims=NN):
    return lax.dot_general(a, b, dims, preferred_element_type=f32)


def cost(flops, nbytes, trans=0):
    return pl.CostEstimate(flops=int(flops), bytes_accessed=int(nbytes), transcendentals=int(trans))


def sds(shape, dtype):
    return jax.ShapeDtypeStruct(shape, dtype)


def whole(shape):
    zeros = (0,) * len(shape)
    return pl.BlockSpec(shape, lambda *_: zeros, pipeline_mode=pl.Buffered(1))


def grid_spec(grid, ins, outs, scratch=()):
    return pltpu.PrefetchScalarGridSpec(
        num_scalar_prefetch=1, grid=grid, in_specs=ins, out_specs=outs, scratch_shapes=scratch
    )


def length_of(m):
    return m[m[2] // 2]


def x_of(m):
    return m[2] // 2


def core_of(m):
    return lax.rem(m[2], 2)


def slot_of(m, b):
    v = jnp.bitwise_xor(m[2], b)
    return lax.rem(v, 2) * 2 + v // 2


def norm(x, gain):
    inv = lax.rsqrt(jnp.mean(x * x, axis=-1, keepdims=True) + EPS)
    n = x * inv
    return n, inv, (n * gain).astype(bf16)


def qkv_body(meta, x0, x1, x2, x3, wa, wb, pack, gain, h_ref, raw_ref, mix_ref, w_ref, taps, ext):
    b = pl.program_id(0)
    rows = x0.shape[0]
    part = w_ref.shape[0] // 4
    width = x0.shape[1]
    tall = wa.shape[0]
    hd = meta[2]

    @pl.when(b == 0)
    def _():
        def put(k, ref, first):
            at = jnp.bitwise_xor(hd, k) * part
            w_ref[pl.ds(pl.multiple_of(at, 64), part), 0:width] = ref[first : first + part, :]
            for n in range(2):
                row = pl.multiple_of(at + n * (part // 2), 32)
                w_ref[pl.ds(row, part // 2), width:] = ref[
                    first + part : first + part + part // 2, n * (width // 2) : (n + 1) * (width // 2)
                ]

        put(0, wa, 0)
        put(1, wb, 0)
        put(2, pack, 0)
        put(3, pack, tall)
        last = lambda ref, end: ref[end - 16 : end, :].astype(f32)
        near = last(wa, tall) + last(wb, tall)
        far = last(pack, tall) + last(pack, 2 * tall)
        t = jnp.where(x_of(meta) == core_of(meta), near, far)
        taps[...] = jnp.zeros_like(taps)
        taps[0:3, 0:width] = t[0:3]
        taps[0:3, width:] = t[3:6, 0 : width // 2]
        ext[0:8, :] = jnp.zeros((8, ext.shape[1]), f32)

    slot = slot_of(meta, b)
    step = ext.shape[0] - 8

    def some(n, carry):
        sl = pl.ds(pl.multiple_of(n * step, step), step)
        x = x0[sl, :]
        for k, other in ((1, x1), (2, x2), (3, x3)):
            x = jnp.where(slot == k, other[sl, :], x)
        _, _, h = norm(x.astype(f32), gain[...].astype(f32))
        h_ref[sl, :] = h
        raw = dot(h, w_ref[...]).astype(bf16)
        raw_ref[sl, :] = raw
        rawf = raw.astype(f32)
        ext[8:, :] = rawf
        t = taps[...]
        mixed = t[0:1] * rawf + t[1:2] * ext[7 : 7 + step, :] + t[2:3] * ext[6 : 6 + step, :]
        mix_ref[sl, :] = mixed.astype(bf16)
        ext[0:8, :] = ext[step:, :]
        return carry

    lax.fori_loop(0, rows // step, some, 0)


def qkv_call(meta, x_own, x_nb, x_core, x_cnb, w_mine, w_core, pack, gain):
    rows, width = x_own.shape
    tall = w_mine.shape[0]
    cols = width * 3 // 2
    length = 4 * rows
    blk = lambda n: pl.BlockSpec((rows, n), lambda b, m: (b, 0))
    const = lambda r: pl.BlockSpec((r, cols), lambda b, m: (0, 0))
    return pl.pallas_call(
        qkv_body,
        out_shape=[
            sds((length, width), bf16),
            sds((length, cols), bf16),
            sds((length, cols), bf16),
            sds((width, cols), bf16),
            sds((8, cols), f32),
        ],
        grid_spec=grid_spec(
            (4,),
            [whole((rows, width))] * 4
            + [whole((tall, width))] * 2
            + [whole(pack.shape), whole((1, width))],
            [
                pl.BlockSpec((rows, width), lambda b, m: (slot_of(m, b), 0)),
                blk(cols),
                blk(cols),
                const(width),
                const(8),
            ],
            [pltpu.VMEM((T + 8, cols), f32)],
        ),
        cost_estimate=cost(2 * length * width * cols, 2 * length * (width * 2 + cols * 2)),
        name="qkv",
    )(meta, x_own, x_nb, x_core, x_cnb, w_mine, w_core, pack, gain)


def two_heads(v):
    lane = lax.broadcasted_iota(jnp.int32, v.shape, 1)
    z = jnp.zeros_like(v)
    return jnp.concatenate([jnp.where(lane < HDIM, v, z), jnp.where(lane < HDIM, z, v)], axis=0)


def causal(first, keys, start, queries):
    key = first + lax.broadcasted_iota(jnp.int32, (keys, queries), 0)
    ok = key <= start + lax.broadcasted_iota(jnp.int32, (keys, queries), 1)
    return jnp.concatenate([ok, ok], axis=1)


def upper(v, axis):
    B = v.shape[axis] // 2
    h = B // 2
    if axis == 0:
        return jnp.concatenate([v[h:B], v[B + h :]], axis=0)
    return jnp.concatenate([v[:, h:B], v[:, B + h :]], axis=1)


def with_bias(k_ref, ka, length):
    L = k_ref.shape[0]
    ka[:, :128] = k_ref[...]
    lane = lax.broadcasted_iota(jnp.int32, (L, 128), 1)
    row = lax.broadcasted_iota(jnp.int32, (L, 128), 0)
    pad = jnp.logical_and(lane == 0, row >= length)
    ka[:, 128:] = jnp.where(pad, -1e9, 0.0).astype(bf16)


def biased(q):
    qq = two_heads(q)
    lane = lax.broadcasted_iota(jnp.int32, qq.shape, 1)
    return jnp.concatenate([qq, jnp.where(lane == 0, 1.0, 0.0).astype(bf16)], axis=1)


def att_fwd_body(meta, q_ref, k_ref, v_ref, mine_ref, theirs_ref, lse_ref, ka, vt, sc):
    i = pl.program_id(1)
    B = q_ref.shape[0]

    @pl.when(i == 0)
    def _():
        vt[...] = v_ref[...].T
        with_bias(k_ref, ka, length_of(meta))

    qq = biased(q_ref[...] * bf16(HDIM**-0.5))
    own = lax.rem(i, 2) == core_of(meta)

    def run(ii):
        m = None
        for j in range(ii + 1):
            ks = slice(j * B, j * B + B)
            s = dot(ka[ks, :], qq, NT)
            if j == ii:
                s = jnp.where(causal(0, B, 0, B), s, -1e9)
            sc[ks, :] = s
            mj = jnp.max(s, axis=0, keepdims=True)
            m = mj if m is None else jnp.maximum(m, mj)
        l = jnp.zeros((1, 2 * B), f32)
        acc = [jnp.zeros((HDIM, B), f32)] * 2
        for j in range(ii + 1):
            ks = slice(j * B, j * B + B)
            p = jnp.exp(sc[ks, :] - m)
            l = l + jnp.sum(p, axis=0, keepdims=True)
            pb = p.astype(bf16)
            for h in range(2):
                r = slice(HDIM * h, HDIM * h + HDIM)
                acc[h] = acc[h] + dot(vt[r, ks], pb[:, h * B : h * B + B])
        inv = 1.0 / l
        out = jnp.concatenate([acc[h] * inv[:, h * B : h * B + B] for h in range(2)], axis=0)
        out = out.T.astype(bf16)

        @pl.when(own)
        def _():
            mine_ref[...] = out

        @pl.when(jnp.logical_not(own))
        def _():
            theirs_ref[...] = out

        ls = m + jnp.log(l)
        lse_ref[0] = jnp.concatenate([ls[:, :B], ls[:, B:]], axis=0)

    for ii in range(4):
        pl.when(i == ii)(functools.partial(run, ii))


def half_map(p, i, m):
    return (jnp.bitwise_xor(i // 2, x_of(m)), p)


def att_fwd_call(meta, mix):
    length, cols = mix.shape
    width = cols // 3
    pairs = width // 128
    B = length // 4
    half = pl.BlockSpec((B, 128), half_map)
    return pl.pallas_call(
        att_fwd_body,
        out_shape=[
            sds((length // 2, width), bf16),
            sds((length // 2, width), bf16),
            sds((pairs, 2, length), f32),
        ],
        grid_spec=grid_spec(
            (pairs, 4),
            [
                pl.BlockSpec((B, 128), lambda p, i, m: (i, p)),
                pl.BlockSpec((length, 128), lambda p, i, m: (0, pairs + p)),
                pl.BlockSpec((length, 128), lambda p, i, m: (0, 2 * pairs + p)),
            ],
            [half, half, pl.BlockSpec((1, 2, B), lambda p, i, m: (p, 0, i))],
            [
                pltpu.VMEM((length, 256), bf16),
                pltpu.VMEM((128, length), bf16),
                pltpu.VMEM((length, 2 * B), f32),
            ],
        ),
        cost_estimate=cost(8 * length * length * width, 8 * length * width, 2 * length * length * pairs),
        name="attn_fwd",
    )(meta, mix, mix, mix)


def att_bwd_body(
    p0, aliased, meta, q_ref, k_ref, v_ref, om, ot, dm, dt, lse_ref, rq, rk, rv, taps, *refs
):
    gm_ref, gt_ref, gt, ka, kt, dkt, dvt, dqt, dqs, ext, stage, sem = refs[2:] if aliased else refs
    i = pl.program_id(1)
    B = q_ref.shape[0]
    L = k_ref.shape[0]
    H = B // 2

    @pl.when(i == 0)
    def _():
        kt[...] = k_ref[...].T
        with_bias(k_ref, ka, length_of(meta))

    own = lax.rem(i, 2) == core_of(meta)
    q = q_ref[...] * bf16(HDIM**-0.5)
    o = jnp.where(own, om[...], ot[...])
    do = jnp.where(own, dm[...], dt[...])
    qq, dd = biased(q), two_heads(do)
    qt, dot_ = q.T, do.T
    od = (o.astype(f32) * do.astype(f32)).T
    delta = jnp.concatenate(
        [jnp.sum(od[:HDIM], axis=0, keepdims=True), jnp.sum(od[HDIM:], axis=0, keepdims=True)],
        axis=1,
    )
    ls = lse_ref[0]
    lse = jnp.concatenate([ls[0:1], ls[1:2]], axis=1)

    dqt[...] = jnp.zeros_like(dqt)

    def tile(st, n, lo, diagonal):
        w = B - lo
        ks = pl.ds(pl.multiple_of(st, H), n)
        part = upper if lo else lambda v, axis: v
        s = dot(ka[ks, :], part(qq, 0), NT)
        dp = dot(v_ref[ks, :], part(dd, 0), NT)
        p = jnp.exp(s - part(lse, 1))
        if diagonal:
            p = jnp.where(causal(lo, n, lo, w), p, 0.0)
        ds = (p * (dp - part(delta, 1))).astype(bf16)
        pb = p.astype(bf16)
        for h in range(2):
            r, c = slice(HDIM * h, HDIM * h + HDIM), slice(h * w, h * w + w)
            dqt[r, lo:] += dot(kt[r, ks], ds[:, c])
            a = dot(qt[r, lo:], ds[:, c], NT)
            b = dot(dot_[r, lo:], pb[:, c], NT)
            if diagonal:
                dkt[r, ks] = a
                dvt[r, ks] = b
            else:
                dkt[r, ks] += a
                dvt[r, ks] += b

    lax.fori_loop(0, i, lambda j, c: (tile(j * B, B, 0, False), c)[1], 0)
    tile(i * B, H, 0, True)
    tile(i * B + H, H, H, True)
    dqs[pl.ds(pl.multiple_of(i * B, B), B), :] = dqt[...].T * HDIM**-0.5

    def copies(pair):
        width = gm_ref.shape[1] // 3
        for b in range(L // B):
            to = pl.ds(pl.multiple_of(jnp.bitwise_xor(b // 2, x_of(meta)) * B, B), B)
            for k in range(3):
                col = pl.ds(pl.multiple_of(k * width + (p0 + pair) * 128, 128), 128)
                src = stage.at[k, pl.ds(b * B, B), :]
                yield b, lambda g, to=to, col=col, src=src, k=k: pltpu.make_async_copy(
                    src, g.at[to, col], sem.at[k]
                )

    def send(pair):
        for b, copy in copies(pair):
            own = core_of(meta) == b % 2

            @pl.when(own)
            def _(copy=copy):
                copy(gm_ref).start()

            @pl.when(jnp.logical_not(own))
            def _(copy=copy):
                copy(gt_ref).start()

    def finish(pair):
        for _, copy in copies(pair):
            copy(gm_ref).wait()

    @pl.when(i == pl.num_programs(1) - 1)
    def _():
        pair = pl.program_id(0)
        gt[...] = jnp.zeros_like(gt)
        ext[...] = jnp.zeros_like(ext)

        @pl.when(pair > 0)
        def _():
            finish(pair)

        def back(n, carry):
            blk = L // B - 1 - n
            sl = pl.ds(pl.multiple_of(blk * B, B), B)
            for which, raw in enumerate((rq, rk, rv)):
                col = which * (taps.shape[1] // 3) + (p0 + pl.program_id(0)) * 128
                t = taps[:, pl.ds(pl.multiple_of(col, 128), 128)]
                g = dqs[sl, :] if which == 0 else (dkt, dvt)[which - 1][:, sl].T
                ext[which, B : B + 8, :] = ext[which, 0:8, :]
                ext[which, 0:B, :] = g
                g1, g2 = ext[which, 1 : B + 1, :], ext[which, 2 : B + 2, :]
                stage[which, sl, :] = (t[0:1] * g + t[1:2] * g1 + t[2:3] * g2).astype(bf16)
                r = raw[sl, :].astype(f32)
                for k, gg in enumerate((g, g1, g2)):
                    row = slice(3 * which + k, 3 * which + k + 1)
                    gt[row, :] += jnp.sum(r * gg, axis=0, keepdims=True)
            return carry

        lax.fori_loop(0, L // B, back, 0)
        send(pair)

        @pl.when(pair == pl.num_programs(0) - 1)
        def _():
            finish(pair)


def att_bwd_call(meta, mix, raw, om, ot, dm, dt, lse, taps, p0, count, into=None):
    length, cols = mix.shape
    pairs = cols // 384
    B = length // 4
    half = pl.BlockSpec((B, 128), lambda p, i, m: (jnp.bitwise_xor(i // 2, x_of(m)), p0 + p))
    full = lambda k: pl.BlockSpec((length, 128), lambda p, i, m: (0, k * pairs + p0 + p))
    return pl.pallas_call(
        functools.partial(att_bwd_body, p0, into is not None),
        out_shape=[sds((length // 2, cols), bf16)] * 2 + [sds((16, 128 * count), f32)],
        grid_spec=grid_spec(
            (count, 4),
            [
                pl.BlockSpec((B, 128), lambda p, i, m: (i, p0 + p)),
                full(1),
                full(2),
                half,
                half,
                half,
                half,
                pl.BlockSpec((1, 2, B), lambda p, i, m: (p0 + p, 0, i)),
                full(0),
                full(1),
                full(2),
                whole((8, cols)),
            ]
            + ([] if into is None else [pl.BlockSpec(memory_space=pl.ANY)] * 2),
            [pl.BlockSpec(memory_space=pl.ANY)] * 2 + [pl.BlockSpec((16, 128), lambda p, i, m: (0, p))],
            [
                pltpu.VMEM((length, 256), bf16),
                pltpu.VMEM((128, length), bf16),
                pltpu.VMEM((128, length), f32),
                pltpu.VMEM((128, length), f32),
                pltpu.VMEM((128, B), f32),
                pltpu.VMEM((length, 128), f32),
                pltpu.VMEM((3, B + 8, 128), f32),
                pltpu.VMEM((3, length, 128), bf16),
                pltpu.SemaphoreType.DMA((3,)),
            ],
        ),
        cost_estimate=cost(
            14 * length * length * 128 * count, 20 * length * 128 * count, 2 * length * length * count
        ),
        name="attn_bwd",
        input_output_aliases={} if into is None else {13: 0, 14: 1},
    )(meta, mix, mix, mix, om, ot, dm, dt, lse, raw, raw, raw, taps, *(into or ()))


T = 256


def valid_rows(meta, i, rows):
    per = rows // T
    block = jnp.where(i < per, meta[2], jnp.bitwise_xor(meta[2], 2))
    start = block * rows + lax.rem(i, per) * T
    return start + lax.broadcasted_iota(jnp.int32, (T, 1), 0) < length_of(meta)


def ffn_body(
    meta, xo, xx, co, cx, am, at, gain, wo_o, wo_c, pack,
    u_o, d_o, f_c, n0, n1, n2, n3, c0, c1, c2, c3,
    oo, ox, dm, dt, gg, dmid, gu0, gu1, gu2, gu3, gd0, gd1, gd2, gd3,
    wo, wus, wds, mid, h_s, g_s, fo, dh, act, du, stu, std, sto, gacc, sw, so, sg, sd, st,
):
    rows, width = xo.shape
    part = wo_o.shape[0]
    half = 2 * part
    n = 2 * rows // T
    per = rows // T
    copies = []
    for k, src in ((0, wo_o), (1, wo_c), (2, pack.at[pl.ds(rows, part), :]), (3, pack.at[pl.ds(rows + part, part), :])):
        shard = jnp.bitwise_xor(meta[2], k)
        row = jnp.where(shard // 2 == core_of(meta), 0, half) + lax.rem(shard, 2) * part
        cp = pltpu.make_async_copy(src, wo.at[pl.ds(pl.multiple_of(row, 64), part), :], so.at[k])
        cp.start()
        copies.append(cp)
    for k, pair in ((0, (f_c.at[0], f_c.at[1])), (2, (u_o, d_o))):
        for n_, src in enumerate(pair):
            pltpu.make_async_copy(src, (wus, wds)[n_].at[k], sw.at[k, n_]).start()
    for k, quarters in ((1, (c0, c1, c2, c3)), (3, (n0, n1, n2, n3))):
        for q_, src in enumerate(quarters):
            count = src.shape[1]
            to = pl.ds(pl.multiple_of(jnp.bitwise_xor(meta[3], q_) * count, 64), count)
            for n_, dst in enumerate((wus, wds)):
                pltpu.make_async_copy(src.at[n_], dst.at[k, to, :], sw.at[k, n_]).start()
    for cp in copies:
        cp.wait()
    gn = gain[...].astype(f32)

    def first_rows(i, carry):
        sl = pl.ds(pl.multiple_of(i * T, T), T)
        src = pl.ds(pl.multiple_of(lax.rem(i, per) * T, T), T)
        own = i < per
        x = jnp.where(own, xo[src, :], xx[src, :]).astype(f32)
        a = jnp.concatenate([am[sl, :], at[sl, :]], axis=1)
        m = x + dot(a, wo[...])
        mid[sl, :] = m
        fo[sl, :] = m
        h_s[sl, :] = norm(m, gn)[2]
        ct = jnp.where(own, co[src, :], cx[src, :])
        g_s[sl, :] = jnp.where(valid_rows(meta, i, rows), ct, jnp.zeros_like(ct))
        dh[sl, :] = jnp.zeros((T, width), f32)
        return carry

    lax.fori_loop(0, n, first_rows, 0)

    R = 512
    C = 768

    gus, gds = (gu0, gu1, gu2, gu3), (gd0, gd1, gd2, gd3)

    def stores(n_, slot):
        return [
            pltpu.make_async_copy(stu.at[slot], gus[n_], sg.at[slot, 0]),
            pltpu.make_async_copy(std.at[slot], gds[n_].at[pl.ds(0, width), :], sg.at[slot, 1]),
        ]

    def shard(k, carry):
        for cp in (
            pltpu.make_async_copy(u_o, wus.at[k], sw.at[k, 0]),
            pltpu.make_async_copy(d_o, wds.at[k], sw.at[k, 1]),
        ):
            cp.wait()

        def rows_step(t, c2):
            sl = pl.ds(pl.multiple_of(t * R, R), R)
            h, g = h_s[sl, :], g_s[sl, :]
            r = jnp.maximum(dot(h, wus[k]), 0.0)
            a = (r * r).astype(bf16)
            d = (dot(g, wds[k], NT) * 2.0 * r).astype(bf16)
            act[sl, :] = a
            du[sl, :] = d
            fo[sl, :] += dot(a, wds[k])
            dh[sl, :] += dot(d, wus[k], NT)
            return c2

        lax.fori_loop(0, 2 * rows // R, rows_step, 0)
        slot = lax.rem(k, 2)

        @pl.when(k >= 2)
        def _():
            for cp in stores(0, slot):
                cp.wait()

        def cols_step(t, c2):
            sl = pl.ds(pl.multiple_of(t * C, C), C)
            stu[slot, :, sl] = dot(h_s[...], du[:, sl], TN).astype(bf16)
            std[slot, sl, :] = dot(act[:, sl], g_s[...], TN).astype(bf16)
            return c2

        lax.fori_loop(0, width // C, cols_step, 0)
        for n_ in range(4):

            @pl.when(k == n_)
            def _(n_=n_):
                for cp in stores(n_, n_ % 2):
                    cp.start()

        return carry

    lax.fori_loop(0, 4, shard, 0)
    gg[...] = jnp.zeros_like(gg)

    def last_rows(i, carry):
        sl = pl.ds(pl.multiple_of(i * T, T), T)
        dst = pl.ds(pl.multiple_of(lax.rem(i, per) * T, T), T)
        ok = valid_rows(meta, i, rows)
        m = mid[sl, :]
        out = jnp.where(ok, fo[sl, :], 0.0)

        fo[sl, :] = out

        @pl.when(i < per)
        def _():
            own = oo.at[meta[2] // 2, dst, :]
            pltpu.make_async_copy(fo.at[sl, :], own, sd.at[1]).start()

        @pl.when(i >= per)
        def _():
            ox[dst, :] = out.astype(bf16)

        nm, inv, _ = norm(m, gn)
        d = dh[sl, :]
        dn = d * gn
        r = g_s[sl, :].astype(f32) + inv * (dn - nm * jnp.mean(dn * nm, axis=-1, keepdims=True))
        mid[sl, :] = r
        pltpu.make_async_copy(mid.at[sl, :], dmid.at[sl, :], sd.at[0]).start()
        db = r.astype(bf16)
        du[sl, :] = db
        da = dot(db, wo[...], NT).astype(bf16)
        dm[sl, :] = da[:, :half]
        dt[sl, :] = da[:, half:]
        gg[...] += jnp.sum(d * nm, axis=0, keepdims=True)
        return carry

    lax.fori_loop(0, n, last_rows, 0)
    gacc[0:half, :] = dot(am[...], du[...], TN)
    gacc[half:, :] = dot(at[...], du[...], TN)
    outs = [
        pltpu.make_async_copy(mid, dmid, sd.at[0]),
        pltpu.make_async_copy(fo.at[pl.ds(0, rows), :], oo.at[meta[2] // 2], sd.at[1]),
    ]
    for k, k_ in enumerate((1, 3, 0, 2)):
        shard_ = jnp.bitwise_xor(meta[2], k_)
        row = jnp.where(shard_ // 2 == core_of(meta), 0, half) + lax.rem(shard_, 2) * part
        sto[k] = gacc[pl.ds(pl.multiple_of(row, 64), part), :].astype(bf16)
        cp = pltpu.make_async_copy(sto.at[k], gds[k].at[pl.ds(width, part), :], st.at[k])
        cp.start()
        outs.append(cp)
    for slot in range(2):
        outs.extend(stores(2 + slot, slot))
    for cp in outs:
        cp.wait()


def ffn_call(meta, xo, xx, co, cx, am, at, gain, wos, ffs):
    rows, width = xo.shape
    half = am.shape[1]
    part = half // 2
    hid = ffs[0].shape[1]
    hbm = pl.BlockSpec(memory_space=pl.ANY)
    vm = lambda *shape: whole(shape)
    all_rows = 2 * rows
    return pl.pallas_call(
        ffn_body,
        out_shape=[
            sds((2, rows, width), f32),
            sds((rows, width), bf16),
            sds((all_rows, half), bf16),
            sds((all_rows, half), bf16),
            sds((1, width), f32),
            sds((all_rows, width), f32),
        ]
        + [sds((width, hid), bf16)] * 4
        + [sds((hid + part, width), bf16)] * 4,
        grid_spec=grid_spec(
            (1,),
            [vm(rows, width)] * 4 + [vm(all_rows, half)] * 2 + [vm(1, width)] + [hbm] * 14,
            [
                hbm,
                vm(rows, width),
                vm(all_rows, half),
                vm(all_rows, half),
                vm(1, width),
            ]
            + [hbm] * 9,
            [
                pltpu.VMEM((width, width), bf16),
                pltpu.VMEM((4, width, hid), bf16),
                pltpu.VMEM((4, hid, width), bf16),
                pltpu.VMEM((all_rows, width), f32),
                pltpu.VMEM((all_rows, width), bf16),
                pltpu.VMEM((all_rows, width), bf16),
                pltpu.VMEM((all_rows, width), f32),
                pltpu.VMEM((all_rows, width), f32),
                pltpu.VMEM((all_rows, hid), bf16),
                pltpu.VMEM((all_rows, hid), bf16),
                pltpu.VMEM((2, width, hid), bf16),
                pltpu.VMEM((2, hid, width), bf16),
                pltpu.VMEM((4, part, width), bf16),
                pltpu.VMEM((width, width), f32),
                pltpu.SemaphoreType.DMA((4, 2)),
                pltpu.SemaphoreType.DMA((4,)),
                pltpu.SemaphoreType.DMA((2, 2)),
                pltpu.SemaphoreType.DMA((2,)),
                pltpu.SemaphoreType.DMA((4,)),
            ],
        ),
        cost_estimate=cost(
            48 * all_rows * width * hid + 6 * all_rows * width * width, 40 * all_rows * width
        ),
        compiler_params=pltpu.CompilerParams(vmem_limit_bytes=62 * 2**20),
        name="ffn",
    )(meta, xo, xx, co, cx, am, at, gain, *wos, *ffs)


def projg_body(meta, h, dm, dt, keep, far, send, acc):
    rows = dm.shape[0]
    acc[...] = dot(h[0:rows, :], dm[...], TN) + dot(h[rows:, :], dt[...], TN)
    part = keep.shape[0]
    for ref, k, row in ((keep, 0, 0), (far, 2, 0), (send, 1, 0), (send, 3, part)):
        at = jnp.bitwise_xor(meta[2], k)
        ref[row : row + part, :] = acc[pl.ds(pl.multiple_of(at * part, 64), part), :].astype(bf16)


def projg_call(meta, h, dm, dt):
    length, width = h.shape
    cols = dm.shape[1]
    step = cols // 3
    d = pl.BlockSpec((length // 2, step), lambda j, m: (0, j))
    g = lambda rows: pl.BlockSpec((rows, step), lambda j, m: (0, j))
    part = width // 4
    return pl.pallas_call(
        projg_body,
        out_shape=[sds((rows, cols), bf16) for rows in (part, part, 2 * part)],
        grid_spec=grid_spec(
            (3,),
            [whole((length, width)), d, d],
            [g(part), g(part), g(2 * part)],
            [pltpu.VMEM((width, step), f32)],
        ),
        cost_estimate=cost(length, length),
        name="projg",
    )(meta, h, dm, dt)


def last_body(meta, xo, xx, dm, dt, wm, wt, dmid, gain, go, gx, gg):
    i = pl.program_id(0)
    per = pl.num_programs(0) // 2
    first = i < per
    x = jnp.where(first, xo[...], xx[...]).astype(f32)
    gn = gain[...].astype(f32)
    n, inv, _ = norm(x, gn)
    dh = dot(dm[...], wm[...], NT) + dot(dt[...], wt[...], NT)
    dn = dh * gn
    out = dmid[...] + inv * (dn - n * jnp.mean(dn * n, axis=-1, keepdims=True))

    @pl.when(first)
    def _():
        go[0] = out

    @pl.when(jnp.logical_not(first))
    def _():
        gx[...] = out.astype(bf16)

    ps = jnp.sum(dh * n, axis=0, keepdims=True)

    @pl.when(i == 0)
    def _():
        gg[...] = ps

    @pl.when(i > 0)
    def _():
        gg[...] += ps


def own_map(per):
    return lambda i, m: (jnp.minimum(i, per - 1), 0)


def nb_map(per):
    return lambda i, m: (jnp.maximum(i - per, 0), 0)


def last_call(meta, xo, xx, dm, dt, wm, wt, dmid, gain):
    rows, width = xo.shape
    cols = dm.shape[1]
    per = rows // T
    fst, snd = pl.BlockSpec((T, width), own_map(per)), pl.BlockSpec((T, width), nb_map(per))
    blk = lambda n: pl.BlockSpec((T, n), lambda i, m: (i, 0))
    return pl.pallas_call(
        last_body,
        out_shape=[sds((2, rows, width), f32), sds((rows, width), bf16), sds((1, width), f32)],
        grid_spec=grid_spec(
            (2 * per,),
            [fst, snd, blk(cols), blk(cols)]
            + [whole((width, cols))] * 2
            + [blk(width), whole((1, width))],
            [
                pl.BlockSpec((1, T, width), lambda i, m: (x_of(m), jnp.minimum(i, per - 1), 0)),
                snd,
                pl.BlockSpec((1, width), lambda i, m: (0, 0)),
            ],
        ),
        cost_estimate=cost(rows, rows),
        name="last",
    )(meta, xo, xx, dm, dt, wm, wt, dmid, gain)


def flip(size, bit):
    return [(i, i ^ bit) for i in range(size)]


def core_swap(v):
    return lax.ppermute(v, "head", CORE)


def x_swap(v):
    return lax.ppermute(v, "head", XNB)


def after(v, *deps):
    return lax.optimization_barrier((v, *deps))[0]


def halve(terms, index, count):
    rows = terms[0].shape[0] // count
    piece = lambda t, k: lax.dynamic_slice_in_dim(t, jnp.bitwise_xor(index, k) * rows, rows, 0)
    total = lambda k: sum(piece(t, k).astype(f32) for t in terms)
    return [total(k).astype(bf16) for k in range(1, count)], total(0)


def strides(dp):
    out = [1]
    while 2 * out[-1] < dp:
        out.append(2 * out[-1])
    return out


def side(stride):
    return lax.axis_index("dp") // stride % 2


def swap(v, stride, dp):
    return lax.ppermute(v, "dp", flip(dp, stride))


def rows_as(got, vs):
    out, row = [], 0
    for v in vs:
        out.append(got[row : row + v.shape[0]])
        row += v.shape[0]
    return out


def swap_both(vs, stride, dp):
    return rows_as(swap(jnp.concatenate(vs, axis=0), stride, dp), vs)


def scatter(sums, stride, dp):
    halves = [halve(terms, side(stride), 2) for terms in sums]
    send = jnp.concatenate([h[0][0] for h in halves], axis=0)
    got = swap(send, stride, dp)
    out, row = [], 0
    for (part,), keep in halves:
        out.append([keep, got[row : row + part.shape[0]]])
        row += part.shape[0]
    return out, send


def join(mine, got, stride):
    upper = side(stride) == 1
    return jnp.concatenate([jnp.where(upper, got, mine), jnp.where(upper, mine, got)], axis=0)


def total(terms):
    return sum(t.astype(f32) for t in terms)


def local(dp, inputs, lengths, w_query, w_key, w_value, w_out, w_up, w_down, conv_taps, gain_attn, gain_ff, cotangent):
    hd = lax.axis_index("head")
    x, c, y = hd // 2, hd % 2, lax.axis_index("dp") % 2
    q = lax.axis_index("dp") % 4
    width = inputs.shape[2]
    part = w_query.shape[0]
    half = 2 * part
    pick = lambda v, k: lax.dynamic_index_in_dim(v, k, 0, keepdims=False)
    y_swap = lambda v: lax.ppermute(v, "dp", flip(dp, 1))
    order = lambda own, nb: lax.dynamic_update_slice_in_dim(own, nb[None].astype(f32), 1 - x, 0)
    meta = jnp.concatenate([lengths, jnp.stack([hd, q])]).astype(jnp.int32)
    gain1, gain2 = gain_attn.reshape(1, width), gain_ff.reshape(1, width)

    mask = (jnp.arange(2) == c)[None, None, :, None]
    tap_rows = jnp.where(mask, conv_taps.transpose(1, 0, 2)[:, :, None, :], 0).reshape(3, 3 * half)
    tap_rows = jnp.concatenate([tap_rows[:, :width], jnp.pad(tap_rows[:, width:], ((0, 0), (0, half)))], axis=0)
    tap_rows = jnp.pad(tap_rows, ((0, 10), (0, 0)))

    def packed(k):
        cut = lambda w: lax.dynamic_slice_in_dim(w, k * half, half, 1)
        fold = cut(w_value)
        return jnp.concatenate(
            [
                jnp.concatenate([cut(w_query), cut(w_key)], axis=1),
                jnp.concatenate([fold[: part // 2], fold[part // 2 :]], axis=1),
                tap_rows,
            ],
            axis=0,
        )

    w_core = core_swap(packed(1 - c))
    w_mine = packed(c)
    x_own = pick(inputs, x)
    rows = x_own.shape[0]
    x_nb = x_swap(pick(inputs, 1 - x))
    pack = x_swap(jnp.concatenate([w_mine, w_core], axis=0))
    x_core = core_swap(x_own)
    count = width // 4
    quarter = lambda w: lax.dynamic_slice_in_dim(w, q * count, count, 0)
    wo_c = core_swap(w_out)
    c_own = pick(cotangent, x)
    ff_src = jnp.stack([quarter(w_up), quarter(w_down)])
    ff_own = jnp.stack([w_up, w_down])
    pack2 = jnp.concatenate([pick(cotangent, 1 - x), w_out, wo_c], axis=0)
    x_nb, ff_src, ff_own, pack2, c_own, meta, x_core, pack = lax.optimization_barrier(
        (x_nb, ff_src, ff_own, pack2, c_own, meta, x_core, pack)
    )
    x_cnb = core_swap(x_nb)
    h1, raw, mix, w_full, taps = qkv_call(meta, x_own, x_nb, x_core, x_cnb, w_mine, w_core, pack, gain1)

    ff_first, pack2 = x_swap(ff_src), x_swap(pack2)
    ff_c = core_swap(ff_own)
    src = after(ff_first, mix)
    ff_n = [swap(src, k, dp) for k in (1, 2, 3)]
    a_mine, a_send, lse = att_fwd_call(meta, after(mix, src, ff_c))
    a_got = core_swap(a_send)
    w_other = core_swap(w_full)
    *ff_n, pack2 = lax.optimization_barrier((*ff_n, pack2, a_mine))[:-1]
    ff_n = [src, *ff_n]
    ff_cn = [core_swap(v) for v in ff_n]
    out_own, out_nb, d_mine, d_send, gg2, dmid, *gw = ffn_call(
        meta, x_own, x_nb, c_own, pack2, a_mine, a_got, after(gain2, w_other),
        (w_out, wo_c, pack2),
        (w_up, w_down, ff_c, *ff_n, *ff_cn),
    )
    d_got = core_swap(d_send)

    _, *rest = strides(dp)
    un, dn, do, uo = [core_swap(gw[k]) for k in (1, 5, 4, 0)]
    nu = total((gw[3], un)).astype(bf16)
    xu = x_swap(nu)
    (dn_send,), dn_keep = halve((gw[7], dn), y, 2)
    (do_send,), do_keep = halve((gw[6], do), y, 2)
    yn, yo = y_swap(dn_send), y_swap(do_send)
    out_x = x_swap(after(out_nb, nu))
    pairs = width // 256
    bwd = lambda m, p, n, into: att_bwd_call(
        meta, m, raw, a_mine, a_send, d_mine, d_got, lse, taps, p, n, into
    )
    *dall, gt_a = bwd(after(mix, nu, dn_send, do_send), 0, pairs - 1, None)
    xu, yn, yo, out_x = lax.optimization_barrier((xu, yn, yo, out_x, gt_a))[:4]
    (u_send,), u_keep = halve((gw[2], uo, xu), y, 2)
    nd = total((dn_keep, yn)).astype(bf16)
    yu, xd = y_swap(u_send), x_swap(nd)
    p_mine, p_theirs, gt_b = bwd(after(mix, u_send, nd), pairs - 1, 1, dall)
    p_got = core_swap(p_theirs)
    gt = jnp.concatenate([gt_a, gt_b], axis=1)
    yu, xd = lax.optimization_barrier((yu, xd, gt_b))[:2]
    sums, sent = scatter([[u_keep, yu], [do_keep, yo, xd]], rest[0], dp)
    keep, far, send = projg_call(meta, after(h1, sent), p_mine, p_theirs)
    far = x_swap(far)
    *flat, far = lax.optimization_barrier((*sums[0], *sums[1], far))
    sums, sent = scatter([flat[:2], flat[2:]], rest[1], dp)
    got = core_swap(after(send, sent))
    far2 = x_swap(got[part:])
    gi_own, gi_nb, gg1 = last_call(
        meta, x_own, x_nb, p_mine, p_got, w_full, w_other, after(dmid, sent, far), gain1
    )
    *flat, gt, gg1 = lax.optimization_barrier((*sums[0], *sums[1], gt, x_swap(core_swap(gg1))))
    sums = [flat[:2], flat[2:]]
    for stride in rest[2:]:
        sums, _ = scatter(sums, stride, dp)
    vs = [total(t).astype(bf16) for t in sums]
    far, far2 = lax.optimization_barrier((far, far2, *vs))[:2]
    ga, gb = keep.astype(f32) + far.astype(f32), got[:part].astype(f32) + far2.astype(f32)
    g_send, g_keep = jnp.where(y == 0, gb, ga).astype(bf16), jnp.where(y == 0, ga, gb)
    pt = [g_keep, y_swap(g_send)]
    gi_got = x_swap(after(gi_nb, g_send))
    for stride in reversed(rest[1:]):
        cat = jnp.concatenate(vs, axis=0)
        first_cat = cat if stride == rest[-1] else first_cat
        got_v = swap(cat, stride, dp)
        vs = [join(v, g, stride) for v, g in zip(vs, rows_as(got_v, vs))]
    (pt,), sent = scatter([pt], rest[0], dp)
    packed_vs = jnp.concatenate(vs, axis=0)
    near_got = swap(packed_vs, rest[0], dp)
    across = rows_as(y_swap(packed_vs), vs)
    for stride in rest[1:]:
        (pt,), _ = scatter([pt], stride, dp)
    others, also = rows_as(near_got, vs), rows_as(y_swap(near_got), vs)
    ps = after(total(pt).astype(bf16), near_got)
    for stride in reversed(rest):
        ps = join(ps, swap(ps, stride, dp), stride)
    ps_got = y_swap(ps)
    whole_of = lambda k: join(
        join(vs[k], others[k], rest[0]), join(across[k], also[k], rest[0]), 1
    ).astype(f32)
    grad_up, gd_all = whole_of(0), whole_of(1)
    grad_down, grad_out = gd_all[: w_down.shape[0]], gd_all[w_down.shape[0] :]
    lo, hi = jnp.where(y == c, ps, ps_got), jnp.where(y == c, ps_got, ps)
    third = lambda v, w: v[:, w * half : w * half + half]
    grads = [jnp.concatenate([third(lo, w), third(hi, w)], axis=1).astype(f32) for w in range(3)]

    gt = gt[:9].reshape(9, 2, part).transpose(1, 0, 2)
    gt = jnp.where(jnp.arange(2)[:, None, None, None] == c, gt[None], 0.0).reshape(4, 9, part)
    gains = jnp.concatenate([gg1, gg2], axis=0).reshape(2, 4, part).transpose(1, 0, 2)
    small = jnp.concatenate([gt, gains, jnp.zeros((4, 5, part), f32)], axis=1)
    small = after(small, first_cat)
    small = jnp.broadcast_to(small[:, None], (4, dp, 16, part)).reshape(4 * dp, 16, part)
    small = jnp.sum(lax.all_to_all(small, ("head", "dp"), 0, 0, tiled=True), axis=0)
    output = order(after(out_own, g_send), out_x)
    grad_input = order(after(gi_own, ps), gi_got)
    return (
        output,
        grad_input,
        *grads,
        grad_out,
        grad_up,
        grad_down,
        small[:9].reshape(3, 3, part),
        small[9],
        small[10],
    )


def solution(mesh):
    placed = (
        P("dp", "head", None),
        P("dp"),
        P("head", None),
        P("head", None),
        P("head", None),
        P("head", None),
        P(None, "head"),
        P("head", None),
        P(None, None, "head"),
        P(),
        P(),
        P("dp", "head", None),
    )
    return jax.shard_map(
        functools.partial(local, mesh.shape["dp"]),
        mesh=mesh,
        in_specs=placed,
        out_specs=(
            P("dp", "head", None),
            P("dp", "head", None),
            P("head", None),
            P("head", None),
            P("head", None),
            P("head", None),
            P(None, "head"),
            P("head", None),
            P(None, None, "head"),
            P("head"),
            P("head"),
        ),
        check_vma=False,
    )
```

```python
import functools

import jax
import jax.numpy as jnp
from jax import lax
from jax.experimental import pallas as pl
from jax.experimental.pallas import tpu as pltpu
from jax.sharding import PartitionSpec as P

HDIM = 64
EPS = 1e-06
bf16 = jnp.bfloat16
f32 = jnp.float32

NN = (((1,), (0,)), ((), ()))
NT = (((1,), (1,)), ((), ()))
TN = (((0,), (0,)), ((), ()))

CORE = [(0, 1), (1, 0), (2, 3), (3, 2)]
XNB = [(0, 2), (2, 0), (1, 3), (3, 1)]


def dot(a, b, dims=NN):
    return lax.dot_general(a, b, dims, preferred_element_type=f32)


def cost(flops, nbytes, trans=0):
    return pl.CostEstimate(flops=int(flops), bytes_accessed=int(nbytes), transcendentals=int(trans))


def sds(shape, dtype):
    return jax.ShapeDtypeStruct(shape, dtype)


def whole(shape):
    zeros = (0,) * len(shape)
    return pl.BlockSpec(shape, lambda *_: zeros, pipeline_mode=pl.Buffered(1))


def grid_spec(grid, ins, outs, scratch=()):
    return pltpu.PrefetchScalarGridSpec(
        num_scalar_prefetch=1, grid=grid, in_specs=ins, out_specs=outs, scratch_shapes=scratch
    )


def length_of(m):
    return m[m[2] // 2]


def x_of(m):
    return m[2] // 2


def core_of(m):
    return lax.rem(m[2], 2)


def slot_of(m, b):
    v = jnp.bitwise_xor(m[2], b)
    return lax.rem(v, 2) * 2 + v // 2


def norm(x, gain):
    inv = lax.rsqrt(jnp.mean(x * x, axis=-1, keepdims=True) + EPS)
    n = x * inv
    return n, inv, (n * gain).astype(bf16)


def qkv_body(meta, x0, x1, x2, x3, wa, wb, pack, gain, h_ref, raw_ref, mix_ref, w_ref, taps, ext):
    b = pl.program_id(0)
    rows = x0.shape[0]
    part = w_ref.shape[0] // 4
    width = x0.shape[1]
    tall = wa.shape[0]
    hd = meta[2]

    @pl.when(b == 0)
    def _():
        def put(k, ref, first):
            at = jnp.bitwise_xor(hd, k) * part
            w_ref[pl.ds(pl.multiple_of(at, 64), part), 0:width] = ref[first : first + part, :]
            for n in range(2):
                row = pl.multiple_of(at + n * (part // 2), 32)
                w_ref[pl.ds(row, part // 2), width:] = ref[
                    first + part : first + part + part // 2, n * (width // 2) : (n + 1) * (width // 2)
                ]

        put(0, wa, 0)
        put(1, wb, 0)
        put(2, pack, 0)
        put(3, pack, tall)
        last = lambda ref, end: ref[end - 16 : end, :].astype(f32)
        near = last(wa, tall) + last(wb, tall)
        far = last(pack, tall) + last(pack, 2 * tall)
        t = jnp.where(x_of(meta) == core_of(meta), near, far)
        taps[...] = jnp.zeros_like(taps)
        taps[0:3, 0:width] = t[0:3]
        taps[0:3, width:] = t[3:6, 0 : width // 2]
        ext[0:8, :] = jnp.zeros((8, ext.shape[1]), f32)

    slot = slot_of(meta, b)
    step = ext.shape[0] - 8

    def some(n, carry):
        sl = pl.ds(pl.multiple_of(n * step, step), step)
        x = x0[sl, :]
        for k, other in ((1, x1), (2, x2), (3, x3)):
            x = jnp.where(slot == k, other[sl, :], x)
        _, _, h = norm(x.astype(f32), gain[...].astype(f32))
        h_ref[sl, :] = h
        raw = dot(h, w_ref[...]).astype(bf16)
        raw_ref[sl, :] = raw
        rawf = raw.astype(f32)
        ext[8:, :] = rawf
        t = taps[...]
        mixed = t[0:1] * rawf + t[1:2] * ext[7 : 7 + step, :] + t[2:3] * ext[6 : 6 + step, :]
        mix_ref[sl, :] = mixed.astype(bf16)
        ext[0:8, :] = ext[step:, :]
        return carry

    lax.fori_loop(0, rows // step, some, 0)


def qkv_call(meta, x_own, x_nb, x_core, x_cnb, w_mine, w_core, pack, gain):
    rows, width = x_own.shape
    tall = w_mine.shape[0]
    cols = width * 3 // 2
    length = 4 * rows
    blk = lambda n: pl.BlockSpec((rows, n), lambda b, m: (b, 0))
    const = lambda r: pl.BlockSpec((r, cols), lambda b, m: (0, 0))
    return pl.pallas_call(
        qkv_body,
        out_shape=[
            sds((length, width), bf16),
            sds((length, cols), bf16),
            sds((length, cols), bf16),
            sds((width, cols), bf16),
            sds((8, cols), f32),
        ],
        grid_spec=grid_spec(
            (4,),
            [whole((rows, width))] * 4
            + [whole((tall, width))] * 2
            + [whole(pack.shape), whole((1, width))],
            [
                pl.BlockSpec((rows, width), lambda b, m: (slot_of(m, b), 0)),
                blk(cols),
                blk(cols),
                const(width),
                const(8),
            ],
            [pltpu.VMEM((T + 8, cols), f32)],
        ),
        cost_estimate=cost(2 * length * width * cols, 2 * length * (width * 2 + cols * 2)),
        name="qkv",
    )(meta, x_own, x_nb, x_core, x_cnb, w_mine, w_core, pack, gain)


def two_heads(v):
    lane = lax.broadcasted_iota(jnp.int32, v.shape, 1)
    z = jnp.zeros_like(v)
    return jnp.concatenate([jnp.where(lane < HDIM, v, z), jnp.where(lane < HDIM, z, v)], axis=0)


def causal(first, keys, start, queries):
    key = first + lax.broadcasted_iota(jnp.int32, (keys, queries), 0)
    ok = key <= start + lax.broadcasted_iota(jnp.int32, (keys, queries), 1)
    return jnp.concatenate([ok, ok], axis=1)


def upper(v, axis):
    B = v.shape[axis] // 2
    h = B // 2
    if axis == 0:
        return jnp.concatenate([v[h:B], v[B + h :]], axis=0)
    return jnp.concatenate([v[:, h:B], v[:, B + h :]], axis=1)


def with_bias(k_ref, ka, length):
    L = k_ref.shape[0]
    ka[:, :128] = k_ref[...]
    lane = lax.broadcasted_iota(jnp.int32, (L, 128), 1)
    row = lax.broadcasted_iota(jnp.int32, (L, 128), 0)
    pad = jnp.logical_and(lane == 0, row >= length)
    ka[:, 128:] = jnp.where(pad, -1e9, 0.0).astype(bf16)


def biased(q):
    qq = two_heads(q)
    lane = lax.broadcasted_iota(jnp.int32, qq.shape, 1)
    return jnp.concatenate([qq, jnp.where(lane == 0, 1.0, 0.0).astype(bf16)], axis=1)


def att_fwd_body(meta, q_ref, k_ref, v_ref, mine_ref, theirs_ref, lse_ref, ka, vt, sc):
    i = pl.program_id(1)
    B = q_ref.shape[0]

    @pl.when(i == 0)
    def _():
        vt[...] = v_ref[...].T
        with_bias(k_ref, ka, length_of(meta))

    qq = biased(q_ref[...] * bf16(HDIM**-0.5))
    own = lax.rem(i, 2) == core_of(meta)

    def run(ii):
        m = None
        for j in range(ii + 1):
            ks = slice(j * B, j * B + B)
            s = dot(ka[ks, :], qq, NT)
            if j == ii:
                s = jnp.where(causal(0, B, 0, B), s, -1e9)
            sc[ks, :] = s
            mj = jnp.max(s, axis=0, keepdims=True)
            m = mj if m is None else jnp.maximum(m, mj)
        l = jnp.zeros((1, 2 * B), f32)
        acc = [jnp.zeros((HDIM, B), f32)] * 2
        for j in range(ii + 1):
            ks = slice(j * B, j * B + B)
            p = jnp.exp(sc[ks, :] - m)
            l = l + jnp.sum(p, axis=0, keepdims=True)
            pb = p.astype(bf16)
            for h in range(2):
                r = slice(HDIM * h, HDIM * h + HDIM)
                acc[h] = acc[h] + dot(vt[r, ks], pb[:, h * B : h * B + B])
        inv = 1.0 / l
        out = jnp.concatenate([acc[h] * inv[:, h * B : h * B + B] for h in range(2)], axis=0)
        out = out.T.astype(bf16)

        @pl.when(own)
        def _():
            mine_ref[...] = out

        @pl.when(jnp.logical_not(own))
        def _():
            theirs_ref[...] = out

        ls = m + jnp.log(l)
        lse_ref[0] = jnp.concatenate([ls[:, :B], ls[:, B:]], axis=0)

    for ii in range(4):
        pl.when(i == ii)(functools.partial(run, ii))


def half_map(p, i, m):
    return (jnp.bitwise_xor(i // 2, x_of(m)), p)


def att_fwd_call(meta, mix):
    length, cols = mix.shape
    width = cols // 3
    pairs = width // 128
    B = length // 4
    half = pl.BlockSpec((B, 128), half_map)
    return pl.pallas_call(
        att_fwd_body,
        out_shape=[
            sds((length // 2, width), bf16),
            sds((length // 2, width), bf16),
            sds((pairs, 2, length), f32),
        ],
        grid_spec=grid_spec(
            (pairs, 4),
            [
                pl.BlockSpec((B, 128), lambda p, i, m: (i, p)),
                pl.BlockSpec((length, 128), lambda p, i, m: (0, pairs + p)),
                pl.BlockSpec((length, 128), lambda p, i, m: (0, 2 * pairs + p)),
            ],
            [half, half, pl.BlockSpec((1, 2, B), lambda p, i, m: (p, 0, i))],
            [
                pltpu.VMEM((length, 256), bf16),
                pltpu.VMEM((128, length), bf16),
                pltpu.VMEM((length, 2 * B), f32),
            ],
        ),
        cost_estimate=cost(8 * length * length * width, 8 * length * width, 2 * length * length * pairs),
        name="attn_fwd",
    )(meta, mix, mix, mix)


def att_bwd_body(
    p0, aliased, meta, q_ref, k_ref, v_ref, om, ot, dm, dt, lse_ref, rq, rk, rv, taps, *refs
):
    gm_ref, gt_ref, gt, ka, kt, dkt, dvt, dqt, dqs, ext, stage, sem = refs[2:] if aliased else refs
    i = pl.program_id(1)
    B = q_ref.shape[0]
    L = k_ref.shape[0]
    H = B // 2

    @pl.when(i == 0)
    def _():
        kt[...] = k_ref[...].T
        with_bias(k_ref, ka, length_of(meta))

    own = lax.rem(i, 2) == core_of(meta)
    q = q_ref[...] * bf16(HDIM**-0.5)
    o = jnp.where(own, om[...], ot[...])
    do = jnp.where(own, dm[...], dt[...])
    qq, dd = biased(q), two_heads(do)
    qt, dot_ = q.T, do.T
    od = (o.astype(f32) * do.astype(f32)).T
    delta = jnp.concatenate(
        [jnp.sum(od[:HDIM], axis=0, keepdims=True), jnp.sum(od[HDIM:], axis=0, keepdims=True)],
        axis=1,
    )
    ls = lse_ref[0]
    lse = jnp.concatenate([ls[0:1], ls[1:2]], axis=1)

    dqt[...] = jnp.zeros_like(dqt)

    def tile(st, n, lo, diagonal):
        w = B - lo
        ks = pl.ds(pl.multiple_of(st, H), n)
        part = upper if lo else lambda v, axis: v
        s = dot(ka[ks, :], part(qq, 0), NT)
        dp = dot(v_ref[ks, :], part(dd, 0), NT)
        p = jnp.exp(s - part(lse, 1))
        if diagonal:
            p = jnp.where(causal(lo, n, lo, w), p, 0.0)
        ds = (p * (dp - part(delta, 1))).astype(bf16)
        pb = p.astype(bf16)
        for h in range(2):
            r, c = slice(HDIM * h, HDIM * h + HDIM), slice(h * w, h * w + w)
            dqt[r, lo:] += dot(kt[r, ks], ds[:, c])
            a = dot(qt[r, lo:], ds[:, c], NT)
            b = dot(dot_[r, lo:], pb[:, c], NT)
            if diagonal:
                dkt[r, ks] = a
                dvt[r, ks] = b
            else:
                dkt[r, ks] += a
                dvt[r, ks] += b

    lax.fori_loop(0, i, lambda j, c: (tile(j * B, B, 0, False), c)[1], 0)
    tile(i * B, H, 0, True)
    tile(i * B + H, H, H, True)
    dqs[pl.ds(pl.multiple_of(i * B, B), B), :] = dqt[...].T * HDIM**-0.5

    def copies(pair):
        width = gm_ref.shape[1] // 3
        for b in range(L // B):
            to = pl.ds(pl.multiple_of(jnp.bitwise_xor(b // 2, x_of(meta)) * B, B), B)
            for k in range(3):
                col = pl.ds(pl.multiple_of(k * width + (p0 + pair) * 128, 128), 128)
                src = stage.at[k, pl.ds(b * B, B), :]
                yield b, lambda g, to=to, col=col, src=src, k=k: pltpu.make_async_copy(
                    src, g.at[to, col], sem.at[k]
                )

    def send(pair):
        for b, copy in copies(pair):
            own = core_of(meta) == b % 2

            @pl.when(own)
            def _(copy=copy):
                copy(gm_ref).start()

            @pl.when(jnp.logical_not(own))
            def _(copy=copy):
                copy(gt_ref).start()

    def finish(pair):
        for _, copy in copies(pair):
            copy(gm_ref).wait()

    @pl.when(i == pl.num_programs(1) - 1)
    def _():
        pair = pl.program_id(0)
        gt[...] = jnp.zeros_like(gt)
        ext[...] = jnp.zeros_like(ext)

        @pl.when(pair > 0)
        def _():
            finish(pair)

        def back(n, carry):
            blk = L // B - 1 - n
            sl = pl.ds(pl.multiple_of(blk * B, B), B)
            for which, raw in enumerate((rq, rk, rv)):
                col = which * (taps.shape[1] // 3) + (p0 + pl.program_id(0)) * 128
                t = taps[:, pl.ds(pl.multiple_of(col, 128), 128)]
                g = dqs[sl, :] if which == 0 else (dkt, dvt)[which - 1][:, sl].T
                ext[which, B : B + 8, :] = ext[which, 0:8, :]
                ext[which, 0:B, :] = g
                g1, g2 = ext[which, 1 : B + 1, :], ext[which, 2 : B + 2, :]
                stage[which, sl, :] = (t[0:1] * g + t[1:2] * g1 + t[2:3] * g2).astype(bf16)
                r = raw[sl, :].astype(f32)
                for k, gg in enumerate((g, g1, g2)):
                    row = slice(3 * which + k, 3 * which + k + 1)
                    gt[row, :] += jnp.sum(r * gg, axis=0, keepdims=True)
            return carry

        lax.fori_loop(0, L // B, back, 0)
        send(pair)

        @pl.when(pair == pl.num_programs(0) - 1)
        def _():
            finish(pair)


def att_bwd_call(meta, mix, raw, om, ot, dm, dt, lse, taps, p0, count, into=None):
    length, cols = mix.shape
    pairs = cols // 384
    B = length // 4
    half = pl.BlockSpec((B, 128), lambda p, i, m: (jnp.bitwise_xor(i // 2, x_of(m)), p0 + p))
    full = lambda k: pl.BlockSpec((length, 128), lambda p, i, m: (0, k * pairs + p0 + p))
    return pl.pallas_call(
        functools.partial(att_bwd_body, p0, into is not None),
        out_shape=[sds((length // 2, cols), bf16)] * 2 + [sds((16, 128 * count), f32)],
        grid_spec=grid_spec(
            (count, 4),
            [
                pl.BlockSpec((B, 128), lambda p, i, m: (i, p0 + p)),
                full(1),
                full(2),
                half,
                half,
                half,
                half,
                pl.BlockSpec((1, 2, B), lambda p, i, m: (p0 + p, 0, i)),
                full(0),
                full(1),
                full(2),
                whole((8, cols)),
            ]
            + ([] if into is None else [pl.BlockSpec(memory_space=pl.ANY)] * 2),
            [pl.BlockSpec(memory_space=pl.ANY)] * 2 + [pl.BlockSpec((16, 128), lambda p, i, m: (0, p))],
            [
                pltpu.VMEM((length, 256), bf16),
                pltpu.VMEM((128, length), bf16),
                pltpu.VMEM((128, length), f32),
                pltpu.VMEM((128, length), f32),
                pltpu.VMEM((128, B), f32),
                pltpu.VMEM((length, 128), f32),
                pltpu.VMEM((3, B + 8, 128), f32),
                pltpu.VMEM((3, length, 128), bf16),
                pltpu.SemaphoreType.DMA((3,)),
            ],
        ),
        cost_estimate=cost(
            14 * length * length * 128 * count, 20 * length * 128 * count, 2 * length * length * count
        ),
        name="attn_bwd",
        input_output_aliases={} if into is None else {13: 0, 14: 1},
    )(meta, mix, mix, mix, om, ot, dm, dt, lse, raw, raw, raw, taps, *(into or ()))


T = 256


def valid_rows(meta, i, rows):
    per = rows // T
    block = jnp.where(i < per, meta[2], jnp.bitwise_xor(meta[2], 2))
    start = block * rows + lax.rem(i, per) * T
    return start + lax.broadcasted_iota(jnp.int32, (T, 1), 0) < length_of(meta)


def ffn_body(
    meta, xo, xx, co, cx, am, at, gain, wo_o, wo_c, pack,
    u_o, d_o, f_c, n0, n1, n2, n3, c0, c1, c2, c3,
    oo, ox, dm, dt, gg, dmid, gu0, gu1, gu2, gu3, gd0, gd1, gd2, gd3,
    wo, wus, wds, mid, h_s, g_s, fo, dh, act, du, stu, std, sto, gacc, sw, so, sg, sd, st,
):
    rows, width = xo.shape
    part = wo_o.shape[0]
    half = 2 * part
    n = 2 * rows // T
    per = rows // T
    copies = []
    for k, src in ((0, wo_o), (1, wo_c), (2, pack.at[pl.ds(rows, part), :]), (3, pack.at[pl.ds(rows + part, part), :])):
        shard = jnp.bitwise_xor(meta[2], k)
        row = jnp.where(shard // 2 == core_of(meta), 0, half) + lax.rem(shard, 2) * part
        cp = pltpu.make_async_copy(src, wo.at[pl.ds(pl.multiple_of(row, 64), part), :], so.at[k])
        cp.start()
        copies.append(cp)
    for k, pair in ((0, (f_c.at[0], f_c.at[1])), (2, (u_o, d_o))):
        for n_, src in enumerate(pair):
            pltpu.make_async_copy(src, (wus, wds)[n_].at[k], sw.at[k, n_]).start()
    for k, quarters in ((1, (c0, c1, c2, c3)), (3, (n0, n1, n2, n3))):
        for q_, src in enumerate(quarters):
            count = src.shape[1]
            to = pl.ds(pl.multiple_of(jnp.bitwise_xor(meta[3], q_) * count, 64), count)
            for n_, dst in enumerate((wus, wds)):
                pltpu.make_async_copy(src.at[n_], dst.at[k, to, :], sw.at[k, n_]).start()
    for cp in copies:
        cp.wait()
    gn = gain[...].astype(f32)

    def first_rows(i, carry):
        sl = pl.ds(pl.multiple_of(i * T, T), T)
        src = pl.ds(pl.multiple_of(lax.rem(i, per) * T, T), T)
        own = i < per
        x = jnp.where(own, xo[src, :], xx[src, :]).astype(f32)
        a = jnp.concatenate([am[sl, :], at[sl, :]], axis=1)
        m = x + dot(a, wo[...])
        mid[sl, :] = m
        fo[sl, :] = m
        h_s[sl, :] = norm(m, gn)[2]
        ct = jnp.where(own, co[src, :], cx[src, :])
        g_s[sl, :] = jnp.where(valid_rows(meta, i, rows), ct, jnp.zeros_like(ct))
        dh[sl, :] = jnp.zeros((T, width), f32)
        return carry

    lax.fori_loop(0, n, first_rows, 0)

    R = 512
    C = 768

    gus, gds = (gu0, gu1, gu2, gu3), (gd0, gd1, gd2, gd3)

    def stores(n_, slot):
        return [
            pltpu.make_async_copy(stu.at[slot], gus[n_], sg.at[slot, 0]),
            pltpu.make_async_copy(std.at[slot], gds[n_].at[pl.ds(0, width), :], sg.at[slot, 1]),
        ]

    def shard(k, carry):
        for cp in (
            pltpu.make_async_copy(u_o, wus.at[k], sw.at[k, 0]),
            pltpu.make_async_copy(d_o, wds.at[k], sw.at[k, 1]),
        ):
            cp.wait()

        def rows_step(t, c2):
            sl = pl.ds(pl.multiple_of(t * R, R), R)
            h, g = h_s[sl, :], g_s[sl, :]
            r = jnp.maximum(dot(h, wus[k]), 0.0)
            a = (r * r).astype(bf16)
            d = (dot(g, wds[k], NT) * 2.0 * r).astype(bf16)
            act[sl, :] = a
            du[sl, :] = d
            fo[sl, :] += dot(a, wds[k])
            dh[sl, :] += dot(d, wus[k], NT)
            return c2

        lax.fori_loop(0, 2 * rows // R, rows_step, 0)
        slot = lax.rem(k, 2)

        @pl.when(k >= 2)
        def _():
            for cp in stores(0, slot):
                cp.wait()

        def cols_step(t, c2):
            sl = pl.ds(pl.multiple_of(t * C, C), C)
            stu[slot, :, sl] = dot(h_s[...], du[:, sl], TN).astype(bf16)
            std[slot, sl, :] = dot(act[:, sl], g_s[...], TN).astype(bf16)
            return c2

        lax.fori_loop(0, width // C, cols_step, 0)
        for n_ in range(4):

            @pl.when(k == n_)
            def _(n_=n_):
                for cp in stores(n_, n_ % 2):
                    cp.start()

        return carry

    lax.fori_loop(0, 4, shard, 0)
    gg[...] = jnp.zeros_like(gg)

    def last_rows(i, carry):
        sl = pl.ds(pl.multiple_of(i * T, T), T)
        dst = pl.ds(pl.multiple_of(lax.rem(i, per) * T, T), T)
        ok = valid_rows(meta, i, rows)
        m = mid[sl, :]
        out = jnp.where(ok, fo[sl, :], 0.0)

        fo[sl, :] = out

        @pl.when(i < per)
        def _():
            own = oo.at[meta[2] // 2, dst, :]
            pltpu.make_async_copy(fo.at[sl, :], own, sd.at[1]).start()

        @pl.when(i >= per)
        def _():
            ox[dst, :] = out.astype(bf16)

        nm, inv, _ = norm(m, gn)
        d = dh[sl, :]
        dn = d * gn
        r = g_s[sl, :].astype(f32) + inv * (dn - nm * jnp.mean(dn * nm, axis=-1, keepdims=True))
        mid[sl, :] = r
        pltpu.make_async_copy(mid.at[sl, :], dmid.at[sl, :], sd.at[0]).start()
        db = r.astype(bf16)
        du[sl, :] = db
        da = dot(db, wo[...], NT).astype(bf16)
        dm[sl, :] = da[:, :half]
        dt[sl, :] = da[:, half:]
        gg[...] += jnp.sum(d * nm, axis=0, keepdims=True)
        return carry

    lax.fori_loop(0, n, last_rows, 0)
    gacc[0:half, :] = dot(am[...], du[...], TN)
    gacc[half:, :] = dot(at[...], du[...], TN)
    outs = [
        pltpu.make_async_copy(mid, dmid, sd.at[0]),
        pltpu.make_async_copy(fo.at[pl.ds(0, rows), :], oo.at[meta[2] // 2], sd.at[1]),
    ]
    for k, k_ in enumerate((1, 3, 0, 2)):
        shard_ = jnp.bitwise_xor(meta[2], k_)
        row = jnp.where(shard_ // 2 == core_of(meta), 0, half) + lax.rem(shard_, 2) * part
        sto[k] = gacc[pl.ds(pl.multiple_of(row, 64), part), :].astype(bf16)
        cp = pltpu.make_async_copy(sto.at[k], gds[k].at[pl.ds(width, part), :], st.at[k])
        cp.start()
        outs.append(cp)
    for slot in range(2):
        outs.extend(stores(2 + slot, slot))
    for cp in outs:
        cp.wait()


def ffn_call(meta, xo, xx, co, cx, am, at, gain, wos, ffs):
    rows, width = xo.shape
    half = am.shape[1]
    part = half // 2
    hid = ffs[0].shape[1]
    hbm = pl.BlockSpec(memory_space=pl.ANY)
    vm = lambda *shape: whole(shape)
    all_rows = 2 * rows
    return pl.pallas_call(
        ffn_body,
        out_shape=[
            sds((2, rows, width), f32),
            sds((rows, width), bf16),
            sds((all_rows, half), bf16),
            sds((all_rows, half), bf16),
            sds((1, width), f32),
            sds((all_rows, width), f32),
        ]
        + [sds((width, hid), bf16)] * 4
        + [sds((hid + part, width), bf16)] * 4,
        grid_spec=grid_spec(
            (1,),
            [vm(rows, width)] * 4 + [vm(all_rows, half)] * 2 + [vm(1, width)] + [hbm] * 14,
            [
                hbm,
                vm(rows, width),
                vm(all_rows, half),
                vm(all_rows, half),
                vm(1, width),
            ]
            + [hbm] * 9,
            [
                pltpu.VMEM((width, width), bf16),
                pltpu.VMEM((4, width, hid), bf16),
                pltpu.VMEM((4, hid, width), bf16),
                pltpu.VMEM((all_rows, width), f32),
                pltpu.VMEM((all_rows, width), bf16),
                pltpu.VMEM((all_rows, width), bf16),
                pltpu.VMEM((all_rows, width), f32),
                pltpu.VMEM((all_rows, width), f32),
                pltpu.VMEM((all_rows, hid), bf16),
                pltpu.VMEM((all_rows, hid), bf16),
                pltpu.VMEM((2, width, hid), bf16),
                pltpu.VMEM((2, hid, width), bf16),
                pltpu.VMEM((4, part, width), bf16),
                pltpu.VMEM((width, width), f32),
                pltpu.SemaphoreType.DMA((4, 2)),
                pltpu.SemaphoreType.DMA((4,)),
                pltpu.SemaphoreType.DMA((2, 2)),
                pltpu.SemaphoreType.DMA((2,)),
                pltpu.SemaphoreType.DMA((4,)),
            ],
        ),
        cost_estimate=cost(
            48 * all_rows * width * hid + 6 * all_rows * width * width, 40 * all_rows * width
        ),
        compiler_params=pltpu.CompilerParams(vmem_limit_bytes=62 * 2**20),
        name="ffn",
    )(meta, xo, xx, co, cx, am, at, gain, *wos, *ffs)


def projg_body(meta, h, dm, dt, keep, far, send, acc):
    rows = dm.shape[0]
    acc[...] = dot(h[0:rows, :], dm[...], TN) + dot(h[rows:, :], dt[...], TN)
    part = keep.shape[0]
    for ref, k, row in ((keep, 0, 0), (far, 2, 0), (send, 1, 0), (send, 3, part)):
        at = jnp.bitwise_xor(meta[2], k)
        ref[row : row + part, :] = acc[pl.ds(pl.multiple_of(at * part, 64), part), :].astype(bf16)


def projg_call(meta, h, dm, dt):
    length, width = h.shape
    cols = dm.shape[1]
    step = cols // 3
    d = pl.BlockSpec((length // 2, step), lambda j, m: (0, j))
    g = lambda rows: pl.BlockSpec((rows, step), lambda j, m: (0, j))
    part = width // 4
    return pl.pallas_call(
        projg_body,
        out_shape=[sds((rows, cols), bf16) for rows in (part, part, 2 * part)],
        grid_spec=grid_spec(
            (3,),
            [whole((length, width)), d, d],
            [g(part), g(part), g(2 * part)],
            [pltpu.VMEM((width, step), f32)],
        ),
        cost_estimate=cost(length, length),
        name="projg",
    )(meta, h, dm, dt)


def last_body(meta, xo, xx, dm, dt, wm, wt, dmid, gain, go, gx, gg):
    i = pl.program_id(0)
    per = pl.num_programs(0) // 2
    first = i < per
    x = jnp.where(first, xo[...], xx[...]).astype(f32)
    gn = gain[...].astype(f32)
    n, inv, _ = norm(x, gn)
    dh = dot(dm[...], wm[...], NT) + dot(dt[...], wt[...], NT)
    dn = dh * gn
    out = dmid[...] + inv * (dn - n * jnp.mean(dn * n, axis=-1, keepdims=True))

    @pl.when(first)
    def _():
        go[0] = out

    @pl.when(jnp.logical_not(first))
    def _():
        gx[...] = out.astype(bf16)

    ps = jnp.sum(dh * n, axis=0, keepdims=True)

    @pl.when(i == 0)
    def _():
        gg[...] = ps

    @pl.when(i > 0)
    def _():
        gg[...] += ps


def own_map(per):
    return lambda i, m: (jnp.minimum(i, per - 1), 0)


def nb_map(per):
    return lambda i, m: (jnp.maximum(i - per, 0), 0)


def last_call(meta, xo, xx, dm, dt, wm, wt, dmid, gain):
    rows, width = xo.shape
    cols = dm.shape[1]
    per = rows // T
    fst, snd = pl.BlockSpec((T, width), own_map(per)), pl.BlockSpec((T, width), nb_map(per))
    blk = lambda n: pl.BlockSpec((T, n), lambda i, m: (i, 0))
    return pl.pallas_call(
        last_body,
        out_shape=[sds((2, rows, width), f32), sds((rows, width), bf16), sds((1, width), f32)],
        grid_spec=grid_spec(
            (2 * per,),
            [fst, snd, blk(cols), blk(cols)]
            + [whole((width, cols))] * 2
            + [blk(width), whole((1, width))],
            [
                pl.BlockSpec((1, T, width), lambda i, m: (x_of(m), jnp.minimum(i, per - 1), 0)),
                snd,
                pl.BlockSpec((1, width), lambda i, m: (0, 0)),
            ],
        ),
        cost_estimate=cost(rows, rows),
        name="last",
    )(meta, xo, xx, dm, dt, wm, wt, dmid, gain)


def flip(size, bit):
    return [(i, i ^ bit) for i in range(size)]


def core_swap(v):
    return lax.ppermute(v, "head", CORE)


def x_swap(v):
    return lax.ppermute(v, "head", XNB)


def after(v, *deps):
    return lax.optimization_barrier((v, *deps))[0]


def halve(terms, index, count):
    rows = terms[0].shape[0] // count
    piece = lambda t, k: lax.dynamic_slice_in_dim(t, jnp.bitwise_xor(index, k) * rows, rows, 0)
    total = lambda k: sum(piece(t, k).astype(f32) for t in terms)
    return [total(k).astype(bf16) for k in range(1, count)], total(0)


def strides(dp):
    out = [1]
    while 2 * out[-1] < dp:
        out.append(2 * out[-1])
    return out


def side(stride):
    return lax.axis_index("dp") // stride % 2


def swap(v, stride, dp):
    return lax.ppermute(v, "dp", flip(dp, stride))


def rows_as(got, vs):
    out, row = [], 0
    for v in vs:
        out.append(got[row : row + v.shape[0]])
        row += v.shape[0]
    return out


def swap_both(vs, stride, dp):
    return rows_as(swap(jnp.concatenate(vs, axis=0), stride, dp), vs)


def scatter(sums, stride, dp):
    halves = [halve(terms, side(stride), 2) for terms in sums]
    send = jnp.concatenate([h[0][0] for h in halves], axis=0)
    got = swap(send, stride, dp)
    out, row = [], 0
    for (part,), keep in halves:
        out.append([keep, got[row : row + part.shape[0]]])
        row += part.shape[0]
    return out, send


def join(mine, got, stride):
    upper = side(stride) == 1
    return jnp.concatenate([jnp.where(upper, got, mine), jnp.where(upper, mine, got)], axis=0)


def total(terms):
    return sum(t.astype(f32) for t in terms)


def local(dp, inputs, lengths, w_query, w_key, w_value, w_out, w_up, w_down, conv_taps, gain_attn, gain_ff, cotangent):
    hd = lax.axis_index("head")
    x, c, y = hd // 2, hd % 2, lax.axis_index("dp") % 2
    q = lax.axis_index("dp") % 4
    width = inputs.shape[2]
    part = w_query.shape[0]
    half = 2 * part
    pick = lambda v, k: lax.dynamic_index_in_dim(v, k, 0, keepdims=False)
    y_swap = lambda v: lax.ppermute(v, "dp", flip(dp, 1))
    order = lambda own, nb: lax.dynamic_update_slice_in_dim(own, nb[None].astype(f32), 1 - x, 0)
    meta = jnp.concatenate([lengths, jnp.stack([hd, q])]).astype(jnp.int32)
    gain1, gain2 = gain_attn.reshape(1, width), gain_ff.reshape(1, width)

    mask = (jnp.arange(2) == c)[None, None, :, None]
    tap_rows = jnp.where(mask, conv_taps.transpose(1, 0, 2)[:, :, None, :], 0).reshape(3, 3 * half)
    tap_rows = jnp.concatenate([tap_rows[:, :width], jnp.pad(tap_rows[:, width:], ((0, 0), (0, half)))], axis=0)
    tap_rows = jnp.pad(tap_rows, ((0, 10), (0, 0)))

    def packed(k):
        cut = lambda w: lax.dynamic_slice_in_dim(w, k * half, half, 1)
        fold = cut(w_value)
        return jnp.concatenate(
            [
                jnp.concatenate([cut(w_query), cut(w_key)], axis=1),
                jnp.concatenate([fold[: part // 2], fold[part // 2 :]], axis=1),
                tap_rows,
            ],
            axis=0,
        )

    w_core = core_swap(packed(1 - c))
    w_mine = packed(c)
    x_own = pick(inputs, x)
    rows = x_own.shape[0]
    x_nb = x_swap(pick(inputs, 1 - x))
    pack = x_swap(jnp.concatenate([w_mine, w_core], axis=0))
    x_core = core_swap(x_own)
    count = width // 4
    quarter = lambda w: lax.dynamic_slice_in_dim(w, q * count, count, 0)
    wo_c = core_swap(w_out)
    c_own = pick(cotangent, x)
    ff_src = jnp.stack([quarter(w_up), quarter(w_down)])
    ff_own = jnp.stack([w_up, w_down])
    pack2 = jnp.concatenate([pick(cotangent, 1 - x), w_out, wo_c], axis=0)
    x_nb, ff_src, ff_own, pack2, c_own, meta, x_core, pack = lax.optimization_barrier(
        (x_nb, ff_src, ff_own, pack2, c_own, meta, x_core, pack)
    )
    x_cnb = core_swap(x_nb)
    h1, raw, mix, w_full, taps = qkv_call(meta, x_own, x_nb, x_core, x_cnb, w_mine, w_core, pack, gain1)

    ff_first, pack2 = x_swap(ff_src), x_swap(pack2)
    ff_c = core_swap(ff_own)
    src = after(ff_first, mix)
    ff_n = [swap(src, k, dp) for k in (1, 2, 3)]
    a_mine, a_send, lse = att_fwd_call(meta, after(mix, src, ff_c))
    a_got = core_swap(a_send)
    w_other = core_swap(w_full)
    *ff_n, pack2 = lax.optimization_barrier((*ff_n, pack2, a_mine))[:-1]
    ff_n = [src, *ff_n]
    ff_cn = [core_swap(v) for v in ff_n]
    out_own, out_nb, d_mine, d_send, gg2, dmid, *gw = ffn_call(
        meta, x_own, x_nb, c_own, pack2, a_mine, a_got, after(gain2, w_other),
        (w_out, wo_c, pack2),
        (w_up, w_down, ff_c, *ff_n, *ff_cn),
    )
    d_got = core_swap(d_send)

    _, *rest = strides(dp)
    un, dn, do, uo = [core_swap(gw[k]) for k in (1, 5, 4, 0)]
    nu = total((gw[3], un)).astype(bf16)
    xu = x_swap(nu)
    (dn_send,), dn_keep = halve((gw[7], dn), y, 2)
    (do_send,), do_keep = halve((gw[6], do), y, 2)
    yn, yo = y_swap(dn_send), y_swap(do_send)
    out_x = x_swap(after(out_nb, nu))
    pairs = width // 256
    bwd = lambda m, p, n, into: att_bwd_call(
        meta, m, raw, a_mine, a_send, d_mine, d_got, lse, taps, p, n, into
    )
    *dall, gt_a = bwd(after(mix, nu, dn_send, do_send), 0, pairs - 1, None)
    xu, yn, yo, out_x = lax.optimization_barrier((xu, yn, yo, out_x, gt_a))[:4]
    (u_send,), u_keep = halve((gw[2], uo, xu), y, 2)
    nd = total((dn_keep, yn)).astype(bf16)
    yu, xd = y_swap(u_send), x_swap(nd)
    p_mine, p_theirs, gt_b = bwd(after(mix, u_send, nd), pairs - 1, 1, dall)
    p_got = core_swap(p_theirs)
    gt = jnp.concatenate([gt_a, gt_b], axis=1)
    yu, xd = lax.optimization_barrier((yu, xd, gt_b))[:2]
    sums, sent = scatter([[u_keep, yu], [do_keep, yo, xd]], rest[0], dp)
    keep, far, send = projg_call(meta, after(h1, sent), p_mine, p_theirs)
    flat = lax.optimization_barrier((*sums[0], *sums[1], keep))[:-1]
    sums, sent = scatter([flat[:2], flat[2:]], rest[1], dp)
    got = core_swap(after(send, sent))
    far, far2 = x_swap(far), x_swap(got[part:])
    gi_own, gi_nb, gg1 = last_call(
        meta, x_own, x_nb, p_mine, p_got, w_full, w_other, after(dmid, sent), gain1
    )
    *flat, gt, gg1 = lax.optimization_barrier((*sums[0], *sums[1], gt, x_swap(core_swap(gg1))))
    sums = [flat[:2], flat[2:]]
    for stride in rest[2:]:
        sums, _ = scatter(sums, stride, dp)
    vs = [total(t).astype(bf16) for t in sums]
    far, far2 = lax.optimization_barrier((far, far2, *vs))[:2]
    ga, gb = keep.astype(f32) + far.astype(f32), got[:part].astype(f32) + far2.astype(f32)
    g_send, g_keep = jnp.where(y == 0, gb, ga).astype(bf16), jnp.where(y == 0, ga, gb)
    pt = [g_keep, y_swap(g_send)]
    gi_got = x_swap(after(gi_nb, g_send))
    for stride in reversed(rest[1:]):
        cat = jnp.concatenate(vs, axis=0)
        first_cat = cat if stride == rest[-1] else first_cat
        got_v = swap(cat, stride, dp)
        vs = [join(v, g, stride) for v, g in zip(vs, rows_as(got_v, vs))]
    (pt,), sent = scatter([pt], rest[0], dp)
    *vs, _ = lax.optimization_barrier((*vs, sent))
    packed_vs = jnp.concatenate(vs, axis=0)
    near_got = swap(packed_vs, rest[0], dp)
    across = rows_as(y_swap(packed_vs), vs)
    for stride in rest[1:]:
        (pt,), _ = scatter([pt], stride, dp)
    others, also = rows_as(near_got, vs), rows_as(y_swap(near_got), vs)
    ps = after(total(pt).astype(bf16), near_got)
    for stride in reversed(rest):
        ps = join(ps, swap(ps, stride, dp), stride)
    ps_got = y_swap(ps)
    whole_of = lambda k: join(
        join(vs[k], others[k], rest[0]), join(across[k], also[k], rest[0]), 1
    ).astype(f32)
    grad_up, gd_all = whole_of(0), whole_of(1)
    grad_down, grad_out = gd_all[: w_down.shape[0]], gd_all[w_down.shape[0] :]
    lo, hi = jnp.where(y == c, ps, ps_got), jnp.where(y == c, ps_got, ps)
    third = lambda v, w: v[:, w * half : w * half + half]
    grads = [jnp.concatenate([third(lo, w), third(hi, w)], axis=1).astype(f32) for w in range(3)]

    gt = gt[:9].reshape(9, 2, part).transpose(1, 0, 2)
    gt = jnp.where(jnp.arange(2)[:, None, None, None] == c, gt[None], 0.0).reshape(4, 9, part)
    gains = jnp.concatenate([gg1, gg2], axis=0).reshape(2, 4, part).transpose(1, 0, 2)
    small = jnp.concatenate([gt, gains, jnp.zeros((4, 5, part), f32)], axis=1)
    small = after(small, first_cat)
    small = jnp.broadcast_to(small[:, None], (4, dp, 16, part)).reshape(4 * dp, 16, part)
    small = jnp.sum(lax.all_to_all(small, ("head", "dp"), 0, 0, tiled=True), axis=0)
    output = order(after(out_own, g_send), out_x)
    grad_input = order(after(gi_own, ps), gi_got)
    return (
        output,
        grad_input,
        *grads,
        grad_out,
        grad_up,
        grad_down,
        small[:9].reshape(3, 3, part),
        small[9],
        small[10],
    )


def solution(mesh):
    placed = (
        P("dp", "head", None),
        P("dp"),
        P("head", None),
        P("head", None),
        P("head", None),
        P("head", None),
        P(None, "head"),
        P("head", None),
        P(None, None, "head"),
        P(),
        P(),
        P("dp", "head", None),
    )
    return jax.shard_map(
        functools.partial(local, mesh.shape["dp"]),
        mesh=mesh,
        in_specs=placed,
        out_specs=(
            P("dp", "head", None),
            P("dp", "head", None),
            P("head", None),
            P("head", None),
            P("head", None),
            P("head", None),
            P(None, "head"),
            P("head", None),
            P(None, None, "head"),
            P("head"),
            P("head"),
        ),
        check_vma=False,
    )
```

```python
import functools

import jax
import jax.numpy as jnp
from jax import lax
from jax.experimental import pallas as pl
from jax.experimental.pallas import tpu as pltpu
from jax.sharding import PartitionSpec as P

HDIM = 64
EPS = 1e-06
bf16 = jnp.bfloat16
f32 = jnp.float32

NN = (((1,), (0,)), ((), ()))
NT = (((1,), (1,)), ((), ()))
TN = (((0,), (0,)), ((), ()))

CORE = [(0, 1), (1, 0), (2, 3), (3, 2)]
XNB = [(0, 2), (2, 0), (1, 3), (3, 1)]


def dot(a, b, dims=NN):
    return lax.dot_general(a, b, dims, preferred_element_type=f32)


def cost(flops, nbytes, trans=0):
    return pl.CostEstimate(flops=int(flops), bytes_accessed=int(nbytes), transcendentals=int(trans))


def sds(shape, dtype):
    return jax.ShapeDtypeStruct(shape, dtype)


def whole(shape):
    zeros = (0,) * len(shape)
    return pl.BlockSpec(shape, lambda *_: zeros, pipeline_mode=pl.Buffered(1))


def grid_spec(grid, ins, outs, scratch=()):
    return pltpu.PrefetchScalarGridSpec(
        num_scalar_prefetch=1, grid=grid, in_specs=ins, out_specs=outs, scratch_shapes=scratch
    )


def length_of(m):
    return m[m[2] // 2]


def x_of(m):
    return m[2] // 2


def core_of(m):
    return lax.rem(m[2], 2)


def slot_of(m, b):
    v = jnp.bitwise_xor(m[2], b)
    return lax.rem(v, 2) * 2 + v // 2


def norm(x, gain):
    inv = lax.rsqrt(jnp.mean(x * x, axis=-1, keepdims=True) + EPS)
    n = x * inv
    return n, inv, (n * gain).astype(bf16)


def qkv_body(meta, x0, x1, x2, x3, wa, wb, pack, gain, h_ref, raw_ref, mix_ref, w_ref, taps, ext):
    b = pl.program_id(0)
    rows = x0.shape[0]
    part = w_ref.shape[0] // 4
    width = x0.shape[1]
    tall = wa.shape[0]
    hd = meta[2]

    @pl.when(b == 0)
    def _():
        def put(k, ref, first):
            at = jnp.bitwise_xor(hd, k) * part
            w_ref[pl.ds(pl.multiple_of(at, 64), part), 0:width] = ref[first : first + part, :]
            for n in range(2):
                row = pl.multiple_of(at + n * (part // 2), 32)
                w_ref[pl.ds(row, part // 2), width:] = ref[
                    first + part : first + part + part // 2, n * (width // 2) : (n + 1) * (width // 2)
                ]

        put(0, wa, 0)
        put(1, wb, 0)
        put(2, pack, 0)
        put(3, pack, tall)
        last = lambda ref, end: ref[end - 16 : end, :].astype(f32)
        near = last(wa, tall) + last(wb, tall)
        far = last(pack, tall) + last(pack, 2 * tall)
        t = jnp.where(x_of(meta) == core_of(meta), near, far)
        taps[...] = jnp.zeros_like(taps)
        taps[0:3, 0:width] = t[0:3]
        taps[0:3, width:] = t[3:6, 0 : width // 2]
        ext[0:8, :] = jnp.zeros((8, ext.shape[1]), f32)

    slot = slot_of(meta, b)
    step = ext.shape[0] - 8

    def some(n, carry):
        sl = pl.ds(pl.multiple_of(n * step, step), step)
        x = x0[sl, :]
        for k, other in ((1, x1), (2, x2), (3, x3)):
            x = jnp.where(slot == k, other[sl, :], x)
        _, _, h = norm(x.astype(f32), gain[...].astype(f32))
        h_ref[sl, :] = h
        raw = dot(h, w_ref[...]).astype(bf16)
        raw_ref[sl, :] = raw
        rawf = raw.astype(f32)
        ext[8:, :] = rawf
        t = taps[...]
        mixed = t[0:1] * rawf + t[1:2] * ext[7 : 7 + step, :] + t[2:3] * ext[6 : 6 + step, :]
        mix_ref[sl, :] = mixed.astype(bf16)
        ext[0:8, :] = ext[step:, :]
        return carry

    lax.fori_loop(0, rows // step, some, 0)


def qkv_call(meta, x_own, x_nb, x_core, x_cnb, w_mine, w_core, pack, gain):
    rows, width = x_own.shape
    tall = w_mine.shape[0]
    cols = width * 3 // 2
    length = 4 * rows
    blk = lambda n: pl.BlockSpec((rows, n), lambda b, m: (b, 0))
    const = lambda r: pl.BlockSpec((r, cols), lambda b, m: (0, 0))
    return pl.pallas_call(
        qkv_body,
        out_shape=[
            sds((length, width), bf16),
            sds((length, cols), bf16),
            sds((length, cols), bf16),
            sds((width, cols), bf16),
            sds((8, cols), f32),
        ],
        grid_spec=grid_spec(
            (4,),
            [whole((rows, width))] * 4
            + [whole((tall, width))] * 2
            + [whole(pack.shape), whole((1, width))],
            [
                pl.BlockSpec((rows, width), lambda b, m: (slot_of(m, b), 0)),
                blk(cols),
                blk(cols),
                const(width),
                const(8),
            ],
            [pltpu.VMEM((T + 8, cols), f32)],
        ),
        cost_estimate=cost(2 * length * width * cols, 2 * length * (width * 2 + cols * 2)),
        name="qkv",
    )(meta, x_own, x_nb, x_core, x_cnb, w_mine, w_core, pack, gain)


def two_heads(v):
    lane = lax.broadcasted_iota(jnp.int32, v.shape, 1)
    z = jnp.zeros_like(v)
    return jnp.concatenate([jnp.where(lane < HDIM, v, z), jnp.where(lane < HDIM, z, v)], axis=0)


def causal(first, keys, start, queries):
    key = first + lax.broadcasted_iota(jnp.int32, (keys, queries), 0)
    ok = key <= start + lax.broadcasted_iota(jnp.int32, (keys, queries), 1)
    return jnp.concatenate([ok, ok], axis=1)


def upper(v, axis):
    B = v.shape[axis] // 2
    h = B // 2
    if axis == 0:
        return jnp.concatenate([v[h:B], v[B + h :]], axis=0)
    return jnp.concatenate([v[:, h:B], v[:, B + h :]], axis=1)


def with_bias(k_ref, ka, length):
    L = k_ref.shape[0]
    ka[:, :128] = k_ref[...]
    lane = lax.broadcasted_iota(jnp.int32, (L, 128), 1)
    row = lax.broadcasted_iota(jnp.int32, (L, 128), 0)
    pad = jnp.logical_and(lane == 0, row >= length)
    ka[:, 128:] = jnp.where(pad, -1e9, 0.0).astype(bf16)


def biased(q):
    qq = two_heads(q)
    lane = lax.broadcasted_iota(jnp.int32, qq.shape, 1)
    return jnp.concatenate([qq, jnp.where(lane == 0, 1.0, 0.0).astype(bf16)], axis=1)


def att_fwd_body(meta, q_ref, k_ref, v_ref, mine_ref, theirs_ref, lse_ref, ka, vt, sc):
    i = pl.program_id(1)
    B = q_ref.shape[0]

    @pl.when(i == 0)
    def _():
        vt[...] = v_ref[...].T
        with_bias(k_ref, ka, length_of(meta))

    qq = biased(q_ref[...] * bf16(HDIM**-0.5))
    own = lax.rem(i, 2) == core_of(meta)

    def run(ii):
        m = None
        for j in range(ii + 1):
            ks = slice(j * B, j * B + B)
            s = dot(ka[ks, :], qq, NT)
            if j == ii:
                s = jnp.where(causal(0, B, 0, B), s, -1e9)
            sc[ks, :] = s
            mj = jnp.max(s, axis=0, keepdims=True)
            m = mj if m is None else jnp.maximum(m, mj)
        l = jnp.zeros((1, 2 * B), f32)
        acc = [jnp.zeros((HDIM, B), f32)] * 2
        for j in range(ii + 1):
            ks = slice(j * B, j * B + B)
            p = jnp.exp(sc[ks, :] - m)
            l = l + jnp.sum(p, axis=0, keepdims=True)
            pb = p.astype(bf16)
            for h in range(2):
                r = slice(HDIM * h, HDIM * h + HDIM)
                acc[h] = acc[h] + dot(vt[r, ks], pb[:, h * B : h * B + B])
        inv = 1.0 / l
        out = jnp.concatenate([acc[h] * inv[:, h * B : h * B + B] for h in range(2)], axis=0)
        out = out.T.astype(bf16)

        @pl.when(own)
        def _():
            mine_ref[...] = out

        @pl.when(jnp.logical_not(own))
        def _():
            theirs_ref[...] = out

        ls = m + jnp.log(l)
        lse_ref[0] = jnp.concatenate([ls[:, :B], ls[:, B:]], axis=0)

    for ii in range(4):
        pl.when(i == ii)(functools.partial(run, ii))


def half_map(p, i, m):
    return (jnp.bitwise_xor(i // 2, x_of(m)), p)


def att_fwd_call(meta, mix):
    length, cols = mix.shape
    width = cols // 3
    pairs = width // 128
    B = length // 4
    half = pl.BlockSpec((B, 128), half_map)
    return pl.pallas_call(
        att_fwd_body,
        out_shape=[
            sds((length // 2, width), bf16),
            sds((length // 2, width), bf16),
            sds((pairs, 2, length), f32),
        ],
        grid_spec=grid_spec(
            (pairs, 4),
            [
                pl.BlockSpec((B, 128), lambda p, i, m: (i, p)),
                pl.BlockSpec((length, 128), lambda p, i, m: (0, pairs + p)),
                pl.BlockSpec((length, 128), lambda p, i, m: (0, 2 * pairs + p)),
            ],
            [half, half, pl.BlockSpec((1, 2, B), lambda p, i, m: (p, 0, i))],
            [
                pltpu.VMEM((length, 256), bf16),
                pltpu.VMEM((128, length), bf16),
                pltpu.VMEM((length, 2 * B), f32),
            ],
        ),
        cost_estimate=cost(8 * length * length * width, 8 * length * width, 2 * length * length * pairs),
        name="attn_fwd",
    )(meta, mix, mix, mix)


def att_bwd_body(
    p0, aliased, meta, q_ref, k_ref, v_ref, om, ot, dm, dt, lse_ref, rq, rk, rv, taps, *refs
):
    gm_ref, gt_ref, gt, ka, kt, dkt, dvt, dqt, dqs, ext, stage, sem = refs[2:] if aliased else refs
    i = pl.program_id(1)
    B = q_ref.shape[0]
    L = k_ref.shape[0]
    H = B // 2

    @pl.when(i == 0)
    def _():
        kt[...] = k_ref[...].T
        with_bias(k_ref, ka, length_of(meta))

    own = lax.rem(i, 2) == core_of(meta)
    q = q_ref[...] * bf16(HDIM**-0.5)
    o = jnp.where(own, om[...], ot[...])
    do = jnp.where(own, dm[...], dt[...])
    qq, dd = biased(q), two_heads(do)
    qt, dot_ = q.T, do.T
    od = (o.astype(f32) * do.astype(f32)).T
    delta = jnp.concatenate(
        [jnp.sum(od[:HDIM], axis=0, keepdims=True), jnp.sum(od[HDIM:], axis=0, keepdims=True)],
        axis=1,
    )
    ls = lse_ref[0]
    lse = jnp.concatenate([ls[0:1], ls[1:2]], axis=1)

    dqt[...] = jnp.zeros_like(dqt)

    def tile(st, n, lo, diagonal):
        w = B - lo
        ks = pl.ds(pl.multiple_of(st, H), n)
        part = upper if lo else lambda v, axis: v
        s = dot(ka[ks, :], part(qq, 0), NT)
        dp = dot(v_ref[ks, :], part(dd, 0), NT)
        p = jnp.exp(s - part(lse, 1))
        if diagonal:
            p = jnp.where(causal(lo, n, lo, w), p, 0.0)
        ds = (p * (dp - part(delta, 1))).astype(bf16)
        pb = p.astype(bf16)
        for h in range(2):
            r, c = slice(HDIM * h, HDIM * h + HDIM), slice(h * w, h * w + w)
            dqt[r, lo:] += dot(kt[r, ks], ds[:, c])
            a = dot(qt[r, lo:], ds[:, c], NT)
            b = dot(dot_[r, lo:], pb[:, c], NT)
            if diagonal:
                dkt[r, ks] = a
                dvt[r, ks] = b
            else:
                dkt[r, ks] += a
                dvt[r, ks] += b

    lax.fori_loop(0, i, lambda j, c: (tile(j * B, B, 0, False), c)[1], 0)
    tile(i * B, H, 0, True)
    tile(i * B + H, H, H, True)
    dqs[pl.ds(pl.multiple_of(i * B, B), B), :] = dqt[...].T * HDIM**-0.5

    def copies(pair):
        width = gm_ref.shape[1] // 3
        for b in range(L // B):
            to = pl.ds(pl.multiple_of(jnp.bitwise_xor(b // 2, x_of(meta)) * B, B), B)
            for k in range(3):
                col = pl.ds(pl.multiple_of(k * width + (p0 + pair) * 128, 128), 128)
                src = stage.at[k, pl.ds(b * B, B), :]
                yield b, lambda g, to=to, col=col, src=src, k=k: pltpu.make_async_copy(
                    src, g.at[to, col], sem.at[k]
                )

    def send(pair):
        for b, copy in copies(pair):
            own = core_of(meta) == b % 2

            @pl.when(own)
            def _(copy=copy):
                copy(gm_ref).start()

            @pl.when(jnp.logical_not(own))
            def _(copy=copy):
                copy(gt_ref).start()

    def finish(pair):
        for _, copy in copies(pair):
            copy(gm_ref).wait()

    @pl.when(i == pl.num_programs(1) - 1)
    def _():
        pair = pl.program_id(0)
        gt[...] = jnp.zeros_like(gt)
        ext[...] = jnp.zeros_like(ext)

        @pl.when(pair > 0)
        def _():
            finish(pair)

        def back(n, carry):
            blk = L // B - 1 - n
            sl = pl.ds(pl.multiple_of(blk * B, B), B)
            for which, raw in enumerate((rq, rk, rv)):
                col = which * (taps.shape[1] // 3) + (p0 + pl.program_id(0)) * 128
                t = taps[:, pl.ds(pl.multiple_of(col, 128), 128)]
                g = dqs[sl, :] if which == 0 else (dkt, dvt)[which - 1][:, sl].T
                ext[which, B : B + 8, :] = ext[which, 0:8, :]
                ext[which, 0:B, :] = g
                g1, g2 = ext[which, 1 : B + 1, :], ext[which, 2 : B + 2, :]
                stage[which, sl, :] = (t[0:1] * g + t[1:2] * g1 + t[2:3] * g2).astype(bf16)
                r = raw[sl, :].astype(f32)
                for k, gg in enumerate((g, g1, g2)):
                    row = slice(3 * which + k, 3 * which + k + 1)
                    gt[row, :] += jnp.sum(r * gg, axis=0, keepdims=True)
            return carry

        lax.fori_loop(0, L // B, back, 0)
        send(pair)

        @pl.when(pair == pl.num_programs(0) - 1)
        def _():
            finish(pair)


def att_bwd_call(meta, mix, raw, om, ot, dm, dt, lse, taps, p0, count, into=None):
    length, cols = mix.shape
    pairs = cols // 384
    B = length // 4
    half = pl.BlockSpec((B, 128), lambda p, i, m: (jnp.bitwise_xor(i // 2, x_of(m)), p0 + p))
    full = lambda k: pl.BlockSpec((length, 128), lambda p, i, m: (0, k * pairs + p0 + p))
    return pl.pallas_call(
        functools.partial(att_bwd_body, p0, into is not None),
        out_shape=[sds((length // 2, cols), bf16)] * 2 + [sds((16, 128 * count), f32)],
        grid_spec=grid_spec(
            (count, 4),
            [
                pl.BlockSpec((B, 128), lambda p, i, m: (i, p0 + p)),
                full(1),
                full(2),
                half,
                half,
                half,
                half,
                pl.BlockSpec((1, 2, B), lambda p, i, m: (p0 + p, 0, i)),
                full(0),
                full(1),
                full(2),
                whole((8, cols)),
            ]
            + ([] if into is None else [pl.BlockSpec(memory_space=pl.ANY)] * 2),
            [pl.BlockSpec(memory_space=pl.ANY)] * 2 + [pl.BlockSpec((16, 128), lambda p, i, m: (0, p))],
            [
                pltpu.VMEM((length, 256), bf16),
                pltpu.VMEM((128, length), bf16),
                pltpu.VMEM((128, length), f32),
                pltpu.VMEM((128, length), f32),
                pltpu.VMEM((128, B), f32),
                pltpu.VMEM((length, 128), f32),
                pltpu.VMEM((3, B + 8, 128), f32),
                pltpu.VMEM((3, length, 128), bf16),
                pltpu.SemaphoreType.DMA((3,)),
            ],
        ),
        cost_estimate=cost(
            14 * length * length * 128 * count, 20 * length * 128 * count, 2 * length * length * count
        ),
        name="attn_bwd",
        input_output_aliases={} if into is None else {13: 0, 14: 1},
    )(meta, mix, mix, mix, om, ot, dm, dt, lse, raw, raw, raw, taps, *(into or ()))


T = 256


def valid_rows(meta, i, rows):
    per = rows // T
    block = jnp.where(i < per, meta[2], jnp.bitwise_xor(meta[2], 2))
    start = block * rows + lax.rem(i, per) * T
    return start + lax.broadcasted_iota(jnp.int32, (T, 1), 0) < length_of(meta)


def ffn_body(
    meta, xo, xx, co, cx, am, at, gain, wo_o, wo_c, pack,
    u_o, d_o, f_c, n0, n1, n2, n3, c0, c1, c2, c3,
    oo, ox, dm, dt, gg, dmid, gu0, gu1, gu2, gu3, gd0, gd1, gd2, gd3,
    wo, wus, wds, mid, h_s, g_s, fo, dh, act, du, stu, std, sto, gacc, sw, so, sg, sd, st,
):
    rows, width = xo.shape
    part = wo_o.shape[0]
    half = 2 * part
    n = 2 * rows // T
    per = rows // T
    copies = []
    for k, src in ((0, wo_o), (1, wo_c), (2, pack.at[pl.ds(rows, part), :]), (3, pack.at[pl.ds(rows + part, part), :])):
        shard = jnp.bitwise_xor(meta[2], k)
        row = jnp.where(shard // 2 == core_of(meta), 0, half) + lax.rem(shard, 2) * part
        cp = pltpu.make_async_copy(src, wo.at[pl.ds(pl.multiple_of(row, 64), part), :], so.at[k])
        cp.start()
        copies.append(cp)
    for k, pair in ((0, (f_c.at[0], f_c.at[1])), (2, (u_o, d_o))):
        for n_, src in enumerate(pair):
            pltpu.make_async_copy(src, (wus, wds)[n_].at[k], sw.at[k, n_]).start()
    for k, quarters in ((1, (c0, c1, c2, c3)), (3, (n0, n1, n2, n3))):
        for q_, src in enumerate(quarters):
            count = src.shape[1]
            to = pl.ds(pl.multiple_of(jnp.bitwise_xor(meta[3], q_) * count, 64), count)
            for n_, dst in enumerate((wus, wds)):
                pltpu.make_async_copy(src.at[n_], dst.at[k, to, :], sw.at[k, n_]).start()
    for cp in copies:
        cp.wait()
    gn = gain[...].astype(f32)

    def first_rows(i, carry):
        sl = pl.ds(pl.multiple_of(i * T, T), T)
        src = pl.ds(pl.multiple_of(lax.rem(i, per) * T, T), T)
        own = i < per
        x = jnp.where(own, xo[src, :], xx[src, :]).astype(f32)
        a = jnp.concatenate([am[sl, :], at[sl, :]], axis=1)
        m = x + dot(a, wo[...])
        mid[sl, :] = m
        fo[sl, :] = m
        h_s[sl, :] = norm(m, gn)[2]
        ct = jnp.where(own, co[src, :], cx[src, :])
        g_s[sl, :] = jnp.where(valid_rows(meta, i, rows), ct, jnp.zeros_like(ct))
        dh[sl, :] = jnp.zeros((T, width), f32)
        return carry

    lax.fori_loop(0, n, first_rows, 0)

    R = 512
    C = 768

    gus, gds = (gu0, gu1, gu2, gu3), (gd0, gd1, gd2, gd3)

    def stores(n_, slot):
        return [
            pltpu.make_async_copy(stu.at[slot], gus[n_], sg.at[slot, 0]),
            pltpu.make_async_copy(std.at[slot], gds[n_].at[pl.ds(0, width), :], sg.at[slot, 1]),
        ]

    def shard(k, carry):
        for cp in (
            pltpu.make_async_copy(u_o, wus.at[k], sw.at[k, 0]),
            pltpu.make_async_copy(d_o, wds.at[k], sw.at[k, 1]),
        ):
            cp.wait()

        def rows_step(t, c2):
            sl = pl.ds(pl.multiple_of(t * R, R), R)
            h, g = h_s[sl, :], g_s[sl, :]
            r = jnp.maximum(dot(h, wus[k]), 0.0)
            a = (r * r).astype(bf16)
            d = (dot(g, wds[k], NT) * 2.0 * r).astype(bf16)
            act[sl, :] = a
            du[sl, :] = d
            fo[sl, :] += dot(a, wds[k])
            dh[sl, :] += dot(d, wus[k], NT)
            return c2

        lax.fori_loop(0, 2 * rows // R, rows_step, 0)
        slot = lax.rem(k, 2)

        @pl.when(k >= 2)
        def _():
            for cp in stores(0, slot):
                cp.wait()

        def cols_step(t, c2):
            sl = pl.ds(pl.multiple_of(t * C, C), C)
            stu[slot, :, sl] = dot(h_s[...], du[:, sl], TN).astype(bf16)
            std[slot, sl, :] = dot(act[:, sl], g_s[...], TN).astype(bf16)
            return c2

        lax.fori_loop(0, width // C, cols_step, 0)
        for n_ in range(4):

            @pl.when(k == n_)
            def _(n_=n_):
                for cp in stores(n_, n_ % 2):
                    cp.start()

        return carry

    lax.fori_loop(0, 4, shard, 0)
    gg[...] = jnp.zeros_like(gg)

    def last_rows(i, carry):
        sl = pl.ds(pl.multiple_of(i * T, T), T)
        dst = pl.ds(pl.multiple_of(lax.rem(i, per) * T, T), T)
        ok = valid_rows(meta, i, rows)
        m = mid[sl, :]
        out = jnp.where(ok, fo[sl, :], 0.0)

        fo[sl, :] = out

        @pl.when(i < per)
        def _():
            own = oo.at[meta[2] // 2, dst, :]
            pltpu.make_async_copy(fo.at[sl, :], own, sd.at[1]).start()

        @pl.when(i >= per)
        def _():
            ox[dst, :] = out.astype(bf16)

        nm, inv, _ = norm(m, gn)
        d = dh[sl, :]
        dn = d * gn
        r = g_s[sl, :].astype(f32) + inv * (dn - nm * jnp.mean(dn * nm, axis=-1, keepdims=True))
        mid[sl, :] = r
        pltpu.make_async_copy(mid.at[sl, :], dmid.at[sl, :], sd.at[0]).start()
        db = r.astype(bf16)
        du[sl, :] = db
        da = dot(db, wo[...], NT).astype(bf16)
        dm[sl, :] = da[:, :half]
        dt[sl, :] = da[:, half:]
        gg[...] += jnp.sum(d * nm, axis=0, keepdims=True)
        return carry

    lax.fori_loop(0, n, last_rows, 0)
    gacc[0:half, :] = dot(am[...], du[...], TN)
    gacc[half:, :] = dot(at[...], du[...], TN)
    outs = [
        pltpu.make_async_copy(mid, dmid, sd.at[0]),
        pltpu.make_async_copy(fo.at[pl.ds(0, rows), :], oo.at[meta[2] // 2], sd.at[1]),
    ]
    for k, k_ in enumerate((1, 3, 0, 2)):
        shard_ = jnp.bitwise_xor(meta[2], k_)
        row = jnp.where(shard_ // 2 == core_of(meta), 0, half) + lax.rem(shard_, 2) * part
        sto[k] = gacc[pl.ds(pl.multiple_of(row, 64), part), :].astype(bf16)
        cp = pltpu.make_async_copy(sto.at[k], gds[k].at[pl.ds(width, part), :], st.at[k])
        cp.start()
        outs.append(cp)
    for slot in range(2):
        outs.extend(stores(2 + slot, slot))
    for cp in outs:
        cp.wait()


def ffn_call(meta, xo, xx, co, cx, am, at, gain, wos, ffs):
    rows, width = xo.shape
    half = am.shape[1]
    part = half // 2
    hid = ffs[0].shape[1]
    hbm = pl.BlockSpec(memory_space=pl.ANY)
    vm = lambda *shape: whole(shape)
    all_rows = 2 * rows
    return pl.pallas_call(
        ffn_body,
        out_shape=[
            sds((2, rows, width), f32),
            sds((rows, width), bf16),
            sds((all_rows, half), bf16),
            sds((all_rows, half), bf16),
            sds((1, width), f32),
            sds((all_rows, width), f32),
        ]
        + [sds((width, hid), bf16)] * 4
        + [sds((hid + part, width), bf16)] * 4,
        grid_spec=grid_spec(
            (1,),
            [vm(rows, width)] * 4 + [vm(all_rows, half)] * 2 + [vm(1, width)] + [hbm] * 14,
            [
                hbm,
                vm(rows, width),
                vm(all_rows, half),
                vm(all_rows, half),
                vm(1, width),
            ]
            + [hbm] * 9,
            [
                pltpu.VMEM((width, width), bf16),
                pltpu.VMEM((4, width, hid), bf16),
                pltpu.VMEM((4, hid, width), bf16),
                pltpu.VMEM((all_rows, width), f32),
                pltpu.VMEM((all_rows, width), bf16),
                pltpu.VMEM((all_rows, width), bf16),
                pltpu.VMEM((all_rows, width), f32),
                pltpu.VMEM((all_rows, width), f32),
                pltpu.VMEM((all_rows, hid), bf16),
                pltpu.VMEM((all_rows, hid), bf16),
                pltpu.VMEM((2, width, hid), bf16),
                pltpu.VMEM((2, hid, width), bf16),
                pltpu.VMEM((4, part, width), bf16),
                pltpu.VMEM((width, width), f32),
                pltpu.SemaphoreType.DMA((4, 2)),
                pltpu.SemaphoreType.DMA((4,)),
                pltpu.SemaphoreType.DMA((2, 2)),
                pltpu.SemaphoreType.DMA((2,)),
                pltpu.SemaphoreType.DMA((4,)),
            ],
        ),
        cost_estimate=cost(
            48 * all_rows * width * hid + 6 * all_rows * width * width, 40 * all_rows * width
        ),
        compiler_params=pltpu.CompilerParams(vmem_limit_bytes=62 * 2**20),
        name="ffn",
    )(meta, xo, xx, co, cx, am, at, gain, *wos, *ffs)


def projg_body(meta, h, dm, dt, keep, far, send, acc):
    rows = dm.shape[0]
    acc[...] = dot(h[0:rows, :], dm[...], TN) + dot(h[rows:, :], dt[...], TN)
    part = keep.shape[0]
    for ref, k, row in ((keep, 0, 0), (far, 2, 0), (send, 1, 0), (send, 3, part)):
        at = jnp.bitwise_xor(meta[2], k)
        ref[row : row + part, :] = acc[pl.ds(pl.multiple_of(at * part, 64), part), :].astype(bf16)


def projg_call(meta, h, dm, dt):
    length, width = h.shape
    cols = dm.shape[1]
    step = cols // 3
    d = pl.BlockSpec((length // 2, step), lambda j, m: (0, j))
    g = lambda rows: pl.BlockSpec((rows, step), lambda j, m: (0, j))
    part = width // 4
    return pl.pallas_call(
        projg_body,
        out_shape=[sds((rows, cols), bf16) for rows in (part, part, 2 * part)],
        grid_spec=grid_spec(
            (3,),
            [whole((length, width)), d, d],
            [g(part), g(part), g(2 * part)],
            [pltpu.VMEM((width, step), f32)],
        ),
        cost_estimate=cost(length, length),
        name="projg",
    )(meta, h, dm, dt)


def last_body(meta, xo, xx, dm, dt, wm, wt, dmid, gain, go, gx, gg):
    i = pl.program_id(0)
    per = pl.num_programs(0) // 2
    first = i < per
    x = jnp.where(first, xo[...], xx[...]).astype(f32)
    gn = gain[...].astype(f32)
    n, inv, _ = norm(x, gn)
    dh = dot(dm[...], wm[...], NT) + dot(dt[...], wt[...], NT)
    dn = dh * gn
    out = dmid[...] + inv * (dn - n * jnp.mean(dn * n, axis=-1, keepdims=True))

    @pl.when(first)
    def _():
        go[0] = out

    @pl.when(jnp.logical_not(first))
    def _():
        gx[...] = out.astype(bf16)

    ps = jnp.sum(dh * n, axis=0, keepdims=True)

    @pl.when(i == 0)
    def _():
        gg[...] = ps

    @pl.when(i > 0)
    def _():
        gg[...] += ps


def own_map(per):
    return lambda i, m: (jnp.minimum(i, per - 1), 0)


def nb_map(per):
    return lambda i, m: (jnp.maximum(i - per, 0), 0)


def last_call(meta, xo, xx, dm, dt, wm, wt, dmid, gain):
    rows, width = xo.shape
    cols = dm.shape[1]
    per = rows // T
    fst, snd = pl.BlockSpec((T, width), own_map(per)), pl.BlockSpec((T, width), nb_map(per))
    blk = lambda n: pl.BlockSpec((T, n), lambda i, m: (i, 0))
    return pl.pallas_call(
        last_body,
        out_shape=[sds((2, rows, width), f32), sds((rows, width), bf16), sds((1, width), f32)],
        grid_spec=grid_spec(
            (2 * per,),
            [fst, snd, blk(cols), blk(cols)]
            + [whole((width, cols))] * 2
            + [blk(width), whole((1, width))],
            [
                pl.BlockSpec((1, T, width), lambda i, m: (x_of(m), jnp.minimum(i, per - 1), 0)),
                snd,
                pl.BlockSpec((1, width), lambda i, m: (0, 0)),
            ],
        ),
        cost_estimate=cost(rows, rows),
        name="last",
    )(meta, xo, xx, dm, dt, wm, wt, dmid, gain)


def flip(size, bit):
    return [(i, i ^ bit) for i in range(size)]


def core_swap(v):
    return lax.ppermute(v, "head", CORE)


def x_swap(v):
    return lax.ppermute(v, "head", XNB)


def after(v, *deps):
    return lax.optimization_barrier((v, *deps))[0]


def halve(terms, index, count):
    rows = terms[0].shape[0] // count
    piece = lambda t, k: lax.dynamic_slice_in_dim(t, jnp.bitwise_xor(index, k) * rows, rows, 0)
    total = lambda k: sum(piece(t, k).astype(f32) for t in terms)
    return [total(k).astype(bf16) for k in range(1, count)], total(0)


def strides(dp):
    out = [1]
    while 2 * out[-1] < dp:
        out.append(2 * out[-1])
    return out


def side(stride):
    return lax.axis_index("dp") // stride % 2


def swap(v, stride, dp):
    return lax.ppermute(v, "dp", flip(dp, stride))


def rows_as(got, vs):
    out, row = [], 0
    for v in vs:
        out.append(got[row : row + v.shape[0]])
        row += v.shape[0]
    return out


def swap_both(vs, stride, dp):
    return rows_as(swap(jnp.concatenate(vs, axis=0), stride, dp), vs)


def scatter(sums, stride, dp):
    halves = [halve(terms, side(stride), 2) for terms in sums]
    send = jnp.concatenate([h[0][0] for h in halves], axis=0)
    got = swap(send, stride, dp)
    out, row = [], 0
    for (part,), keep in halves:
        out.append([keep, got[row : row + part.shape[0]]])
        row += part.shape[0]
    return out, send


def join(mine, got, stride):
    upper = side(stride) == 1
    return jnp.concatenate([jnp.where(upper, got, mine), jnp.where(upper, mine, got)], axis=0)


def total(terms):
    return sum(t.astype(f32) for t in terms)


def local(dp, inputs, lengths, w_query, w_key, w_value, w_out, w_up, w_down, conv_taps, gain_attn, gain_ff, cotangent):
    hd = lax.axis_index("head")
    x, c, y = hd // 2, hd % 2, lax.axis_index("dp") % 2
    q = lax.axis_index("dp") % 4
    width = inputs.shape[2]
    part = w_query.shape[0]
    half = 2 * part
    pick = lambda v, k: lax.dynamic_index_in_dim(v, k, 0, keepdims=False)
    y_swap = lambda v: lax.ppermute(v, "dp", flip(dp, 1))
    order = lambda own, nb: lax.dynamic_update_slice_in_dim(own, nb[None].astype(f32), 1 - x, 0)
    meta = jnp.concatenate([lengths, jnp.stack([hd, q])]).astype(jnp.int32)
    gain1, gain2 = gain_attn.reshape(1, width), gain_ff.reshape(1, width)

    mask = (jnp.arange(2) == c)[None, None, :, None]
    tap_rows = jnp.where(mask, conv_taps.transpose(1, 0, 2)[:, :, None, :], 0).reshape(3, 3 * half)
    tap_rows = jnp.concatenate([tap_rows[:, :width], jnp.pad(tap_rows[:, width:], ((0, 0), (0, half)))], axis=0)
    tap_rows = jnp.pad(tap_rows, ((0, 10), (0, 0)))

    def packed(k):
        cut = lambda w: lax.dynamic_slice_in_dim(w, k * half, half, 1)
        fold = cut(w_value)
        return jnp.concatenate(
            [
                jnp.concatenate([cut(w_query), cut(w_key)], axis=1),
                jnp.concatenate([fold[: part // 2], fold[part // 2 :]], axis=1),
                tap_rows,
            ],
            axis=0,
        )

    w_core = core_swap(packed(1 - c))
    w_mine = packed(c)
    x_own = pick(inputs, x)
    rows = x_own.shape[0]
    x_nb = x_swap(pick(inputs, 1 - x))
    pack = x_swap(jnp.concatenate([w_mine, w_core], axis=0))
    x_core = core_swap(x_own)
    count = width // 4
    quarter = lambda w: lax.dynamic_slice_in_dim(w, q * count, count, 0)
    wo_c = core_swap(w_out)
    c_own = pick(cotangent, x)
    ff_src = jnp.stack([quarter(w_up), quarter(w_down)])
    ff_own = jnp.stack([w_up, w_down])
    pack2 = jnp.concatenate([pick(cotangent, 1 - x), w_out, wo_c], axis=0)
    x_nb, ff_src, ff_own, pack2, c_own, meta, x_core, pack = lax.optimization_barrier(
        (x_nb, ff_src, ff_own, pack2, c_own, meta, x_core, pack)
    )
    x_cnb = core_swap(x_nb)
    h1, raw, mix, w_full, taps = qkv_call(meta, x_own, x_nb, x_core, x_cnb, w_mine, w_core, pack, gain1)

    ff_first, pack2 = x_swap(ff_src), x_swap(pack2)
    ff_c = core_swap(ff_own)
    src = after(ff_first, mix)
    ff_n = [swap(src, k, dp) for k in (1, 2, 3)]
    a_mine, a_send, lse = att_fwd_call(meta, after(mix, src, ff_c))
    a_got = core_swap(a_send)
    w_other = core_swap(w_full)
    *ff_n, pack2 = lax.optimization_barrier((*ff_n, pack2, a_mine))[:-1]
    ff_n = [src, *ff_n]
    ff_cn = [core_swap(v) for v in ff_n]
    out_own, out_nb, d_mine, d_send, gg2, dmid, *gw = ffn_call(
        meta, x_own, x_nb, c_own, pack2, a_mine, a_got, after(gain2, w_other),
        (w_out, wo_c, pack2),
        (w_up, w_down, ff_c, *ff_n, *ff_cn),
    )
    d_got = core_swap(d_send)

    _, *rest = strides(dp)
    un, dn, do, uo = [core_swap(gw[k]) for k in (1, 5, 4, 0)]
    nu = total((gw[3], un)).astype(bf16)
    xu = x_swap(nu)
    (dn_send,), dn_keep = halve((gw[7], dn), y, 2)
    (do_send,), do_keep = halve((gw[6], do), y, 2)
    yn, yo = y_swap(dn_send), y_swap(do_send)
    out_x = x_swap(after(out_nb, nu))
    pairs = width // 256
    bwd = lambda m, p, n, into: att_bwd_call(
        meta, m, raw, a_mine, a_send, d_mine, d_got, lse, taps, p, n, into
    )
    *dall, gt_a = bwd(after(mix, nu, dn_send, do_send), 0, pairs - 1, None)
    xu, yn, yo, out_x = lax.optimization_barrier((xu, yn, yo, out_x, gt_a))[:4]
    (u_send,), u_keep = halve((gw[2], uo, xu), y, 2)
    nd = total((dn_keep, yn)).astype(bf16)
    yu, xd = y_swap(u_send), x_swap(nd)
    p_mine, p_theirs, gt_b = bwd(after(mix, u_send, nd), pairs - 1, 1, dall)
    p_got = core_swap(p_theirs)
    gt = jnp.concatenate([gt_a, gt_b], axis=1)
    yu, xd = lax.optimization_barrier((yu, xd, gt_b))[:2]
    sums, sent = scatter([[u_keep, yu], [do_keep, yo, xd]], rest[0], dp)
    keep, far, send = projg_call(meta, after(h1, sent), p_mine, p_theirs)
    flat = lax.optimization_barrier((*sums[0], *sums[1], keep))[:-1]
    sums, sent = scatter([flat[:2], flat[2:]], rest[1], dp)
    got = core_swap(after(send, sent))
    far, far2 = x_swap(far), x_swap(got[part:])
    gi_own, gi_nb, gg1 = last_call(
        meta, x_own, x_nb, p_mine, p_got, w_full, w_other, after(dmid, sent), gain1
    )
    *flat, gt, gg1 = lax.optimization_barrier((*sums[0], *sums[1], gt, x_swap(core_swap(gg1))))
    sums = [flat[:2], flat[2:]]
    for stride in rest[2:]:
        sums, _ = scatter(sums, stride, dp)
    vs = [total(t).astype(bf16) for t in sums]
    far, far2 = lax.optimization_barrier((far, far2, *vs))[:2]
    ga, gb = keep.astype(f32) + far.astype(f32), got[:part].astype(f32) + far2.astype(f32)
    g_send, g_keep = jnp.where(y == 0, gb, ga).astype(bf16), jnp.where(y == 0, ga, gb)
    pt = [g_keep, y_swap(g_send)]
    gi_got = x_swap(after(gi_nb, g_send))
    for stride in reversed(rest[1:]):
        cat = jnp.concatenate(vs, axis=0)
        first_cat = cat if stride == rest[-1] else first_cat
        got_v = swap(cat, stride, dp)
        vs = [join(v, g, stride) for v, g in zip(vs, rows_as(got_v, vs))]
    (pt,), sent = scatter([pt], rest[0], dp)
    packed_vs = jnp.concatenate(vs, axis=0)
    near_got = swap(packed_vs, rest[0], dp)
    across = rows_as(y_swap(packed_vs), vs)
    for stride in rest[1:]:
        (pt,), _ = scatter([pt], stride, dp)
    others, also = rows_as(near_got, vs), rows_as(y_swap(near_got), vs)
    ps = after(total(pt).astype(bf16), near_got)
    for stride in reversed(rest):
        ps = join(ps, swap(ps, stride, dp), stride)
    ps_got = y_swap(ps)
    whole_of = lambda k: join(
        join(vs[k], others[k], rest[0]), join(across[k], also[k], rest[0]), 1
    ).astype(f32)
    grad_up, gd_all = whole_of(0), whole_of(1)
    grad_down, grad_out = gd_all[: w_down.shape[0]], gd_all[w_down.shape[0] :]
    lo, hi = jnp.where(y == c, ps, ps_got), jnp.where(y == c, ps_got, ps)
    third = lambda v, w: v[:, w * half : w * half + half]
    grads = [jnp.concatenate([third(lo, w), third(hi, w)], axis=1).astype(f32) for w in range(3)]

    gt = gt[:9].reshape(9, 2, part).transpose(1, 0, 2)
    gt = jnp.where(jnp.arange(2)[:, None, None, None] == c, gt[None], 0.0).reshape(4, 9, part)
    gains = jnp.concatenate([gg1, gg2], axis=0).reshape(2, 4, part).transpose(1, 0, 2)
    small = jnp.concatenate([gt, gains, jnp.zeros((4, 5, part), f32)], axis=1)
    small = after(small, near_got)
    small = jnp.broadcast_to(small[:, None], (4, dp, 16, part)).reshape(4 * dp, 16, part)
    small = jnp.sum(lax.all_to_all(small, ("head", "dp"), 0, 0, tiled=True), axis=0)
    output = order(after(out_own, g_send), out_x)
    grad_input = order(after(gi_own, ps), gi_got)
    return (
        output,
        grad_input,
        *grads,
        grad_out,
        grad_up,
        grad_down,
        small[:9].reshape(3, 3, part),
        small[9],
        small[10],
    )


def solution(mesh):
    placed = (
        P("dp", "head", None),
        P("dp"),
        P("head", None),
        P("head", None),
        P("head", None),
        P("head", None),
        P(None, "head"),
        P("head", None),
        P(None, None, "head"),
        P(),
        P(),
        P("dp", "head", None),
    )
    return jax.shard_map(
        functools.partial(local, mesh.shape["dp"]),
        mesh=mesh,
        in_specs=placed,
        out_specs=(
            P("dp", "head", None),
            P("dp", "head", None),
            P("head", None),
            P("head", None),
            P("head", None),
            P("head", None),
            P(None, "head"),
            P("head", None),
            P(None, None, "head"),
            P("head"),
            P("head"),
        ),
        check_vma=False,
    )
```

```python
import functools

import jax
import jax.numpy as jnp
from jax import lax
from jax.experimental import pallas as pl
from jax.experimental.pallas import tpu as pltpu
from jax.sharding import PartitionSpec as P

HDIM = 64
EPS = 1e-06
bf16 = jnp.bfloat16
f32 = jnp.float32

NN = (((1,), (0,)), ((), ()))
NT = (((1,), (1,)), ((), ()))
TN = (((0,), (0,)), ((), ()))

CORE = [(0, 1), (1, 0), (2, 3), (3, 2)]
XNB = [(0, 2), (2, 0), (1, 3), (3, 1)]


def dot(a, b, dims=NN):
    return lax.dot_general(a, b, dims, preferred_element_type=f32)


def cost(flops, nbytes, trans=0):
    return pl.CostEstimate(flops=int(flops), bytes_accessed=int(nbytes), transcendentals=int(trans))


def sds(shape, dtype):
    return jax.ShapeDtypeStruct(shape, dtype)


def whole(shape):
    zeros = (0,) * len(shape)
    return pl.BlockSpec(shape, lambda *_: zeros, pipeline_mode=pl.Buffered(1))


def grid_spec(grid, ins, outs, scratch=()):
    return pltpu.PrefetchScalarGridSpec(
        num_scalar_prefetch=1, grid=grid, in_specs=ins, out_specs=outs, scratch_shapes=scratch
    )


def length_of(m):
    return m[m[2] // 2]


def x_of(m):
    return m[2] // 2


def core_of(m):
    return lax.rem(m[2], 2)


def slot_of(m, b):
    v = jnp.bitwise_xor(m[2], b)
    return lax.rem(v, 2) * 2 + v // 2


def norm(x, gain):
    inv = lax.rsqrt(jnp.mean(x * x, axis=-1, keepdims=True) + EPS)
    n = x * inv
    return n, inv, (n * gain).astype(bf16)


def qkv_body(meta, x0, x1, x2, x3, wa, wb, pack, gain, h_ref, raw_ref, mix_ref, w_ref, taps, ext):
    b = pl.program_id(0)
    rows = x0.shape[0]
    part = w_ref.shape[0] // 4
    width = x0.shape[1]
    tall = wa.shape[0]
    hd = meta[2]

    @pl.when(b == 0)
    def _():
        def put(k, ref, first):
            at = jnp.bitwise_xor(hd, k) * part
            w_ref[pl.ds(pl.multiple_of(at, 64), part), 0:width] = ref[first : first + part, :]
            for n in range(2):
                row = pl.multiple_of(at + n * (part // 2), 32)
                w_ref[pl.ds(row, part // 2), width:] = ref[
                    first + part : first + part + part // 2, n * (width // 2) : (n + 1) * (width // 2)
                ]

        put(0, wa, 0)
        put(1, wb, 0)
        put(2, pack, 0)
        put(3, pack, tall)
        last = lambda ref, end: ref[end - 16 : end, :].astype(f32)
        near = last(wa, tall) + last(wb, tall)
        far = last(pack, tall) + last(pack, 2 * tall)
        t = jnp.where(x_of(meta) == core_of(meta), near, far)
        taps[...] = jnp.zeros_like(taps)
        taps[0:3, 0:width] = t[0:3]
        taps[0:3, width:] = t[3:6, 0 : width // 2]
        ext[0:8, :] = jnp.zeros((8, ext.shape[1]), f32)

    slot = slot_of(meta, b)
    step = ext.shape[0] - 8

    def some(n, carry):
        sl = pl.ds(pl.multiple_of(n * step, step), step)
        x = x0[sl, :]
        for k, other in ((1, x1), (2, x2), (3, x3)):
            x = jnp.where(slot == k, other[sl, :], x)
        _, _, h = norm(x.astype(f32), gain[...].astype(f32))
        h_ref[sl, :] = h
        raw = dot(h, w_ref[...]).astype(bf16)
        raw_ref[sl, :] = raw
        rawf = raw.astype(f32)
        ext[8:, :] = rawf
        t = taps[...]
        mixed = t[0:1] * rawf + t[1:2] * ext[7 : 7 + step, :] + t[2:3] * ext[6 : 6 + step, :]
        mix_ref[sl, :] = mixed.astype(bf16)
        ext[0:8, :] = ext[step:, :]
        return carry

    lax.fori_loop(0, rows // step, some, 0)


def qkv_call(meta, x_own, x_nb, x_core, x_cnb, w_mine, w_core, pack, gain):
    rows, width = x_own.shape
    tall = w_mine.shape[0]
    cols = width * 3 // 2
    length = 4 * rows
    blk = lambda n: pl.BlockSpec((rows, n), lambda b, m: (b, 0))
    const = lambda r: pl.BlockSpec((r, cols), lambda b, m: (0, 0))
    return pl.pallas_call(
        qkv_body,
        out_shape=[
            sds((length, width), bf16),
            sds((length, cols), bf16),
            sds((length, cols), bf16),
            sds((width, cols), bf16),
            sds((8, cols), f32),
        ],
        grid_spec=grid_spec(
            (4,),
            [whole((rows, width))] * 4
            + [whole((tall, width))] * 2
            + [whole(pack.shape), whole((1, width))],
            [
                pl.BlockSpec((rows, width), lambda b, m: (slot_of(m, b), 0)),
                blk(cols),
                blk(cols),
                const(width),
                const(8),
            ],
            [pltpu.VMEM((T + 8, cols), f32)],
        ),
        cost_estimate=cost(2 * length * width * cols, 2 * length * (width * 2 + cols * 2)),
        name="qkv",
    )(meta, x_own, x_nb, x_core, x_cnb, w_mine, w_core, pack, gain)


def two_heads(v):
    lane = lax.broadcasted_iota(jnp.int32, v.shape, 1)
    z = jnp.zeros_like(v)
    return jnp.concatenate([jnp.where(lane < HDIM, v, z), jnp.where(lane < HDIM, z, v)], axis=0)


def causal(first, keys, start, queries):
    key = first + lax.broadcasted_iota(jnp.int32, (keys, queries), 0)
    ok = key <= start + lax.broadcasted_iota(jnp.int32, (keys, queries), 1)
    return jnp.concatenate([ok, ok], axis=1)


def upper(v, axis):
    B = v.shape[axis] // 2
    h = B // 2
    if axis == 0:
        return jnp.concatenate([v[h:B], v[B + h :]], axis=0)
    return jnp.concatenate([v[:, h:B], v[:, B + h :]], axis=1)


def with_bias(k_ref, ka, length):
    L = k_ref.shape[0]
    ka[:, :128] = k_ref[...]
    lane = lax.broadcasted_iota(jnp.int32, (L, 128), 1)
    row = lax.broadcasted_iota(jnp.int32, (L, 128), 0)
    pad = jnp.logical_and(lane == 0, row >= length)
    ka[:, 128:] = jnp.where(pad, -1e9, 0.0).astype(bf16)


def biased(q):
    qq = two_heads(q)
    lane = lax.broadcasted_iota(jnp.int32, qq.shape, 1)
    return jnp.concatenate([qq, jnp.where(lane == 0, 1.0, 0.0).astype(bf16)], axis=1)


def att_fwd_body(meta, q_ref, k_ref, v_ref, mine_ref, theirs_ref, lse_ref, ka, vt, sc):
    i = pl.program_id(1)
    B = q_ref.shape[0]

    @pl.when(i == 0)
    def _():
        vt[...] = v_ref[...].T
        with_bias(k_ref, ka, length_of(meta))

    qq = biased(q_ref[...] * bf16(HDIM**-0.5))
    own = lax.rem(i, 2) == core_of(meta)

    def run(ii):
        m = None
        for j in range(ii + 1):
            ks = slice(j * B, j * B + B)
            s = dot(ka[ks, :], qq, NT)
            if j == ii:
                s = jnp.where(causal(0, B, 0, B), s, -1e9)
            sc[ks, :] = s
            mj = jnp.max(s, axis=0, keepdims=True)
            m = mj if m is None else jnp.maximum(m, mj)
        l = jnp.zeros((1, 2 * B), f32)
        acc = [jnp.zeros((HDIM, B), f32)] * 2
        for j in range(ii + 1):
            ks = slice(j * B, j * B + B)
            p = jnp.exp(sc[ks, :] - m)
            l = l + jnp.sum(p, axis=0, keepdims=True)
            pb = p.astype(bf16)
            for h in range(2):
                r = slice(HDIM * h, HDIM * h + HDIM)
                acc[h] = acc[h] + dot(vt[r, ks], pb[:, h * B : h * B + B])
        inv = 1.0 / l
        out = jnp.concatenate([acc[h] * inv[:, h * B : h * B + B] for h in range(2)], axis=0)
        out = out.T.astype(bf16)

        @pl.when(own)
        def _():
            mine_ref[...] = out

        @pl.when(jnp.logical_not(own))
        def _():
            theirs_ref[...] = out

        ls = m + jnp.log(l)
        lse_ref[0] = jnp.concatenate([ls[:, :B], ls[:, B:]], axis=0)

    for ii in range(4):
        pl.when(i == ii)(functools.partial(run, ii))


def half_map(p, i, m):
    return (jnp.bitwise_xor(i // 2, x_of(m)), p)


def att_fwd_call(meta, mix):
    length, cols = mix.shape
    width = cols // 3
    pairs = width // 128
    B = length // 4
    half = pl.BlockSpec((B, 128), half_map)
    return pl.pallas_call(
        att_fwd_body,
        out_shape=[
            sds((length // 2, width), bf16),
            sds((length // 2, width), bf16),
            sds((pairs, 2, length), f32),
        ],
        grid_spec=grid_spec(
            (pairs, 4),
            [
                pl.BlockSpec((B, 128), lambda p, i, m: (i, p)),
                pl.BlockSpec((length, 128), lambda p, i, m: (0, pairs + p)),
                pl.BlockSpec((length, 128), lambda p, i, m: (0, 2 * pairs + p)),
            ],
            [half, half, pl.BlockSpec((1, 2, B), lambda p, i, m: (p, 0, i))],
            [
                pltpu.VMEM((length, 256), bf16),
                pltpu.VMEM((128, length), bf16),
                pltpu.VMEM((length, 2 * B), f32),
            ],
        ),
        cost_estimate=cost(8 * length * length * width, 8 * length * width, 2 * length * length * pairs),
        name="attn_fwd",
    )(meta, mix, mix, mix)


def att_bwd_body(
    p0, aliased, meta, q_ref, k_ref, v_ref, om, ot, dm, dt, lse_ref, rq, rk, rv, taps, *refs
):
    gm_ref, gt_ref, gt, ka, kt, dkt, dvt, dqt, dqs, ext, stage, sem = refs[2:] if aliased else refs
    i = pl.program_id(1)
    B = q_ref.shape[0]
    L = k_ref.shape[0]
    H = B // 2

    @pl.when(i == 0)
    def _():
        kt[...] = k_ref[...].T
        with_bias(k_ref, ka, length_of(meta))

    own = lax.rem(i, 2) == core_of(meta)
    q = q_ref[...] * bf16(HDIM**-0.5)
    o = jnp.where(own, om[...], ot[...])
    do = jnp.where(own, dm[...], dt[...])
    qq, dd = biased(q), two_heads(do)
    qt, dot_ = q.T, do.T
    od = (o.astype(f32) * do.astype(f32)).T
    delta = jnp.concatenate(
        [jnp.sum(od[:HDIM], axis=0, keepdims=True), jnp.sum(od[HDIM:], axis=0, keepdims=True)],
        axis=1,
    )
    ls = lse_ref[0]
    lse = jnp.concatenate([ls[0:1], ls[1:2]], axis=1)

    dqt[...] = jnp.zeros_like(dqt)

    def tile(st, n, lo, diagonal):
        w = B - lo
        ks = pl.ds(pl.multiple_of(st, H), n)
        part = upper if lo else lambda v, axis: v
        s = dot(ka[ks, :], part(qq, 0), NT)
        dp = dot(v_ref[ks, :], part(dd, 0), NT)
        p = jnp.exp(s - part(lse, 1))
        if diagonal:
            p = jnp.where(causal(lo, n, lo, w), p, 0.0)
        ds = (p * (dp - part(delta, 1))).astype(bf16)
        pb = p.astype(bf16)
        for h in range(2):
            r, c = slice(HDIM * h, HDIM * h + HDIM), slice(h * w, h * w + w)
            dqt[r, lo:] += dot(kt[r, ks], ds[:, c])
            a = dot(qt[r, lo:], ds[:, c], NT)
            b = dot(dot_[r, lo:], pb[:, c], NT)
            if diagonal:
                dkt[r, ks] = a
                dvt[r, ks] = b
            else:
                dkt[r, ks] += a
                dvt[r, ks] += b

    lax.fori_loop(0, i, lambda j, c: (tile(j * B, B, 0, False), c)[1], 0)
    tile(i * B, H, 0, True)
    tile(i * B + H, H, H, True)
    dqs[pl.ds(pl.multiple_of(i * B, B), B), :] = dqt[...].T * HDIM**-0.5

    def copies(pair):
        width = gm_ref.shape[1] // 3
        for b in range(L // B):
            to = pl.ds(pl.multiple_of(jnp.bitwise_xor(b // 2, x_of(meta)) * B, B), B)
            for k in range(3):
                col = pl.ds(pl.multiple_of(k * width + (p0 + pair) * 128, 128), 128)
                src = stage.at[k, pl.ds(b * B, B), :]
                yield b, lambda g, to=to, col=col, src=src, k=k: pltpu.make_async_copy(
                    src, g.at[to, col], sem.at[k]
                )

    def send(pair):
        for b, copy in copies(pair):
            own = core_of(meta) == b % 2

            @pl.when(own)
            def _(copy=copy):
                copy(gm_ref).start()

            @pl.when(jnp.logical_not(own))
            def _(copy=copy):
                copy(gt_ref).start()

    def finish(pair):
        for _, copy in copies(pair):
            copy(gm_ref).wait()

    @pl.when(i == pl.num_programs(1) - 1)
    def _():
        pair = pl.program_id(0)
        gt[...] = jnp.zeros_like(gt)
        ext[...] = jnp.zeros_like(ext)

        @pl.when(pair > 0)
        def _():
            finish(pair)

        def back(n, carry):
            blk = L // B - 1 - n
            sl = pl.ds(pl.multiple_of(blk * B, B), B)
            for which, raw in enumerate((rq, rk, rv)):
                col = which * (taps.shape[1] // 3) + (p0 + pl.program_id(0)) * 128
                t = taps[:, pl.ds(pl.multiple_of(col, 128), 128)]
                g = dqs[sl, :] if which == 0 else (dkt, dvt)[which - 1][:, sl].T
                ext[which, B : B + 8, :] = ext[which, 0:8, :]
                ext[which, 0:B, :] = g
                g1, g2 = ext[which, 1 : B + 1, :], ext[which, 2 : B + 2, :]
                stage[which, sl, :] = (t[0:1] * g + t[1:2] * g1 + t[2:3] * g2).astype(bf16)
                r = raw[sl, :].astype(f32)
                for k, gg in enumerate((g, g1, g2)):
                    row = slice(3 * which + k, 3 * which + k + 1)
                    gt[row, :] += jnp.sum(r * gg, axis=0, keepdims=True)
            return carry

        lax.fori_loop(0, L // B, back, 0)
        send(pair)

        @pl.when(pair == pl.num_programs(0) - 1)
        def _():
            finish(pair)


def att_bwd_call(meta, mix, raw, om, ot, dm, dt, lse, taps, p0, count, into=None):
    length, cols = mix.shape
    pairs = cols // 384
    B = length // 4
    half = pl.BlockSpec((B, 128), lambda p, i, m: (jnp.bitwise_xor(i // 2, x_of(m)), p0 + p))
    full = lambda k: pl.BlockSpec((length, 128), lambda p, i, m: (0, k * pairs + p0 + p))
    return pl.pallas_call(
        functools.partial(att_bwd_body, p0, into is not None),
        out_shape=[sds((length // 2, cols), bf16)] * 2 + [sds((16, 128 * count), f32)],
        grid_spec=grid_spec(
            (count, 4),
            [
                pl.BlockSpec((B, 128), lambda p, i, m: (i, p0 + p)),
                full(1),
                full(2),
                half,
                half,
                half,
                half,
                pl.BlockSpec((1, 2, B), lambda p, i, m: (p0 + p, 0, i)),
                full(0),
                full(1),
                full(2),
                whole((8, cols)),
            ]
            + ([] if into is None else [pl.BlockSpec(memory_space=pl.ANY)] * 2),
            [pl.BlockSpec(memory_space=pl.ANY)] * 2 + [pl.BlockSpec((16, 128), lambda p, i, m: (0, p))],
            [
                pltpu.VMEM((length, 256), bf16),
                pltpu.VMEM((128, length), bf16),
                pltpu.VMEM((128, length), f32),
                pltpu.VMEM((128, length), f32),
                pltpu.VMEM((128, B), f32),
                pltpu.VMEM((length, 128), f32),
                pltpu.VMEM((3, B + 8, 128), f32),
                pltpu.VMEM((3, length, 128), bf16),
                pltpu.SemaphoreType.DMA((3,)),
            ],
        ),
        cost_estimate=cost(
            14 * length * length * 128 * count, 20 * length * 128 * count, 2 * length * length * count
        ),
        name="attn_bwd",
        input_output_aliases={} if into is None else {13: 0, 14: 1},
    )(meta, mix, mix, mix, om, ot, dm, dt, lse, raw, raw, raw, taps, *(into or ()))


T = 256


def valid_rows(meta, i, rows):
    per = rows // T
    block = jnp.where(i < per, meta[2], jnp.bitwise_xor(meta[2], 2))
    start = block * rows + lax.rem(i, per) * T
    return start + lax.broadcasted_iota(jnp.int32, (T, 1), 0) < length_of(meta)


def ffn_body(
    meta, xo, xx, co, cx, am, at, gain, wo_o, wo_c, pack,
    u_o, d_o, f_c, n0, n1, n2, n3, c0, c1, c2, c3,
    oo, ox, dm, dt, gg, dmid, gu0, gu1, gu2, gu3, gd0, gd1, gd2, gd3,
    wo, wus, wds, mid, h_s, g_s, fo, dh, act, du, stu, std, sto, gacc, sw, so, sg, sd, st,
):
    rows, width = xo.shape
    part = wo_o.shape[0]
    half = 2 * part
    n = 2 * rows // T
    per = rows // T
    copies = []
    for k, src in ((0, wo_o), (1, wo_c), (2, pack.at[pl.ds(rows, part), :]), (3, pack.at[pl.ds(rows + part, part), :])):
        shard = jnp.bitwise_xor(meta[2], k)
        row = jnp.where(shard // 2 == core_of(meta), 0, half) + lax.rem(shard, 2) * part
        cp = pltpu.make_async_copy(src, wo.at[pl.ds(pl.multiple_of(row, 64), part), :], so.at[k])
        cp.start()
        copies.append(cp)
    for k, pair in ((0, (f_c.at[0], f_c.at[1])), (2, (u_o, d_o))):
        for n_, src in enumerate(pair):
            pltpu.make_async_copy(src, (wus, wds)[n_].at[k], sw.at[k, n_]).start()
    for k, quarters in ((1, (c0, c1, c2, c3)), (3, (n0, n1, n2, n3))):
        for q_, src in enumerate(quarters):
            count = src.shape[1]
            to = pl.ds(pl.multiple_of(jnp.bitwise_xor(meta[3], q_) * count, 64), count)
            for n_, dst in enumerate((wus, wds)):
                pltpu.make_async_copy(src.at[n_], dst.at[k, to, :], sw.at[k, n_]).start()
    for cp in copies:
        cp.wait()
    gn = gain[...].astype(f32)

    def first_rows(i, carry):
        sl = pl.ds(pl.multiple_of(i * T, T), T)
        src = pl.ds(pl.multiple_of(lax.rem(i, per) * T, T), T)
        own = i < per
        x = jnp.where(own, xo[src, :], xx[src, :]).astype(f32)
        a = jnp.concatenate([am[sl, :], at[sl, :]], axis=1)
        m = x + dot(a, wo[...])
        mid[sl, :] = m
        fo[sl, :] = m
        h_s[sl, :] = norm(m, gn)[2]
        ct = jnp.where(own, co[src, :], cx[src, :])
        g_s[sl, :] = jnp.where(valid_rows(meta, i, rows), ct, jnp.zeros_like(ct))
        dh[sl, :] = jnp.zeros((T, width), f32)
        return carry

    lax.fori_loop(0, n, first_rows, 0)

    R = 512
    C = 768

    gus, gds = (gu0, gu1, gu2, gu3), (gd0, gd1, gd2, gd3)

    def stores(n_, slot):
        return [
            pltpu.make_async_copy(stu.at[slot], gus[n_], sg.at[slot, 0]),
            pltpu.make_async_copy(std.at[slot], gds[n_].at[pl.ds(0, width), :], sg.at[slot, 1]),
        ]

    def shard(k, carry):
        for cp in (
            pltpu.make_async_copy(u_o, wus.at[k], sw.at[k, 0]),
            pltpu.make_async_copy(d_o, wds.at[k], sw.at[k, 1]),
        ):
            cp.wait()

        def rows_step(t, c2):
            sl = pl.ds(pl.multiple_of(t * R, R), R)
            h, g = h_s[sl, :], g_s[sl, :]
            r = jnp.maximum(dot(h, wus[k]), 0.0)
            a = (r * r).astype(bf16)
            d = (dot(g, wds[k], NT) * 2.0 * r).astype(bf16)
            act[sl, :] = a
            du[sl, :] = d
            fo[sl, :] += dot(a, wds[k])
            dh[sl, :] += dot(d, wus[k], NT)
            return c2

        lax.fori_loop(0, 2 * rows // R, rows_step, 0)
        slot = lax.rem(k, 2)

        @pl.when(k >= 2)
        def _():
            for cp in stores(0, slot):
                cp.wait()

        def cols_step(t, c2):
            sl = pl.ds(pl.multiple_of(t * C, C), C)
            stu[slot, :, sl] = dot(h_s[...], du[:, sl], TN).astype(bf16)
            std[slot, sl, :] = dot(act[:, sl], g_s[...], TN).astype(bf16)
            return c2

        lax.fori_loop(0, width // C, cols_step, 0)
        for n_ in range(4):

            @pl.when(k == n_)
            def _(n_=n_):
                for cp in stores(n_, n_ % 2):
                    cp.start()

        return carry

    lax.fori_loop(0, 4, shard, 0)
    gg[...] = jnp.zeros_like(gg)

    def last_rows(i, carry):
        sl = pl.ds(pl.multiple_of(i * T, T), T)
        dst = pl.ds(pl.multiple_of(lax.rem(i, per) * T, T), T)
        ok = valid_rows(meta, i, rows)
        m = mid[sl, :]
        out = jnp.where(ok, fo[sl, :], 0.0)

        fo[sl, :] = out

        @pl.when(i < per)
        def _():
            own = oo.at[meta[2] // 2, dst, :]
            pltpu.make_async_copy(fo.at[sl, :], own, sd.at[1]).start()

        @pl.when(i >= per)
        def _():
            ox[dst, :] = out.astype(bf16)

        nm, inv, _ = norm(m, gn)
        d = dh[sl, :]
        dn = d * gn
        r = g_s[sl, :].astype(f32) + inv * (dn - nm * jnp.mean(dn * nm, axis=-1, keepdims=True))
        mid[sl, :] = r
        pltpu.make_async_copy(mid.at[sl, :], dmid.at[sl, :], sd.at[0]).start()
        db = r.astype(bf16)
        du[sl, :] = db
        da = dot(db, wo[...], NT).astype(bf16)
        dm[sl, :] = da[:, :half]
        dt[sl, :] = da[:, half:]
        gg[...] += jnp.sum(d * nm, axis=0, keepdims=True)
        return carry

    lax.fori_loop(0, n, last_rows, 0)
    gacc[0:half, :] = dot(am[...], du[...], TN)
    gacc[half:, :] = dot(at[...], du[...], TN)
    outs = [
        pltpu.make_async_copy(mid, dmid, sd.at[0]),
        pltpu.make_async_copy(fo.at[pl.ds(0, rows), :], oo.at[meta[2] // 2], sd.at[1]),
    ]
    for k, k_ in enumerate((1, 3, 0, 2)):
        shard_ = jnp.bitwise_xor(meta[2], k_)
        row = jnp.where(shard_ // 2 == core_of(meta), 0, half) + lax.rem(shard_, 2) * part
        sto[k] = gacc[pl.ds(pl.multiple_of(row, 64), part), :].astype(bf16)
        cp = pltpu.make_async_copy(sto.at[k], gds[k].at[pl.ds(width, part), :], st.at[k])
        cp.start()
        outs.append(cp)
    for slot in range(2):
        outs.extend(stores(2 + slot, slot))
    for cp in outs:
        cp.wait()


def ffn_call(meta, xo, xx, co, cx, am, at, gain, wos, ffs):
    rows, width = xo.shape
    half = am.shape[1]
    part = half // 2
    hid = ffs[0].shape[1]
    hbm = pl.BlockSpec(memory_space=pl.ANY)
    vm = lambda *shape: whole(shape)
    all_rows = 2 * rows
    return pl.pallas_call(
        ffn_body,
        out_shape=[
            sds((2, rows, width), f32),
            sds((rows, width), bf16),
            sds((all_rows, half), bf16),
            sds((all_rows, half), bf16),
            sds((1, width), f32),
            sds((all_rows, width), f32),
        ]
        + [sds((width, hid), bf16)] * 4
        + [sds((hid + part, width), bf16)] * 4,
        grid_spec=grid_spec(
            (1,),
            [vm(rows, width)] * 4 + [vm(all_rows, half)] * 2 + [vm(1, width)] + [hbm] * 14,
            [
                hbm,
                vm(rows, width),
                vm(all_rows, half),
                vm(all_rows, half),
                vm(1, width),
            ]
            + [hbm] * 9,
            [
                pltpu.VMEM((width, width), bf16),
                pltpu.VMEM((4, width, hid), bf16),
                pltpu.VMEM((4, hid, width), bf16),
                pltpu.VMEM((all_rows, width), f32),
                pltpu.VMEM((all_rows, width), bf16),
                pltpu.VMEM((all_rows, width), bf16),
                pltpu.VMEM((all_rows, width), f32),
                pltpu.VMEM((all_rows, width), f32),
                pltpu.VMEM((all_rows, hid), bf16),
                pltpu.VMEM((all_rows, hid), bf16),
                pltpu.VMEM((2, width, hid), bf16),
                pltpu.VMEM((2, hid, width), bf16),
                pltpu.VMEM((4, part, width), bf16),
                pltpu.VMEM((width, width), f32),
                pltpu.SemaphoreType.DMA((4, 2)),
                pltpu.SemaphoreType.DMA((4,)),
                pltpu.SemaphoreType.DMA((2, 2)),
                pltpu.SemaphoreType.DMA((2,)),
                pltpu.SemaphoreType.DMA((4,)),
            ],
        ),
        cost_estimate=cost(
            48 * all_rows * width * hid + 6 * all_rows * width * width, 40 * all_rows * width
        ),
        compiler_params=pltpu.CompilerParams(vmem_limit_bytes=62 * 2**20),
        name="ffn",
    )(meta, xo, xx, co, cx, am, at, gain, *wos, *ffs)


def projg_body(meta, h, dm, dt, keep, far, send, acc):
    rows = dm.shape[0]
    acc[...] = dot(h[0:rows, :], dm[...], TN) + dot(h[rows:, :], dt[...], TN)
    part = keep.shape[0]
    for ref, k, row in ((keep, 0, 0), (far, 2, 0), (send, 1, 0), (send, 3, part)):
        at = jnp.bitwise_xor(meta[2], k)
        ref[row : row + part, :] = acc[pl.ds(pl.multiple_of(at * part, 64), part), :].astype(bf16)


def projg_call(meta, h, dm, dt):
    length, width = h.shape
    cols = dm.shape[1]
    step = cols // 3
    d = pl.BlockSpec((length // 2, step), lambda j, m: (0, j))
    g = lambda rows: pl.BlockSpec((rows, step), lambda j, m: (0, j))
    part = width // 4
    return pl.pallas_call(
        projg_body,
        out_shape=[sds((rows, cols), bf16) for rows in (part, part, 2 * part)],
        grid_spec=grid_spec(
            (3,),
            [whole((length, width)), d, d],
            [g(part), g(part), g(2 * part)],
            [pltpu.VMEM((width, step), f32)],
        ),
        cost_estimate=cost(length, length),
        name="projg",
    )(meta, h, dm, dt)


def last_body(meta, xo, xx, dm, dt, wm, wt, dmid, gain, go, gx, gg):
    i = pl.program_id(0)
    per = pl.num_programs(0) // 2
    first = i < per
    x = jnp.where(first, xo[...], xx[...]).astype(f32)
    gn = gain[...].astype(f32)
    n, inv, _ = norm(x, gn)
    dh = dot(dm[...], wm[...], NT) + dot(dt[...], wt[...], NT)
    dn = dh * gn
    out = dmid[...] + inv * (dn - n * jnp.mean(dn * n, axis=-1, keepdims=True))

    @pl.when(first)
    def _():
        go[0] = out

    @pl.when(jnp.logical_not(first))
    def _():
        gx[...] = out.astype(bf16)

    ps = jnp.sum(dh * n, axis=0, keepdims=True)

    @pl.when(i == 0)
    def _():
        gg[...] = ps

    @pl.when(i > 0)
    def _():
        gg[...] += ps


def own_map(per):
    return lambda i, m: (jnp.minimum(i, per - 1), 0)


def nb_map(per):
    return lambda i, m: (jnp.maximum(i - per, 0), 0)


def last_call(meta, xo, xx, dm, dt, wm, wt, dmid, gain):
    rows, width = xo.shape
    cols = dm.shape[1]
    per = rows // T
    fst, snd = pl.BlockSpec((T, width), own_map(per)), pl.BlockSpec((T, width), nb_map(per))
    blk = lambda n: pl.BlockSpec((T, n), lambda i, m: (i, 0))
    return pl.pallas_call(
        last_body,
        out_shape=[sds((2, rows, width), f32), sds((rows, width), bf16), sds((1, width), f32)],
        grid_spec=grid_spec(
            (2 * per,),
            [fst, snd, blk(cols), blk(cols)]
            + [whole((width, cols))] * 2
            + [blk(width), whole((1, width))],
            [
                pl.BlockSpec((1, T, width), lambda i, m: (x_of(m), jnp.minimum(i, per - 1), 0)),
                snd,
                pl.BlockSpec((1, width), lambda i, m: (0, 0)),
            ],
        ),
        cost_estimate=cost(rows, rows),
        name="last",
    )(meta, xo, xx, dm, dt, wm, wt, dmid, gain)


def flip(size, bit):
    return [(i, i ^ bit) for i in range(size)]


def core_swap(v):
    return lax.ppermute(v, "head", CORE)


def x_swap(v):
    return lax.ppermute(v, "head", XNB)


def after(v, *deps):
    return lax.optimization_barrier((v, *deps))[0]


def halve(terms, index, count):
    rows = terms[0].shape[0] // count
    piece = lambda t, k: lax.dynamic_slice_in_dim(t, jnp.bitwise_xor(index, k) * rows, rows, 0)
    total = lambda k: sum(piece(t, k).astype(f32) for t in terms)
    return [total(k).astype(bf16) for k in range(1, count)], total(0)


def strides(dp):
    out = [1]
    while 2 * out[-1] < dp:
        out.append(2 * out[-1])
    return out


def side(stride):
    return lax.axis_index("dp") // stride % 2


def swap(v, stride, dp):
    return lax.ppermute(v, "dp", flip(dp, stride))


def rows_as(got, vs):
    out, row = [], 0
    for v in vs:
        out.append(got[row : row + v.shape[0]])
        row += v.shape[0]
    return out


def swap_both(vs, stride, dp):
    return rows_as(swap(jnp.concatenate(vs, axis=0), stride, dp), vs)


def scatter(sums, stride, dp):
    halves = [halve(terms, side(stride), 2) for terms in sums]
    send = jnp.concatenate([h[0][0] for h in halves], axis=0)
    got = swap(send, stride, dp)
    out, row = [], 0
    for (part,), keep in halves:
        out.append([keep, got[row : row + part.shape[0]]])
        row += part.shape[0]
    return out, send


def join(mine, got, stride):
    upper = side(stride) == 1
    return jnp.concatenate([jnp.where(upper, got, mine), jnp.where(upper, mine, got)], axis=0)


def total(terms):
    return sum(t.astype(f32) for t in terms)


def local(dp, inputs, lengths, w_query, w_key, w_value, w_out, w_up, w_down, conv_taps, gain_attn, gain_ff, cotangent):
    hd = lax.axis_index("head")
    x, c, y = hd // 2, hd % 2, lax.axis_index("dp") % 2
    q = lax.axis_index("dp") % 4
    width = inputs.shape[2]
    part = w_query.shape[0]
    half = 2 * part
    pick = lambda v, k: lax.dynamic_index_in_dim(v, k, 0, keepdims=False)
    y_swap = lambda v: lax.ppermute(v, "dp", flip(dp, 1))
    order = lambda own, nb: lax.dynamic_update_slice_in_dim(own, nb[None].astype(f32), 1 - x, 0)
    meta = jnp.concatenate([lengths, jnp.stack([hd, q])]).astype(jnp.int32)
    gain1, gain2 = gain_attn.reshape(1, width), gain_ff.reshape(1, width)

    mask = (jnp.arange(2) == c)[None, None, :, None]
    tap_rows = jnp.where(mask, conv_taps.transpose(1, 0, 2)[:, :, None, :], 0).reshape(3, 3 * half)
    tap_rows = jnp.concatenate([tap_rows[:, :width], jnp.pad(tap_rows[:, width:], ((0, 0), (0, half)))], axis=0)
    tap_rows = jnp.pad(tap_rows, ((0, 10), (0, 0)))

    def packed(k):
        cut = lambda w: lax.dynamic_slice_in_dim(w, k * half, half, 1)
        fold = cut(w_value)
        return jnp.concatenate(
            [
                jnp.concatenate([cut(w_query), cut(w_key)], axis=1),
                jnp.concatenate([fold[: part // 2], fold[part // 2 :]], axis=1),
                tap_rows,
            ],
            axis=0,
        )

    w_core = core_swap(packed(1 - c))
    w_mine = packed(c)
    x_own = pick(inputs, x)
    rows = x_own.shape[0]
    x_nb = x_swap(pick(inputs, 1 - x))
    pack = x_swap(jnp.concatenate([w_mine, w_core], axis=0))
    x_core = core_swap(x_own)
    count = width // 4
    quarter = lambda w: lax.dynamic_slice_in_dim(w, q * count, count, 0)
    wo_c = core_swap(w_out)
    c_own = pick(cotangent, x)
    ff_src = jnp.stack([quarter(w_up), quarter(w_down)])
    ff_own = jnp.stack([w_up, w_down])
    pack2 = jnp.concatenate([pick(cotangent, 1 - x), w_out, wo_c], axis=0)
    x_nb, ff_src, ff_own, pack2, c_own, meta, x_core, pack = lax.optimization_barrier(
        (x_nb, ff_src, ff_own, pack2, c_own, meta, x_core, pack)
    )
    x_cnb = core_swap(x_nb)
    h1, raw, mix, w_full, taps = qkv_call(meta, x_own, x_nb, x_core, x_cnb, w_mine, w_core, pack, gain1)

    ff_first, pack2 = x_swap(ff_src), x_swap(pack2)
    ff_c = core_swap(ff_own)
    src = after(ff_first, mix)
    ff_n = [swap(src, k, dp) for k in (1, 2, 3)]
    a_mine, a_send, lse = att_fwd_call(meta, after(mix, src, ff_c))
    a_got = core_swap(a_send)
    w_other = core_swap(w_full)
    *ff_n, pack2 = lax.optimization_barrier((*ff_n, pack2, a_mine))[:-1]
    ff_n = [src, *ff_n]
    ff_cn = [core_swap(v) for v in ff_n]
    out_own, out_nb, d_mine, d_send, gg2, dmid, *gw = ffn_call(
        meta, x_own, x_nb, c_own, pack2, a_mine, a_got, after(gain2, w_other),
        (w_out, wo_c, pack2),
        (w_up, w_down, ff_c, *ff_n, *ff_cn),
    )
    d_got = core_swap(d_send)

    _, *rest = strides(dp)
    un, dn, do, uo = [core_swap(gw[k]) for k in (1, 5, 4, 0)]
    nu = total((gw[3], un)).astype(bf16)
    xu = x_swap(nu)
    (dn_send,), dn_keep = halve((gw[7], dn), y, 2)
    (do_send,), do_keep = halve((gw[6], do), y, 2)
    yn, yo = y_swap(dn_send), y_swap(do_send)
    out_x = x_swap(after(out_nb, nu))
    pairs = width // 256
    bwd = lambda m, p, n, into: att_bwd_call(
        meta, m, raw, a_mine, a_send, d_mine, d_got, lse, taps, p, n, into
    )
    *dall, gt_a = bwd(after(mix, nu, dn_send, do_send), 0, pairs - 1, None)
    xu, yn, yo, out_x = lax.optimization_barrier((xu, yn, yo, out_x, gt_a))[:4]
    (u_send,), u_keep = halve((gw[2], uo, xu), y, 2)
    nd = total((dn_keep, yn)).astype(bf16)
    yu, xd = y_swap(u_send), x_swap(nd)
    p_mine, p_theirs, gt_b = bwd(after(mix, u_send, nd), pairs - 1, 1, dall)
    p_got = core_swap(p_theirs)
    gt = jnp.concatenate([gt_a, gt_b], axis=1)
    yu, xd = lax.optimization_barrier((yu, xd, gt_b))[:2]
    sums, sent = scatter([[u_keep, yu], [do_keep, yo, xd]], rest[0], dp)
    keep, far, send = projg_call(meta, after(h1, sent), p_mine, p_theirs)
    flat = lax.optimization_barrier((*sums[0], *sums[1], keep))[:-1]
    sums, sent = scatter([flat[:2], flat[2:]], rest[1], dp)
    got = core_swap(after(send, sent))
    far, far2 = x_swap(far), x_swap(got[part:])
    gi_own, gi_nb, gg1 = last_call(
        meta, x_own, x_nb, p_mine, p_got, w_full, w_other, after(dmid, sent), gain1
    )
    *flat, gt, gg1 = lax.optimization_barrier((*sums[0], *sums[1], gt, x_swap(core_swap(gg1))))
    sums = [flat[:2], flat[2:]]
    for stride in rest[2:]:
        sums, _ = scatter(sums, stride, dp)
    vs = [total(t).astype(bf16) for t in sums]
    far, far2 = lax.optimization_barrier((far, far2, *vs))[:2]
    ga, gb = keep.astype(f32) + far.astype(f32), got[:part].astype(f32) + far2.astype(f32)
    g_send, g_keep = jnp.where(y == 0, gb, ga).astype(bf16), jnp.where(y == 0, ga, gb)
    pt = [g_keep, y_swap(g_send)]
    gi_got = x_swap(after(gi_nb, g_send))
    for stride in reversed(rest[1:]):
        cat = jnp.concatenate(vs, axis=0)
        first_cat = cat if stride == rest[-1] else first_cat
        got_v = swap(cat, stride, dp)
        vs = [join(v, g, stride) for v, g in zip(vs, rows_as(got_v, vs))]
    (pt,), sent = scatter([pt], rest[0], dp)
    packed_vs = jnp.concatenate(vs, axis=0)
    near_got = swap(packed_vs, rest[0], dp)
    across = rows_as(y_swap(packed_vs), vs)
    for stride in rest[1:]:
        (pt,), _ = scatter([pt], stride, dp)
    others, also = rows_as(near_got, vs), rows_as(y_swap(near_got), vs)
    ps = after(total(pt).astype(bf16), near_got)
    for stride in reversed(rest):
        ps = join(ps, swap(ps, stride, dp), stride)
    ps_got = y_swap(ps)
    whole_of = lambda k: join(
        join(vs[k], others[k], rest[0]), join(across[k], also[k], rest[0]), 1
    ).astype(f32)
    grad_up, gd_all = whole_of(0), whole_of(1)
    grad_down, grad_out = gd_all[: w_down.shape[0]], gd_all[w_down.shape[0] :]
    lo, hi = jnp.where(y == c, ps, ps_got), jnp.where(y == c, ps_got, ps)
    third = lambda v, w: v[:, w * half : w * half + half]
    grads = [jnp.concatenate([third(lo, w), third(hi, w)], axis=1).astype(f32) for w in range(3)]

    gt = gt[:9].reshape(9, 2, part).transpose(1, 0, 2)
    gt = jnp.where(jnp.arange(2)[:, None, None, None] == c, gt[None], 0.0).reshape(4, 9, part)
    gains = jnp.concatenate([gg1, gg2], axis=0).reshape(2, 4, part).transpose(1, 0, 2)
    small = jnp.concatenate([gt, gains, jnp.zeros((4, 5, part), f32)], axis=1)
    small = after(small, first_cat)
    small = jnp.broadcast_to(small[:, None], (4, dp, 16, part)).reshape(4 * dp, 16, part)
    small = lax.all_to_all(small.astype(bf16), ("head", "dp"), 0, 0, tiled=True)
    small = jnp.sum(small.astype(f32), axis=0)
    output = order(after(out_own, g_send), out_x)
    grad_input = order(after(gi_own, ps), gi_got)
    return (
        output,
        grad_input,
        *grads,
        grad_out,
        grad_up,
        grad_down,
        small[:9].reshape(3, 3, part),
        small[9],
        small[10],
    )


def solution(mesh):
    placed = (
        P("dp", "head", None),
        P("dp"),
        P("head", None),
        P("head", None),
        P("head", None),
        P("head", None),
        P(None, "head"),
        P("head", None),
        P(None, None, "head"),
        P(),
        P(),
        P("dp", "head", None),
    )
    return jax.shard_map(
        functools.partial(local, mesh.shape["dp"]),
        mesh=mesh,
        in_specs=placed,
        out_specs=(
            P("dp", "head", None),
            P("dp", "head", None),
            P("head", None),
            P("head", None),
            P("head", None),
            P("head", None),
            P(None, "head"),
            P("head", None),
            P(None, None, "head"),
            P("head"),
            P("head"),
        ),
        check_vma=False,
    )
```

```python
import functools

import jax
import jax.numpy as jnp
from jax import lax
from jax.experimental import pallas as pl
from jax.experimental.pallas import tpu as pltpu
from jax.sharding import PartitionSpec as P

HDIM = 64
EPS = 1e-06
bf16 = jnp.bfloat16
f32 = jnp.float32

NN = (((1,), (0,)), ((), ()))
NT = (((1,), (1,)), ((), ()))
TN = (((0,), (0,)), ((), ()))

CORE = [(0, 1), (1, 0), (2, 3), (3, 2)]
XNB = [(0, 2), (2, 0), (1, 3), (3, 1)]


def dot(a, b, dims=NN):
    return lax.dot_general(a, b, dims, preferred_element_type=f32)


def cost(flops, nbytes, trans=0):
    return pl.CostEstimate(flops=int(flops), bytes_accessed=int(nbytes), transcendentals=int(trans))


def sds(shape, dtype):
    return jax.ShapeDtypeStruct(shape, dtype)


def whole(shape):
    zeros = (0,) * len(shape)
    return pl.BlockSpec(shape, lambda *_: zeros, pipeline_mode=pl.Buffered(1))


def grid_spec(grid, ins, outs, scratch=()):
    return pltpu.PrefetchScalarGridSpec(
        num_scalar_prefetch=1, grid=grid, in_specs=ins, out_specs=outs, scratch_shapes=scratch
    )


def length_of(m):
    return m[m[2] // 2]


def x_of(m):
    return m[2] // 2


def core_of(m):
    return lax.rem(m[2], 2)


def slot_of(m, b):
    v = jnp.bitwise_xor(m[2], b)
    return lax.rem(v, 2) * 2 + v // 2


def norm(x, gain):
    inv = lax.rsqrt(jnp.mean(x * x, axis=-1, keepdims=True) + EPS)
    n = x * inv
    return n, inv, (n * gain).astype(bf16)


def qkv_body(meta, x0, x1, x2, x3, wa, wb, pack, gain, h_ref, raw_ref, mix_ref, w_ref, taps, ext):
    b = pl.program_id(0)
    rows = x0.shape[0]
    part = w_ref.shape[0] // 4
    width = x0.shape[1]
    tall = wa.shape[0]
    hd = meta[2]

    @pl.when(b == 0)
    def _():
        def put(k, ref, first):
            at = jnp.bitwise_xor(hd, k) * part
            w_ref[pl.ds(pl.multiple_of(at, 64), part), 0:width] = ref[first : first + part, :]
            for n in range(2):
                row = pl.multiple_of(at + n * (part // 2), 32)
                w_ref[pl.ds(row, part // 2), width:] = ref[
                    first + part : first + part + part // 2, n * (width // 2) : (n + 1) * (width // 2)
                ]

        put(0, wa, 0)
        put(1, wb, 0)
        put(2, pack, 0)
        put(3, pack, tall)
        last = lambda ref, end: ref[end - 16 : end, :].astype(f32)
        near = last(wa, tall) + last(wb, tall)
        far = last(pack, tall) + last(pack, 2 * tall)
        t = jnp.where(x_of(meta) == core_of(meta), near, far)
        taps[...] = jnp.zeros_like(taps)
        taps[0:3, 0:width] = t[0:3]
        taps[0:3, width:] = t[3:6, 0 : width // 2]
        ext[0:8, :] = jnp.zeros((8, ext.shape[1]), f32)

    slot = slot_of(meta, b)
    step = ext.shape[0] - 8

    def some(n, carry):
        sl = pl.ds(pl.multiple_of(n * step, step), step)
        x = x0[sl, :]
        for k, other in ((1, x1), (2, x2), (3, x3)):
            x = jnp.where(slot == k, other[sl, :], x)
        _, _, h = norm(x.astype(f32), gain[...].astype(f32))
        h_ref[sl, :] = h
        raw = dot(h, w_ref[...]).astype(bf16)
        raw_ref[sl, :] = raw
        rawf = raw.astype(f32)
        ext[8:, :] = rawf
        t = taps[...]
        mixed = t[0:1] * rawf + t[1:2] * ext[7 : 7 + step, :] + t[2:3] * ext[6 : 6 + step, :]
        mix_ref[sl, :] = mixed.astype(bf16)
        ext[0:8, :] = ext[step:, :]
        return carry

    lax.fori_loop(0, rows // step, some, 0)


def qkv_call(meta, x_own, x_nb, x_core, x_cnb, w_mine, w_core, pack, gain):
    rows, width = x_own.shape
    tall = w_mine.shape[0]
    cols = width * 3 // 2
    length = 4 * rows
    blk = lambda n: pl.BlockSpec((rows, n), lambda b, m: (b, 0))
    const = lambda r: pl.BlockSpec((r, cols), lambda b, m: (0, 0))
    return pl.pallas_call(
        qkv_body,
        out_shape=[
            sds((length, width), bf16),
            sds((length, cols), bf16),
            sds((length, cols), bf16),
            sds((width, cols), bf16),
            sds((8, cols), f32),
        ],
        grid_spec=grid_spec(
            (4,),
            [whole((rows, width))] * 4
            + [whole((tall, width))] * 2
            + [whole(pack.shape), whole((1, width))],
            [
                pl.BlockSpec((rows, width), lambda b, m: (slot_of(m, b), 0)),
                blk(cols),
                blk(cols),
                const(width),
                const(8),
            ],
            [pltpu.VMEM((T + 8, cols), f32)],
        ),
        cost_estimate=cost(2 * length * width * cols, 2 * length * (width * 2 + cols * 2)),
        name="qkv",
    )(meta, x_own, x_nb, x_core, x_cnb, w_mine, w_core, pack, gain)


def two_heads(v):
    lane = lax.broadcasted_iota(jnp.int32, v.shape, 1)
    z = jnp.zeros_like(v)
    return jnp.concatenate([jnp.where(lane < HDIM, v, z), jnp.where(lane < HDIM, z, v)], axis=0)


def causal(first, keys, start, queries):
    key = first + lax.broadcasted_iota(jnp.int32, (keys, queries), 0)
    ok = key <= start + lax.broadcasted_iota(jnp.int32, (keys, queries), 1)
    return jnp.concatenate([ok, ok], axis=1)


def upper(v, axis):
    B = v.shape[axis] // 2
    h = B // 2
    if axis == 0:
        return jnp.concatenate([v[h:B], v[B + h :]], axis=0)
    return jnp.concatenate([v[:, h:B], v[:, B + h :]], axis=1)


def with_bias(k_ref, ka, length):
    L = k_ref.shape[0]
    ka[:, :128] = k_ref[...]
    lane = lax.broadcasted_iota(jnp.int32, (L, 128), 1)
    row = lax.broadcasted_iota(jnp.int32, (L, 128), 0)
    pad = jnp.logical_and(lane == 0, row >= length)
    ka[:, 128:] = jnp.where(pad, -1e9, 0.0).astype(bf16)


def biased(q):
    qq = two_heads(q)
    lane = lax.broadcasted_iota(jnp.int32, qq.shape, 1)
    return jnp.concatenate([qq, jnp.where(lane == 0, 1.0, 0.0).astype(bf16)], axis=1)


def att_fwd_body(meta, q_ref, k_ref, v_ref, mine_ref, theirs_ref, lse_ref, ka, vt, sc):
    i = pl.program_id(1)
    B = q_ref.shape[0]

    @pl.when(i == 0)
    def _():
        vt[...] = v_ref[...].T
        with_bias(k_ref, ka, length_of(meta))

    qq = biased(q_ref[...] * bf16(HDIM**-0.5))
    own = lax.rem(i, 2) == core_of(meta)

    def run(ii):
        m = None
        for j in range(ii + 1):
            ks = slice(j * B, j * B + B)
            s = dot(ka[ks, :], qq, NT)
            if j == ii:
                s = jnp.where(causal(0, B, 0, B), s, -1e9)
            sc[ks, :] = s
            mj = jnp.max(s, axis=0, keepdims=True)
            m = mj if m is None else jnp.maximum(m, mj)
        l = jnp.zeros((1, 2 * B), f32)
        acc = [jnp.zeros((HDIM, B), f32)] * 2
        for j in range(ii + 1):
            ks = slice(j * B, j * B + B)
            p = jnp.exp(sc[ks, :] - m)
            l = l + jnp.sum(p, axis=0, keepdims=True)
            pb = p.astype(bf16)
            for h in range(2):
                r = slice(HDIM * h, HDIM * h + HDIM)
                acc[h] = acc[h] + dot(vt[r, ks], pb[:, h * B : h * B + B])
        inv = 1.0 / l
        out = jnp.concatenate([acc[h] * inv[:, h * B : h * B + B] for h in range(2)], axis=0)
        out = out.T.astype(bf16)

        @pl.when(own)
        def _():
            mine_ref[...] = out

        @pl.when(jnp.logical_not(own))
        def _():
            theirs_ref[...] = out

        ls = m + jnp.log(l)
        lse_ref[0] = jnp.concatenate([ls[:, :B], ls[:, B:]], axis=0)

    for ii in range(4):
        pl.when(i == ii)(functools.partial(run, ii))


def half_map(p, i, m):
    return (jnp.bitwise_xor(i // 2, x_of(m)), p)


def att_fwd_call(meta, mix):
    length, cols = mix.shape
    width = cols // 3
    pairs = width // 128
    B = length // 4
    half = pl.BlockSpec((B, 128), half_map)
    return pl.pallas_call(
        att_fwd_body,
        out_shape=[
            sds((length // 2, width), bf16),
            sds((length // 2, width), bf16),
            sds((pairs, 2, length), f32),
        ],
        grid_spec=grid_spec(
            (pairs, 4),
            [
                pl.BlockSpec((B, 128), lambda p, i, m: (i, p)),
                pl.BlockSpec((length, 128), lambda p, i, m: (0, pairs + p)),
                pl.BlockSpec((length, 128), lambda p, i, m: (0, 2 * pairs + p)),
            ],
            [half, half, pl.BlockSpec((1, 2, B), lambda p, i, m: (p, 0, i))],
            [
                pltpu.VMEM((length, 256), bf16),
                pltpu.VMEM((128, length), bf16),
                pltpu.VMEM((length, 2 * B), f32),
            ],
        ),
        cost_estimate=cost(8 * length * length * width, 8 * length * width, 2 * length * length * pairs),
        name="attn_fwd",
    )(meta, mix, mix, mix)


def att_bwd_body(
    p0, aliased, meta, q_ref, k_ref, v_ref, om, ot, dm, dt, lse_ref, rq, rk, rv, taps, *refs
):
    gm_ref, gt_ref, gt, ka, kt, dkt, dvt, dqt, dqs, ext, stage, sem = refs[2:] if aliased else refs
    i = pl.program_id(1)
    B = q_ref.shape[0]
    L = k_ref.shape[0]
    H = B // 2

    @pl.when(i == 0)
    def _():
        kt[...] = k_ref[...].T
        with_bias(k_ref, ka, length_of(meta))

    own = lax.rem(i, 2) == core_of(meta)
    q = q_ref[...] * bf16(HDIM**-0.5)
    o = jnp.where(own, om[...], ot[...])
    do = jnp.where(own, dm[...], dt[...])
    qq, dd = biased(q), two_heads(do)
    qt, dot_ = q.T, do.T
    od = (o.astype(f32) * do.astype(f32)).T
    delta = jnp.concatenate(
        [jnp.sum(od[:HDIM], axis=0, keepdims=True), jnp.sum(od[HDIM:], axis=0, keepdims=True)],
        axis=1,
    )
    ls = lse_ref[0]
    lse = jnp.concatenate([ls[0:1], ls[1:2]], axis=1)

    dqt[...] = jnp.zeros_like(dqt)

    def tile(st, n, lo, diagonal):
        w = B - lo
        ks = pl.ds(pl.multiple_of(st, H), n)
        part = upper if lo else lambda v, axis: v
        s = dot(ka[ks, :], part(qq, 0), NT)
        dp = dot(v_ref[ks, :], part(dd, 0), NT)
        p = jnp.exp(s - part(lse, 1))
        if diagonal:
            p = jnp.where(causal(lo, n, lo, w), p, 0.0)
        ds = (p * (dp - part(delta, 1))).astype(bf16)
        pb = p.astype(bf16)
        for h in range(2):
            r, c = slice(HDIM * h, HDIM * h + HDIM), slice(h * w, h * w + w)
            dqt[r, lo:] += dot(kt[r, ks], ds[:, c])
            a = dot(qt[r, lo:], ds[:, c], NT)
            b = dot(dot_[r, lo:], pb[:, c], NT)
            if diagonal:
                dkt[r, ks] = a
                dvt[r, ks] = b
            else:
                dkt[r, ks] += a
                dvt[r, ks] += b

    lax.fori_loop(0, i, lambda j, c: (tile(j * B, B, 0, False), c)[1], 0)
    tile(i * B, H, 0, True)
    tile(i * B + H, H, H, True)
    dqs[pl.ds(pl.multiple_of(i * B, B), B), :] = dqt[...].T * HDIM**-0.5

    def copies(pair):
        width = gm_ref.shape[1] // 3
        for b in range(L // B):
            to = pl.ds(pl.multiple_of(jnp.bitwise_xor(b // 2, x_of(meta)) * B, B), B)
            for k in range(3):
                col = pl.ds(pl.multiple_of(k * width + (p0 + pair) * 128, 128), 128)
                src = stage.at[k, pl.ds(b * B, B), :]
                yield b, lambda g, to=to, col=col, src=src, k=k: pltpu.make_async_copy(
                    src, g.at[to, col], sem.at[k]
                )

    def send(pair):
        for b, copy in copies(pair):
            own = core_of(meta) == b % 2

            @pl.when(own)
            def _(copy=copy):
                copy(gm_ref).start()

            @pl.when(jnp.logical_not(own))
            def _(copy=copy):
                copy(gt_ref).start()

    def finish(pair):
        for _, copy in copies(pair):
            copy(gm_ref).wait()

    @pl.when(i == pl.num_programs(1) - 1)
    def _():
        pair = pl.program_id(0)
        gt[...] = jnp.zeros_like(gt)
        ext[...] = jnp.zeros_like(ext)

        @pl.when(pair > 0)
        def _():
            finish(pair)

        def back(n, carry):
            blk = L // B - 1 - n
            sl = pl.ds(pl.multiple_of(blk * B, B), B)
            for which, raw in enumerate((rq, rk, rv)):
                col = which * (taps.shape[1] // 3) + (p0 + pl.program_id(0)) * 128
                t = taps[:, pl.ds(pl.multiple_of(col, 128), 128)]
                g = dqs[sl, :] if which == 0 else (dkt, dvt)[which - 1][:, sl].T
                ext[which, B : B + 8, :] = ext[which, 0:8, :]
                ext[which, 0:B, :] = g
                g1, g2 = ext[which, 1 : B + 1, :], ext[which, 2 : B + 2, :]
                stage[which, sl, :] = (t[0:1] * g + t[1:2] * g1 + t[2:3] * g2).astype(bf16)
                r = raw[sl, :].astype(f32)
                for k, gg in enumerate((g, g1, g2)):
                    row = slice(3 * which + k, 3 * which + k + 1)
                    gt[row, :] += jnp.sum(r * gg, axis=0, keepdims=True)
            return carry

        lax.fori_loop(0, L // B, back, 0)
        send(pair)

        @pl.when(pair == pl.num_programs(0) - 1)
        def _():
            finish(pair)


def att_bwd_call(meta, mix, raw, om, ot, dm, dt, lse, taps, p0, count, into=None):
    length, cols = mix.shape
    pairs = cols // 384
    B = length // 4
    half = pl.BlockSpec((B, 128), lambda p, i, m: (jnp.bitwise_xor(i // 2, x_of(m)), p0 + p))
    full = lambda k: pl.BlockSpec((length, 128), lambda p, i, m: (0, k * pairs + p0 + p))
    return pl.pallas_call(
        functools.partial(att_bwd_body, p0, into is not None),
        out_shape=[sds((length // 2, cols), bf16)] * 2 + [sds((16, 128 * count), f32)],
        grid_spec=grid_spec(
            (count, 4),
            [
                pl.BlockSpec((B, 128), lambda p, i, m: (i, p0 + p)),
                full(1),
                full(2),
                half,
                half,
                half,
                half,
                pl.BlockSpec((1, 2, B), lambda p, i, m: (p0 + p, 0, i)),
                full(0),
                full(1),
                full(2),
                whole((8, cols)),
            ]
            + ([] if into is None else [pl.BlockSpec(memory_space=pl.ANY)] * 2),
            [pl.BlockSpec(memory_space=pl.ANY)] * 2 + [pl.BlockSpec((16, 128), lambda p, i, m: (0, p))],
            [
                pltpu.VMEM((length, 256), bf16),
                pltpu.VMEM((128, length), bf16),
                pltpu.VMEM((128, length), f32),
                pltpu.VMEM((128, length), f32),
                pltpu.VMEM((128, B), f32),
                pltpu.VMEM((length, 128), f32),
                pltpu.VMEM((3, B + 8, 128), f32),
                pltpu.VMEM((3, length, 128), bf16),
                pltpu.SemaphoreType.DMA((3,)),
            ],
        ),
        cost_estimate=cost(
            14 * length * length * 128 * count, 20 * length * 128 * count, 2 * length * length * count
        ),
        name="attn_bwd",
        input_output_aliases={} if into is None else {13: 0, 14: 1},
    )(meta, mix, mix, mix, om, ot, dm, dt, lse, raw, raw, raw, taps, *(into or ()))


T = 256


def valid_rows(meta, i, rows):
    per = rows // T
    block = jnp.where(i < per, meta[2], jnp.bitwise_xor(meta[2], 2))
    start = block * rows + lax.rem(i, per) * T
    return start + lax.broadcasted_iota(jnp.int32, (T, 1), 0) < length_of(meta)


def ffn_body(
    meta, xo, xx, co, cx, am, at, gain, wo_o, wo_c, pack,
    u_o, d_o, f_c, n0, n1, n2, n3, c0, c1, c2, c3,
    oo, ox, dm, dt, gg, dmid, gu0, gu1, gu2, gu3, gd0, gd1, gd2, gd3,
    wo, wus, wds, mid, h_s, g_s, fo, dh, act, du, stu, std, sto, gacc, sw, so, sg, sd, st,
):
    rows, width = xo.shape
    part = wo_o.shape[0]
    half = 2 * part
    n = 2 * rows // T
    per = rows // T
    copies = []
    for k, src in ((0, wo_o), (1, wo_c), (2, pack.at[pl.ds(rows, part), :]), (3, pack.at[pl.ds(rows + part, part), :])):
        shard = jnp.bitwise_xor(meta[2], k)
        row = jnp.where(shard // 2 == core_of(meta), 0, half) + lax.rem(shard, 2) * part
        cp = pltpu.make_async_copy(src, wo.at[pl.ds(pl.multiple_of(row, 64), part), :], so.at[k])
        cp.start()
        copies.append(cp)
    for k, pair in ((0, (f_c.at[0], f_c.at[1])), (2, (u_o, d_o))):
        for n_, src in enumerate(pair):
            pltpu.make_async_copy(src, (wus, wds)[n_].at[k], sw.at[k, n_]).start()
    for k, quarters in ((1, (c0, c1, c2, c3)), (3, (n0, n1, n2, n3))):
        for q_, src in enumerate(quarters):
            count = src.shape[1]
            to = pl.ds(pl.multiple_of(jnp.bitwise_xor(meta[3], q_) * count, 64), count)
            for n_, dst in enumerate((wus, wds)):
                pltpu.make_async_copy(src.at[n_], dst.at[k, to, :], sw.at[k, n_]).start()
    for cp in copies:
        cp.wait()
    gn = gain[...].astype(f32)

    def first_rows(i, carry):
        sl = pl.ds(pl.multiple_of(i * T, T), T)
        src = pl.ds(pl.multiple_of(lax.rem(i, per) * T, T), T)
        own = i < per
        x = jnp.where(own, xo[src, :], xx[src, :]).astype(f32)
        a = jnp.concatenate([am[sl, :], at[sl, :]], axis=1)
        m = x + dot(a, wo[...])
        mid[sl, :] = m
        fo[sl, :] = m
        h_s[sl, :] = norm(m, gn)[2]
        ct = jnp.where(own, co[src, :], cx[src, :])
        g_s[sl, :] = jnp.where(valid_rows(meta, i, rows), ct, jnp.zeros_like(ct))
        dh[sl, :] = jnp.zeros((T, width), f32)
        return carry

    lax.fori_loop(0, n, first_rows, 0)

    R = 512
    C = 768

    gus, gds = (gu0, gu1, gu2, gu3), (gd0, gd1, gd2, gd3)

    def stores(n_, slot):
        return [
            pltpu.make_async_copy(stu.at[slot], gus[n_], sg.at[slot, 0]),
            pltpu.make_async_copy(std.at[slot], gds[n_].at[pl.ds(0, width), :], sg.at[slot, 1]),
        ]

    def shard(k, carry):
        for cp in (
            pltpu.make_async_copy(u_o, wus.at[k], sw.at[k, 0]),
            pltpu.make_async_copy(d_o, wds.at[k], sw.at[k, 1]),
        ):
            cp.wait()

        def rows_step(t, c2):
            sl = pl.ds(pl.multiple_of(t * R, R), R)
            h, g = h_s[sl, :], g_s[sl, :]
            r = jnp.maximum(dot(h, wus[k]), 0.0)
            a = (r * r).astype(bf16)
            d = (dot(g, wds[k], NT) * 2.0 * r).astype(bf16)
            act[sl, :] = a
            du[sl, :] = d
            fo[sl, :] += dot(a, wds[k])
            dh[sl, :] += dot(d, wus[k], NT)
            return c2

        lax.fori_loop(0, 2 * rows // R, rows_step, 0)
        slot = lax.rem(k, 2)

        @pl.when(k >= 2)
        def _():
            for cp in stores(0, slot):
                cp.wait()

        def cols_step(t, c2):
            sl = pl.ds(pl.multiple_of(t * C, C), C)
            stu[slot, :, sl] = dot(h_s[...], du[:, sl], TN).astype(bf16)
            std[slot, sl, :] = dot(act[:, sl], g_s[...], TN).astype(bf16)
            return c2

        lax.fori_loop(0, width // C, cols_step, 0)
        for n_ in range(4):

            @pl.when(k == n_)
            def _(n_=n_):
                for cp in stores(n_, n_ % 2):
                    cp.start()

        return carry

    lax.fori_loop(0, 4, shard, 0)
    gg[...] = jnp.zeros_like(gg)

    def last_rows(i, carry):
        sl = pl.ds(pl.multiple_of(i * T, T), T)
        dst = pl.ds(pl.multiple_of(lax.rem(i, per) * T, T), T)
        ok = valid_rows(meta, i, rows)
        m = mid[sl, :]
        out = jnp.where(ok, fo[sl, :], 0.0)

        fo[sl, :] = out

        @pl.when(i < per)
        def _():
            own = oo.at[meta[2] // 2, dst, :]
            pltpu.make_async_copy(fo.at[sl, :], own, sd.at[1]).start()

        @pl.when(i >= per)
        def _():
            ox[dst, :] = out.astype(bf16)

        nm, inv, _ = norm(m, gn)
        d = dh[sl, :]
        dn = d * gn
        r = g_s[sl, :].astype(f32) + inv * (dn - nm * jnp.mean(dn * nm, axis=-1, keepdims=True))
        mid[sl, :] = r
        pltpu.make_async_copy(mid.at[sl, :], dmid.at[sl, :], sd.at[0]).start()
        db = r.astype(bf16)
        du[sl, :] = db
        da = dot(db, wo[...], NT).astype(bf16)
        dm[sl, :] = da[:, :half]
        dt[sl, :] = da[:, half:]
        gg[...] += jnp.sum(d * nm, axis=0, keepdims=True)
        return carry

    lax.fori_loop(0, n, last_rows, 0)
    gacc[0:half, :] = dot(am[...], du[...], TN)
    gacc[half:, :] = dot(at[...], du[...], TN)
    outs = [
        pltpu.make_async_copy(mid, dmid, sd.at[0]),
        pltpu.make_async_copy(fo.at[pl.ds(0, rows), :], oo.at[meta[2] // 2], sd.at[1]),
    ]
    for k, k_ in enumerate((1, 3, 0, 2)):
        shard_ = jnp.bitwise_xor(meta[2], k_)
        row = jnp.where(shard_ // 2 == core_of(meta), 0, half) + lax.rem(shard_, 2) * part
        sto[k] = gacc[pl.ds(pl.multiple_of(row, 64), part), :].astype(bf16)
        cp = pltpu.make_async_copy(sto.at[k], gds[k].at[pl.ds(width, part), :], st.at[k])
        cp.start()
        outs.append(cp)
    for slot in range(2):
        outs.extend(stores(2 + slot, slot))
    for cp in outs:
        cp.wait()


def ffn_call(meta, xo, xx, co, cx, am, at, gain, wos, ffs):
    rows, width = xo.shape
    half = am.shape[1]
    part = half // 2
    hid = ffs[0].shape[1]
    hbm = pl.BlockSpec(memory_space=pl.ANY)
    vm = lambda *shape: whole(shape)
    all_rows = 2 * rows
    return pl.pallas_call(
        ffn_body,
        out_shape=[
            sds((2, rows, width), f32),
            sds((rows, width), bf16),
            sds((all_rows, half), bf16),
            sds((all_rows, half), bf16),
            sds((1, width), f32),
            sds((all_rows, width), f32),
        ]
        + [sds((width, hid), bf16)] * 4
        + [sds((hid + part, width), bf16)] * 4,
        grid_spec=grid_spec(
            (1,),
            [vm(rows, width)] * 4 + [vm(all_rows, half)] * 2 + [vm(1, width)] + [hbm] * 14,
            [
                hbm,
                vm(rows, width),
                vm(all_rows, half),
                vm(all_rows, half),
                vm(1, width),
            ]
            + [hbm] * 9,
            [
                pltpu.VMEM((width, width), bf16),
                pltpu.VMEM((4, width, hid), bf16),
                pltpu.VMEM((4, hid, width), bf16),
                pltpu.VMEM((all_rows, width), f32),
                pltpu.VMEM((all_rows, width), bf16),
                pltpu.VMEM((all_rows, width), bf16),
                pltpu.VMEM((all_rows, width), f32),
                pltpu.VMEM((all_rows, width), f32),
                pltpu.VMEM((all_rows, hid), bf16),
                pltpu.VMEM((all_rows, hid), bf16),
                pltpu.VMEM((2, width, hid), bf16),
                pltpu.VMEM((2, hid, width), bf16),
                pltpu.VMEM((4, part, width), bf16),
                pltpu.VMEM((width, width), f32),
                pltpu.SemaphoreType.DMA((4, 2)),
                pltpu.SemaphoreType.DMA((4,)),
                pltpu.SemaphoreType.DMA((2, 2)),
                pltpu.SemaphoreType.DMA((2,)),
                pltpu.SemaphoreType.DMA((4,)),
            ],
        ),
        cost_estimate=cost(
            48 * all_rows * width * hid + 6 * all_rows * width * width, 40 * all_rows * width
        ),
        compiler_params=pltpu.CompilerParams(vmem_limit_bytes=62 * 2**20),
        name="ffn",
    )(meta, xo, xx, co, cx, am, at, gain, *wos, *ffs)


def projg_body(meta, h, dm, dt, keep, far, send, acc):
    rows = dm.shape[0]
    acc[...] = dot(h[0:rows, :], dm[...], TN) + dot(h[rows:, :], dt[...], TN)
    part = keep.shape[0]
    for ref, k, row in ((keep, 0, 0), (far, 2, 0), (send, 1, 0), (send, 3, part)):
        at = jnp.bitwise_xor(meta[2], k)
        ref[row : row + part, :] = acc[pl.ds(pl.multiple_of(at * part, 64), part), :].astype(bf16)


def projg_call(meta, h, dm, dt):
    length, width = h.shape
    cols = dm.shape[1]
    step = cols // 3
    d = pl.BlockSpec((length // 2, step), lambda j, m: (0, j))
    g = lambda rows: pl.BlockSpec((rows, step), lambda j, m: (0, j))
    part = width // 4
    return pl.pallas_call(
        projg_body,
        out_shape=[sds((rows, cols), bf16) for rows in (part, part, 2 * part)],
        grid_spec=grid_spec(
            (3,),
            [whole((length, width)), d, d],
            [g(part), g(part), g(2 * part)],
            [pltpu.VMEM((width, step), f32)],
        ),
        cost_estimate=cost(length, length),
        name="projg",
    )(meta, h, dm, dt)


def last_body(meta, xo, xx, dm, dt, wm, wt, dmid, gain, go, gx, gg):
    i = pl.program_id(0)
    per = pl.num_programs(0) // 2
    first = i < per
    x = jnp.where(first, xo[...], xx[...]).astype(f32)
    gn = gain[...].astype(f32)
    n, inv, _ = norm(x, gn)
    dh = dot(dm[...], wm[...], NT) + dot(dt[...], wt[...], NT)
    dn = dh * gn
    out = dmid[...] + inv * (dn - n * jnp.mean(dn * n, axis=-1, keepdims=True))

    @pl.when(first)
    def _():
        go[0] = out

    @pl.when(jnp.logical_not(first))
    def _():
        gx[...] = out.astype(bf16)

    ps = jnp.sum(dh * n, axis=0, keepdims=True)

    @pl.when(i == 0)
    def _():
        gg[...] = ps

    @pl.when(i > 0)
    def _():
        gg[...] += ps


def own_map(per):
    return lambda i, m: (jnp.minimum(i, per - 1), 0)


def nb_map(per):
    return lambda i, m: (jnp.maximum(i - per, 0), 0)


def last_call(meta, xo, xx, dm, dt, wm, wt, dmid, gain):
    rows, width = xo.shape
    cols = dm.shape[1]
    per = rows // T
    fst, snd = pl.BlockSpec((T, width), own_map(per)), pl.BlockSpec((T, width), nb_map(per))
    blk = lambda n: pl.BlockSpec((T, n), lambda i, m: (i, 0))
    return pl.pallas_call(
        last_body,
        out_shape=[sds((2, rows, width), f32), sds((rows, width), bf16), sds((1, width), f32)],
        grid_spec=grid_spec(
            (2 * per,),
            [fst, snd, blk(cols), blk(cols)]
            + [whole((width, cols))] * 2
            + [blk(width), whole((1, width))],
            [
                pl.BlockSpec((1, T, width), lambda i, m: (x_of(m), jnp.minimum(i, per - 1), 0)),
                snd,
                pl.BlockSpec((1, width), lambda i, m: (0, 0)),
            ],
        ),
        cost_estimate=cost(rows, rows),
        name="last",
    )(meta, xo, xx, dm, dt, wm, wt, dmid, gain)


def flip(size, bit):
    return [(i, i ^ bit) for i in range(size)]


def core_swap(v):
    return lax.ppermute(v, "head", CORE)


def x_swap(v):
    return lax.ppermute(v, "head", XNB)


def after(v, *deps):
    return lax.optimization_barrier((v, *deps))[0]


def halve(terms, index, count):
    rows = terms[0].shape[0] // count
    piece = lambda t, k: lax.dynamic_slice_in_dim(t, jnp.bitwise_xor(index, k) * rows, rows, 0)
    total = lambda k: sum(piece(t, k).astype(f32) for t in terms)
    return [total(k).astype(bf16) for k in range(1, count)], total(0)


def strides(dp):
    out = [1]
    while 2 * out[-1] < dp:
        out.append(2 * out[-1])
    return out


def side(stride):
    return lax.axis_index("dp") // stride % 2


def swap(v, stride, dp):
    return lax.ppermute(v, "dp", flip(dp, stride))


def rows_as(got, vs):
    out, row = [], 0
    for v in vs:
        out.append(got[row : row + v.shape[0]])
        row += v.shape[0]
    return out


def swap_both(vs, stride, dp):
    return rows_as(swap(jnp.concatenate(vs, axis=0), stride, dp), vs)


def scatter(sums, stride, dp):
    halves = [halve(terms, side(stride), 2) for terms in sums]
    send = jnp.concatenate([h[0][0] for h in halves], axis=0)
    got = swap(send, stride, dp)
    out, row = [], 0
    for (part,), keep in halves:
        out.append([keep, got[row : row + part.shape[0]]])
        row += part.shape[0]
    return out, send


def join(mine, got, stride):
    upper = side(stride) == 1
    return jnp.concatenate([jnp.where(upper, got, mine), jnp.where(upper, mine, got)], axis=0)


def total(terms):
    return sum(t.astype(f32) for t in terms)


def local(dp, inputs, lengths, w_query, w_key, w_value, w_out, w_up, w_down, conv_taps, gain_attn, gain_ff, cotangent):
    hd = lax.axis_index("head")
    x, c, y = hd // 2, hd % 2, lax.axis_index("dp") % 2
    q = lax.axis_index("dp") % 4
    width = inputs.shape[2]
    part = w_query.shape[0]
    half = 2 * part
    pick = lambda v, k: lax.dynamic_index_in_dim(v, k, 0, keepdims=False)
    y_swap = lambda v: lax.ppermute(v, "dp", flip(dp, 1))
    order = lambda own, nb: lax.dynamic_update_slice_in_dim(own, nb[None].astype(f32), 1 - x, 0)
    meta = jnp.concatenate([lengths, jnp.stack([hd, q])]).astype(jnp.int32)
    gain1, gain2 = gain_attn.reshape(1, width), gain_ff.reshape(1, width)

    mask = (jnp.arange(2) == c)[None, None, :, None]
    tap_rows = jnp.where(mask, conv_taps.transpose(1, 0, 2)[:, :, None, :], 0).reshape(3, 3 * half)
    tap_rows = jnp.concatenate([tap_rows[:, :width], jnp.pad(tap_rows[:, width:], ((0, 0), (0, half)))], axis=0)
    tap_rows = jnp.pad(tap_rows, ((0, 10), (0, 0)))

    def packed(k):
        cut = lambda w: lax.dynamic_slice_in_dim(w, k * half, half, 1)
        fold = cut(w_value)
        return jnp.concatenate(
            [
                jnp.concatenate([cut(w_query), cut(w_key)], axis=1),
                jnp.concatenate([fold[: part // 2], fold[part // 2 :]], axis=1),
                tap_rows,
            ],
            axis=0,
        )

    w_core = core_swap(packed(1 - c))
    w_mine = packed(c)
    x_own = pick(inputs, x)
    rows = x_own.shape[0]
    x_nb = x_swap(pick(inputs, 1 - x))
    pack = x_swap(jnp.concatenate([w_mine, w_core], axis=0))
    x_core = core_swap(x_own)
    count = width // 4
    quarter = lambda w: lax.dynamic_slice_in_dim(w, q * count, count, 0)
    wo_c = core_swap(w_out)
    c_own = pick(cotangent, x)
    ff_src = jnp.stack([quarter(w_up), quarter(w_down)])
    ff_own = jnp.stack([w_up, w_down])
    pack2 = jnp.concatenate([pick(cotangent, 1 - x), w_out, wo_c], axis=0)
    x_nb, ff_src, ff_own, pack2, c_own, meta, x_core, pack = lax.optimization_barrier(
        (x_nb, ff_src, ff_own, pack2, c_own, meta, x_core, pack)
    )
    x_cnb = core_swap(x_nb)
    h1, raw, mix, w_full, taps = qkv_call(meta, x_own, x_nb, x_core, x_cnb, w_mine, w_core, pack, gain1)

    ff_first, pack2 = x_swap(ff_src), x_swap(pack2)
    ff_c = core_swap(ff_own)
    src = after(ff_first, mix)
    ff_n = [swap(src, k, dp) for k in (1, 2, 3)]
    a_mine, a_send, lse = att_fwd_call(meta, after(mix, src, ff_c))
    a_got = core_swap(a_send)
    w_other = core_swap(w_full)
    *ff_n, pack2 = lax.optimization_barrier((*ff_n, pack2, a_mine))[:-1]
    ff_n = [src, *ff_n]
    ff_cn = [core_swap(v) for v in ff_n]
    out_own, out_nb, d_mine, d_send, gg2, dmid, *gw = ffn_call(
        meta, x_own, x_nb, c_own, pack2, a_mine, a_got, after(gain2, w_other),
        (w_out, wo_c, pack2),
        (w_up, w_down, ff_c, *ff_n, *ff_cn),
    )
    d_got = core_swap(d_send)

    _, *rest = strides(dp)
    un, dn, do, uo = [core_swap(gw[k]) for k in (1, 5, 4, 0)]
    nu = total((gw[3], un)).astype(bf16)
    xu = x_swap(nu)
    (dn_send,), dn_keep = halve((gw[7], dn), y, 2)
    (do_send,), do_keep = halve((gw[6], do), y, 2)
    yn, yo = y_swap(dn_send), y_swap(do_send)
    out_x = x_swap(after(out_nb, nu))
    pairs = width // 256
    bwd = lambda m, p, n, into: att_bwd_call(
        meta, m, raw, a_mine, a_send, d_mine, d_got, lse, taps, p, n, into
    )
    *dall, gt_a = bwd(after(mix, nu, dn_send, do_send), 0, pairs - 1, None)
    xu, yn, yo, out_x = lax.optimization_barrier((xu, yn, yo, out_x, gt_a))[:4]
    (u_send,), u_keep = halve((gw[2], uo, xu), y, 2)
    nd = total((dn_keep, yn)).astype(bf16)
    yu, xd = y_swap(u_send), x_swap(nd)
    p_mine, p_theirs, gt_b = bwd(after(mix, u_send, nd), pairs - 1, 1, dall)
    p_got = core_swap(p_theirs)
    gt = jnp.concatenate([gt_a, gt_b], axis=1)
    yu, xd = lax.optimization_barrier((yu, xd, gt_b))[:2]
    sums, sent = scatter([[u_keep, yu], [do_keep, yo, xd]], rest[0], dp)
    keep, far, send = projg_call(meta, after(h1, sent), p_mine, p_theirs)
    flat = lax.optimization_barrier((*sums[0], *sums[1], keep))[:-1]
    sums, sent = scatter([flat[:2], flat[2:]], rest[1], dp)
    got = core_swap(after(send, sent))
    far, far2 = x_swap(far), x_swap(got[part:])
    gi_own, gi_nb, gg1 = last_call(
        meta, x_own, x_nb, p_mine, p_got, w_full, w_other, after(dmid, sent), gain1
    )
    *flat, gt, gg1 = lax.optimization_barrier((*sums[0], *sums[1], gt, x_swap(core_swap(gg1))))
    sums = [flat[:2], flat[2:]]
    for stride in rest[2:]:
        sums, _ = scatter(sums, stride, dp)
    vs = [total(t).astype(bf16) for t in sums]
    far, far2 = lax.optimization_barrier((far, far2, *vs))[:2]
    ga, gb = keep.astype(f32) + far.astype(f32), got[:part].astype(f32) + far2.astype(f32)
    g_send, g_keep = jnp.where(y == 0, gb, ga).astype(bf16), jnp.where(y == 0, ga, gb)
    pt = [g_keep, y_swap(g_send)]
    gi_got = x_swap(after(gi_nb, g_send))
    for stride in reversed(rest[1:]):
        cat = jnp.concatenate(vs, axis=0)
        first_cat = cat if stride == rest[-1] else first_cat
        got_v = swap(cat, stride, dp)
        vs = [join(v, g, stride) for v, g in zip(vs, rows_as(got_v, vs))]
    (pt,), sent = scatter([pt], rest[0], dp)
    packed_vs = jnp.concatenate(vs, axis=0)
    near_got = swap(packed_vs, rest[0], dp)
    across = rows_as(y_swap(packed_vs), vs)
    for stride in rest[1:]:
        (pt,), _ = scatter([pt], stride, dp)
    others, also = rows_as(near_got, vs), rows_as(y_swap(near_got), vs)
    ps = after(total(pt).astype(bf16), near_got)
    for stride in reversed(rest):
        ps = join(ps, swap(ps, stride, dp), stride)
    ps_got = y_swap(ps)
    whole_of = lambda k: join(
        join(vs[k], others[k], rest[0]), join(across[k], also[k], rest[0]), 1
    ).astype(f32)
    grad_up, gd_all = whole_of(0), whole_of(1)
    grad_down, grad_out = gd_all[: w_down.shape[0]], gd_all[w_down.shape[0] :]
    lo, hi = jnp.where(y == c, ps, ps_got), jnp.where(y == c, ps_got, ps)
    third = lambda v, w: v[:, w * half : w * half + half]
    grads = [jnp.concatenate([third(lo, w), third(hi, w)], axis=1).astype(f32) for w in range(3)]

    gt = gt[:9].reshape(9, 2, part).transpose(1, 0, 2)
    gt = jnp.where(jnp.arange(2)[:, None, None, None] == c, gt[None], 0.0).reshape(4, 9, part)
    gains = jnp.concatenate([gg1, gg2], axis=0).reshape(2, 4, part).transpose(1, 0, 2)
    small = jnp.concatenate([gt, gains, jnp.zeros((4, 5, part), f32)], axis=1)
    small = after(small, first_cat)
    small = jnp.broadcast_to(small[:, None], (4, dp, 16, part)).reshape(4 * dp, 16, part)
    small = lax.all_to_all(small.astype(bf16).reshape(4 * dp, 8, 2 * part), ("head", "dp"), 0, 0, tiled=True)
    small = small.reshape(4 * dp, 16, part)
    small = jnp.sum(small.astype(f32), axis=0)
    output = order(after(out_own, g_send), out_x)
    grad_input = order(after(gi_own, ps), gi_got)
    return (
        output,
        grad_input,
        *grads,
        grad_out,
        grad_up,
        grad_down,
        small[:9].reshape(3, 3, part),
        small[9],
        small[10],
    )


def solution(mesh):
    placed = (
        P("dp", "head", None),
        P("dp"),
        P("head", None),
        P("head", None),
        P("head", None),
        P("head", None),
        P(None, "head"),
        P("head", None),
        P(None, None, "head"),
        P(),
        P(),
        P("dp", "head", None),
    )
    return jax.shard_map(
        functools.partial(local, mesh.shape["dp"]),
        mesh=mesh,
        in_specs=placed,
        out_specs=(
            P("dp", "head", None),
            P("dp", "head", None),
            P("head", None),
            P("head", None),
            P("head", None),
            P("head", None),
            P(None, "head"),
            P("head", None),
            P(None, None, "head"),
            P("head"),
            P("head"),
        ),
        check_vma=False,
    )
```
